32 devices in a mesh: wide: 4 (over x, core), narrow: 8 (over z, y).
Axes of the slice: x: 2, y: 2, z: 4, core: 2. Of those that a mesh axis runs over, the one named last changes fastest.
Arguments:
- tokens: bfloat16 [32768, 768], P(('wide', 'narrow')), may hold values from -60 to 60
- cotangent: bfloat16 [32768, 768], P(('wide', 'narrow')), may hold values from -8 to 8
- segment_ids: int32 [32768], P(('wide', 'narrow')), may hold values from 0 to 14, as said below
- pad_mask: int32 [32768], P(('wide', 'narrow')), may hold values from 0 to 1, as said below
- lengths: int32 [32], P(('wide', 'narrow')), may hold values from 706 to 966, as said below
- params: float32 [55424, 128], P(('wide', 'narrow')), may hold values from -10 to 10
Outputs:
- output: bfloat16 [32768, 768], P(('wide', 'narrow'))
- grad_input: float32 [32768, 768], P(('wide', 'narrow'))
- grad_params: float32 [55424, 128], P(('wide', 'narrow'))
The draws below stay inside these ranges and needn't reach their ends.
Inputs may be any that keep to these rules, and one draw needn't show every extreme that they name: `segment_ids`: within each sequence of 1024 slots the numbers start at 0 and never fall. An image is one class token, 4 registers and h * w patches with h and w from 8 to 16; images are packed in order while they fit in 1024 - 1024 % (69) slots, and slots past the length carry the number after the last image. The first sequence holds only images of 8 x 8 patches. `pad_mask`: 1 exactly at the positions below its sequence's length. `lengths`: A sequence's length is the number of tokens of its images.
All inputs are finite; a program needn't handle non-finite values.
Results may differ from the reference program's by a relative error of at most 0.0097.
Values may be sent and summed in bfloat16 or wider, within the bound.
No kernel may reach another device: no remote copies, remote signals or barrier semaphores. Data moves between devices by JAX's collectives and lax.ppermute only.
A program may use at most 256 MiB of HBM per device.

```python
import math
import jax
import jax.numpy as jnp
from jax import lax

D = 768
FF = 3072
HEADS = 12
REGISTERS = 4
SIDE_LO = 8
SIDE_HI = 16
LEN = 1024
SEQS = 32
TOKENS = 32768
ATT_COUNT = 2363904
MLP_COUNT = 4724736
ATT_ROWS = 578
MLP_ROWS = 1154
PROWS = 55424
N_WIDE = 4
N_NARROW = 8


def packing(key):
    smallest = 1 + REGISTERS + SIDE_LO * SIDE_LO
    capacity = LEN - LEN % smallest
    images = LEN // smallest + 1
    patch_sides = jax.random.randint(jax.random.fold_in(key, 17), (SEQS, images, 2), SIDE_LO, SIDE_HI + 1)
    first_row = jnp.arange(SEQS, dtype=jnp.int32)[:, None, None] == 0
    patch_sides = jnp.where(first_row, SIDE_LO, patch_sides).astype(jnp.int32)
    image_tokens = 1 + REGISTERS + patch_sides[..., 0] * patch_sides[..., 1]
    image_ends = jnp.cumsum(image_tokens, axis=1)
    image_fits = image_ends <= capacity
    sequence_lengths = jnp.max(jnp.where(image_fits, image_ends, 0), axis=1).astype(jnp.int32)
    positions = jnp.arange(LEN, dtype=jnp.int32)
    before = (image_ends[:, None, :] <= positions[None, :, None]) & image_fits[:, None, :]
    segment_numbers = jnp.sum(before.astype(jnp.int32), axis=2).astype(jnp.int32)
    real_slots = (positions[None, :] < sequence_lengths[:, None]).astype(jnp.int32)
    return (segment_numbers.reshape(-1), real_slots.reshape(-1), sequence_lengths)


def draw_segment_ids(key, part):
    return packing(key)[0]


def draw_pad_mask(key, part):
    return packing(key)[1]


def draw_lengths(key, part):
    return packing(key)[2]


def draw_tokens(key, part):
    noise_key = jax.random.fold_in(key, 1)
    column_key = jax.random.fold_in(key, 2)
    row_key = jax.random.fold_in(key, 3)
    columns = jnp.exp(jax.random.uniform(column_key, (1, D), jnp.float32, -1.15, 1.15))
    base_values = jax.random.normal(noise_key, (TOKENS, D), jnp.float32)
    row_scale = jnp.exp(jax.random.uniform(row_key, (TOKENS, 1), jnp.float32, -0.693, 0.693))
    return (base_values * columns * row_scale).astype(jnp.bfloat16)


def draw_cotangent(key, part):
    noise_key = jax.random.fold_in(key, 31)
    base_values = jnp.clip(jax.random.normal(noise_key, (TOKENS, D), jnp.float32), -6.0, 6.0)
    return base_values.astype(jnp.bfloat16)


def draw_params(key, part):
    devices = N_WIDE * N_NARROW

    def random_part(number, amount):
        sub_key = jax.random.fold_in(key, number)
        return jax.random.normal(sub_key, (amount,), jnp.float32)
    model_width = D
    attention = jnp.concatenate([1.0 + 0.15 * random_part(1, model_width), 0.3 * random_part(2, model_width), random_part(3, 3 * model_width * model_width) * model_width ** (-0.5), 0.3 * random_part(4, model_width), 0.3 * random_part(5, model_width), 4.0 * model_width ** (-0.5) * random_part(6, model_width * model_width), 0.3 * random_part(7, model_width), jnp.exp(0.35 * random_part(8, model_width)), random_part(9, devices * ATT_ROWS * 128 - ATT_COUNT)])
    feedforward = jnp.concatenate([1.0 + 0.15 * random_part(11, model_width), 0.3 * random_part(12, model_width), random_part(13, model_width * FF) * model_width ** (-0.5), 0.3 * random_part(14, FF), 1.5 * FF ** (-0.5) * random_part(15, FF * model_width), 0.3 * random_part(16, model_width), jnp.exp(0.35 * random_part(17, model_width)), random_part(18, devices * MLP_ROWS * 128 - MLP_COUNT)])
    layout = jnp.concatenate([attention.reshape(devices, ATT_ROWS, 128), feedforward.reshape(devices, MLP_ROWS, 128)], axis=1)
    return layout.reshape(PROWS, 128)


def setup_inputs(seed: int = 0) -> dict:
    streams_of = jax.random.split(jax.random.key(seed), 7)
    return {
        "tokens": draw_tokens(jax.random.fold_in(streams_of[6], 71), 0),
        "cotangent": draw_cotangent(jax.random.fold_in(streams_of[6], 71), 0),
        "segment_ids": draw_segment_ids(jax.random.fold_in(streams_of[6], 71), 0),
        "pad_mask": draw_pad_mask(jax.random.fold_in(streams_of[6], 71), 0),
        "lengths": draw_lengths(jax.random.fold_in(streams_of[6], 71), 0),
        "params": draw_params(jax.random.fold_in(streams_of[6], 71), 0),
    }


HIGH = lax.Precision.HIGHEST
EPSILON = 1e-06
NEGATIVE = -1e+30

@jax.custom_vjp
def low(v):
    return lax.optimization_barrier(v.astype(jnp.bfloat16)).astype(jnp.float32)

@jax.custom_vjp
def low_back(v):
    return v

def low_keep(v):
    return (low(v), None)

def low_pass(kept, grad):
    return (grad,)

def back_keep(v):
    return (v, None)

def back_low(kept, grad):
    return (low(grad),)
low.defvjp(low_keep, low_pass)
low_back.defvjp(back_keep, back_low)

def layer_norm(values, norm_gain, norm_shift):
    center = values - lax.optimization_barrier(jnp.mean(values, axis=-1, keepdims=True))
    spread = lax.optimization_barrier(jnp.mean(center * center, axis=-1, keepdims=True))
    return center * lax.rsqrt(spread + EPSILON) * norm_gain + norm_shift

def split_vector(vector, amounts):
    pieces = []
    offset = 0
    for amount in amounts:
        pieces.append(vector[offset:offset + amount])
        offset = offset + amount
    return pieces

def forward(inputs, attention_vector, feedforward_vector, segments, validity):
    groups = inputs.shape[0]
    head_dim = D // HEADS
    score_scale = head_dim ** (-0.5)
    first_gain, first_shift, triple_weight, query_bias, value_bias, output_weight, output_bias, first_scale = split_vector(low(attention_vector), [D, D, 3 * D * D, D, D, D * D, D, D])
    second_gain, second_shift, expand_weight, expand_bias, contract_weight, contract_bias, second_scale = split_vector(low(feedforward_vector), [D, D, D * FF, FF, FF * D, D, D])
    normed_one = low(layer_norm(inputs, first_gain, first_shift))
    bias_row = jnp.concatenate([query_bias, jnp.zeros((D,), jnp.float32), value_bias])
    triple = jnp.einsum('gld,de->gle', normed_one, triple_weight.reshape(D, 3 * D), precision=HIGH) + bias_row
    triple = low(low_back(triple))
    query_part = triple[..., :D].reshape(groups, LEN, HEADS, head_dim)
    key_part = triple[..., D:2 * D].reshape(groups, LEN, HEADS, head_dim)
    value_part = triple[..., 2 * D:].reshape(groups, LEN, HEADS, head_dim)
    scores = low_back(jnp.einsum('gqhe,gkhe->ghqk', query_part, key_part, precision=HIGH) * score_scale)
    same_image = (segments[:, :, None] == segments[:, None, :]) & (validity[:, None, :] > 0)
    allowed = same_image | jnp.eye(LEN, dtype=bool)[None]
    scores = jnp.where(allowed[:, None], scores, NEGATIVE)
    softmax_probs = low(jax.nn.softmax(scores, axis=-1))
    mixed_heads = jnp.einsum('ghqk,gkhe->gqhe', softmax_probs, value_part, precision=HIGH).reshape(groups, LEN, D)
    mixed_heads = low(low_back(mixed_heads))
    branch = low_back(jnp.einsum('gld,de->gle', mixed_heads, output_weight.reshape(D, D), precision=HIGH) + output_bias)
    middle = inputs + first_scale * branch
    normed_two = low(layer_norm(middle, second_gain, second_shift))
    expanded = low_back(jnp.einsum('gld,df->glf', normed_two, expand_weight.reshape(D, FF), precision=HIGH) + expand_bias)
    activated = low(jax.nn.gelu(expanded, approximate=False))
    contracted = low_back(jnp.einsum('glf,fd->gld', activated, contract_weight.reshape(FF, D), precision=HIGH) + contract_bias)
    return middle + second_scale * contracted

def reference(tokens, cotangent, segment_ids, pad_mask, lengths, params):
    devices = N_WIDE * N_NARROW
    sequence_count = lengths.shape[0]
    per_group = math.gcd(sequence_count, max(1, 4096 // LEN))
    group_count = sequence_count // per_group
    layout = params.reshape(devices, ATT_ROWS + MLP_ROWS, 128)
    attention_vector = layout[:, :ATT_ROWS].reshape(-1)[:ATT_COUNT]
    feedforward_vector = layout[:, ATT_ROWS:].reshape(-1)[:MLP_COUNT]
    positions = jnp.arange(LEN, dtype=jnp.int32)
    validity = ((pad_mask.reshape(sequence_count, LEN) > 0) & (positions[None, :] < lengths[:, None])).astype(jnp.int32)
    inputs = tokens.astype(jnp.float32).reshape(group_count, per_group, LEN, D)
    upstream = cotangent.astype(jnp.float32).reshape(group_count, per_group, LEN, D)
    segments = segment_ids.reshape(group_count, per_group, LEN)
    validity = validity.reshape(group_count, per_group, LEN)

    def group_step(carry, pieces):
        inputs_group, upstream_group, segment_group, valid_group = pieces

        def apply_layer(values, attention_part, feedforward_part):
            return forward(values, attention_part, feedforward_part, segment_group, valid_group)
        result, pullback = jax.vjp(apply_layer, inputs_group, attention_vector, feedforward_vector)
        grad_inputs, grad_attention, grad_feedforward = pullback(upstream_group)
        return ((carry[0] + grad_attention, carry[1] + grad_feedforward), (result.astype(jnp.bfloat16), grad_inputs))
    initial = (jnp.zeros((ATT_COUNT,), jnp.float32), jnp.zeros((MLP_COUNT,), jnp.float32))
    totals, outcome = lax.scan(group_step, initial, (inputs, upstream, segments, validity))
    output = outcome[0].reshape(TOKENS, D)
    grad_input = outcome[1].reshape(TOKENS, D)
    attention_layout = jnp.pad(totals[0], (0, devices * ATT_ROWS * 128 - ATT_COUNT)).reshape(devices, ATT_ROWS, 128)
    feedforward_layout = jnp.pad(totals[1], (0, devices * MLP_ROWS * 128 - MLP_COUNT)).reshape(devices, MLP_ROWS, 128)
    grad_params = jnp.concatenate([attention_layout, feedforward_layout], axis=1).reshape(-1, 128)
    grad_params = grad_params * (1.0 / math.sqrt(tokens.shape[0]))
    return (output, grad_input, grad_params)
```

```python
import math
from functools import partial

import jax
import jax.numpy as jnp
from jax import lax
from jax.experimental import pallas as pl
from jax.experimental.pallas import tpu as pltpu
from jax.sharding import PartitionSpec as P

FF = 3072
HEADS = 12
EPSILON = 1e-06
NEGATIVE = -1e30
AXES = ("wide", "narrow")
LANES = 128
SUB = 16
QB = 128
MEGA = 1 << 20
F32 = jnp.float32
BF16 = jnp.bfloat16

BLOCKS = 32
QKV_BLOCKS, QKV_RT, QKV_CT = 24, 2, 18
WO_BLOCKS, WO_RT, WO_CT = 8, 6, 6
W1_BLOCKS, W1_RT, W1_CT = 16, 3, 24
W2_BLOCKS, W2_RT, W2_CT = 16, 12, 6
ATT_HALF, MLP_HALF = 18, 36
CHUNK = 768
CHUNKS = FF // CHUNK

G1, C1, BQ, BV, BO, S1 = 0, 6, 12, 18, 24, 30
G2, C2, B1, B2, S2 = 36, 42, 48, 72, 78
SMALL = 88

NT = (((1,), (1,)), ((), ()))
NN = (((1,), (0,)), ((), ()))
TN = (((0,), (0,)), ((), ()))


def mm(lhs, rhs, dims):
    return lax.dot_general(lhs, rhs, dims, preferred_element_type=F32)


def row_of(ref, first, count):
    return jnp.concatenate([ref[first + k : first + k + 1, :] for k in range(count)], axis=1)


def put_row(ref, first, values):
    for k in range(values.shape[1] // LANES):
        ref[first + k : first + k + 1, :] = values[:, k * LANES : (k + 1) * LANES]


def fold8(values):
    rows, columns = values.shape
    return jnp.sum(values.reshape(rows // 8, 8, columns), axis=0)


def total(values):
    return jnp.sum(values, axis=0, keepdims=True)


def vmem():
    return pl.BlockSpec(memory_space=pltpu.VMEM)


def smem():
    return pl.BlockSpec(memory_space=pltpu.SMEM)


def anywhere():
    return pl.BlockSpec(memory_space=pl.ANY)


def shape(dims, kind):
    return jax.ShapeDtypeStruct(dims, kind)


def cost(flops, moved, exps=0):
    return pl.CostEstimate(flops=int(flops), transcendentals=int(exps), bytes_accessed=int(moved))


def normalized(values):
    center = values - jnp.mean(values, axis=-1, keepdims=True)
    inverse = lax.rsqrt(jnp.mean(center * center, axis=-1, keepdims=True) + EPSILON)
    return center * inverse, inverse


def norm_pullback(unit, inverse, grad, gain):
    scaled = grad * gain
    first = jnp.mean(scaled, axis=-1, keepdims=True)
    second = jnp.mean(scaled * unit, axis=-1, keepdims=True)
    return inverse * (scaled - first - unit * second)


def gelu_pair(z):
    magnitude = jnp.abs(z)
    t = 1.0 / (1.0 + (0.3275911 * math.sqrt(0.5)) * magnitude)
    density = jnp.exp(z * z * -0.5)
    tail = 0.5 * 1.061405429
    tail = tail * t + 0.5 * -1.453152027
    tail = tail * t + 0.5 * 1.421413741
    tail = tail * t + 0.5 * -0.284496736
    tail = tail * t + 0.5 * 0.254829592
    tail = tail * t * density
    cumulative = jnp.where(z < 0, tail, 1.0 - tail)
    return z * cumulative, cumulative + z * density * (1.0 / math.sqrt(2.0 * math.pi))


def fetch(copies):
    for copy in copies:
        copy.start()


def settle(copies):
    for copy in copies:
        copy.wait()


ATT_BEFORE, ATT_AFTER = 64, 32
MLP_BEFORE, MLP_AFTER = 64, 40


def window_offsets(me, att_rows, mlp_rows):
    att = ATT_BEFORE + 12 + me * (576 - att_rows) + jnp.where(me < QKV_BLOCKS, 0, 12)
    mlp = MLP_BEFORE + 12 + me * (1152 - mlp_rows) + jnp.where(me < W1_BLOCKS, 0, 24)
    return att, mlp


def each_tile(me, act):
    @pl.when(me < QKV_BLOCKS)
    def _():
        for ct in range(QKV_CT):
            for rt in range(QKV_RT):
                act("att", ct // 9, (ct % 9) * QKV_RT + rt, rt * SUB * QKV_CT + ct, QKV_CT)

    @pl.when(me >= QKV_BLOCKS)
    def _():
        for rt in range(WO_RT):
            for ct in range(WO_CT):
                act("att", rt // 3, (rt % 3) * WO_CT + ct, rt * SUB * WO_CT + ct, WO_CT)

    @pl.when(me < W1_BLOCKS)
    def _():
        for ct in range(W1_CT):
            for rt in range(W1_RT):
                act("mlp", ct // 12, (ct % 12) * W1_RT + rt, rt * SUB * W1_CT + ct, W1_CT)

    @pl.when(me >= W1_BLOCKS)
    def _():
        for rt in range(W2_RT):
            for ct in range(W2_CT):
                act("mlp", rt // 6, (rt % 6) * W2_CT + ct, rt * SUB * W2_CT + ct, W2_CT)


def small_rows(me, act):
    @pl.when(me == 0)
    def _():
        act("att", True, 12, G1)
        act("mlp", True, 12, G2)

    @pl.when(me == QKV_BLOCKS - 1)
    def _():
        act("att", False, 12, BQ)

    @pl.when(me == W1_BLOCKS - 1)
    def _():
        act("mlp", False, 24, B1)

    @pl.when(me == BLOCKS - 1)
    def _():
        act("att", False, 12, BO)
        act("mlp", False, 12, B2)


def pack_kernel(att_rows, me_ref, own, tails, heads, att, mlp, small, win_a, win_m):
    me = me_ref[0]
    mlp_rows = own.shape[0] - att_rows
    win_a[0:ATT_BEFORE, :] = tails[0:ATT_BEFORE, :]
    win_a[ATT_BEFORE : ATT_BEFORE + att_rows, :] = own[0:att_rows, :]
    win_a[ATT_BEFORE + att_rows :, :] = heads[0:ATT_AFTER, :]
    win_m[0:MLP_BEFORE, :] = tails[ATT_BEFORE:, :]
    win_m[MLP_BEFORE : MLP_BEFORE + mlp_rows, :] = own[att_rows:, :]
    win_m[MLP_BEFORE + mlp_rows :, :] = heads[ATT_AFTER:, :]
    att_off, mlp_off = window_offsets(me, att_rows, mlp_rows)

    def tile(kind, half, index, first, stride):
        window, out, off = (win_a, att, att_off) if kind == "att" else (win_m, mlp, mlp_off)
        out[half, index] = window[pl.ds(off + first, SUB, stride=stride), :].astype(BF16)

    each_tile(me, tile)
    small[...] = jnp.zeros_like(small)

    def vector(kind, before, rows, first):
        window, off, size = (win_a, att_off, 576) if kind == "att" else (win_m, mlp_off, 1152)
        start = off - 12 if before else off + size
        rounded = window[pl.ds(start, rows), :].astype(BF16).astype(F32)
        small[first : first + rows, :] = rounded

    small_rows(me, vector)


def pack(me, own, tails, heads, att_rows):
    mlp_rows = own.shape[0] - att_rows
    return pl.pallas_call(
        partial(pack_kernel, att_rows),
        out_shape=(
            shape((2, ATT_HALF, SUB, LANES), BF16),
            shape((2, MLP_HALF, SUB, LANES), BF16),
            shape((SMALL, LANES), F32),
        ),
        in_specs=[smem(), vmem(), vmem(), vmem()],
        out_specs=(vmem(), vmem(), vmem()),
        scratch_shapes=[
            pltpu.VMEM((ATT_BEFORE + att_rows + ATT_AFTER, LANES), F32),
            pltpu.VMEM((MLP_BEFORE + mlp_rows + MLP_AFTER, LANES), F32),
        ],
        name="pack",
    )(me, own, tails, heads)


def spread_kernel(att_rows, mlp_rows, scale, me_ref, att_a, att_b, mlp_a, mlp_b, small, win_a, win_m):
    me = me_ref[0]
    att_off, mlp_off = window_offsets(me, att_rows, mlp_rows)
    win_a[...] = jnp.zeros_like(win_a)
    win_m[...] = jnp.zeros_like(win_m)

    def tile(kind, half, index, first, stride):
        window, off = (win_a, att_off) if kind == "att" else (win_m, mlp_off)
        source = {"att": (att_a, att_b), "mlp": (mlp_a, mlp_b)}[kind][half]
        window[pl.ds(off + first, SUB, stride=stride), :] = source[index] * scale

    each_tile(me, tile)

    def vector(kind, before, rows, first):
        window, off, size = (win_a, att_off, 576) if kind == "att" else (win_m, mlp_off, 1152)
        start = off - 12 if before else off + size
        window[pl.ds(start, rows), :] = small[first : first + rows, :] * scale

    small_rows(me, vector)


def spread(me, att_a, att_b, mlp_a, mlp_b, small, att_rows, mlp_rows, scale):
    return pl.pallas_call(
        partial(spread_kernel, att_rows, mlp_rows, scale),
        out_shape=(
            shape((ATT_BEFORE + att_rows + ATT_AFTER, LANES), F32),
            shape((MLP_BEFORE + mlp_rows + MLP_AFTER, LANES), F32),
        ),
        in_specs=[smem()] + [vmem()] * 5,
        out_specs=(vmem(), vmem()),
        name="spread",
    )(me, att_a, att_b, mlp_a, mlp_b, small)


def half_copies(me, first, count, halves, scratch, sems, base=0):
    copies = []
    for i in range(count):
        slot = jnp.bitwise_xor(me, first + i)
        for h, half in enumerate(halves):
            size = half.shape[1]
            copies.append(
                pltpu.make_async_copy(
                    half.at[slot], scratch.at[i, pl.ds(h * size, size)], sems.at[base + 2 * i + h]
                )
            )
    return copies


def qkv_column(w, ct):
    tiles = [w[d, ct * QKV_RT + rt] for d in range(QKV_BLOCKS) for rt in range(QKV_RT)]
    return jnp.concatenate(tiles, axis=0)


def wo_column(w, ct):
    tiles = [w[i, rt * WO_CT + ct] for i in range(WO_BLOCKS) for rt in range(WO_RT)]
    return jnp.concatenate(tiles, axis=0)


def norm_rows(rows, gain, shift, source, target, step=32):
    def one(i, carry):
        at = pl.ds(pl.multiple_of(i * step, step), step)
        unit, _ = normalized(source[at, :].astype(F32))
        target[at, :] = (unit * gain + shift).astype(BF16)
        return carry

    lax.fori_loop(0, rows // step, one, 0)


def qkv_kernel(me_ref, tokens, small, wa, wb, n1, qkv, w, sems):
    copies = half_copies(me_ref[0], 0, QKV_BLOCKS, (wa, wb), w, sems)
    fetch(copies)
    rows = tokens.shape[0]
    norm_rows(rows, row_of(small, G1, 6), row_of(small, C1, 6), tokens, n1)
    settle(copies)
    bias = jnp.concatenate(
        [row_of(small, BQ, 6), jnp.zeros((1, 768), F32), row_of(small, BV, 6)], axis=1
    )
    for c in range(QKV_CT // 2):
        weight = jnp.concatenate([qkv_column(w, 2 * c), qkv_column(w, 2 * c + 1)], axis=1)
        lanes = slice(256 * c, 256 * c + 256)
        qkv[:, lanes] = (mm(n1[...], weight, NN) + bias[:, lanes]).astype(BF16)


def project_qkv(me, tokens, small, att):
    rows, width = tokens.shape
    return pl.pallas_call(
        qkv_kernel,
        out_shape=(shape((rows, width), BF16), shape((rows, 3 * width), BF16)),
        in_specs=[smem(), vmem(), vmem(), anywhere(), anywhere()],
        out_specs=(vmem(), vmem()),
        scratch_shapes=[
            pltpu.VMEM((QKV_BLOCKS, 2 * ATT_HALF, SUB, LANES), BF16),
            pltpu.SemaphoreType.DMA((2 * QKV_BLOCKS,)),
        ],
        compiler_params=pltpu.CompilerParams(vmem_limit_bytes=40 * MEGA),
        cost_estimate=cost(6 * rows * width * width, 12 * rows * width),
        name="qkv_forward",
    )(me, tokens, small, att[0], att[1])


CLASSES = (128, 256, 384, 512, 768)


def head_masked(block):
    lane = lax.broadcasted_iota(jnp.int32, block.shape, 1)
    zero = jnp.zeros_like(block)
    return jnp.concatenate(
        [jnp.where(lane < 64, block, zero), jnp.where(lane >= 64, block, zero)], axis=0
    )


def pick_heads(both):
    return jnp.concatenate([both[0:64, 0:QB], both[64:128, QB : 2 * QB]], axis=0)


def lane_block(p, group):
    return pl.ds(pl.multiple_of((group * 6 + p) * LANES, LANES), LANES)


def mask_bias(start, width, b, key_ids, query_ids, bias):
    for j in range(width // QB):
        at = pl.ds(pl.multiple_of(start + j * QB, SUB), QB)
        same = key_ids[at, :] == query_ids[pl.ds(b, 1), :]
        bias[j * QB : (j + 1) * QB, :] = jnp.where(same, 0.0, NEGATIVE)


def attend_kernel(windows, qkv, key_ids, query_ids, mixed, stats, bias, scores):
    blocks = qkv.shape[0] // QB

    def one_block(b, carry):
        start = pl.multiple_of(windows[0, b], SUB)
        rows = pl.ds(pl.multiple_of(b * QB, QB), QB)
        for index, width in enumerate(CLASSES):

            @pl.when(windows[1, b] == index)
            def _(width=width):
                mask_bias(start, width, b, key_ids, query_ids, bias)
                pieces = [slice(j * QB, (j + 1) * QB) for j in range(width // QB)]

                def one_pair(p, inner):
                    queries = head_masked(qkv[rows, lane_block(p, 0)] * 0.125)
                    highest = jnp.full((8, 2 * QB), NEGATIVE, F32)
                    for piece in pieces:
                        at = pl.ds(pl.multiple_of(start + piece.start, SUB), QB)
                        part = mm(qkv[at, lane_block(p, 1)], queries, NT)
                        part = part + jnp.concatenate([bias[piece, :]] * 2, axis=1)
                        scores[piece, :] = part
                        highest = jnp.maximum(
                            highest, jnp.max(part.reshape(QB // 8, 8, 2 * QB), axis=0)
                        )
                    highest = jnp.max(highest, axis=0, keepdims=True)
                    summed = jnp.zeros((8, 2 * QB), F32)
                    both = jnp.zeros((LANES, 2 * QB), F32)
                    for piece in pieces:
                        at = pl.ds(pl.multiple_of(start + piece.start, SUB), QB)
                        raised = jnp.exp(scores[piece, :] - highest)
                        summed = summed + fold8(raised)
                        both = both + mm(qkv[at, lane_block(p, 2)], raised.astype(BF16), TN)
                    inverse = 1.0 / total(summed)
                    out = pick_heads(both * inverse)
                    mixed[rows, lane_block(p, 0)] = out.T.astype(BF16)
                    stats[b * 6 + p, 0:1, :] = highest
                    stats[b * 6 + p, 1:2, :] = inverse
                    return inner

                lax.fori_loop(0, 6, one_pair, 0, unroll=2)

        return carry

    lax.fori_loop(0, blocks, one_block, 0)


def attend(windows, qkv, key_ids, query_ids):
    rows = qkv.shape[0]
    width = qkv.shape[1] // 3
    return pl.pallas_call(
        attend_kernel,
        out_shape=(shape((rows, width), BF16), shape((rows // QB * 6, 2, 2 * QB), F32)),
        in_specs=[smem(), vmem(), vmem(), vmem()],
        out_specs=(vmem(), vmem()),
        scratch_shapes=[
            pltpu.VMEM((CLASSES[-1], QB), F32),
            pltpu.VMEM((CLASSES[-1], 2 * QB), F32),
        ],
        compiler_params=pltpu.CompilerParams(vmem_limit_bytes=40 * MEGA),
        cost_estimate=cost(2 * rows * rows * width, 8 * rows * width, 4 * rows * rows),
        name="attend_forward",
    )(windows, qkv, key_ids, query_ids)


def join_kernel(me_ref, tokens, mixed, small, wa, wb, x1, branch, n2, w, sems):
    copies = half_copies(me_ref[0], QKV_BLOCKS, WO_BLOCKS, (wa, wb), w, sems)
    fetch(copies)
    rows = tokens.shape[0]
    bias, scale = row_of(small, BO, 6), row_of(small, S1, 6)
    gain, shift = row_of(small, G2, 6), row_of(small, C2, 6)
    settle(copies)
    for c in range(3):
        weight = jnp.concatenate([wo_column(w, 2 * c), wo_column(w, 2 * c + 1)], axis=1)
        lanes = slice(256 * c, 256 * c + 256)
        branch[:, lanes] = mm(mixed[...], weight, NN) + bias[:, lanes]
    step = 32

    def one(i, carry):
        at = pl.ds(pl.multiple_of(i * step, step), step)
        values = tokens[at, :].astype(F32) + scale * branch[at, :]
        x1[at, :] = values
        unit, _ = normalized(values)
        n2[at, :] = (unit * gain + shift).astype(BF16)
        return carry

    lax.fori_loop(0, rows // step, one, 0)


def join(me, tokens, mixed, small, att):
    rows, width = tokens.shape
    return pl.pallas_call(
        join_kernel,
        out_shape=(
            shape((rows, width), F32),
            shape((rows, width), F32),
            shape((rows, width), BF16),
        ),
        in_specs=[smem(), vmem(), vmem(), vmem(), anywhere(), anywhere()],
        out_specs=(vmem(), vmem(), vmem()),
        scratch_shapes=[
            pltpu.VMEM((WO_BLOCKS, 2 * ATT_HALF, SUB, LANES), BF16),
            pltpu.SemaphoreType.DMA((2 * WO_BLOCKS,)),
        ],
        compiler_params=pltpu.CompilerParams(vmem_limit_bytes=40 * MEGA),
        cost_estimate=cost(2 * rows * width * width, 14 * rows * width),
        name="project_and_norm",
    )(me, tokens, mixed, small, att[0], att[1])


def w1_matrix(w1, f):
    columns = []
    for ct in range(6):
        tiles = [w1[f, d, ct * W1_RT + rt] for d in range(W1_BLOCKS) for rt in range(W1_RT)]
        columns.append(jnp.concatenate(tiles, axis=0))
    return jnp.concatenate(columns, axis=1)


def w2_matrix(w2, f):
    columns = []
    for ct in range(W2_CT):
        tiles = [w2[4 * f + k, rt * W2_CT + ct] for k in range(4) for rt in range(W2_RT)]
        columns.append(jnp.concatenate(tiles, axis=0))
    return jnp.concatenate(columns, axis=1)


def mlp_kernel(
    me_ref, n2, cot, x1, small, wa, wb,
    out, dx1, vectors, grads,
    w1, w2, macc, dnacc, dm, u, dz, gb1, sems1, sems2,
):
    me = me_ref[0]
    rows = n2.shape[0]
    slots1 = [jnp.bitwise_xor(me, d) for d in range(W1_BLOCKS)]

    def into_w1(f):
        half = (wa, wb)[f // 2]
        part = pl.ds(MLP_HALF // 2 * (f % 2), MLP_HALF // 2)
        return [
            pltpu.make_async_copy(half.at[slots1[d], part], w1.at[f, d], sems1.at[f, d])
            for d in range(W1_BLOCKS)
        ]

    def into_w2(f):
        return [
            pltpu.make_async_copy(
                (wa, wb)[h].at[jnp.bitwise_xor(me, W1_BLOCKS + 4 * f + k)],
                w2.at[4 * f + k, pl.ds(h * MLP_HALF, MLP_HALF)],
                sems2.at[f, 2 * k + h],
            )
            for k in range(4)
            for h in range(2)
        ]

    arriving = [into_w1(f) + into_w2(f) for f in range(CHUNKS)]
    for f in range(CHUNKS):
        fetch(arriving[f])

    def out_copies(f):
        copies = []
        for d in range(W1_BLOCKS):
            part = pl.ds(MLP_HALF // 2 * (f % 2), MLP_HALF // 2)
            target = grads.at[f // 2, slots1[d], part]
            copies.append(pltpu.make_async_copy(w1.at[f, d], target, sems1.at[f, d]))
        for k in range(4):
            slot = jnp.bitwise_xor(me, W1_BLOCKS + 4 * f + k)
            for h in range(2):
                source = w2.at[4 * f + k, pl.ds(h * MLP_HALF, MLP_HALF)]
                copies.append(
                    pltpu.make_async_copy(source, grads.at[h, slot], sems2.at[f, 2 * k + h])
                )
        return copies

    scale = row_of(small, S2, 6)
    step = 32

    def prepare(i, carry):
        at = pl.ds(pl.multiple_of(i * step, step), step)
        rounded = (cot[at, :].astype(F32) * scale).astype(BF16)
        dm[at, :] = rounded
        macc[at, :] = jnp.zeros((step, macc.shape[1]), F32)
        dnacc[at, :] = jnp.zeros((step, macc.shape[1]), F32)
        return carry + fold8(rounded.astype(F32))

    zero = jnp.zeros((8, 768), F32)
    gb2 = lax.fori_loop(0, rows // step, prepare, zero)
    gb1[...] = jnp.zeros_like(gb1)
    tall = 256

    for f in range(CHUNKS):
        settle(arriving[f])

        def one_tile(i, carry, f=f):
            at = pl.ds(pl.multiple_of(i * tall, tall), tall)
            first = w1_matrix(w1, f)
            second = w2_matrix(w2, f)
            for c in range(CHUNK // 256):
                lanes = slice(256 * c, 256 * c + 256)
                bias = row_of(small, B1 + 6 * f + 2 * c, 2)
                z = mm(n2[at, :], first[:, lanes], NN) + bias
                du = mm(dm[at, :], second[lanes, :], NT)
                for r in range(tall // 32):
                    part = slice(32 * r, 32 * r + 32)
                    place = pl.ds(pl.multiple_of(i * tall + 32 * r, 32), 32)
                    value, slope = gelu_pair(z[part, :])
                    u[place, lanes] = value.astype(BF16)
                    rounded = (du[part, :] * slope).astype(BF16)
                    dz[place, lanes] = rounded
                    gb1[f, :, lanes] += fold8(rounded.astype(F32))
            macc[at, :] += mm(u[at, :], second, NN)
            dnacc[at, :] += mm(dz[at, :], first, NT)
            return carry

        lax.fori_loop(0, rows // tall, one_tile, 0)
        for c in range(CHUNK // 256):
            lanes = slice(256 * c, 256 * c + 256)
            grad = mm(u[:, lanes], dm[...], TN)
            for r in range(SUB):
                tile_row = SUB * c + r
                k, rt = tile_row // W2_RT, tile_row % W2_RT
                for ct in range(W2_CT):
                    tile = grad[SUB * r : SUB * r + SUB, LANES * ct : LANES * ct + LANES]
                    w2[4 * f + k, rt * W2_CT + ct] = tile.astype(BF16)
        for c in range(CHUNK // 256):
            lanes = slice(256 * c, 256 * c + 256)
            grad = mm(n2[:, lanes], dz[...], TN)
            for r in range(SUB):
                tile_row = SUB * c + r
                d, rt = tile_row // W1_RT, tile_row % W1_RT
                for ct in range(6):
                    tile = grad[SUB * r : SUB * r + SUB, LANES * ct : LANES * ct + LANES]
                    w1[f, d, ct * W1_RT + rt] = tile.astype(BF16)
        leaving = out_copies(f)
        fetch(leaving)
        arriving[f] = leaving

    bias, gain = row_of(small, B2, 6), row_of(small, G2, 6)

    def finish(i, carry):
        gs2, gg2, gc2 = carry
        at = pl.ds(pl.multiple_of(i * SUB, SUB), SUB)
        upstream = cot[at, :].astype(F32)
        values = x1[at, :]
        contracted = macc[at, :] + bias
        out[at, :] = (values + scale * contracted).astype(BF16)
        unit, inverse = normalized(values)
        grad = dnacc[at, :]
        dx1[at, :] = upstream + norm_pullback(unit, inverse, grad, gain)
        return (
            gs2 + fold8(upstream * contracted),
            gg2 + fold8(grad * unit),
            gc2 + fold8(grad),
        )

    gs2, gg2, gc2 = lax.fori_loop(0, rows // SUB, finish, (zero, zero, zero))
    put_row(vectors, G2 - G2, total(gg2))
    put_row(vectors, C2 - G2, total(gc2))
    for f in range(CHUNKS):
        put_row(vectors, B1 - G2 + 6 * f, total(gb1[f]))
    put_row(vectors, B2 - G2, total(gb2))
    put_row(vectors, S2 - G2, total(gs2))
    for f in range(CHUNKS):
        settle(arriving[f])


def feed_forward(me, n2, cot, x1, small, mlp):
    rows, width = n2.shape
    return pl.pallas_call(
        mlp_kernel,
        out_shape=(
            shape((rows, width), BF16),
            shape((rows, width), F32),
            shape((48, LANES), F32),
            shape((2, BLOCKS, MLP_HALF, SUB, LANES), BF16),
        ),
        in_specs=[smem(), vmem(), vmem(), vmem(), vmem(), anywhere(), anywhere()],
        out_specs=(vmem(), vmem(), vmem(), anywhere()),
        scratch_shapes=[
            pltpu.VMEM((CHUNKS, W1_BLOCKS, MLP_HALF // 2, SUB, LANES), BF16),
            pltpu.VMEM((W2_BLOCKS, 2 * MLP_HALF, SUB, LANES), BF16),
            pltpu.VMEM((rows, width), F32),
            pltpu.VMEM((rows, width), F32),
            pltpu.VMEM((rows, width), BF16),
            pltpu.VMEM((rows, CHUNK), BF16),
            pltpu.VMEM((rows, CHUNK), BF16),
            pltpu.VMEM((CHUNKS, 8, CHUNK), F32),
            pltpu.SemaphoreType.DMA((CHUNKS, W1_BLOCKS)),
            pltpu.SemaphoreType.DMA((CHUNKS, 8)),
        ],
        compiler_params=pltpu.CompilerParams(vmem_limit_bytes=58 * MEGA),
        cost_estimate=cost(12 * rows * width * FF, 40 * MEGA),
        name="feed_forward",
    )(me, n2, cot, x1, small, mlp[0], mlp[1])


def split_kernel(me_ref, dx1, branch, mixed, small, wa, wb, da, vectors, grads, w, db, sems):
    me = me_ref[0]
    copies = half_copies(me, QKV_BLOCKS, WO_BLOCKS, (wa, wb), w, sems)
    fetch(copies)
    rows = dx1.shape[0]
    scale = row_of(small, S1, 6)
    step = 32

    def one(i, carry):
        gs1, gbo = carry
        at = pl.ds(pl.multiple_of(i * step, step), step)
        grad = dx1[at, :]
        rounded = (grad * scale).astype(BF16)
        db[at, :] = rounded
        return gs1 + fold8(grad * branch[at, :]), gbo + fold8(rounded.astype(F32))

    zero = jnp.zeros((8, 768), F32)
    gs1, gbo = lax.fori_loop(0, rows // step, one, (zero, zero))
    put_row(vectors, 0, total(gbo))
    put_row(vectors, 6, total(gs1))
    vectors[12:16, :] = jnp.zeros((4, LANES), F32)
    settle(copies)
    weight = jnp.concatenate([wo_column(w, ct) for ct in range(WO_CT)], axis=1)
    for c in range(3):
        lanes = slice(256 * c, 256 * c + 256)
        da[:, lanes] = mm(db[...], weight[lanes, :], NT).astype(BF16)
    for c in range(3):
        grad = mm(mixed[:, 256 * c : 256 * c + 256], db[...], TN)
        for r in range(SUB):
            tile_row = SUB * c + r
            i, rt = tile_row // WO_RT, tile_row % WO_RT
            for ct in range(WO_CT):
                tile = grad[SUB * r : SUB * r + SUB, LANES * ct : LANES * ct + LANES]
                w[i, rt * WO_CT + ct] = tile.astype(BF16)
    leaving = []
    for i in range(WO_BLOCKS):
        slot = jnp.bitwise_xor(me, QKV_BLOCKS + i)
        for h in range(2):
            source = w.at[i, pl.ds(h * ATT_HALF, ATT_HALF)]
            leaving.append(pltpu.make_async_copy(source, grads.at[h, slot], sems.at[2 * i + h]))
    fetch(leaving)
    settle(leaving)


def split(me, dx1, branch, mixed, small, att):
    rows, width = dx1.shape
    return pl.pallas_call(
        split_kernel,
        out_shape=(
            shape((rows, width), BF16),
            shape((16, LANES), F32),
            shape((2, BLOCKS, ATT_HALF, SUB, LANES), BF16),
        ),
        in_specs=[smem(), vmem(), vmem(), vmem(), vmem(), anywhere(), anywhere()],
        out_specs=(vmem(), vmem(), anywhere()),
        scratch_shapes=[
            pltpu.VMEM((WO_BLOCKS, 2 * ATT_HALF, SUB, LANES), BF16),
            pltpu.VMEM((rows, width), BF16),
            pltpu.SemaphoreType.DMA((2 * WO_BLOCKS,)),
        ],
        compiler_params=pltpu.CompilerParams(vmem_limit_bytes=40 * MEGA),
        cost_estimate=cost(4 * rows * width * width, 14 * rows * width),
        name="project_backward",
    )(me, dx1, branch, mixed, small, att[0], att[1])


def attend_back_kernel(
    windows, qkv, da, stats, key_ids, query_ids, dqkv, bias, probs, dprobs, dkeys, dvalues
):
    blocks = qkv.shape[0] // QB

    def clear(b, carry):
        rows = pl.ds(pl.multiple_of(b * QB, QB), QB)
        dkeys[rows, :] = jnp.zeros((QB, dkeys.shape[1]), F32)
        dvalues[rows, :] = jnp.zeros((QB, dkeys.shape[1]), F32)
        return carry

    lax.fori_loop(0, blocks, clear, 0)

    def one_block(b, carry):
        start = pl.multiple_of(windows[0, b], SUB)
        rows = pl.ds(pl.multiple_of(b * QB, QB), QB)
        for index, width in enumerate(CLASSES):

            @pl.when(windows[1, b] == index)
            def _(width=width):
                mask_bias(start, width, b, key_ids, query_ids, bias)
                pieces = [slice(j * QB, (j + 1) * QB) for j in range(width // QB)]

                def one_pair(p, inner):
                    queries = head_masked(qkv[rows, lane_block(p, 0)] * 0.125)
                    grads = head_masked(da[rows, lane_block(p, 0)])
                    highest = stats[b * 6 + p, 0:1, :]
                    inverse = stats[b * 6 + p, 1:2, :]
                    inner_sum = jnp.zeros((8, 2 * QB), F32)
                    for piece in pieces:
                        at = pl.ds(pl.multiple_of(start + piece.start, SUB), QB)
                        part = mm(qkv[at, lane_block(p, 1)], queries, NT)
                        part = part + jnp.concatenate([bias[piece, :]] * 2, axis=1)
                        weight = jnp.exp(part - highest) * inverse
                        dweight = mm(qkv[at, lane_block(p, 2)], grads, NT)
                        inner_sum = inner_sum + fold8(weight * dweight)
                        probs[piece, :] = weight
                        dprobs[piece, :] = dweight
                        dvalues[at, lane_block(p, 0)] += mm(weight.astype(BF16), grads, NN)
                    inner_sum = total(inner_sum)
                    both = jnp.zeros((LANES, 2 * QB), F32)
                    for piece in pieces:
                        at = pl.ds(pl.multiple_of(start + piece.start, SUB), QB)
                        dscore = probs[piece, :] * (dprobs[piece, :] - inner_sum)
                        dscore = dscore.astype(BF16)
                        dkeys[at, lane_block(p, 0)] += mm(dscore, queries, NN)
                        both = both + mm(qkv[at, lane_block(p, 1)], dscore, TN)
                    out = pick_heads(both) * 0.125
                    dqkv[rows, lane_block(p, 0)] = out.T.astype(BF16)
                    return inner

                lax.fori_loop(0, 6, one_pair, 0, unroll=2)

        return carry

    lax.fori_loop(0, blocks, one_block, 0)
    width = dkeys.shape[1]

    def store(b, carry):
        rows = pl.ds(pl.multiple_of(b * 32, 32), 32)
        dqkv[rows, width : 2 * width] = dkeys[rows, :].astype(BF16)
        dqkv[rows, 2 * width :] = dvalues[rows, :].astype(BF16)
        return carry

    lax.fori_loop(0, qkv.shape[0] // 32, store, 0)


def attend_back(windows, qkv, da, stats, key_ids, query_ids):
    rows, triple = qkv.shape
    width = triple // 3
    return pl.pallas_call(
        attend_back_kernel,
        out_shape=shape((rows, triple), BF16),
        in_specs=[smem()] + [vmem()] * 5,
        out_specs=vmem(),
        scratch_shapes=[
            pltpu.VMEM((CLASSES[-1], QB), F32),
            pltpu.VMEM((CLASSES[-1], 2 * QB), F32),
            pltpu.VMEM((CLASSES[-1], 2 * QB), F32),
            pltpu.VMEM((rows, width), F32),
            pltpu.VMEM((rows, width), F32),
        ],
        compiler_params=pltpu.CompilerParams(vmem_limit_bytes=48 * MEGA),
        cost_estimate=cost(6 * rows * rows * width, 14 * rows * width, 4 * rows * rows),
        name="attend_backward",
    )(windows, qkv, da, stats, key_ids, query_ids)


def weight_grad_kernel(me_ref, n1, dqkv, given, grads, w, sems):
    me = me_ref[0]
    for c in range(3):
        for half in range(2):
            columns = slice(1152 * half, 1152 * half + 1152)
            grad = mm(n1[:, 256 * c : 256 * c + 256], dqkv[:, columns], TN)
            for r in range(SUB):
                tile_row = SUB * c + r
                d, rt = tile_row // QKV_RT, tile_row % QKV_RT
                for ct in range(9):
                    tile = grad[SUB * r : SUB * r + SUB, LANES * ct : LANES * ct + LANES]
                    w[d, (9 * half + ct) * QKV_RT + rt] = tile.astype(BF16)
    leaving = []
    for d in range(QKV_BLOCKS):
        slot = jnp.bitwise_xor(me, d)
        for h in range(2):
            source = w.at[d, pl.ds(h * ATT_HALF, ATT_HALF)]
            leaving.append(pltpu.make_async_copy(source, grads.at[h, slot], sems.at[2 * d + h]))
    fetch(leaving)
    settle(leaving)


def weight_grad(me, n1, dqkv, given):
    rows, width = n1.shape
    return pl.pallas_call(
        weight_grad_kernel,
        out_shape=shape(given.shape, BF16),
        in_specs=[smem(), vmem(), vmem(), anywhere()],
        out_specs=anywhere(),
        scratch_shapes=[
            pltpu.VMEM((QKV_BLOCKS, 2 * ATT_HALF, SUB, LANES), BF16),
            pltpu.SemaphoreType.DMA((2 * QKV_BLOCKS,)),
        ],
        input_output_aliases={3: 0},
        compiler_params=pltpu.CompilerParams(vmem_limit_bytes=40 * MEGA),
        cost_estimate=cost(6 * rows * width * width, 10 * rows * width),
        name="qkv_weight_grad",
    )(me, n1, dqkv, given)


def input_grad_kernel(me_ref, tokens, dx1, dqkv, small, wa, wb, dx, vectors, w, dn, sems):
    copies = half_copies(me_ref[0], 0, QKV_BLOCKS, (wa, wb), w, sems)
    fetch(copies)
    rows = tokens.shape[0]
    zero = jnp.zeros((8, 768), F32)

    def sums(i, carry):
        at = pl.ds(pl.multiple_of(i * 32, 32), 32)
        return (
            carry[0] + fold8(dqkv[at, 0:768].astype(F32)),
            carry[1] + fold8(dqkv[at, 1536:2304].astype(F32)),
        )

    gbq, gbv = lax.fori_loop(0, rows // 32, sums, (zero, zero))
    settle(copies)
    weight = jnp.concatenate([qkv_column(w, ct) for ct in range(QKV_CT)], axis=1)
    for c in range(3):
        lanes = slice(256 * c, 256 * c + 256)
        dn[:, lanes] = mm(dqkv[...], weight[lanes, :], NT)
    gain = row_of(small, G1, 6)

    def finish(i, carry):
        at = pl.ds(pl.multiple_of(i * SUB, SUB), SUB)
        unit, inverse = normalized(tokens[at, :].astype(F32))
        grad = dn[at, :]
        dx[at, :] = dx1[at, :] + norm_pullback(unit, inverse, grad, gain)
        return carry[0] + fold8(grad * unit), carry[1] + fold8(grad)

    gg1, gc1 = lax.fori_loop(0, rows // SUB, finish, (zero, zero))
    put_row(vectors, 0, total(gg1))
    put_row(vectors, 6, total(gc1))
    put_row(vectors, 12, total(gbq))
    put_row(vectors, 18, total(gbv))


def input_grad(me, tokens, dx1, dqkv, small, att):
    rows, width = tokens.shape
    return pl.pallas_call(
        input_grad_kernel,
        out_shape=(shape((rows, width), F32), shape((24, LANES), F32)),
        in_specs=[smem(), vmem(), vmem(), vmem(), vmem(), anywhere(), anywhere()],
        out_specs=(vmem(), vmem()),
        scratch_shapes=[
            pltpu.VMEM((QKV_BLOCKS, 2 * ATT_HALF, SUB, LANES), BF16),
            pltpu.VMEM((rows, width), F32),
            pltpu.SemaphoreType.DMA((2 * QKV_BLOCKS,)),
        ],
        compiler_params=pltpu.CompilerParams(vmem_limit_bytes=44 * MEGA),
        cost_estimate=cost(6 * rows * width * width, 18 * rows * width),
        name="input_grad",
    )(me, tokens, dx1, dqkv, small, att[0], att[1])


X, C, Z1, Z0, Y = 16, 8, 4, 2, 1


def exchange(values, bit):
    return lax.ppermute(values, AXES, [(d, d ^ bit) for d in range(BLOCKS)])


def shifted(values, by):
    pairs = [(d, d + by) for d in range(BLOCKS) if 0 <= d + by < BLOCKS]
    return lax.ppermute(values, AXES, pairs)


def widen(values, bit, axis):
    return jnp.stack([values, exchange(values, bit)], axis=axis)


def spread_blocks(halves):
    values = widen(halves, Z1, 0)
    values = widen(values, Z0, 1)
    first, second = values[:, :, 0], values[:, :, 1]
    first = widen(first, X, 0)
    second = widen(second, Y, 2)
    first = widen(first, Y, 3)
    second = widen(second, X, 0)
    first = widen(first, C, 1)
    second = widen(second, C, 1)
    flat = (BLOCKS,) + halves.shape[1:]
    return first.reshape(flat), second.reshape(flat)


def narrow_step(values, bit, axis, last=False):
    keep = lax.index_in_dim(values, 0, axis, keepdims=False)
    send = lax.index_in_dim(values, 1, axis, keepdims=False)
    summed = keep.astype(F32) + exchange(send, bit).astype(F32)
    return summed if last else summed.astype(BF16)


def reduce_blocks(grads):
    parts = []
    for half in range(2):
        values = grads[half].reshape((2, 2, 2, 2, 2) + grads.shape[2:])
        parts.append(narrow_step(values, C, 1))
    first, second = parts
    first = narrow_step(first, X, 0)
    second = narrow_step(second, Y, 3)
    first = narrow_step(first, Y, 2)
    second = narrow_step(second, X, 0)
    out = []
    for values in (first, second):
        values = narrow_step(values, Z0, 1)
        out.append(narrow_step(values, Z1, 0, last=True))
    return out


def attention_amounts(width):
    return [width, width, 3 * width * width, width, width, width * width, width, width]


def feedforward_amounts(width):
    return [width, width, width * FF, FF, FF * width, width, width]


def pieces_of(vector, amounts):
    out, offset = [], 0
    for amount in amounts:
        out.append(vector[offset : offset + amount])
        offset += amount
    return out


def tiles_by_column(matrix, blocks, rt):
    ct = matrix.shape[1] // LANES
    return matrix.reshape(blocks, rt, SUB, ct, LANES).transpose(0, 3, 1, 2, 4)


def tiles_by_row(matrix, blocks, rt):
    ct = matrix.shape[1] // LANES
    return matrix.reshape(blocks, rt, SUB, ct, LANES).transpose(0, 1, 3, 2, 4)


def gather_plainly(params, att_rows, width):
    rounded = params.astype(BF16)
    att = lax.all_gather(rounded[:att_rows], AXES, axis=0, tiled=True).reshape(-1)
    mlp = lax.all_gather(rounded[att_rows:], AXES, axis=0, tiled=True).reshape(-1)
    g1, c1, wqkv, bq, bv, wo, bo, s1 = pieces_of(att, attention_amounts(width))
    g2, c2, w1, b1, w2, b2, s2 = pieces_of(mlp, feedforward_amounts(width))
    tile = (SUB, LANES)
    att = jnp.concatenate(
        [
            tiles_by_column(wqkv.reshape(width, -1), QKV_BLOCKS, QKV_RT).reshape((-1, 36) + tile),
            tiles_by_row(wo.reshape(width, -1), WO_BLOCKS, WO_RT).reshape((-1, 36) + tile),
        ]
    )
    mlp = jnp.concatenate(
        [
            tiles_by_column(w1.reshape(width, -1), W1_BLOCKS, W1_RT).reshape((-1, 72) + tile),
            tiles_by_row(w2.reshape(FF, -1), W2_BLOCKS, W2_RT).reshape((-1, 72) + tile),
        ]
    )
    vectors = jnp.concatenate([g1, c1, bq, bv, bo, s1, g2, c2, b1, b2, s2]).astype(F32)
    small = jnp.pad(vectors.reshape(-1, LANES), ((0, SMALL - 84), (0, 0)))
    return (att[:, :18], att[:, 18:]), (mlp[:, :36], mlp[:, 36:]), small


def reduce_plainly(gatt, gmlp, small, att_rows, mlp_rows, width, devices):
    att = jnp.concatenate([gatt[0], gatt[1]], axis=1).astype(F32)
    mlp = jnp.concatenate([gmlp[0], gmlp[1]], axis=1).astype(F32)
    five = lambda v, dims: v.reshape((v.shape[0],) + dims + (SUB, LANES))
    wqkv = five(att[:QKV_BLOCKS], (QKV_CT, QKV_RT)).transpose(0, 2, 3, 1, 4).reshape(-1)
    wo = five(att[QKV_BLOCKS:], (WO_RT, WO_CT)).transpose(0, 1, 3, 2, 4).reshape(-1)
    w1 = five(mlp[:W1_BLOCKS], (W1_CT, W1_RT)).transpose(0, 2, 3, 1, 4).reshape(-1)
    w2 = five(mlp[W1_BLOCKS:], (W2_RT, W2_CT)).transpose(0, 1, 3, 2, 4).reshape(-1)
    line = lambda first, count: small[first : first + count].reshape(-1)
    att = [line(G1, 12), wqkv, line(BQ, 12), wo, line(BO, 12)]
    mlp = [line(G2, 12), w1, line(B1, 24), w2, line(B2, 12)]

    def lay(parts, rows):
        vector = jnp.concatenate(parts)
        vector = jnp.pad(vector, (0, devices * rows * LANES - vector.shape[0]))
        return vector.reshape(devices, rows, LANES)

    whole = jnp.concatenate([lay(att, att_rows), lay(mlp, mlp_rows)], axis=1)
    return lax.psum_scatter(whole.reshape(-1, LANES), AXES, scatter_dimension=0, tiled=True)


def key_windows(segments, real):
    length = segments.shape[0]
    position = jnp.arange(length, dtype=jnp.int32)
    ids = jnp.where(real, segments, length + position)
    first = segments[0::QB]
    final = segments[QB - 1 :: QB]
    begin = jnp.sum((segments[None, :] < first[:, None]).astype(jnp.int32), axis=1)
    begin = jnp.where(real[0::QB], begin, position[0::QB])
    end = jnp.sum(((segments[None, :] <= final[:, None]) & real[None, :]).astype(jnp.int32), axis=1)
    end = jnp.where(real[QB - 1 :: QB], end, position[QB - 1 :: QB] + 1)
    begin = begin // SUB * SUB
    need = end - begin
    kind = sum((need > width).astype(jnp.int32) for width in CLASSES[:-1])
    widths = sum(
        jnp.where(kind == i, width, 0) for i, width in enumerate(CLASSES)
    )
    begin = jnp.minimum(begin, length - widths)
    return ids, jnp.stack([begin, kind]).astype(jnp.int32)


def local(tokens, cotangent, segment_ids, pad_mask, lengths, params):
    rows, width = tokens.shape
    wide, narrow = lax.axis_size("wide"), lax.axis_size("narrow")
    devices = wide * narrow
    att_count = 4 * width * width + 6 * width
    att_rows = (att_count // LANES + devices - 1) // devices
    mlp_rows = params.shape[0] - att_rows
    paired = (wide, narrow) == (4, 8)
    scale = 1.0 / math.sqrt(rows * devices)

    position = jnp.arange(rows, dtype=jnp.int32)
    real = (pad_mask > 0) & (position < lengths[0])
    ids, windows = key_windows(segment_ids, real)
    key_ids = ids.reshape(rows, 1)
    query_ids = ids.reshape(rows // QB, QB)

    if paired:
        me = lax.axis_index(AXES).astype(jnp.int32).reshape(1)
        tails = jnp.concatenate([params[att_rows - ATT_BEFORE : att_rows], params[-MLP_BEFORE:]])
        heads = jnp.concatenate([params[:ATT_AFTER], params[att_rows : att_rows + MLP_AFTER]])
        tails, heads = shifted(tails, 1), shifted(heads, -1)
        att_own, mlp_own, small_own = pack(me, params, tails, heads, att_rows)
        small = lax.psum(small_own, AXES)
        att = spread_blocks(att_own)
        mlp = spread_blocks(mlp_own)
    else:
        me = jnp.zeros((1,), jnp.int32)
        att, mlp, small = gather_plainly(params, att_rows, width)

    n1, qkv = project_qkv(me, tokens, small, att)
    mixed, stats = attend(windows, qkv, key_ids, query_ids)
    x1, branch, n2 = join(me, tokens, mixed, small, att)
    output, dx1, small_mlp, gmlp = feed_forward(me, n2, cotangent, x1, small, mlp)
    da, small_proj, gatt = split(me, dx1, branch, mixed, small, att)
    dqkv = attend_back(windows, qkv, da, stats, key_ids, query_ids)
    gatt = weight_grad(me, n1, dqkv, gatt)
    grad_input, small_norm = input_grad(me, tokens, dx1, dqkv, small, att)
    small_grads = jnp.concatenate(
        [small_norm, small_proj[:12], small_mlp, jnp.zeros((SMALL - 84, LANES), F32)]
    )

    if paired:
        mlp_sums = reduce_blocks(gmlp)
        att_sums = reduce_blocks(gatt)
        small_sums = lax.psum(small_grads, AXES)
        win_a, win_m = spread(
            me, *att_sums, *mlp_sums, small_sums, att_rows, mlp_rows, scale
        )
        before = shifted(jnp.concatenate([win_a[:ATT_BEFORE], win_m[:MLP_BEFORE]]), -1)
        after = shifted(jnp.concatenate([win_a[-ATT_AFTER:], win_m[-MLP_AFTER:]]), 1)
        out_a = win_a[ATT_BEFORE : ATT_BEFORE + att_rows]
        out_m = win_m[MLP_BEFORE : MLP_BEFORE + mlp_rows]
        out_a = out_a + jnp.pad(after[:ATT_AFTER], ((0, att_rows - ATT_AFTER), (0, 0)))
        out_a = out_a + jnp.pad(before[:ATT_BEFORE], ((att_rows - ATT_BEFORE, 0), (0, 0)))
        out_m = out_m + jnp.pad(after[ATT_AFTER:], ((0, mlp_rows - MLP_AFTER), (0, 0)))
        out_m = out_m + jnp.pad(before[ATT_BEFORE:], ((mlp_rows - MLP_BEFORE, 0), (0, 0)))
        grad_params = jnp.concatenate([out_a, out_m])
    else:
        owned = reduce_plainly(gatt, gmlp, small_grads, att_rows, mlp_rows, width, devices)
        grad_params = owned * scale
    return output, grad_input, grad_params


def solution(mesh):
    return jax.shard_map(
        local,
        mesh=mesh,
        in_specs=(
            P(AXES, None),
            P(AXES, None),
            P(AXES),
            P(AXES),
            P(AXES),
            P(AXES, None),
        ),
        out_specs=(P(AXES, None), P(AXES, None), P(AXES, None)),
        check_vma=False,
    )
```

```python
import math
from functools import partial

import jax
import jax.numpy as jnp
from jax import lax
from jax.experimental import pallas as pl
from jax.experimental.pallas import tpu as pltpu
from jax.sharding import PartitionSpec as P

FF = 3072
HEADS = 12
EPSILON = 1e-06
NEGATIVE = -1e30
AXES = ("wide", "narrow")
LANES = 128
SUB = 16
QB = 128
MEGA = 1 << 20
F32 = jnp.float32
BF16 = jnp.bfloat16

BLOCKS = 32
QKV_BLOCKS, QKV_RT, QKV_CT = 24, 2, 18
WO_BLOCKS, WO_RT, WO_CT = 8, 6, 6
W1_BLOCKS, W1_RT, W1_CT = 16, 3, 24
W2_BLOCKS, W2_RT, W2_CT = 16, 12, 6
ATT_HALF, MLP_HALF = 18, 36
ATT_SENT = ATT_HALF + 1
HALF_BLOCKS = BLOCKS // 2
CHUNK = 768
CHUNKS = FF // CHUNK

G1, C1, BQ, BV, BO, S1 = 0, 6, 12, 18, 24, 30
G2, C2, B1, B2, S2 = 36, 42, 48, 72, 78
SMALL = 88

NT = (((1,), (1,)), ((), ()))
NN = (((1,), (0,)), ((), ()))
TN = (((0,), (0,)), ((), ()))


def mm(lhs, rhs, dims):
    return lax.dot_general(lhs, rhs, dims, preferred_element_type=F32)


def row_of(ref, first, count):
    return jnp.concatenate([ref[first + k : first + k + 1, :] for k in range(count)], axis=1)


def put_row(ref, first, values):
    for k in range(values.shape[1] // LANES):
        ref[first + k : first + k + 1, :] = values[:, k * LANES : (k + 1) * LANES]


def fold8(values):
    rows, columns = values.shape
    return jnp.sum(values.reshape(rows // 8, 8, columns), axis=0)


def total(values):
    return jnp.sum(values, axis=0, keepdims=True)


def vmem():
    return pl.BlockSpec(memory_space=pltpu.VMEM)


def smem():
    return pl.BlockSpec(memory_space=pltpu.SMEM)


def anywhere():
    return pl.BlockSpec(memory_space=pl.ANY)


def shape(dims, kind):
    return jax.ShapeDtypeStruct(dims, kind)


def cost(flops, moved, exps=0):
    return pl.CostEstimate(flops=int(flops), transcendentals=int(exps), bytes_accessed=int(moved))


def normalized(values):
    center = values - jnp.mean(values, axis=-1, keepdims=True)
    inverse = lax.rsqrt(jnp.mean(center * center, axis=-1, keepdims=True) + EPSILON)
    return center * inverse, inverse


def norm_pullback(unit, inverse, grad, gain):
    scaled = grad * gain
    first = jnp.mean(scaled, axis=-1, keepdims=True)
    second = jnp.mean(scaled * unit, axis=-1, keepdims=True)
    return inverse * (scaled - first - unit * second)


def gelu_pair(z):
    magnitude = jnp.abs(z)
    t = 1.0 / (1.0 + (0.3275911 * math.sqrt(0.5)) * magnitude)
    density = jnp.exp(z * z * -0.5)
    tail = 0.5 * 1.061405429
    tail = tail * t + 0.5 * -1.453152027
    tail = tail * t + 0.5 * 1.421413741
    tail = tail * t + 0.5 * -0.284496736
    tail = tail * t + 0.5 * 0.254829592
    tail = tail * t * density
    cumulative = jnp.where(z < 0, tail, 1.0 - tail)
    return z * cumulative, cumulative + z * density * (1.0 / math.sqrt(2.0 * math.pi))


def fetch(copies):
    for copy in copies:
        copy.start()


def settle(copies):
    for copy in copies:
        copy.wait()


ATT_BEFORE, ATT_AFTER = 64, 32
MLP_BEFORE, MLP_AFTER = 64, 40


def window_offsets(me, att_rows, mlp_rows):
    att = ATT_BEFORE + 12 + me * (576 - att_rows) + jnp.where(me < QKV_BLOCKS, 0, 12)
    mlp = MLP_BEFORE + 12 + me * (1152 - mlp_rows) + jnp.where(me < W1_BLOCKS, 0, 24)
    return att, mlp


def each_tile(me, act):
    @pl.when(me < QKV_BLOCKS)
    def _():
        for ct in range(QKV_CT):
            for rt in range(QKV_RT):
                act("att", ct // 9, (ct % 9) * QKV_RT + rt, rt * SUB * QKV_CT + ct, QKV_CT)

    @pl.when(me >= QKV_BLOCKS)
    def _():
        for rt in range(WO_RT):
            for ct in range(WO_CT):
                act("att", rt // 3, (rt % 3) * WO_CT + ct, rt * SUB * WO_CT + ct, WO_CT)

    @pl.when(me < W1_BLOCKS)
    def _():
        for ct in range(W1_CT):
            for rt in range(W1_RT):
                act("mlp", ct // 12, (ct % 12) * W1_RT + rt, rt * SUB * W1_CT + ct, W1_CT)

    @pl.when(me >= W1_BLOCKS)
    def _():
        for rt in range(W2_RT):
            for ct in range(W2_CT):
                act("mlp", rt // 6, (rt % 6) * W2_CT + ct, rt * SUB * W2_CT + ct, W2_CT)


def small_rows(me, act):
    @pl.when(me == 0)
    def _():
        act("att", True, 12, G1)
        act("mlp", True, 12, G2)

    @pl.when(me == QKV_BLOCKS - 1)
    def _():
        act("att", False, 12, BQ)

    @pl.when(me == W1_BLOCKS - 1)
    def _():
        act("mlp", False, 24, B1)

    @pl.when(me == BLOCKS - 1)
    def _():
        act("att", False, 12, BO)
        act("mlp", False, 12, B2)


OWNERS = (0, W1_BLOCKS - 1, QKV_BLOCKS - 1, BLOCKS - 1)


def sent_rows(kind, first):
    return 12 if kind == "mlp" and first in (G2, B2) else 0


def pack_kernel(att_rows, me_ref, own, tails, heads, att, mlp, win_a, win_m, table):
    me = me_ref[0]
    mlp_rows = own.shape[0] - att_rows
    win_a[0:ATT_BEFORE, :] = tails[0:ATT_BEFORE, :]
    win_a[ATT_BEFORE : ATT_BEFORE + att_rows, :] = own[0:att_rows, :]
    win_a[ATT_BEFORE + att_rows :, :] = heads[0:ATT_AFTER, :]
    win_m[0:MLP_BEFORE, :] = tails[ATT_BEFORE:, :]
    win_m[MLP_BEFORE : MLP_BEFORE + mlp_rows, :] = own[att_rows:, :]
    win_m[MLP_BEFORE + mlp_rows :, :] = heads[ATT_AFTER:, :]
    att_off, mlp_off = window_offsets(me, att_rows, mlp_rows)

    def tile(kind, half, index, first, stride):
        window, out, off = (win_a, att, att_off) if kind == "att" else (win_m, mlp, mlp_off)
        out[half, index] = window[pl.ds(off + first, SUB, stride=stride), :].astype(BF16)

    each_tile(me, tile)
    table[...] = jnp.zeros_like(table)

    def vector(kind, before, rows, first):
        window, off, size = (win_a, att_off, 576) if kind == "att" else (win_m, mlp_off, 1152)
        start = off - 12 if before else off + size
        place = sent_rows(kind, first)
        table[place : place + rows, :] = window[pl.ds(start, rows), :]

    small_rows(me, vector)
    att[0, ATT_HALF] = table[0:SUB, :].astype(BF16)
    att[1, ATT_HALF] = table[SUB : 2 * SUB, :].astype(BF16)


def pack(me, own, tails, heads, att_rows):
    mlp_rows = own.shape[0] - att_rows
    return pl.pallas_call(
        partial(pack_kernel, att_rows),
        out_shape=(
            shape((2, ATT_SENT, SUB, LANES), BF16),
            shape((2, MLP_HALF, SUB, LANES), BF16),
        ),
        in_specs=[smem(), vmem(), vmem(), vmem()],
        out_specs=(vmem(), vmem()),
        scratch_shapes=[
            pltpu.VMEM((ATT_BEFORE + att_rows + ATT_AFTER, LANES), F32),
            pltpu.VMEM((MLP_BEFORE + mlp_rows + MLP_AFTER, LANES), F32),
            pltpu.VMEM((2 * SUB, LANES), F32),
        ],
        name="pack",
    )(me, own, tails, heads)


def spread_kernel(
    att_rows, scale, me_ref, att, mlp, mine, to_before, to_after, win_a, win_m, table
):
    me = me_ref[0]
    mlp_rows = mine.shape[0] - att_rows
    att_off, mlp_off = window_offsets(me, att_rows, mlp_rows)
    win_a[...] = jnp.zeros_like(win_a)
    win_m[...] = jnp.zeros_like(win_m)

    def tile(kind, half, index, first, stride):
        window, off = (win_a, att_off) if kind == "att" else (win_m, mlp_off)
        source = att if kind == "att" else mlp
        window[pl.ds(off + first, SUB, stride=stride), :] = source[half, index] * scale

    each_tile(me, tile)
    for h in range(2):
        table[SUB * h : SUB * h + SUB, :] = att[h, ATT_HALF] * scale

    def vector(kind, before, rows, first):
        window, off, size = (win_a, att_off, 576) if kind == "att" else (win_m, mlp_off, 1152)
        start = off - 12 if before else off + size
        place = sent_rows(kind, first)
        window[pl.ds(start, rows), :] = table[place : place + rows, :]

    small_rows(me, vector)
    mine[0:att_rows, :] = win_a[ATT_BEFORE : ATT_BEFORE + att_rows, :]
    mine[att_rows:, :] = win_m[MLP_BEFORE : MLP_BEFORE + mlp_rows, :]
    to_before[0:ATT_BEFORE, :] = win_a[0:ATT_BEFORE, :]
    to_before[ATT_BEFORE:, :] = win_m[0:MLP_BEFORE, :]
    to_after[0:ATT_AFTER, :] = win_a[ATT_BEFORE + att_rows :, :]
    to_after[ATT_AFTER:, :] = win_m[MLP_BEFORE + mlp_rows :, :]


def spread(me, att, mlp, att_rows, mlp_rows, scale):
    return pl.pallas_call(
        partial(spread_kernel, att_rows, scale),
        out_shape=(
            shape((att_rows + mlp_rows, LANES), F32),
            shape((ATT_BEFORE + MLP_BEFORE, LANES), F32),
            shape((ATT_AFTER + MLP_AFTER, LANES), F32),
        ),
        in_specs=[smem(), vmem(), vmem()],
        out_specs=(vmem(), vmem(), vmem()),
        scratch_shapes=[
            pltpu.VMEM((ATT_BEFORE + att_rows + ATT_AFTER, LANES), F32),
            pltpu.VMEM((MLP_BEFORE + mlp_rows + MLP_AFTER, LANES), F32),
            pltpu.VMEM((2 * SUB, LANES), F32),
        ],
        name="spread",
    )(me, att, mlp)


def close_kernel(att_rows, mine, below, above, out):
    rows = mine.shape[0]
    out[...] = mine[...]
    out[0:ATT_AFTER, :] += below[0:ATT_AFTER, :]
    out[att_rows : att_rows + MLP_AFTER, :] += below[ATT_AFTER:, :]
    out[att_rows - ATT_BEFORE : att_rows, :] += above[0:ATT_BEFORE, :]
    out[rows - MLP_BEFORE : rows, :] += above[ATT_BEFORE:, :]


def close(mine, below, above, att_rows):
    return pl.pallas_call(
        partial(close_kernel, att_rows),
        out_shape=shape(mine.shape, F32),
        in_specs=[vmem()] * 3,
        out_specs=vmem(),
        name="close",
    )(mine, below, above)


def slot_of(x, c, z, y):
    return x * 16 + c * 8 + z * 2 + y


GATHERED = [
    [
        [slot_of(i, c, z, s) if h == 0 else slot_of(s, c, z, i) for i in range(2) for z in range(4)]
        for c in range(2)
        for s in range(2)
    ]
    for h in range(2)
]
REDUCED = [
    [
        [slot_of(i, c, z, j) if h == 0 else slot_of(j, c, z, i)
         for i in range(2) for j in range(2) for z in range(4)]
        for c in range(2)
    ]
    for h in range(2)
]


def fetch_blocks(me, buffers, w, sems, first=0):
    for h in range(2):
        for k, slots in enumerate(GATHERED[h]):
            for index, slot in enumerate(slots):
                d = jnp.bitwise_xor(me, slot)

                def start(d=d, h=h, k=k, index=index):
                    source = buffers[4 * h + k].at[index]
                    pltpu.make_async_copy(source, w.at[d - first, h], sems.at[h, d]).start()

                if first:
                    pl.when(d >= first)(start)
                else:
                    start()


def wait_block(buffers, w, sems, d, h, first=0):
    pltpu.make_async_copy(buffers[0].at[0], w.at[d - first, h], sems.at[h, d]).wait()


def leaving_copies(me, buffers, w, sems):
    return [
        pltpu.make_async_copy(
            w.at[jnp.bitwise_xor(me, slot), h],
            buffers[2 * h + c].at[index],
            sems.at[h, jnp.bitwise_xor(me, slot)],
        )
        for h in range(2)
        for c in range(2)
        for index, slot in enumerate(REDUCED[h][c])
    ]


def att_scratch():
    return pltpu.VMEM((BLOCKS, 2, ATT_SENT, SUB, LANES), BF16)


def block_sems():
    return pltpu.SemaphoreType.DMA((2, BLOCKS))


def qkv_column(w, ct):
    h, place = ct // 9, ct % 9 * QKV_RT
    tiles = [w[d, h, place + rt] for d in range(QKV_BLOCKS) for rt in range(QKV_RT)]
    return jnp.concatenate(tiles, axis=0)


def wo_column(w, ct, first=QKV_BLOCKS):
    tiles = [
        w[QKV_BLOCKS - first + i, rt // 3, rt % 3 * WO_CT + ct]
        for i in range(WO_BLOCKS)
        for rt in range(WO_RT)
    ]
    return jnp.concatenate(tiles, axis=0)


def norm_rows(rows, gain, shift, source, target, step=256):
    def one(i, carry):
        at = pl.ds(pl.multiple_of(i * step, step), step)
        unit, _ = normalized(source[at, :].astype(F32))
        target[at, :] = (unit * gain + shift).astype(BF16)
        return carry

    lax.fori_loop(0, rows // step, one, 0)


def qkv_kernel(me_ref, tokens, *refs):
    buffers, (n1, qkv, small, w, sems) = refs[:8], refs[8:]
    fetch_blocks(me_ref[0], buffers, w, sems)
    for owner in OWNERS:
        for h in range(2):
            wait_block(buffers, w, sems, owner, h)
    tables = [
        jnp.concatenate([w[d, h, ATT_HALF] for h in range(2)], axis=0).astype(F32) for d in OWNERS
    ]
    small[G1 : G1 + 12, :] = tables[0][0:12]
    small[G2 : G2 + 12, :] = tables[0][12:24]
    small[B1 : B1 + 24, :] = tables[1][0:24]
    small[BQ : BQ + 12, :] = tables[2][0:12]
    small[BO : BO + 12, :] = tables[3][0:12]
    small[B2 : B2 + 12, :] = tables[3][12:24]
    small[SMALL - 4 :, :] = jnp.zeros((4, LANES), F32)
    rows = tokens.shape[0]
    norm_rows(rows, row_of(small, G1, 6), row_of(small, C1, 6), tokens, n1)
    for d in range(BLOCKS):
        for h in range(2):
            if d not in OWNERS:
                wait_block(buffers, w, sems, d, h)
    bias = jnp.concatenate(
        [row_of(small, BQ, 6), jnp.zeros((1, 768), F32), row_of(small, BV, 6)], axis=1
    )
    for c in range(QKV_CT // 2):
        weight = jnp.concatenate([qkv_column(w, 2 * c), qkv_column(w, 2 * c + 1)], axis=1)
        lanes = slice(256 * c, 256 * c + 256)
        qkv[:, lanes] = (mm(n1[...], weight, NN) + bias[:, lanes]).astype(BF16)


def project_qkv(me, tokens, att):
    rows, width = tokens.shape
    return pl.pallas_call(
        qkv_kernel,
        out_shape=(
            shape((rows, width), BF16),
            shape((rows, 3 * width), BF16),
            shape((SMALL, LANES), F32),
        ),
        in_specs=[smem(), vmem()] + [anywhere()] * 8,
        out_specs=(vmem(), vmem(), vmem()),
        scratch_shapes=[att_scratch(), block_sems()],
        compiler_params=pltpu.CompilerParams(vmem_limit_bytes=40 * MEGA),
        cost_estimate=cost(6 * rows * width * width, 12 * rows * width),
        name="qkv_forward",
    )(me, tokens, *att)


CLASSES = (128, 256, 384, 512, 768)


def head_masked(block):
    lane = lax.broadcasted_iota(jnp.int32, block.shape, 1)
    zero = jnp.zeros_like(block)
    return jnp.concatenate(
        [jnp.where(lane < 64, block, zero), jnp.where(lane >= 64, block, zero)], axis=0
    )


def pick_heads(both):
    return jnp.concatenate([both[0:64, 0:QB], both[64:128, QB : 2 * QB]], axis=0)


def lane_block(p, group):
    return pl.ds(pl.multiple_of((group * 6 + p) * LANES, LANES), LANES)


def mask_bias(start, width, b, key_ids, query_ids, bias):
    for j in range(width // QB):
        at = pl.ds(pl.multiple_of(start + j * QB, SUB), QB)
        same = key_ids[at, :] == query_ids[pl.ds(b, 1), :]
        bias[j * QB : (j + 1) * QB, :] = jnp.where(same, 0.0, NEGATIVE)


def attend_kernel(windows, qkv, key_ids, query_ids, mixed, stats, bias, scores):
    blocks = qkv.shape[0] // QB

    def one_block(b, carry):
        start = pl.multiple_of(windows[0, b], SUB)
        rows = pl.ds(pl.multiple_of(b * QB, QB), QB)
        for index, width in enumerate(CLASSES):

            @pl.when(windows[1, b] == index)
            def _(width=width):
                mask_bias(start, width, b, key_ids, query_ids, bias)
                pieces = [slice(j * QB, (j + 1) * QB) for j in range(width // QB)]

                def one_pair(p, inner):
                    queries = head_masked(qkv[rows, lane_block(p, 0)] * 0.125)
                    highest = jnp.full((8, 2 * QB), NEGATIVE, F32)
                    for piece in pieces:
                        at = pl.ds(pl.multiple_of(start + piece.start, SUB), QB)
                        part = mm(qkv[at, lane_block(p, 1)], queries, NT)
                        part = part + jnp.concatenate([bias[piece, :]] * 2, axis=1)
                        scores[piece, :] = part
                        highest = jnp.maximum(
                            highest, jnp.max(part.reshape(QB // 8, 8, 2 * QB), axis=0)
                        )
                    highest = jnp.max(highest, axis=0, keepdims=True)
                    summed = jnp.zeros((8, 2 * QB), F32)
                    both = jnp.zeros((LANES, 2 * QB), F32)
                    for piece in pieces:
                        at = pl.ds(pl.multiple_of(start + piece.start, SUB), QB)
                        raised = jnp.exp(scores[piece, :] - highest)
                        summed = summed + fold8(raised)
                        both = both + mm(qkv[at, lane_block(p, 2)], raised.astype(BF16), TN)
                    inverse = 1.0 / total(summed)
                    out = pick_heads(both * inverse)
                    mixed[rows, lane_block(p, 0)] = out.T.astype(BF16)
                    stats[b * 6 + p, 0:1, :] = highest
                    stats[b * 6 + p, 1:2, :] = inverse
                    return inner

                lax.fori_loop(0, 6, one_pair, 0, unroll=2)

        return carry

    lax.fori_loop(0, blocks, one_block, 0)


def attend(windows, qkv, key_ids, query_ids):
    rows = qkv.shape[0]
    width = qkv.shape[1] // 3
    return pl.pallas_call(
        attend_kernel,
        out_shape=(shape((rows, width), BF16), shape((rows // QB * 6, 2, 2 * QB), F32)),
        in_specs=[smem(), vmem(), vmem(), vmem()],
        out_specs=(vmem(), vmem()),
        scratch_shapes=[
            pltpu.VMEM((CLASSES[-1], QB), F32),
            pltpu.VMEM((CLASSES[-1], 2 * QB), F32),
        ],
        compiler_params=pltpu.CompilerParams(vmem_limit_bytes=40 * MEGA),
        cost_estimate=cost(2 * rows * rows * width, 8 * rows * width, 4 * rows * rows),
        name="attend_forward",
    )(windows, qkv, key_ids, query_ids)


def wo_scratch():
    return pltpu.VMEM((WO_BLOCKS, 2, ATT_SENT, SUB, LANES), BF16)


def wait_wo(buffers, w, sems):
    for i in range(WO_BLOCKS):
        for h in range(2):
            wait_block(buffers, w, sems, QKV_BLOCKS + i, h, QKV_BLOCKS)


def join_kernel(me_ref, tokens, mixed, small, *refs):
    buffers, (x1, branch, n2, w, sems) = refs[:8], refs[8:]
    fetch_blocks(me_ref[0], buffers, w, sems, QKV_BLOCKS)
    rows = tokens.shape[0]
    bias, scale = row_of(small, BO, 6), row_of(small, S1, 6)
    gain, shift = row_of(small, G2, 6), row_of(small, C2, 6)
    wait_wo(buffers, w, sems)
    for c in range(3):
        weight = jnp.concatenate([wo_column(w, 2 * c), wo_column(w, 2 * c + 1)], axis=1)
        lanes = slice(256 * c, 256 * c + 256)
        branch[:, lanes] = mm(mixed[...], weight, NN) + bias[:, lanes]
    step = 128

    def one(i, carry):
        at = pl.ds(pl.multiple_of(i * step, step), step)
        values = tokens[at, :].astype(F32) + scale * branch[at, :]
        x1[at, :] = values
        unit, _ = normalized(values)
        n2[at, :] = (unit * gain + shift).astype(BF16)
        return carry

    lax.fori_loop(0, rows // step, one, 0)


def join(me, tokens, mixed, small, att):
    rows, width = tokens.shape
    return pl.pallas_call(
        join_kernel,
        out_shape=(
            shape((rows, width), F32),
            shape((rows, width), F32),
            shape((rows, width), BF16),
        ),
        in_specs=[smem(), vmem(), vmem(), vmem()] + [anywhere()] * 8,
        out_specs=(vmem(), vmem(), vmem()),
        scratch_shapes=[
            wo_scratch(),
            block_sems(),
        ],
        compiler_params=pltpu.CompilerParams(vmem_limit_bytes=40 * MEGA),
        cost_estimate=cost(2 * rows * width * width, 14 * rows * width),
        name="project_and_norm",
    )(me, tokens, mixed, small, *att)


def w1_columns(w, f, c):
    columns = []
    for ct in (2 * c, 2 * c + 1):
        place = MLP_HALF // 2 * (f % 2) + ct * W1_RT
        tiles = [w[d, f // 2, place + rt] for d in range(W1_BLOCKS) for rt in range(W1_RT)]
        columns.append(jnp.concatenate(tiles, axis=0))
    return jnp.concatenate(columns, axis=1)


def w2_place(f, row, ct):
    rt = row % W2_RT
    return W1_BLOCKS + 4 * f + row // W2_RT, rt // 6, rt % 6 * W2_CT + ct


def w2_rows(w, f, c):
    columns = []
    for ct in range(W2_CT):
        tiles = [w[w2_place(f, row, ct)] for row in range(SUB * c, SUB * c + SUB)]
        columns.append(jnp.concatenate(tiles, axis=0))
    return jnp.concatenate(columns, axis=1)


TALL = 256
PARTS = CHUNK // 256


def mlp_kernel(me_ref, n2, cot, x1, small, *refs):
    arriving, refs = refs[:8], refs[8:]
    out, dx1, vectors, *leaving = refs[:7]
    w, macc, dnacc, dm, u, dz, zs, dus, bias_sums, b1_lines, sums, sems = refs[7:]
    me = me_ref[0]
    rows, width = n2.shape
    tiles = rows // TALL
    fetch_blocks(me, arriving, w, sems)
    scale = row_of(small, S2, 6)
    step = 128

    def prepare(i, carry):
        at = pl.ds(pl.multiple_of(i * step, step), step)
        rounded = (cot[at, :].astype(F32) * scale).astype(BF16)
        dm[at, :] = rounded
        return carry + fold8(rounded.astype(F32))

    zero = jnp.zeros((8, width), F32)
    gb2 = lax.fori_loop(0, rows // step, prepare, zero)
    bias_sums[...] = jnp.zeros_like(bias_sums)

    units = [(t, c) for c in range(PARTS) for t in range(tiles)]

    def lanes_of(f, c):
        return pl.ds(pl.multiple_of(CHUNK * f + 256 * c, 256), 256)

    def one_chunk(f, carry):
        @pl.when((f & 1) == 0)
        def _():
            for d in range(W1_BLOCKS):
                wait_block(arriving, w, sems, d, f >> 1)

        for k in range(4):
            for h in range(2):
                wait_block(arriving, w, sems, W1_BLOCKS + 4 * f + k, h)

        def multiply(unit, slot):
            t, c = unit
            at = slice(TALL * t, TALL * t + TALL)
            zs[slot] = mm(n2[at, :], w1_columns(w, f, c), NN)
            dus[slot] = mm(dm[at, :], w2_rows(w, f, c), NT)

        def activate(unit, slot):
            t, c = unit
            lanes = lanes_of(f, c)
            bias = b1_lines[pl.ds(f, 1), 256 * c : 256 * c + 256]
            folded = jnp.zeros((8, 256), F32)
            for r in range(TALL // 32):
                part = slice(32 * r, 32 * r + 32)
                place = slice(TALL * t + 32 * r, TALL * t + 32 * r + 32)
                value, slope = gelu_pair(zs[slot, part, :] + bias)
                u[place, lanes] = value.astype(BF16)
                rounded = (dus[slot, part, :] * slope).astype(BF16)
                dz[place, lanes] = rounded
                folded = folded + fold8(rounded.astype(F32))
            bias_sums[:, lanes] += folded

        multiply(units[0], 0)
        for i, unit in enumerate(units):
            if i + 1 < len(units):
                multiply(units[i + 1], (i + 1) % 2)
            activate(unit, i % 2)
        return carry

    for f in range(CHUNKS):
        b1_lines[f : f + 1, :] = row_of(small, B1 + 6 * f, 6)
    lax.fori_loop(0, CHUNKS, one_chunk, 0)

    bias, gain = row_of(small, B2, 6), row_of(small, G2, 6)
    sums[...] = jnp.zeros_like(sums)

    def finish(t):
        for half in range(TALL // step):
            at = pl.ds(pl.multiple_of(TALL * t + step * half, step), step)
            upstream = cot[at, :].astype(F32)
            values = x1[at, :]
            contracted = macc[at, :] + bias
            out[at, :] = (values + scale * contracted).astype(BF16)
            unit, inverse = normalized(values)
            grad = dnacc[at, :]
            dx1[at, :] = upstream + norm_pullback(unit, inverse, grad, gain)
            sums[0:8, :] += fold8(grad * unit)
            sums[8:16, :] += fold8(grad)
            sums[16:24, :] += fold8(upstream * contracted)

    every = [(f, c) for f in range(CHUNKS) for c in range(PARTS)]

    def contract(t):
        at = pl.ds(pl.multiple_of(TALL * t, TALL), TALL)
        second = jnp.concatenate([w2_rows(w, f, c) for f, c in every], axis=0)
        first = jnp.concatenate([w1_columns(w, f, c) for f, c in every], axis=1)
        macc[at, :] = mm(u[at, :], second, NN)
        dnacc[at, :] = mm(dz[at, :], first, NT)

    def one_tile(t, carry):
        contract(t)
        finish(t - 1)
        return carry

    contract(0)
    lax.fori_loop(1, tiles, one_tile, 0)
    finish(tiles - 1)

    def one_grad(f, carry):
        for c in range(PARTS):
            grad = mm(u[:, lanes_of(f, c)], dm[...], TN)
            for r in range(SUB):
                for ct in range(W2_CT):
                    tile = grad[SUB * r : SUB * r + SUB, LANES * ct : LANES * ct + LANES]
                    w[w2_place(f, SUB * c + r, ct)] = tile.astype(BF16)
        chunk = pl.ds(pl.multiple_of(CHUNK * f, CHUNK), CHUNK)
        base = MLP_HALF // 2 * (f & 1)
        for c in range(PARTS):
            lanes = slice(256 * c, 256 * c + 256)
            grad = mm(n2[:, lanes], dz[:, chunk], TN)
            for r in range(SUB):
                d, rt = (SUB * c + r) // W1_RT, (SUB * c + r) % W1_RT
                for ct in range(6):
                    tile = grad[SUB * r : SUB * r + SUB, LANES * ct : LANES * ct + LANES]
                    w[d, f >> 1, base + ct * W1_RT + rt] = tile.astype(BF16)
        return carry

    lax.fori_loop(0, CHUNKS, one_grad, 0)
    copies = leaving_copies(me, leaving, w, sems)
    fetch(copies)
    put_row(vectors, G2 - G2, total(sums[0:8, :]))
    put_row(vectors, C2 - G2, total(sums[8:16, :]))
    put_row(vectors, B1 - G2, total(bias_sums[...]))
    put_row(vectors, B2 - G2, total(gb2))
    put_row(vectors, S2 - G2, total(sums[16:24, :]))
    settle(copies)


def feed_forward(me, n2, cot, x1, small, mlp):
    rows, width = n2.shape
    half = shape((HALF_BLOCKS, MLP_HALF, SUB, LANES), BF16)
    return pl.pallas_call(
        mlp_kernel,
        out_shape=(
            shape((rows, width), BF16),
            shape((rows, width), F32),
            shape((48, LANES), F32),
            half,
            half,
            half,
            half,
        ),
        in_specs=[smem(), vmem(), vmem(), vmem(), vmem()] + [anywhere()] * 8,
        out_specs=(vmem(), vmem(), vmem()) + (anywhere(),) * 4,
        scratch_shapes=[
            pltpu.VMEM((BLOCKS, 2, MLP_HALF, SUB, LANES), BF16),
            pltpu.VMEM((rows, width), F32),
            pltpu.VMEM((rows, width), F32),
            pltpu.VMEM((rows, width), BF16),
            pltpu.VMEM((rows, FF), BF16),
            pltpu.VMEM((rows, FF), BF16),
            pltpu.VMEM((2, TALL, 256), F32),
            pltpu.VMEM((2, TALL, 256), F32),
            pltpu.VMEM((8, FF), F32),
            pltpu.VMEM((CHUNKS, CHUNK), F32),
            pltpu.VMEM((24, width), F32),
            block_sems(),
        ],
        compiler_params=pltpu.CompilerParams(vmem_limit_bytes=58 * MEGA),
        cost_estimate=cost(12 * rows * width * FF, 40 * MEGA),
        name="feed_forward",
    )(me, n2, cot, x1, small, *mlp)


def split_kernel(me_ref, dx1, branch, mixed, small, *refs):
    buffers, (da, vectors, gwo, w, db, sems) = refs[:8], refs[8:]
    fetch_blocks(me_ref[0], buffers, w, sems, QKV_BLOCKS)
    rows = dx1.shape[0]
    scale = row_of(small, S1, 6)
    step = 128

    def one(i, carry):
        gs1, gbo = carry
        at = pl.ds(pl.multiple_of(i * step, step), step)
        grad = dx1[at, :]
        rounded = (grad * scale).astype(BF16)
        db[at, :] = rounded
        return gs1 + fold8(grad * branch[at, :]), gbo + fold8(rounded.astype(F32))

    zero = jnp.zeros((8, 768), F32)
    gs1, gbo = lax.fori_loop(0, rows // step, one, (zero, zero))
    put_row(vectors, 0, total(gbo))
    put_row(vectors, 6, total(gs1))
    wait_wo(buffers, w, sems)
    weight = jnp.concatenate([wo_column(w, ct) for ct in range(WO_CT)], axis=1)
    for c in range(3):
        lanes = slice(256 * c, 256 * c + 256)
        da[:, lanes] = mm(db[...], weight[lanes, :], NT).astype(BF16)
    for c in range(3):
        grad = mm(mixed[:, 256 * c : 256 * c + 256], db[...], TN)
        for r in range(SUB):
            tile_row = SUB * c + r
            i, rt = tile_row // WO_RT, tile_row % WO_RT
            for ct in range(WO_CT):
                tile = grad[SUB * r : SUB * r + SUB, LANES * ct : LANES * ct + LANES]
                gwo[i, rt // 3, rt % 3 * WO_CT + ct] = tile.astype(BF16)


def split(me, dx1, branch, mixed, small, att):
    rows, width = dx1.shape
    return pl.pallas_call(
        split_kernel,
        out_shape=(
            shape((rows, width), BF16),
            shape((12, LANES), F32),
            shape((WO_BLOCKS, 2, ATT_HALF, SUB, LANES), BF16),
        ),
        in_specs=[smem(), vmem(), vmem(), vmem(), vmem()] + [anywhere()] * 8,
        out_specs=(vmem(), vmem(), vmem()),
        scratch_shapes=[wo_scratch(), pltpu.VMEM((rows, width), BF16), block_sems()],
        compiler_params=pltpu.CompilerParams(vmem_limit_bytes=40 * MEGA),
        cost_estimate=cost(4 * rows * width * width, 14 * rows * width),
        name="project_backward",
    )(me, dx1, branch, mixed, small, *att)


def attend_back_kernel(
    windows, qkv, da, stats, key_ids, query_ids, dqkv, bias, probs, dprobs, dkeys, dvalues
):
    blocks = qkv.shape[0] // QB

    def clear(b, carry):
        rows = pl.ds(pl.multiple_of(b * QB, QB), QB)
        dkeys[rows, :] = jnp.zeros((QB, dkeys.shape[1]), F32)
        dvalues[rows, :] = jnp.zeros((QB, dkeys.shape[1]), F32)
        return carry

    lax.fori_loop(0, blocks, clear, 0)

    def one_block(b, carry):
        start = pl.multiple_of(windows[0, b], SUB)
        rows = pl.ds(pl.multiple_of(b * QB, QB), QB)
        for index, width in enumerate(CLASSES):

            @pl.when(windows[1, b] == index)
            def _(width=width):
                mask_bias(start, width, b, key_ids, query_ids, bias)
                pieces = [slice(j * QB, (j + 1) * QB) for j in range(width // QB)]

                def one_pair(p, inner):
                    queries = head_masked(qkv[rows, lane_block(p, 0)] * 0.125)
                    grads = head_masked(da[rows, lane_block(p, 0)])
                    highest = stats[b * 6 + p, 0:1, :]
                    inverse = stats[b * 6 + p, 1:2, :]
                    inner_sum = jnp.zeros((8, 2 * QB), F32)
                    for piece in pieces:
                        at = pl.ds(pl.multiple_of(start + piece.start, SUB), QB)
                        part = mm(qkv[at, lane_block(p, 1)], queries, NT)
                        part = part + jnp.concatenate([bias[piece, :]] * 2, axis=1)
                        weight = jnp.exp(part - highest) * inverse
                        dweight = mm(qkv[at, lane_block(p, 2)], grads, NT)
                        inner_sum = inner_sum + fold8(weight * dweight)
                        probs[piece, :] = weight
                        dprobs[piece, :] = dweight
                        dvalues[at, lane_block(p, 0)] += mm(weight.astype(BF16), grads, NN)
                    inner_sum = total(inner_sum)
                    both = jnp.zeros((LANES, 2 * QB), F32)
                    for piece in pieces:
                        at = pl.ds(pl.multiple_of(start + piece.start, SUB), QB)
                        dscore = probs[piece, :] * (dprobs[piece, :] - inner_sum)
                        dscore = dscore.astype(BF16)
                        dkeys[at, lane_block(p, 0)] += mm(dscore, queries, NN)
                        both = both + mm(qkv[at, lane_block(p, 1)], dscore, TN)
                    out = pick_heads(both) * 0.125
                    dqkv[rows, lane_block(p, 0)] = out.T.astype(BF16)
                    return inner

                lax.fori_loop(0, 6, one_pair, 0, unroll=2)

        return carry

    lax.fori_loop(0, blocks, one_block, 0)
    width = dkeys.shape[1]

    def store(b, carry):
        rows = pl.ds(pl.multiple_of(b * 32, 32), 32)
        dqkv[rows, width : 2 * width] = dkeys[rows, :].astype(BF16)
        dqkv[rows, 2 * width :] = dvalues[rows, :].astype(BF16)
        return carry

    lax.fori_loop(0, qkv.shape[0] // 32, store, 0)


def attend_back(windows, qkv, da, stats, key_ids, query_ids):
    rows, triple = qkv.shape
    width = triple // 3
    return pl.pallas_call(
        attend_back_kernel,
        out_shape=shape((rows, triple), BF16),
        in_specs=[smem()] + [vmem()] * 5,
        out_specs=vmem(),
        scratch_shapes=[
            pltpu.VMEM((CLASSES[-1], QB), F32),
            pltpu.VMEM((CLASSES[-1], 2 * QB), F32),
            pltpu.VMEM((CLASSES[-1], 2 * QB), F32),
            pltpu.VMEM((rows, width), F32),
            pltpu.VMEM((rows, width), F32),
        ],
        compiler_params=pltpu.CompilerParams(vmem_limit_bytes=48 * MEGA),
        cost_estimate=cost(6 * rows * rows * width, 14 * rows * width, 4 * rows * rows),
        name="attend_backward",
    )(windows, qkv, da, stats, key_ids, query_ids)


def qkv_back_kernel(me_ref, tokens, n1, dx1, dqkv, small, proj, mlp, gwo, *refs):
    arriving, refs = refs[:8], refs[8:]
    dx, *leaving = refs[:5]
    w, dn, sums, table, sems = refs[5:]
    me = me_ref[0]
    fetch_blocks(me, arriving, w, sems)
    rows = tokens.shape[0]
    zero = jnp.zeros((8, 768), F32)

    def column_sums(i, carry):
        at = pl.ds(pl.multiple_of(i * 128, 128), 128)
        return (
            carry[0] + fold8(dqkv[at, 0:768].astype(F32)),
            carry[1] + fold8(dqkv[at, 1536:2304].astype(F32)),
        )

    gbq, gbv = lax.fori_loop(0, rows // 128, column_sums, (zero, zero))
    sums[...] = jnp.zeros_like(sums)
    gain = row_of(small, G1, 6)
    for d in range(BLOCKS):
        for h in range(2):
            wait_block(arriving, w, sems, d, h)

    def contract(t):
        at = pl.ds(pl.multiple_of(TALL * t, TALL), TALL)
        weight = jnp.concatenate([qkv_column(w, ct) for ct in range(QKV_CT)], axis=1)
        dn[at, :] = mm(dqkv[at, :], weight, NT)

    def finish(t):
        for half in range(TALL // 128):
            at = pl.ds(pl.multiple_of(TALL * t + 128 * half, 128), 128)
            unit, inverse = normalized(tokens[at, :].astype(F32))
            grad = dn[at, :]
            dx[at, :] = dx1[at, :] + norm_pullback(unit, inverse, grad, gain)
            sums[0:8, :] += fold8(grad * unit)
            sums[8:16, :] += fold8(grad)

    def one_tile(t, carry):
        contract(t)
        finish(t - 1)
        return carry

    contract(0)
    lax.fori_loop(1, rows // TALL, one_tile, 0)
    finish(rows // TALL - 1)

    def put_table(owner, *places):
        table[...] = jnp.zeros_like(table)
        for place, values in places:
            if values.shape[1] == LANES:
                table[place : place + values.shape[0], :] = values
            else:
                put_row(table, place, values)
        for h in range(2):
            w[owner, h, ATT_HALF] = table[SUB * h : SUB * h + SUB, :].astype(BF16)

    put_table(
        OWNERS[0], (0, total(sums[0:8, :])), (6, total(sums[8:16, :])), (12, mlp[0:12, :])
    )
    put_table(OWNERS[1], (0, mlp[B1 - G2 : B1 - G2 + 24, :]))
    put_table(OWNERS[2], (0, total(gbq)), (6, total(gbv)))
    put_table(OWNERS[3], (0, proj[...]), (12, mlp[B2 - G2 : B2 - G2 + 12, :]))
    for i in range(WO_BLOCKS):
        for h in range(2):
            w[QKV_BLOCKS + i, h, 0:ATT_HALF] = gwo[i, h]
    for c in range(3):
        for half in range(2):
            columns = slice(1152 * half, 1152 * half + 1152)
            grad = mm(n1[:, 256 * c : 256 * c + 256], dqkv[:, columns], TN)
            for r in range(SUB):
                d, rt = (SUB * c + r) // QKV_RT, (SUB * c + r) % QKV_RT
                for ct in range(9):
                    tile = grad[SUB * r : SUB * r + SUB, LANES * ct : LANES * ct + LANES]
                    w[d, half, ct * QKV_RT + rt] = tile.astype(BF16)
    copies = leaving_copies(me, leaving, w, sems)
    fetch(copies)
    settle(copies)


def qkv_back(me, tokens, n1, dx1, dqkv, small, proj, mlp, gwo, att):
    rows, width = tokens.shape
    half = shape((HALF_BLOCKS, ATT_SENT, SUB, LANES), BF16)
    return pl.pallas_call(
        qkv_back_kernel,
        out_shape=(shape((rows, width), F32), half, half, half, half),
        in_specs=[smem()] + [vmem()] * 8 + [anywhere()] * 8,
        out_specs=(vmem(),) + (anywhere(),) * 4,
        scratch_shapes=[
            att_scratch(),
            pltpu.VMEM((rows, width), F32),
            pltpu.VMEM((16, width), F32),
            pltpu.VMEM((2 * SUB, LANES), F32),
            block_sems(),
        ],
        compiler_params=pltpu.CompilerParams(vmem_limit_bytes=48 * MEGA),
        cost_estimate=cost(12 * rows * width * width, 30 * rows * width),
        name="qkv_backward",
    )(me, tokens, n1, dx1, dqkv, small, proj, mlp, gwo, *att)


X, C, Z1, Z0, Y = 16, 8, 4, 2, 1


def exchange(values, bit):
    return lax.ppermute(values, AXES, [(d, d ^ bit) for d in range(BLOCKS)])


def shifted(values, by):
    pairs = [(d, d + by) for d in range(BLOCKS) if 0 <= d + by < BLOCKS]
    return lax.ppermute(values, AXES, pairs)


def together(*values):
    return lax.optimization_barrier(values)


def along_z(first, second, received):
    return (
        jnp.stack([first] + [r[0] for r in received]),
        jnp.stack([second] + [r[1] for r in received]),
    )


def joined(own, received):
    return jnp.concatenate([own, received])


def sum_terms(terms):
    summed = terms[0].astype(F32)
    for term in terms[1:]:
        summed = summed + term.astype(F32)
    return summed


def kept(terms):
    return [t[: t.shape[0] // 2] for t in terms]


def sent(terms):
    return sum_terms([t[t.shape[0] // 2 :] for t in terms]).astype(BF16)


def attention_amounts(width):
    return [width, width, 3 * width * width, width, width, width * width, width, width]


def feedforward_amounts(width):
    return [width, width, width * FF, FF, FF * width, width, width]


def pieces_of(vector, amounts):
    out, offset = [], 0
    for amount in amounts:
        out.append(vector[offset : offset + amount])
        offset += amount
    return out


def tiles_by_column(matrix, blocks, rt):
    ct = matrix.shape[1] // LANES
    return matrix.reshape(blocks, rt, SUB, ct, LANES).transpose(0, 3, 1, 2, 4)


def tiles_by_row(matrix, blocks, rt):
    ct = matrix.shape[1] // LANES
    return matrix.reshape(blocks, rt, SUB, ct, LANES).transpose(0, 1, 3, 2, 4)


def gather_plainly(params, att_rows, width):
    rounded = params.astype(BF16)
    att = lax.all_gather(rounded[:att_rows], AXES, axis=0, tiled=True).reshape(-1)
    mlp = lax.all_gather(rounded[att_rows:], AXES, axis=0, tiled=True).reshape(-1)
    g1, c1, wqkv, bq, bv, wo, bo, s1 = pieces_of(att, attention_amounts(width))
    g2, c2, w1, b1, w2, b2, s2 = pieces_of(mlp, feedforward_amounts(width))
    tile = (SUB, LANES)
    att = jnp.concatenate(
        [
            tiles_by_column(wqkv.reshape(width, -1), QKV_BLOCKS, QKV_RT).reshape((-1, 36) + tile),
            tiles_by_row(wo.reshape(width, -1), WO_BLOCKS, WO_RT).reshape((-1, 36) + tile),
        ]
    )
    mlp = jnp.concatenate(
        [
            tiles_by_column(w1.reshape(width, -1), W1_BLOCKS, W1_RT).reshape((-1, 72) + tile),
            tiles_by_row(w2.reshape(FF, -1), W2_BLOCKS, W2_RT).reshape((-1, 72) + tile),
        ]
    )
    vectors = jnp.concatenate([g1, c1, bq, bv, bo, s1, g2, c2, b1, b2, s2]).astype(F32)
    lines = vectors.reshape(-1, LANES)
    sent = jnp.zeros((BLOCKS, 2 * SUB, LANES), F32)
    for owner, place, first, count in (
        (OWNERS[0], 0, G1, 12),
        (OWNERS[0], 12, G2, 12),
        (OWNERS[1], 0, B1, 24),
        (OWNERS[2], 0, BQ, 12),
        (OWNERS[3], 0, BO, 12),
        (OWNERS[3], 12, B2, 12),
    ):
        sent = sent.at[owner, place : place + count].set(lines[first : first + count])
    sent = sent.astype(BF16).reshape((BLOCKS, 2, 1) + tile)
    att = [jnp.concatenate([att[:, 18 * h : 18 * h + 18], sent[:, h]], axis=1) for h in range(2)]
    return by_slot(*att), by_slot(mlp[:, :36], mlp[:, 36:])


def by_slot(first, second):
    halves = (first, second)
    return [
        jnp.stack([halves[h][slot] for slot in slots]) for h in range(2) for slots in GATHERED[h]
    ]


def from_slots(buffers):
    halves = []
    for h in range(2):
        blocks = [None] * BLOCKS
        for c in range(2):
            for index, slot in enumerate(REDUCED[h][c]):
                blocks[slot] = buffers[2 * h + c][index]
        halves.append(jnp.stack(blocks))
    return halves


def reduce_plainly(gatt, gmlp, att_rows, mlp_rows, width, devices):
    first, second = from_slots(gatt)
    vectors = jnp.concatenate([first[:, ATT_HALF:], second[:, ATT_HALF:]], axis=1).astype(F32)
    vectors = vectors.reshape(BLOCKS, 2 * SUB, LANES)
    att = jnp.concatenate([first[:, :ATT_HALF], second[:, :ATT_HALF]], axis=1).astype(F32)
    mlp = jnp.concatenate(from_slots(gmlp), axis=1).astype(F32)
    five = lambda v, dims: v.reshape((v.shape[0],) + dims + (SUB, LANES))
    wqkv = five(att[:QKV_BLOCKS], (QKV_CT, QKV_RT)).transpose(0, 2, 3, 1, 4).reshape(-1)
    wo = five(att[QKV_BLOCKS:], (WO_RT, WO_CT)).transpose(0, 1, 3, 2, 4).reshape(-1)
    w1 = five(mlp[:W1_BLOCKS], (W1_CT, W1_RT)).transpose(0, 2, 3, 1, 4).reshape(-1)
    w2 = five(mlp[W1_BLOCKS:], (W2_RT, W2_CT)).transpose(0, 1, 3, 2, 4).reshape(-1)
    line = lambda owner, first, count: vectors[owner, first : first + count].reshape(-1)
    att = [line(OWNERS[0], 0, 12), wqkv, line(OWNERS[2], 0, 12), wo, line(OWNERS[3], 0, 12)]
    mlp = [line(OWNERS[0], 12, 12), w1, line(OWNERS[1], 0, 24), w2, line(OWNERS[3], 12, 12)]

    def lay(parts, rows):
        vector = jnp.concatenate(parts)
        vector = jnp.pad(vector, (0, devices * rows * LANES - vector.shape[0]))
        return vector.reshape(devices, rows, LANES)

    whole = jnp.concatenate([lay(att, att_rows), lay(mlp, mlp_rows)], axis=1)
    return lax.psum_scatter(whole.reshape(-1, LANES), AXES, scatter_dimension=0, tiled=True)


def key_windows(segments, real):
    length = segments.shape[0]
    position = jnp.arange(length, dtype=jnp.int32)
    ids = jnp.where(real, segments, length + position)
    first = segments[0::QB]
    final = segments[QB - 1 :: QB]
    begin = jnp.sum((segments[None, :] < first[:, None]).astype(jnp.int32), axis=1)
    begin = jnp.where(real[0::QB], begin, position[0::QB])
    end = jnp.sum(((segments[None, :] <= final[:, None]) & real[None, :]).astype(jnp.int32), axis=1)
    end = jnp.where(real[QB - 1 :: QB], end, position[QB - 1 :: QB] + 1)
    begin = begin // SUB * SUB
    need = end - begin
    kind = sum((need > width).astype(jnp.int32) for width in CLASSES[:-1])
    widths = sum(
        jnp.where(kind == i, width, 0) for i, width in enumerate(CLASSES)
    )
    begin = jnp.minimum(begin, length - widths)
    return ids, jnp.stack([begin, kind]).astype(jnp.int32)


def local(tokens, cotangent, segment_ids, pad_mask, lengths, params):
    rows, width = tokens.shape
    wide, narrow = lax.axis_size("wide"), lax.axis_size("narrow")
    devices = wide * narrow
    att_count = 4 * width * width + 6 * width
    att_rows = (att_count // LANES + devices - 1) // devices
    mlp_rows = params.shape[0] - att_rows
    paired = (wide, narrow) == (4, 8)
    scale = 1.0 / math.sqrt(rows * devices)

    position = jnp.arange(rows, dtype=jnp.int32)
    real = (pad_mask > 0) & (position < lengths[0])
    ids, windows = key_windows(segment_ids, real)
    key_ids = ids.reshape(rows, 1)
    query_ids = ids.reshape(rows // QB, QB)

    if not paired:
        me = jnp.zeros((1,), jnp.int32)
        att, mlp = gather_plainly(params, att_rows, width)
        n1, qkv, small = project_qkv(me, tokens, att)
        mixed, stats = attend(windows, qkv, key_ids, query_ids)
        x1, branch, n2 = join(me, tokens, mixed, small, att)
        output, dx1, small_mlp, *gmlp = feed_forward(me, n2, cotangent, x1, small, mlp)
        da, small_proj, gwo = split(me, dx1, branch, mixed, small, att)
        dqkv = attend_back(windows, qkv, da, stats, key_ids, query_ids)
        grad_input, *gatt = qkv_back(
            me, tokens, n1, dx1, dqkv, small, small_proj, small_mlp, gwo, att
        )
        owned = reduce_plainly(gatt, gmlp, att_rows, mlp_rows, width, devices)
        return output, grad_input, owned * scale

    me = lax.axis_index(AXES).astype(jnp.int32).reshape(1)
    tails = jnp.concatenate([params[att_rows - ATT_BEFORE : att_rows], params[-MLP_BEFORE:]])
    heads = jnp.concatenate([params[:ATT_AFTER], params[att_rows : att_rows + MLP_AFTER]])
    tails, heads = shifted(tails, 1), shifted(heads, -1)
    att_own, mlp_own = pack(me, params, tails, heads, att_rows)

    got = [exchange(att_own, k * Z0) for k in range(1, 4)]
    a, b = along_z(att_own[0], att_own[1], got)
    a, b, mlp_own = together(a, b, mlp_own)
    ax, by = exchange(a, X), exchange(b, Y)
    z1, z3 = exchange(mlp_own, Z0), exchange(mlp_own, 3 * Z0)
    a, b = joined(a, ax), joined(b, by)
    a, b, z1, z3, mlp_own = together(a, b, z1, z3, mlp_own)
    ay, bx = exchange(a, Y), exchange(b, X)
    ac, bc = exchange(a, C), exchange(b, C)
    z2 = exchange(mlp_own, 2 * Z0)
    m, n = along_z(mlp_own[0], mlp_own[1], [z1, z2, z3])
    ay, bx, ac, bc, m, n = together(ay, bx, ac, bc, m, n)
    ayc, bxc = exchange(ay, C), exchange(bx, C)
    att = together(a, ay, ac, ayc, b, bx, bc, bxc, m, n, tokens)
    *att, m, n, tokens_now = att
    mx, ny = exchange(m, X), exchange(n, Y)
    n1, qkv, small = project_qkv(me, tokens_now, att)
    m, n = joined(m, mx), joined(n, ny)
    m, n, qkv = together(m, n, qkv)
    my, nx = exchange(m, Y), exchange(n, X)
    mc, nc = exchange(m, C), exchange(n, C)
    mixed, stats = attend(windows, qkv, key_ids, query_ids)
    x1, branch, n2 = join(me, tokens, mixed, small, att)
    m, n, my, nx, mc, nc, n2 = together(m, n, my, nx, mc, nc, n2)
    myc, nxc = exchange(my, C), exchange(nx, C)
    mlp = (m, my, mc, myc, n, nx, nc, nxc)

    output, dx1, small_mlp, *gmlp = feed_forward(me, n2, cotangent, x1, small, mlp)

    mc, nc = exchange(gmlp[1], C), exchange(gmlp[3], C)
    da, small_proj, gwo = split(me, dx1, branch, mixed, small, att)
    mc, nc, da = together(mc, nc, da)
    m, n = [gmlp[0], mc], [gmlp[2], nc]
    mx, ny, da = together(sent(m), sent(n), da)
    mx, ny = exchange(mx, X), exchange(ny, Y)
    dqkv = attend_back(windows, qkv, da, stats, key_ids, query_ids)
    mx, ny, dqkv = together(mx, ny, dqkv)
    m, n = kept(m) + [mx], kept(n) + [ny]
    my, nx, dqkv = together(sent(m), sent(n), dqkv)
    my, nx = exchange(my, Y), exchange(nx, X)
    grad_input, *gatt = qkv_back(
        me, tokens, n1, dx1, dqkv, small, small_proj, small_mlp, gwo, att
    )
    my, nx, *gatt = together(my, nx, *gatt)
    m, n = sum_terms(kept(m) + [my]), sum_terms(kept(n) + [nx])
    m_sums = jnp.stack([m, n], axis=1)
    z1, z2, z3 = [m_sums[k].astype(BF16) for k in range(1, 4)]
    z1, z2, z3, *gatt = together(z1, z2, z3, *gatt)
    ac, bc = exchange(gatt[1], C), exchange(gatt[3], C)
    z1 = exchange(z1, Z0)
    a, b = [gatt[0], ac], [gatt[2], bc]
    ax, by, z1, z2, z3 = together(sent(a), sent(b), z1, z2, z3)
    ax, by = exchange(ax, X), exchange(by, Y)
    z2 = exchange(z2, 2 * Z0)
    a, b = kept(a) + [ax], kept(b) + [by]
    ay, bx, z2, z3 = together(sent(a), sent(b), z2, z3)
    ay, bx = exchange(ay, Y), exchange(bx, X)
    z3 = exchange(z3, 3 * Z0)
    a, b = sum_terms(kept(a) + [ay]), sum_terms(kept(b) + [bx])
    a_sums = jnp.stack([a, b], axis=1)
    m_own = sum_terms([m_sums[0], z1, z2, z3])
    s1, s2, s3 = [a_sums[k].astype(BF16) for k in range(1, 4)]
    s1, s2, s3, m_own = together(s1, s2, s3, m_own)
    got = [exchange(s1, Z0), exchange(s2, 2 * Z0), exchange(s3, 3 * Z0)]
    a_own = sum_terms([a_sums[0]] + got)
    mine, to_before, to_after = spread(me, a_own, m_own, att_rows, mlp_rows, scale)
    grad_params = close(mine, shifted(to_after, 1), shifted(to_before, -1), att_rows)
    return output, grad_input, grad_params


def solution(mesh):
    return jax.shard_map(
        local,
        mesh=mesh,
        in_specs=(
            P(AXES, None),
            P(AXES, None),
            P(AXES),
            P(AXES),
            P(AXES),
            P(AXES, None),
        ),
        out_specs=(P(AXES, None), P(AXES, None), P(AXES, None)),
        check_vma=False,
    )
```

```python
import math
from functools import partial

import jax
import jax.numpy as jnp
from jax import lax
from jax.experimental import pallas as pl
from jax.experimental.pallas import tpu as pltpu
from jax.sharding import PartitionSpec as P

FF = 3072
HEADS = 12
EPSILON = 1e-06
NEGATIVE = -1e30
AXES = ("wide", "narrow")
LANES = 128
SUB = 16
QB = 128
MEGA = 1 << 20
F32 = jnp.float32
BF16 = jnp.bfloat16

BLOCKS = 32
QKV_BLOCKS, QKV_RT, QKV_CT = 24, 2, 18
WO_BLOCKS, WO_RT, WO_CT = 8, 6, 6
W1_BLOCKS, W1_RT, W1_CT = 16, 3, 24
W2_BLOCKS, W2_RT, W2_CT = 16, 12, 6
ATT_HALF, MLP_HALF = 18, 36
ATT_SENT = ATT_HALF + 1
ATT_PART = 9
HALF_BLOCKS = BLOCKS // 2
CHUNK = 768
CHUNKS = FF // CHUNK

G1, C1, BQ, BV, BO, S1 = 0, 6, 12, 18, 24, 30
G2, C2, B1, B2, S2 = 36, 42, 48, 72, 78
SMALL = 88

NT = (((1,), (1,)), ((), ()))
NN = (((1,), (0,)), ((), ()))
TN = (((0,), (0,)), ((), ()))


def mm(lhs, rhs, dims):
    return lax.dot_general(lhs, rhs, dims, preferred_element_type=F32)


def row_of(ref, first, count):
    return jnp.concatenate([ref[first + k : first + k + 1, :] for k in range(count)], axis=1)


def put_row(ref, first, values):
    for k in range(values.shape[1] // LANES):
        ref[first + k : first + k + 1, :] = values[:, k * LANES : (k + 1) * LANES]


def fold8(values):
    rows, columns = values.shape
    return jnp.sum(values.reshape(rows // 8, 8, columns), axis=0)


def total(values):
    return jnp.sum(values, axis=0, keepdims=True)


def vmem():
    return pl.BlockSpec(memory_space=pltpu.VMEM)


def smem():
    return pl.BlockSpec(memory_space=pltpu.SMEM)


def hbm():
    return pl.BlockSpec(memory_space=pltpu.HBM)


def shape(dims, kind):
    return jax.ShapeDtypeStruct(dims, kind)


def cost(flops, moved, exps=0):
    return pl.CostEstimate(flops=int(flops), transcendentals=int(exps), bytes_accessed=int(moved))


def normalized(values):
    center = values - jnp.mean(values, axis=-1, keepdims=True)
    inverse = lax.rsqrt(jnp.mean(center * center, axis=-1, keepdims=True) + EPSILON)
    return center * inverse, inverse


def norm_pullback(unit, inverse, grad, gain):
    scaled = grad * gain
    first = jnp.mean(scaled, axis=-1, keepdims=True)
    second = jnp.mean(scaled * unit, axis=-1, keepdims=True)
    return inverse * (scaled - first - unit * second)


def gelu_pair(z):
    magnitude = jnp.abs(z)
    t = 1.0 / (1.0 + (0.3275911 * math.sqrt(0.5)) * magnitude)
    density = jnp.exp(z * z * -0.5)
    tail = 0.5 * 1.061405429
    tail = tail * t + 0.5 * -1.453152027
    tail = tail * t + 0.5 * 1.421413741
    tail = tail * t + 0.5 * -0.284496736
    tail = tail * t + 0.5 * 0.254829592
    tail = tail * t * density
    cumulative = jnp.where(z < 0, tail, 1.0 - tail)
    return z * cumulative, cumulative + z * density * (1.0 / math.sqrt(2.0 * math.pi))


def fetch(copies):
    for copy in copies:
        copy.start()


def settle(copies):
    for copy in copies:
        copy.wait()


ATT_BEFORE, ATT_AFTER = 64, 32
MLP_BEFORE, MLP_AFTER = 64, 40


def window_offsets(me, att_rows, mlp_rows):
    att = ATT_BEFORE + 12 + me * (576 - att_rows) + jnp.where(me < QKV_BLOCKS, 0, 12)
    mlp = MLP_BEFORE + 12 + me * (1152 - mlp_rows) + jnp.where(me < W1_BLOCKS, 0, 24)
    return att, mlp


def each_tile(me, act):
    for name, blocks, rt_count, ct_count, mine in (
        ("qkv", QKV_BLOCKS, QKV_RT, QKV_CT, me < QKV_BLOCKS),
        ("wo", WO_BLOCKS, WO_RT, WO_CT, me >= QKV_BLOCKS),
        ("w1", W1_BLOCKS, W1_RT, W1_CT, me < W1_BLOCKS),
        ("w2", W2_BLOCKS, W2_RT, W2_CT, me >= W1_BLOCKS),
    ):

        @pl.when(mine)
        def _(name=name, rt_count=rt_count, ct_count=ct_count):
            for ct in range(ct_count):
                for rt in range(rt_count):
                    act(name, rt, ct, rt * SUB * ct_count + ct, ct_count)


def half_place(name, rt, ct):
    if name == "qkv":
        return ct // 9, ct % 9 * QKV_RT + rt
    if name == "wo":
        return rt // 3, rt % 3 * WO_CT + ct
    if name == "w1":
        return ct // 12, ct % 12 * W1_RT + rt
    return rt // 6, rt % 6 * W2_CT + ct


def part_place(name, rt, ct):
    if name == "qkv":
        return ct % 6 // 3, rt, ct // 6 * 3 + ct % 3
    place = rt * WO_CT + ct
    return place // 18, place // ATT_PART % 2, place % ATT_PART


def qkv_group(g):
    return [6 * third + 3 * g + i for third in range(3) for i in range(3)]


def small_rows(me, act):
    @pl.when(me == 0)
    def _():
        act("att", True, 12, G1)
        act("mlp", True, 12, G2)

    @pl.when(me == QKV_BLOCKS - 1)
    def _():
        act("att", False, 12, BQ)

    @pl.when(me == W1_BLOCKS - 1)
    def _():
        act("mlp", False, 24, B1)

    @pl.when(me == BLOCKS - 1)
    def _():
        act("att", False, 12, BO)
        act("mlp", False, 12, B2)


OWNERS = (0, W1_BLOCKS - 1, QKV_BLOCKS - 1, BLOCKS - 1)


def sent_rows(kind, first):
    return 12 if kind == "mlp" and first in (G2, B2) else 0


def pack_kernel(att_rows, me_ref, own, tails, heads, att, mlp, win_a, win_m, table):
    me = me_ref[0]
    mlp_rows = own.shape[0] - att_rows
    win_a[0:ATT_BEFORE, :] = tails[0:ATT_BEFORE, :]
    win_a[ATT_BEFORE : ATT_BEFORE + att_rows, :] = own[0:att_rows, :]
    win_a[ATT_BEFORE + att_rows :, :] = heads[0:ATT_AFTER, :]
    win_m[0:MLP_BEFORE, :] = tails[ATT_BEFORE:, :]
    win_m[MLP_BEFORE : MLP_BEFORE + mlp_rows, :] = own[att_rows:, :]
    win_m[MLP_BEFORE + mlp_rows :, :] = heads[ATT_AFTER:, :]
    att_off, mlp_off = window_offsets(me, att_rows, mlp_rows)

    def tile(name, rt, ct, first, stride):
        attention = name in ("qkv", "wo")
        window, out, off = (win_a, att, att_off) if attention else (win_m, mlp, mlp_off)
        values = window[pl.ds(off + first, SUB, stride=stride), :]
        out[half_place(name, rt, ct)] = values.astype(BF16)

    each_tile(me, tile)
    table[...] = jnp.zeros_like(table)

    def vector(kind, before, rows, first):
        window, off, size = (win_a, att_off, 576) if kind == "att" else (win_m, mlp_off, 1152)
        start = off - 12 if before else off + size
        place = sent_rows(kind, first)
        table[place : place + rows, :] = window[pl.ds(start, rows), :]

    small_rows(me, vector)
    att[0, ATT_HALF] = table[0:SUB, :].astype(BF16)
    att[1, ATT_HALF] = table[SUB : 2 * SUB, :].astype(BF16)


def pack(me, own, tails, heads, att_rows):
    mlp_rows = own.shape[0] - att_rows
    return pl.pallas_call(
        partial(pack_kernel, att_rows),
        out_shape=(
            shape((2, ATT_SENT, SUB, LANES), BF16),
            shape((2, MLP_HALF, SUB, LANES), BF16),
        ),
        in_specs=[smem(), vmem(), vmem(), vmem()],
        out_specs=(vmem(), vmem()),
        scratch_shapes=[
            pltpu.VMEM((ATT_BEFORE + att_rows + ATT_AFTER, LANES), F32),
            pltpu.VMEM((MLP_BEFORE + mlp_rows + MLP_AFTER, LANES), F32),
            pltpu.VMEM((2 * SUB, LANES), F32),
        ],
        name="pack",
    )(me, own, tails, heads)


def spread_kernel(
    att_rows, scale, me_ref, group0, group1, mlp, mine, to_before, to_after, win_a, win_m, table
):
    me = me_ref[0]
    mlp_rows = mine.shape[0] - att_rows
    att_off, mlp_off = window_offsets(me, att_rows, mlp_rows)
    win_a[...] = jnp.zeros_like(win_a)
    win_m[...] = jnp.zeros_like(win_m)

    def tile(name, rt, ct, first, stride):
        if name in ("qkv", "wo"):
            g, half, index = part_place(name, rt, ct)
            values = (group0, group1)[g][half, index]
            win_a[pl.ds(att_off + first, SUB, stride=stride), :] = values * scale
        else:
            values = mlp[half_place(name, rt, ct)]
            win_m[pl.ds(mlp_off + first, SUB, stride=stride), :] = values * scale

    each_tile(me, tile)
    for h in range(2):
        table[SUB * h : SUB * h + SUB, :] = group1[h, ATT_PART] * scale

    def vector(kind, before, rows, first):
        window, off, size = (win_a, att_off, 576) if kind == "att" else (win_m, mlp_off, 1152)
        start = off - 12 if before else off + size
        place = sent_rows(kind, first)
        window[pl.ds(start, rows), :] = table[place : place + rows, :]

    small_rows(me, vector)
    mine[0:att_rows, :] = win_a[ATT_BEFORE : ATT_BEFORE + att_rows, :]
    mine[att_rows:, :] = win_m[MLP_BEFORE : MLP_BEFORE + mlp_rows, :]
    to_before[0:ATT_BEFORE, :] = win_a[0:ATT_BEFORE, :]
    to_before[ATT_BEFORE:, :] = win_m[0:MLP_BEFORE, :]
    to_after[0:ATT_AFTER, :] = win_a[ATT_BEFORE + att_rows :, :]
    to_after[ATT_AFTER:, :] = win_m[MLP_BEFORE + mlp_rows :, :]


def spread(me, group0, group1, mlp, att_rows, mlp_rows, scale):
    return pl.pallas_call(
        partial(spread_kernel, att_rows, scale),
        out_shape=(
            shape((att_rows + mlp_rows, LANES), F32),
            shape((ATT_BEFORE + MLP_BEFORE, LANES), F32),
            shape((ATT_AFTER + MLP_AFTER, LANES), F32),
        ),
        in_specs=[smem(), vmem(), vmem(), vmem()],
        out_specs=(vmem(), vmem(), vmem()),
        scratch_shapes=[
            pltpu.VMEM((ATT_BEFORE + att_rows + ATT_AFTER, LANES), F32),
            pltpu.VMEM((MLP_BEFORE + mlp_rows + MLP_AFTER, LANES), F32),
            pltpu.VMEM((2 * SUB, LANES), F32),
        ],
        name="spread",
    )(me, group0, group1, mlp)


def close_kernel(att_rows, mine, below, above, out):
    rows = mine.shape[0]
    out[...] = mine[...]
    out[0:ATT_AFTER, :] += below[0:ATT_AFTER, :]
    out[att_rows : att_rows + MLP_AFTER, :] += below[ATT_AFTER:, :]
    out[att_rows - ATT_BEFORE : att_rows, :] += above[0:ATT_BEFORE, :]
    out[rows - MLP_BEFORE : rows, :] += above[ATT_BEFORE:, :]


def close(mine, below, above, att_rows):
    return pl.pallas_call(
        partial(close_kernel, att_rows),
        out_shape=shape(mine.shape, F32),
        in_specs=[vmem()] * 3,
        out_specs=vmem(),
        name="close",
    )(mine, below, above)


def slot_of(x, c, z, y):
    return x * 16 + c * 8 + z * 2 + y


GATHERED = [
    [
        [slot_of(i, c, z, s) if h == 0 else slot_of(s, c, z, i) for i in range(2) for z in range(4)]
        for c in range(2)
        for s in range(2)
    ]
    for h in range(2)
]
REDUCED = [
    [
        [slot_of(i, c, z, j) if h == 0 else slot_of(j, c, z, i)
         for i in range(2) for j in range(2) for z in range(4)]
        for c in range(2)
    ]
    for h in range(2)
]


def fetch_blocks(me, buffers, w, sems, first=0):
    for h in range(2):
        for k, slots in enumerate(GATHERED[h]):
            for index, slot in enumerate(slots):
                d = jnp.bitwise_xor(me, slot)

                def start(d=d, h=h, k=k, index=index):
                    source = buffers[4 * h + k].at[index]
                    pltpu.make_async_copy(source, w.at[d - first, h], sems.at[h, d]).start()

                if first:
                    pl.when(d >= first)(start)
                else:
                    start()


def wait_block(buffers, w, sems, d, h, first=0):
    pltpu.make_async_copy(buffers[0].at[0], w.at[d - first, h], sems.at[h, d]).wait()


def leaving_copies(me, buffers, w, sems):
    return [
        pltpu.make_async_copy(
            w.at[jnp.bitwise_xor(me, slot), h],
            buffers[2 * h + c].at[index],
            sems.at[h, jnp.bitwise_xor(me, slot)],
        )
        for h in range(2)
        for c in range(2)
        for index, slot in enumerate(REDUCED[h][c])
    ]


def leave_block(me, buffers, w, sems, d, h):
    slot = jnp.bitwise_xor(me, d)
    x, core, z, y = slot >> 4, (slot >> 3) & 1, (slot >> 1) & 3, slot & 1
    index = x * 8 + y * 4 + z if h == 0 else y * 8 + x * 4 + z
    for c in range(2):

        @pl.when(core == c)
        def _(c=c):
            target = buffers[2 * h + c].at[index]
            pltpu.make_async_copy(w.at[d, h], target, sems.at[h, d]).start()


def await_left(buffers, w, sems):
    for d in range(BLOCKS):
        for h in range(2):
            pltpu.make_async_copy(w.at[d, h], buffers[0].at[0], sems.at[h, d]).wait()


def att_scratch():
    return pltpu.VMEM((BLOCKS, 2, ATT_SENT, SUB, LANES), BF16)


def block_sems():
    return pltpu.SemaphoreType.DMA((2, BLOCKS))


def qkv_column(w, ct):
    h, place = ct // 9, ct % 9 * QKV_RT
    tiles = [w[d, h, place + rt] for d in range(QKV_BLOCKS) for rt in range(QKV_RT)]
    return jnp.concatenate(tiles, axis=0)


def wo_column(w, ct, first=QKV_BLOCKS):
    tiles = [
        w[QKV_BLOCKS - first + i, rt // 3, rt % 3 * WO_CT + ct]
        for i in range(WO_BLOCKS)
        for rt in range(WO_RT)
    ]
    return jnp.concatenate(tiles, axis=0)


def dma(count):
    return pltpu.SemaphoreType.DMA((count,))


def norm_rows(rows, gain, shift, source, target, step=256):
    def one(i, carry):
        at = pl.ds(pl.multiple_of(i * step, step), step)
        unit, _ = normalized(source[at, :].astype(F32))
        target[at, :] = (unit * gain + shift).astype(BF16)
        return carry

    lax.fori_loop(0, rows // step, one, 0)


def qkv_kernel(me_ref, tokens, *refs):
    buffers, (n1, qkv, small, w, x, unit, triple, sems, own) = refs[:8], refs[8:]
    coming = pltpu.make_async_copy(tokens, x, own.at[0])
    coming.start()
    fetch_blocks(me_ref[0], buffers, w, sems)
    for owner in OWNERS:
        for h in range(2):
            wait_block(buffers, w, sems, owner, h)
    tables = [
        jnp.concatenate([w[d, h, ATT_HALF] for h in range(2)], axis=0).astype(F32) for d in OWNERS
    ]
    small[G1 : G1 + 12, :] = tables[0][0:12]
    small[G2 : G2 + 12, :] = tables[0][12:24]
    small[B1 : B1 + 24, :] = tables[1][0:24]
    small[BQ : BQ + 12, :] = tables[2][0:12]
    small[BO : BO + 12, :] = tables[3][0:12]
    small[B2 : B2 + 12, :] = tables[3][12:24]
    small[SMALL - 4 :, :] = jnp.zeros((4, LANES), F32)
    coming.wait()
    norm_rows(x.shape[0], row_of(small, G1, 6), row_of(small, C1, 6), x, unit)
    going = [pltpu.make_async_copy(unit, n1, own.at[0])]
    going[0].start()
    for d in range(BLOCKS):
        for h in range(2):
            if d not in OWNERS:
                wait_block(buffers, w, sems, d, h)
    bias = jnp.concatenate(
        [row_of(small, BQ, 6), jnp.zeros((1, 768), F32), row_of(small, BV, 6)], axis=1
    )
    for c in range(QKV_CT // 2):
        weight = jnp.concatenate([qkv_column(w, 2 * c), qkv_column(w, 2 * c + 1)], axis=1)
        lanes = slice(256 * c, 256 * c + 256)
        triple[:, lanes] = (mm(unit[...], weight, NN) + bias[:, lanes]).astype(BF16)
        going.append(
            pltpu.make_async_copy(triple.at[:, lanes], qkv.at[:, lanes], own.at[1 + c])
        )
        going[-1].start()
    settle(going)


def project_qkv(me, tokens, att):
    rows, width = tokens.shape
    return pl.pallas_call(
        qkv_kernel,
        out_shape=(
            shape((rows, width), BF16),
            shape((rows, 3 * width), BF16),
            shape((SMALL, LANES), F32),
        ),
        in_specs=[smem(), hbm()] + [hbm()] * 8,
        out_specs=(hbm(), hbm(), vmem()),
        scratch_shapes=[
            att_scratch(),
            pltpu.VMEM((rows, width), BF16),
            pltpu.VMEM((rows, width), BF16),
            pltpu.VMEM((rows, 3 * width), BF16),
            block_sems(),
            dma(1 + QKV_CT // 2),
        ],
        compiler_params=pltpu.CompilerParams(vmem_limit_bytes=32 * MEGA),
        cost_estimate=cost(6 * rows * width * width, 12 * rows * width),
        name="qkv_forward",
    )(me, tokens, *att)


CLASSES = (128, 256, 384, 512, 768)


def head_masked(block):
    lane = lax.broadcasted_iota(jnp.int32, block.shape, 1)
    zero = jnp.zeros_like(block)
    return jnp.concatenate(
        [jnp.where(lane < 64, block, zero), jnp.where(lane >= 64, block, zero)], axis=0
    )


def pick_heads(both):
    return jnp.concatenate([both[0:64, 0:QB], both[64:128, QB : 2 * QB]], axis=0)


def mask_bias(start, width, b, key_ids, query_ids, bias):
    for j in range(width // QB):
        at = pl.ds(pl.multiple_of(start + j * QB, SUB), QB)
        same = key_ids[at, :] == query_ids[pl.ds(b, 1), :]
        bias[j * QB : (j + 1) * QB, :] = jnp.where(same, 0.0, NEGATIVE)


PAIRS = HEADS // 2


def attend_block(b, start, width, qkv, mixed, stats, bias, scores):
    rows = pl.ds(pl.multiple_of(b * QB, QB), QB)
    pieces = [slice(j * QB, (j + 1) * QB) for j in range(width // QB)]
    for p in range(PAIRS):
        lanes, key_lanes, value_lanes = [
            slice(LANES * (PAIRS * third + p), LANES * (PAIRS * third + p + 1))
            for third in range(3)
        ]
        queries = head_masked(qkv[rows, lanes] * 0.125)
        highest = jnp.full((8, 2 * QB), NEGATIVE, F32)
        for piece in pieces:
            at = pl.ds(pl.multiple_of(start + piece.start, SUB), QB)
            part = mm(qkv[at, key_lanes], queries, NT)
            part = part + jnp.concatenate([bias[piece, :]] * 2, axis=1)
            scores[p, piece, :] = part
            highest = jnp.maximum(highest, jnp.max(part.reshape(QB // 8, 8, 2 * QB), axis=0))
        highest = jnp.max(highest, axis=0, keepdims=True)
        summed = jnp.zeros((8, 2 * QB), F32)
        both = jnp.zeros((LANES, 2 * QB), F32)
        for piece in pieces:
            at = pl.ds(pl.multiple_of(start + piece.start, SUB), QB)
            raised = jnp.exp(scores[p, piece, :] - highest)
            summed = summed + fold8(raised)
            both = both + mm(qkv[at, value_lanes], raised.astype(BF16), TN)
        inverse = 1.0 / total(summed)
        mixed[rows, lanes] = pick_heads(both * inverse).T.astype(BF16)
        stats[b * PAIRS + p, 0:1, :] = highest
        stats[b * PAIRS + p, 1:2, :] = inverse


def wo_scratch():
    return pltpu.VMEM((WO_BLOCKS, 2, ATT_SENT, SUB, LANES), BF16)


def wait_wo(buffers, w, sems):
    for i in range(WO_BLOCKS):
        for h in range(2):
            wait_block(buffers, w, sems, QKV_BLOCKS + i, h, QKV_BLOCKS)


def attend_kernel(me_ref, windows, qkv, tokens, cot, key_ids, query_ids, small, *refs):
    buffers, refs = refs[:8], refs[8:]
    mixed, x1, branch, n2, dm, stats, gb2 = refs[:7]
    triple, x, g, mix, mid, out, unit, scaled, bias, scores, w, sems, own, chunk_sems = refs[7:]
    rows = tokens.shape[0]
    blocks = rows // QB

    def chunk(i):
        at = pl.ds(pl.multiple_of(i * QB, QB), QB)
        return pltpu.make_async_copy(qkv.at[at, :], triple.at[at, :], chunk_sems.at[i])

    for i in range(blocks):
        chunk(i).start()
    coming = [
        pltpu.make_async_copy(tokens, x, own.at[0]),
        pltpu.make_async_copy(cot, g, own.at[1]),
    ]
    fetch(coming)
    fetch_blocks(me_ref[0], buffers, w, sems, QKV_BLOCKS)

    def one_block(b, loaded):
        start = pl.multiple_of(windows[0, b], SUB)
        needed = jnp.maximum(windows[2, b], loaded)

        def arrived(i, carry):
            chunk(i).wait()
            return carry

        lax.fori_loop(loaded, needed, arrived, 0)
        for index, width in enumerate(CLASSES):

            @pl.when(windows[1, b] == index)
            def _(width=width):
                mask_bias(start, width, b, key_ids, query_ids, bias)
                attend_block(b, start, width, triple, mix, stats, bias, scores)

        return needed

    loaded = lax.fori_loop(0, blocks, one_block, jnp.int32(0))

    def arrived(i, carry):
        chunk(i).wait()
        return carry

    lax.fori_loop(loaded, blocks, arrived, 0)
    going = [pltpu.make_async_copy(mix, mixed, own.at[2])]
    going[0].start()
    wait_wo(buffers, w, sems)
    settle(coming)
    bo, s1 = row_of(small, BO, 6), row_of(small, S1, 6)
    gain, shift = row_of(small, G2, 6), row_of(small, C2, 6)
    s2 = row_of(small, S2, 6)
    weight = jnp.concatenate([wo_column(w, ct) for ct in range(WO_CT)], axis=1)
    step = 256
    sums = jnp.zeros((8, 768), F32)
    for i in range(rows // step):
        at = slice(i * step, (i + 1) * step)
        made = mm(mix[at, :], weight, NN) + bo
        out[at, :] = made.astype(BF16)
        values = x[at, :].astype(F32) + s1 * made
        mid[at, :] = values
        normal, _ = normalized(values)
        unit[at, :] = (normal * gain + shift).astype(BF16)
        rounded = (g[at, :].astype(F32) * s2).astype(BF16)
        scaled[at, :] = rounded
        sums = sums + fold8(rounded.astype(F32))
        for k, (source, target) in enumerate(
            ((out, branch), (mid, x1), (unit, n2), (scaled, dm))
        ):
            sem = own.at[3 + 4 * i + k]
            going.append(pltpu.make_async_copy(source.at[at, :], target.at[at, :], sem))
            going[-1].start()
    put_row(gb2, 0, total(sums))
    settle(going)


def attend(me, windows, qkv, tokens, cot, key_ids, query_ids, small, att):
    rows, width = tokens.shape
    row = lambda kind: pltpu.VMEM((rows, width), kind)
    return pl.pallas_call(
        attend_kernel,
        out_shape=(
            shape((rows, width), BF16),
            shape((rows, width), F32),
            shape((rows, width), BF16),
            shape((rows, width), BF16),
            shape((rows, width), BF16),
            shape((rows // QB * PAIRS, 2, 2 * QB), F32),
            shape((6, LANES), F32),
        ),
        in_specs=[smem(), smem(), hbm(), hbm(), hbm(), vmem(), vmem(), vmem()] + [hbm()] * 8,
        out_specs=(hbm(),) * 5 + (vmem(), vmem()),
        scratch_shapes=[
            pltpu.VMEM((rows, 3 * width), BF16),
            row(BF16),
            row(BF16),
            row(BF16),
            row(F32),
            row(BF16),
            row(BF16),
            row(BF16),
            pltpu.VMEM((CLASSES[-1], QB), F32),
            pltpu.VMEM((PAIRS, CLASSES[-1], 2 * QB), F32),
            wo_scratch(),
            block_sems(),
            dma(3 + 4 * rows // 256),
            dma(rows // QB),
        ],
        compiler_params=pltpu.CompilerParams(vmem_limit_bytes=46 * MEGA),
        cost_estimate=cost(2 * rows * rows * width, 20 * rows * width, 4 * rows * rows),
        name="attend_forward",
    )(me, windows, qkv, tokens, cot, key_ids, query_ids, small, *att)


def w1_columns(w, f, c):
    columns = []
    for ct in (2 * c, 2 * c + 1):
        place = MLP_HALF // 2 * (f % 2) + ct * W1_RT
        tiles = [w[d, f // 2, place + rt] for d in range(W1_BLOCKS) for rt in range(W1_RT)]
        columns.append(jnp.concatenate(tiles, axis=0))
    return jnp.concatenate(columns, axis=1)


def w2_place(f, row, ct):
    rt = row % W2_RT
    return W1_BLOCKS + 4 * f + row // W2_RT, rt // 6, rt % 6 * W2_CT + ct


def w2_rows(w, f, c):
    columns = []
    for ct in range(W2_CT):
        tiles = [w[w2_place(f, row, ct)] for row in range(SUB * c, SUB * c + SUB)]
        columns.append(jnp.concatenate(tiles, axis=0))
    return jnp.concatenate(columns, axis=1)


TALL = 256
PARTS = CHUNK // 256


def mlp_scratch():
    return pltpu.VMEM((BLOCKS, 2, MLP_HALF, SUB, LANES), BF16)


def mlp_kernel(me_ref, n2_in, dm_in, small, *refs):
    arriving, refs = refs[:8], refs[8:]
    u_out, dz_out, vectors, *leaving = refs[:7]
    w, n2, dm, u, dz, zs, dus, bias_sums, b1_lines, sems, own = refs[7:]
    me = me_ref[0]
    rows, width = n2.shape
    tiles = rows // TALL
    coming = [
        pltpu.make_async_copy(n2_in, n2, own.at[0]),
        pltpu.make_async_copy(dm_in, dm, own.at[1]),
    ]
    fetch(coming)
    fetch_blocks(me, arriving, w, sems)
    bias_sums[...] = jnp.zeros_like(bias_sums)
    for f in range(CHUNKS):
        b1_lines[f : f + 1, :] = row_of(small, B1 + 6 * f, 6)
    settle(coming)

    units = [(t, c) for c in range(PARTS) for t in range(tiles)]

    def lanes_of(f, c):
        return pl.ds(pl.multiple_of(CHUNK * f + 256 * c, 256), 256)

    def outward(f):
        chunk = pl.ds(pl.multiple_of(CHUNK * f, CHUNK), CHUNK)
        return [
            pltpu.make_async_copy(u.at[:, chunk], u_out.at[:, chunk], own.at[2 * f]),
            pltpu.make_async_copy(dz.at[:, chunk], dz_out.at[:, chunk], own.at[2 * f + 1]),
        ]

    def one_chunk(f, carry):
        @pl.when((f & 1) == 0)
        def _():
            for d in range(W1_BLOCKS):
                wait_block(arriving, w, sems, d, f >> 1)

        for k in range(4):
            for h in range(2):
                wait_block(arriving, w, sems, W1_BLOCKS + 4 * f + k, h)

        def multiply(unit, slot):
            t, c = unit
            at = slice(TALL * t, TALL * t + TALL)
            zs[slot] = mm(n2[at, :], w1_columns(w, f, c), NN)
            dus[slot] = mm(dm[at, :], w2_rows(w, f, c), NT)

        def activate(unit, slot):
            t, c = unit
            lanes = lanes_of(f, c)
            bias = b1_lines[pl.ds(f, 1), 256 * c : 256 * c + 256]
            folded = jnp.zeros((8, 256), F32)
            for r in range(TALL // 32):
                part = slice(32 * r, 32 * r + 32)
                place = slice(TALL * t + 32 * r, TALL * t + 32 * r + 32)
                value, slope = gelu_pair(zs[slot, part, :] + bias)
                u[place, lanes] = value.astype(BF16)
                rounded = (dus[slot, part, :] * slope).astype(BF16)
                dz[place, lanes] = rounded
                folded = folded + fold8(rounded.astype(F32))
            bias_sums[:, lanes] += folded

        multiply(units[0], 0)
        for i, unit in enumerate(units):
            if i + 1 < len(units):
                multiply(units[i + 1], (i + 1) % 2)
            activate(unit, i % 2)
        fetch(outward(f))
        return carry

    lax.fori_loop(0, CHUNKS, one_chunk, 0)
    put_row(vectors, 0, total(bias_sums[...]))

    def one_grad(f, carry):
        for c in range(PARTS):
            grad = mm(u[:, lanes_of(f, c)], dm[...], TN)
            for r in range(SUB):
                for ct in range(W2_CT):
                    tile = grad[SUB * r : SUB * r + SUB, LANES * ct : LANES * ct + LANES]
                    w[w2_place(f, SUB * c + r, ct)] = tile.astype(BF16)
        for k in range(4):
            for h in range(2):
                leave_block(me, leaving, w, sems, W1_BLOCKS + 4 * f + k, h)
        chunk = pl.ds(pl.multiple_of(CHUNK * f, CHUNK), CHUNK)
        base = MLP_HALF // 2 * (f & 1)
        for c in range(PARTS):
            lanes = slice(256 * c, 256 * c + 256)
            grad = mm(n2[:, lanes], dz[:, chunk], TN)
            for r in range(SUB):
                d, rt = (SUB * c + r) // W1_RT, (SUB * c + r) % W1_RT
                for ct in range(6):
                    tile = grad[SUB * r : SUB * r + SUB, LANES * ct : LANES * ct + LANES]
                    w[d, f >> 1, base + ct * W1_RT + rt] = tile.astype(BF16)
        for h in range(2):

            @pl.when(f == 2 * h + 1)
            def _(h=h):
                for d in range(W1_BLOCKS):
                    leave_block(me, leaving, w, sems, d, h)

        return carry

    lax.fori_loop(0, CHUNKS, one_grad, 0)
    for f in range(CHUNKS):
        settle(outward(f))
    await_left(leaving, w, sems)


def feed_forward(me, n2, dm, small, mlp):
    rows, width = n2.shape
    half = shape((HALF_BLOCKS, MLP_HALF, SUB, LANES), BF16)
    return pl.pallas_call(
        mlp_kernel,
        out_shape=(
            shape((rows, FF), BF16),
            shape((rows, FF), BF16),
            shape((24, LANES), F32),
            half,
            half,
            half,
            half,
        ),
        in_specs=[smem(), hbm(), hbm(), vmem()] + [hbm()] * 8,
        out_specs=(hbm(), hbm(), vmem()) + (hbm(),) * 4,
        scratch_shapes=[
            mlp_scratch(),
            pltpu.VMEM((rows, width), BF16),
            pltpu.VMEM((rows, width), BF16),
            pltpu.VMEM((rows, FF), BF16),
            pltpu.VMEM((rows, FF), BF16),
            pltpu.VMEM((2, TALL, 256), F32),
            pltpu.VMEM((2, TALL, 256), F32),
            pltpu.VMEM((8, FF), F32),
            pltpu.VMEM((CHUNKS, CHUNK), F32),
            block_sems(),
            dma(2 * CHUNKS),
        ],
        compiler_params=pltpu.CompilerParams(vmem_limit_bytes=44 * MEGA),
        cost_estimate=cost(8 * rows * width * FF, 40 * MEGA),
        name="feed_forward",
    )(me, n2, dm, small, *mlp)


def mlp_out_kernel(me_ref, u_in, dz_in, x1_in, cot_in, small, *refs):
    arriving, refs = refs[:8], refs[8:]
    out, dx1, vectors = refs[:3]
    w, u, dz, x1, cot, macc, dnacc, done, grad_x, sums, sems, own = refs[3:]
    rows, width = x1.shape
    tiles = rows // TALL

    def rows_of(t):
        return pl.ds(pl.multiple_of(TALL * t, TALL), TALL)

    def tile_copy(source, target, t, k):
        at = rows_of(t)
        return pltpu.make_async_copy(source.at[at, :], target.at[at, :], own.at[k, t])

    for t in range(tiles):
        tile_copy(u_in, u, t, 0).start()
    fetch_blocks(me_ref[0], arriving, w, sems)
    for t in range(tiles):
        tile_copy(dz_in, dz, t, 1).start()
        tile_copy(x1_in, x1, t, 2).start()
        tile_copy(cot_in, cot, t, 3).start()
    bias, gain, scale = row_of(small, B2, 6), row_of(small, G2, 6), row_of(small, S2, 6)
    sums[...] = jnp.zeros_like(sums)
    for d in range(BLOCKS):
        for h in range(2):
            wait_block(arriving, w, sems, d, h)
    every = [(f, c) for f in range(CHUNKS) for c in range(PARTS)]

    def contract(t):
        at = rows_of(t)
        tile_copy(u_in, u, t, 0).wait()
        second = jnp.concatenate([w2_rows(w, f, c) for f, c in every], axis=0)
        macc[at, :] = mm(u[at, :], second, NN)
        tile_copy(dz_in, dz, t, 1).wait()
        first = jnp.concatenate([w1_columns(w, f, c) for f, c in every], axis=1)
        dnacc[at, :] = mm(dz[at, :], first, NT)

    def finish(t):
        tile_copy(x1_in, x1, t, 2).wait()
        tile_copy(cot_in, cot, t, 3).wait()
        for half in range(2):
            at = pl.ds(pl.multiple_of(TALL * t + TALL // 2 * half, TALL // 2), TALL // 2)
            upstream = cot[at, :].astype(F32)
            values = x1[at, :]
            contracted = macc[at, :] + bias
            done[at, :] = (values + scale * contracted).astype(BF16)
            unit, inverse = normalized(values)
            grad = dnacc[at, :]
            grad_x[at, :] = upstream + norm_pullback(unit, inverse, grad, gain)
            sums[0:8, :] += fold8(grad * unit)
            sums[8:16, :] += fold8(grad)
            sums[16:24, :] += fold8(upstream * contracted)
        tile_copy(done, out, t, 2).start()
        tile_copy(grad_x, dx1, t, 3).start()

    def one_tile(t, carry):
        contract(t)
        finish(t - 1)
        return carry

    contract(0)
    lax.fori_loop(1, tiles, one_tile, 0)
    finish(tiles - 1)
    for k in range(3):
        put_row(vectors, 6 * k, total(sums[8 * k : 8 * k + 8, :]))
    for t in range(tiles):
        tile_copy(done, out, t, 2).wait()
        tile_copy(grad_x, dx1, t, 3).wait()


def feed_forward_out(me, u, dz, x1, cot, small, mlp):
    rows, width = x1.shape
    row = lambda kind: pltpu.VMEM((rows, width), kind)
    return pl.pallas_call(
        mlp_out_kernel,
        out_shape=(
            shape((rows, width), BF16),
            shape((rows, width), F32),
            shape((18, LANES), F32),
        ),
        in_specs=[smem()] + [hbm()] * 4 + [vmem()] + [hbm()] * 8,
        out_specs=(hbm(), hbm(), vmem()),
        scratch_shapes=[
            mlp_scratch(),
            pltpu.VMEM((rows, FF), BF16),
            pltpu.VMEM((rows, FF), BF16),
            row(F32),
            row(BF16),
            row(F32),
            row(F32),
            row(BF16),
            row(F32),
            pltpu.VMEM((24, width), F32),
            block_sems(),
            pltpu.SemaphoreType.DMA((4, rows // TALL)),
        ],
        compiler_params=pltpu.CompilerParams(vmem_limit_bytes=54 * MEGA),
        cost_estimate=cost(4 * rows * width * FF, 40 * MEGA),
        name="feed_forward_out",
    )(me, u, dz, x1, cot, small, *mlp)


def split_kernel(me_ref, dx1_in, branch_in, mixed_in, small, *refs):
    buffers, refs = refs[:8], refs[8:]
    da_out, gwo0, gwo1, vectors = refs[:4]
    w, dx1, branch, mixed, db, da, parts, sems, own = refs[4:]
    rows = dx1.shape[0]
    step = 256
    steps = rows // step

    def tile_copy(source, target, t, k):
        at = pl.ds(pl.multiple_of(step * t, step), step)
        return pltpu.make_async_copy(source.at[at, :], target.at[at, :], own.at[k, t])

    for t in range(steps):
        tile_copy(dx1_in, dx1, t, 0).start()
        tile_copy(branch_in, branch, t, 1).start()
    fetch_blocks(me_ref[0], buffers, w, sems, QKV_BLOCKS)
    for t in range(steps):
        tile_copy(mixed_in, mixed, t, 2).start()
    scale = row_of(small, S1, 6)

    def one(t, carry):
        gs1, gbo = carry
        tile_copy(dx1_in, dx1, t, 0).wait()
        tile_copy(branch_in, branch, t, 1).wait()
        at = pl.ds(pl.multiple_of(t * step, step), step)
        grad = dx1[at, :]
        rounded = (grad * scale).astype(BF16)
        db[at, :] = rounded
        return gs1 + fold8(grad * branch[at, :].astype(F32)), gbo + fold8(rounded.astype(F32))

    zero = jnp.zeros((8, 768), F32)
    gs1, gbo = lax.fori_loop(0, steps, one, (zero, zero))
    put_row(vectors, 0, total(gbo))
    put_row(vectors, 6, total(gs1))
    wait_wo(buffers, w, sems)
    weight = jnp.concatenate([wo_column(w, ct) for ct in range(WO_CT)], axis=1)
    going = []
    for c in range(3):
        lanes = slice(256 * c, 256 * c + 256)
        da[:, lanes] = mm(db[...], weight[lanes, :], NT).astype(BF16)
        going.append(pltpu.make_async_copy(da.at[:, lanes], da_out.at[:, lanes], own.at[3, c]))
        going[-1].start()
    for t in range(steps):
        tile_copy(mixed_in, mixed, t, 2).wait()
    for c in range(3):
        grad = mm(mixed[:, 256 * c : 256 * c + 256], db[...], TN)
        for r in range(SUB):
            i, rt = (SUB * c + r) // WO_RT, (SUB * c + r) % WO_RT
            for ct in range(WO_CT):
                tile = grad[SUB * r : SUB * r + SUB, LANES * ct : LANES * ct + LANES]
                g, half, index = part_place("wo", rt, ct)
                parts[g, i, half, index] = tile.astype(BF16)
    for g, target in enumerate((gwo0, gwo1)):
        going.append(pltpu.make_async_copy(parts.at[g], target, own.at[4, g]))
        going[-1].start()
    settle(going)


def split(me, dx1, branch, mixed, small, att):
    rows, width = dx1.shape
    part = (WO_BLOCKS, 2, ATT_PART, SUB, LANES)
    row = lambda kind: pltpu.VMEM((rows, width), kind)
    return pl.pallas_call(
        split_kernel,
        out_shape=(
            shape((rows, width), BF16),
            shape(part, BF16),
            shape(part, BF16),
            shape((12, LANES), F32),
        ),
        in_specs=[smem()] + [hbm()] * 3 + [vmem()] + [hbm()] * 8,
        out_specs=(hbm(), hbm(), hbm(), vmem()),
        scratch_shapes=[
            wo_scratch(),
            row(F32),
            row(BF16),
            row(BF16),
            row(BF16),
            row(BF16),
            pltpu.VMEM((2,) + part, BF16),
            block_sems(),
            pltpu.SemaphoreType.DMA((5, rows // 256)),
        ],
        compiler_params=pltpu.CompilerParams(vmem_limit_bytes=24 * MEGA),
        cost_estimate=cost(4 * rows * width * width, 14 * rows * width),
        name="project_backward",
    )(me, dx1, branch, mixed, small, *att)


GROUP = PAIRS // 2
GROUP_LANES = GROUP * LANES


def attend_back_block(b, start, width, group, refs):
    q, k, v, da, stats, dq, dkeys, dvalues, bias = refs
    rows = pl.ds(pl.multiple_of(b * QB, QB), QB)
    at = pl.ds(start, width)
    mask = jnp.concatenate([bias[0:width, :]] * 2, axis=1)
    for p in range(GROUP):
        lanes = slice(LANES * p, LANES * p + LANES)
        place = b * PAIRS + GROUP * group + p
        queries = head_masked(q[rows, lanes] * 0.125)
        grads = head_masked(da[rows, lanes])
        highest = stats[place, 0:1, :]
        inverse = stats[place, 1:2, :]
        keys, values = k[at, lanes], v[at, lanes]
        weight = jnp.exp(mm(keys, queries, NT) + mask - highest) * inverse
        dweight = mm(values, grads, NT)
        inner_sum = total(fold8(weight * dweight))
        dvalues[at, lanes] += mm(weight.astype(BF16), grads, NN)
        dscore = (weight * (dweight - inner_sum)).astype(BF16)
        dkeys[at, lanes] += mm(dscore, queries, NN)
        both = mm(keys, dscore, TN)
        dq[rows, lanes] = (pick_heads(both) * 0.125).T.astype(BF16)


def attend_back_kernel(group, windows, qkv, da_in, stats, key_ids, query_ids, dqkv, *refs):
    q, k, v, da, out, dkeys, dvalues, bias, own = refs
    rows = q.shape[0]
    blocks = rows // QB
    lanes = slice(GROUP_LANES * group, GROUP_LANES * group + GROUP_LANES)
    coming = [pltpu.make_async_copy(da_in.at[:, lanes], da, own.at[3])]
    for third, target in enumerate((q, k, v)):
        first = LANES * PAIRS * third + GROUP_LANES * group
        source = qkv.at[:, first : first + GROUP_LANES]
        coming.append(pltpu.make_async_copy(source, target, own.at[third]))
    fetch(coming)
    dkeys[...] = jnp.zeros_like(dkeys)
    dvalues[...] = jnp.zeros_like(dvalues)
    settle(coming)
    dq = out.at[:, 0:GROUP_LANES]

    def one_block(b, carry):
        start = pl.multiple_of(windows[0, b], SUB)
        for index, width in enumerate(CLASSES):

            @pl.when(windows[1, b] == index)
            def _(width=width):
                mask_bias(start, width, b, key_ids, query_ids, bias)
                parts = (q, k, v, da, stats, dq, dkeys, dvalues, bias)
                attend_back_block(b, start, width, group, parts)

        return carry

    lax.fori_loop(0, blocks, one_block, 0)
    going = []
    for i in range(rows // 256):
        at = slice(256 * i, 256 * i + 256)
        out[at, GROUP_LANES : 2 * GROUP_LANES] = dkeys[at, :].astype(BF16)
        out[at, 2 * GROUP_LANES :] = dvalues[at, :].astype(BF16)
        going.append(pltpu.make_async_copy(out.at[at, :], dqkv.at[at, :], own.at[i]))
        going[-1].start()
    settle(going)


def attend_back(group, windows, qkv, da, stats, key_ids, query_ids):
    rows = qkv.shape[0]
    part = lambda kind: pltpu.VMEM((rows, GROUP_LANES), kind)
    return pl.pallas_call(
        partial(attend_back_kernel, group),
        out_shape=shape((rows, 3 * GROUP_LANES), BF16),
        in_specs=[smem(), hbm(), hbm(), vmem(), vmem(), vmem()],
        out_specs=hbm(),
        scratch_shapes=[
            part(BF16),
            part(BF16),
            part(BF16),
            part(BF16),
            pltpu.VMEM((rows, 3 * GROUP_LANES), BF16),
            part(F32),
            part(F32),
            pltpu.VMEM((CLASSES[-1], QB), F32),
            dma(4),
        ],
        compiler_params=pltpu.CompilerParams(vmem_limit_bytes=32 * MEGA),
        cost_estimate=cost(3 * rows * rows * rows, 14 * rows * rows, 4 * rows * rows),
        name="attend_backward",
    )(windows, qkv, da, stats, key_ids, query_ids)


def put_qkv_grad(n1, dqkv, w):
    for c in range(3):
        grad = mm(n1[:, 256 * c : 256 * c + 256], dqkv[...], TN)
        for r in range(SUB):
            d, rt = (SUB * c + r) // QKV_RT, (SUB * c + r) % QKV_RT
            for index in range(ATT_PART):
                tile = grad[SUB * r : SUB * r + SUB, LANES * index : LANES * index + LANES]
                w[d, rt, index] = tile.astype(BF16)


def weight_grad_kernel(me_ref, n1_in, dqkv_in, gwo, *refs):
    leaving, (w, n1, dqkv, sems, own) = refs[:4], refs[4:]
    coming = [
        pltpu.make_async_copy(n1_in, n1, own.at[0]),
        pltpu.make_async_copy(dqkv_in, dqkv, own.at[1]),
        pltpu.make_async_copy(gwo, w.at[QKV_BLOCKS:], own.at[2]),
    ]
    fetch(coming)
    settle(coming)
    put_qkv_grad(n1, dqkv, w)
    copies = leaving_copies(me_ref[0], leaving, w, sems)
    fetch(copies)
    settle(copies)


def weight_grad(me, n1, dqkv, gwo):
    rows, width = n1.shape
    half = shape((HALF_BLOCKS, ATT_PART, SUB, LANES), BF16)
    return pl.pallas_call(
        weight_grad_kernel,
        out_shape=(half,) * 4,
        in_specs=[smem()] + [hbm()] * 3,
        out_specs=(hbm(),) * 4,
        scratch_shapes=[
            pltpu.VMEM((BLOCKS, 2, ATT_PART, SUB, LANES), BF16),
            pltpu.VMEM((rows, width), BF16),
            pltpu.VMEM(dqkv.shape, BF16),
            block_sems(),
            dma(3),
        ],
        compiler_params=pltpu.CompilerParams(vmem_limit_bytes=20 * MEGA),
        cost_estimate=cost(3 * rows * width * width, 10 * rows * width),
        name="qkv_weight_grad",
    )(me, n1, dqkv, gwo)


def qkv_back_kernel(
    me_ref, tokens_in, n1_in, dx1_in, dqkv0_in, dqkv1_in, small, proj, mlp, gwo, *refs
):
    arriving, refs = refs[:8], refs[8:]
    dx_out, *leaving = refs[:5]
    w, gw, tokens, n1, dx1, dqkv0, dqkv1, dn, dx, sums, table, sems, out_sems, own = refs[5:]
    me = me_ref[0]
    rows = tokens.shape[0]
    tiles = rows // TALL

    def tile_copy(source, target, t, k):
        at = pl.ds(pl.multiple_of(TALL * t, TALL), TALL)
        return pltpu.make_async_copy(source.at[at, :], target.at[at, :], own.at[k, t])

    for t in range(tiles):
        tile_copy(dqkv0_in, dqkv0, t, 0).start()
        tile_copy(dqkv1_in, dqkv1, t, 1).start()
    fetch_blocks(me, arriving, w, sems)
    for t in range(tiles):
        tile_copy(tokens_in, tokens, t, 2).start()
        tile_copy(dx1_in, dx1, t, 3).start()
    late = [
        pltpu.make_async_copy(n1_in, n1, own.at[4, 0]),
        pltpu.make_async_copy(gwo, gw.at[QKV_BLOCKS:, :, 0:ATT_PART], own.at[4, 1]),
    ]
    fetch(late)
    sums[...] = jnp.zeros_like(sums)
    gain = row_of(small, G1, 6)
    for d in range(BLOCKS):
        for h in range(2):
            wait_block(arriving, w, sems, d, h)

    def contract(t):
        at = pl.ds(pl.multiple_of(TALL * t, TALL), TALL)
        for g, (source, part) in enumerate(((dqkv0_in, dqkv0), (dqkv1_in, dqkv1))):
            tile_copy(source, part, t, g).wait()
            lanes = slice(384 * g, 384 * g + 384)
            sums[16:24, lanes] += fold8(part[at, 0:384].astype(F32))
            sums[24:32, lanes] += fold8(part[at, 768:1152].astype(F32))
        weight = jnp.concatenate(
            [qkv_column(w, ct) for g in range(2) for ct in qkv_group(g)], axis=1
        )
        both = jnp.concatenate([dqkv0[at, :], dqkv1[at, :]], axis=1)
        dn[at, :] = mm(both, weight, NT)

    def finish(t):
        tile_copy(tokens_in, tokens, t, 2).wait()
        tile_copy(dx1_in, dx1, t, 3).wait()
        for half in range(2):
            at = pl.ds(pl.multiple_of(TALL * t + TALL // 2 * half, TALL // 2), TALL // 2)
            unit, inverse = normalized(tokens[at, :].astype(F32))
            grad = dn[at, :]
            dx[at, :] = dx1[at, :] + norm_pullback(unit, inverse, grad, gain)
            sums[0:8, :] += fold8(grad * unit)
            sums[8:16, :] += fold8(grad)
        tile_copy(dx, dx_out, t, 3).start()

    def one_tile(t, carry):
        contract(t)
        finish(t - 1)
        return carry

    contract(0)
    lax.fori_loop(1, tiles, one_tile, 0)
    finish(tiles - 1)

    def put_table(owner, *places):
        table[...] = jnp.zeros_like(table)
        for place, values in places:
            if values.shape[1] == LANES:
                table[place : place + values.shape[0], :] = values
            else:
                put_row(table, place, values)
        for h in range(2):
            gw[owner, h, ATT_PART] = table[SUB * h : SUB * h + SUB, :].astype(BF16)

    put_table(
        OWNERS[0], (0, total(sums[0:8, :])), (6, total(sums[8:16, :])), (12, mlp[0:12, :])
    )
    put_table(OWNERS[1], (0, mlp[12:36, :]))
    put_table(OWNERS[2], (0, total(sums[16:24, :])), (6, total(sums[24:32, :])))
    put_table(OWNERS[3], (0, proj[...]), (12, mlp[36:48, :]))
    settle(late)
    put_qkv_grad(n1, dqkv1, gw)
    copies = leaving_copies(me, leaving, gw, out_sems)
    fetch(copies)
    for t in range(tiles):
        tile_copy(dx, dx_out, t, 3).wait()
    settle(copies)


def qkv_back(me, tokens, n1, dx1, dqkv0, dqkv1, small, proj, mlp, gwo, att):
    rows, width = tokens.shape
    tiles = ATT_PART + 1
    half = shape((HALF_BLOCKS, tiles, SUB, LANES), BF16)
    row = lambda kind: pltpu.VMEM((rows, width), kind)
    return pl.pallas_call(
        qkv_back_kernel,
        out_shape=(shape((rows, width), F32), half, half, half, half),
        in_specs=[smem()] + [hbm()] * 5 + [vmem()] * 3 + [hbm()] * 9,
        out_specs=(hbm(),) * 5,
        scratch_shapes=[
            att_scratch(),
            pltpu.VMEM((BLOCKS, 2, tiles, SUB, LANES), BF16),
            row(BF16),
            row(BF16),
            row(F32),
            pltpu.VMEM(dqkv0.shape, BF16),
            pltpu.VMEM(dqkv1.shape, BF16),
            row(F32),
            row(F32),
            pltpu.VMEM((32, width), F32),
            pltpu.VMEM((2 * SUB, LANES), F32),
            block_sems(),
            block_sems(),
            pltpu.SemaphoreType.DMA((5, rows // TALL)),
        ],
        compiler_params=pltpu.CompilerParams(vmem_limit_bytes=44 * MEGA),
        cost_estimate=cost(9 * rows * width * width, 30 * rows * width),
        name="qkv_backward",
    )(me, tokens, n1, dx1, dqkv0, dqkv1, small, proj, mlp, gwo, *att)


X, C, Z1, Z0, Y = 16, 8, 4, 2, 1


def exchange(values, bit):
    return lax.ppermute(values, AXES, [(d, d ^ bit) for d in range(BLOCKS)])


def shifted(values, by):
    pairs = [(d, d + by) for d in range(BLOCKS) if 0 <= d + by < BLOCKS]
    return lax.ppermute(values, AXES, pairs)


def together(*values):
    return lax.optimization_barrier(values)


def along_z(first, second, received):
    return (
        jnp.stack([first] + [r[0] for r in received]),
        jnp.stack([second] + [r[1] for r in received]),
    )


def joined(own, received):
    return jnp.concatenate([own, received])


def sum_terms(terms):
    summed = terms[0].astype(F32)
    for term in terms[1:]:
        summed = summed + term.astype(F32)
    return summed


def kept(terms):
    return [t[: t.shape[0] // 2] for t in terms]


def z_part(first, second, k):
    return jnp.stack([sum_terms([t[k] for t in terms]) for terms in (first, second)])


def sent(terms):
    return sum_terms([t[t.shape[0] // 2 :] for t in terms]).astype(BF16)


def attention_amounts(width):
    return [width, width, 3 * width * width, width, width, width * width, width, width]


def feedforward_amounts(width):
    return [width, width, width * FF, FF, FF * width, width, width]


def pieces_of(vector, amounts):
    out, offset = [], 0
    for amount in amounts:
        out.append(vector[offset : offset + amount])
        offset += amount
    return out


def tiles_by_column(matrix, blocks, rt):
    ct = matrix.shape[1] // LANES
    return matrix.reshape(blocks, rt, SUB, ct, LANES).transpose(0, 3, 1, 2, 4)


def tiles_by_row(matrix, blocks, rt):
    ct = matrix.shape[1] // LANES
    return matrix.reshape(blocks, rt, SUB, ct, LANES).transpose(0, 1, 3, 2, 4)


def gather_plainly(params, att_rows, width):
    rounded = params.astype(BF16)
    att = lax.all_gather(rounded[:att_rows], AXES, axis=0, tiled=True).reshape(-1)
    mlp = lax.all_gather(rounded[att_rows:], AXES, axis=0, tiled=True).reshape(-1)
    g1, c1, wqkv, bq, bv, wo, bo, s1 = pieces_of(att, attention_amounts(width))
    g2, c2, w1, b1, w2, b2, s2 = pieces_of(mlp, feedforward_amounts(width))
    tile = (SUB, LANES)
    att = jnp.concatenate(
        [
            tiles_by_column(wqkv.reshape(width, -1), QKV_BLOCKS, QKV_RT).reshape((-1, 36) + tile),
            tiles_by_row(wo.reshape(width, -1), WO_BLOCKS, WO_RT).reshape((-1, 36) + tile),
        ]
    )
    mlp = jnp.concatenate(
        [
            tiles_by_column(w1.reshape(width, -1), W1_BLOCKS, W1_RT).reshape((-1, 72) + tile),
            tiles_by_row(w2.reshape(FF, -1), W2_BLOCKS, W2_RT).reshape((-1, 72) + tile),
        ]
    )
    vectors = jnp.concatenate([g1, c1, bq, bv, bo, s1, g2, c2, b1, b2, s2]).astype(F32)
    lines = vectors.reshape(-1, LANES)
    sent = jnp.zeros((BLOCKS, 2 * SUB, LANES), F32)
    for owner, place, first, count in (
        (OWNERS[0], 0, G1, 12),
        (OWNERS[0], 12, G2, 12),
        (OWNERS[1], 0, B1, 24),
        (OWNERS[2], 0, BQ, 12),
        (OWNERS[3], 0, BO, 12),
        (OWNERS[3], 12, B2, 12),
    ):
        sent = sent.at[owner, place : place + count].set(lines[first : first + count])
    sent = sent.astype(BF16).reshape((BLOCKS, 2, 1) + tile)
    att = [jnp.concatenate([att[:, 18 * h : 18 * h + 18], sent[:, h]], axis=1) for h in range(2)]
    return by_slot(*att), by_slot(mlp[:, :36], mlp[:, 36:])


def by_slot(first, second):
    halves = (first, second)
    return [
        jnp.stack([halves[h][slot] for slot in slots]) for h in range(2) for slots in GATHERED[h]
    ]


def from_slots(buffers):
    halves = []
    for h in range(2):
        blocks = [None] * BLOCKS
        for c in range(2):
            for index, slot in enumerate(REDUCED[h][c]):
                blocks[slot] = buffers[2 * h + c][index]
        halves.append(jnp.stack(blocks))
    return halves


def reduce_plainly(gatt0, gatt1, gmlp, att_rows, mlp_rows, width, devices):
    groups = [from_slots(gatt0), from_slots(gatt1)]
    vectors = jnp.concatenate([groups[1][h][:, ATT_PART:] for h in range(2)], axis=1)
    vectors = vectors.astype(F32).reshape(BLOCKS, 2 * SUB, LANES)

    def matrix(name, first, last, rt_count, ct_count):
        rows = []
        for rt in range(rt_count):
            places = [part_place(name, rt, ct) for ct in range(ct_count)]
            rows.append(jnp.stack([groups[g][h][first:last, i] for g, h, i in places], axis=2))
        return jnp.stack(rows, axis=1).astype(F32).reshape(-1)

    wqkv = matrix("qkv", 0, QKV_BLOCKS, QKV_RT, QKV_CT)
    wo = matrix("wo", QKV_BLOCKS, BLOCKS, WO_RT, WO_CT)
    mlp = jnp.concatenate(from_slots(gmlp), axis=1).astype(F32)
    five = lambda v, dims: v.reshape((v.shape[0],) + dims + (SUB, LANES))
    w1 = five(mlp[:W1_BLOCKS], (W1_CT, W1_RT)).transpose(0, 2, 3, 1, 4).reshape(-1)
    w2 = five(mlp[W1_BLOCKS:], (W2_RT, W2_CT)).transpose(0, 1, 3, 2, 4).reshape(-1)
    line = lambda owner, first, count: vectors[owner, first : first + count].reshape(-1)
    att = [line(OWNERS[0], 0, 12), wqkv, line(OWNERS[2], 0, 12), wo, line(OWNERS[3], 0, 12)]
    mlp = [line(OWNERS[0], 12, 12), w1, line(OWNERS[1], 0, 24), w2, line(OWNERS[3], 12, 12)]

    def lay(parts, rows):
        vector = jnp.concatenate(parts)
        vector = jnp.pad(vector, (0, devices * rows * LANES - vector.shape[0]))
        return vector.reshape(devices, rows, LANES)

    whole = jnp.concatenate([lay(att, att_rows), lay(mlp, mlp_rows)], axis=1)
    return lax.psum_scatter(whole.reshape(-1, LANES), AXES, scatter_dimension=0, tiled=True)


def key_windows(segments, real):
    length = segments.shape[0]
    position = jnp.arange(length, dtype=jnp.int32)
    ids = jnp.where(real, segments, length + position)
    first = segments[0::QB]
    final = segments[QB - 1 :: QB]
    begin = jnp.sum((segments[None, :] < first[:, None]).astype(jnp.int32), axis=1)
    begin = jnp.where(real[0::QB], begin, position[0::QB])
    end = jnp.sum(((segments[None, :] <= final[:, None]) & real[None, :]).astype(jnp.int32), axis=1)
    end = jnp.where(real[QB - 1 :: QB], end, position[QB - 1 :: QB] + 1)
    begin = begin // SUB * SUB
    need = end - begin
    kind = sum((need > width).astype(jnp.int32) for width in CLASSES[:-1])
    widths = sum(
        jnp.where(kind == i, width, 0) for i, width in enumerate(CLASSES)
    )
    begin = jnp.minimum(begin, length - widths)
    chunks = (begin + widths + QB - 1) // QB
    return ids, jnp.stack([begin, kind, chunks]).astype(jnp.int32)


def local(tokens, cotangent, segment_ids, pad_mask, lengths, params):
    rows, width = tokens.shape
    wide, narrow = lax.axis_size("wide"), lax.axis_size("narrow")
    devices = wide * narrow
    att_count = 4 * width * width + 6 * width
    att_rows = (att_count // LANES + devices - 1) // devices
    mlp_rows = params.shape[0] - att_rows
    paired = (wide, narrow) == (4, 8)
    scale = 1.0 / math.sqrt(rows * devices)

    position = jnp.arange(rows, dtype=jnp.int32)
    real = (pad_mask > 0) & (position < lengths[0])
    ids, windows = key_windows(segment_ids, real)
    key_ids = ids.reshape(rows, 1)
    query_ids = ids.reshape(rows // QB, QB)

    if not paired:
        me = jnp.zeros((1,), jnp.int32)
        att, mlp = gather_plainly(params, att_rows, width)
        n1, qkv, small = project_qkv(me, tokens, att)
        mixed, x1, branch, n2, dm, stats, gb2 = attend(
            me, windows, qkv, tokens, cotangent, key_ids, query_ids, small, att
        )
        u, dz, gb1, *gmlp = feed_forward(me, n2, dm, small, mlp)
        output, dx1, others = feed_forward_out(me, u, dz, x1, cotangent, small, mlp)
        small_mlp = jnp.concatenate([others[:12], gb1, gb2, others[12:]])
        da, gwo0, gwo1, small_proj = split(me, dx1, branch, mixed, small, att)
        dqkv0 = attend_back(0, windows, qkv, da, stats, key_ids, query_ids)
        dqkv1 = attend_back(1, windows, qkv, da, stats, key_ids, query_ids)
        gatt0 = weight_grad(me, n1, dqkv0, gwo0)
        grad_input, *gatt1 = qkv_back(
            me, tokens, n1, dx1, dqkv0, dqkv1, small, small_proj, small_mlp, gwo1, att
        )
        owned = reduce_plainly(gatt0, gatt1, gmlp, att_rows, mlp_rows, width, devices)
        return output, grad_input, owned * scale

    me = lax.axis_index(AXES).astype(jnp.int32).reshape(1)
    tails = jnp.concatenate([params[att_rows - ATT_BEFORE : att_rows], params[-MLP_BEFORE:]])
    heads = jnp.concatenate([params[:ATT_AFTER], params[att_rows : att_rows + MLP_AFTER]])
    tails, heads = shifted(tails, 1), shifted(heads, -1)
    att_own, mlp_own = pack(me, params, tails, heads, att_rows)

    got = [exchange(att_own, k * Z0) for k in range(1, 4)]
    a, b = along_z(att_own[0], att_own[1], got)
    a, b, mlp_own, windows, key_ids, query_ids = together(
        a, b, mlp_own, windows, key_ids, query_ids
    )
    ax, by = exchange(a, X), exchange(b, Y)
    z1, z3 = exchange(mlp_own, Z0), exchange(mlp_own, 3 * Z0)
    a, b = joined(a, ax), joined(b, by)
    a, b, z1, z3, mlp_own = together(a, b, z1, z3, mlp_own)
    ay, bx = exchange(a, Y), exchange(b, X)
    ac, bc = exchange(a, C), exchange(b, C)
    z2 = exchange(mlp_own, 2 * Z0)
    m, n = along_z(mlp_own[0], mlp_own[1], [z1, z2, z3])
    ay, bx, ac, bc, m, n = together(ay, bx, ac, bc, m, n)
    ayc, bxc = exchange(ay, C), exchange(bx, C)
    att = together(a, ay, ac, ayc, b, bx, bc, bxc, m, n, tokens)
    *att, m, n, tokens_now = att
    mx, ny = exchange(m, X), exchange(n, Y)
    n1, qkv, small = project_qkv(me, tokens_now, att)
    m, n = joined(m, mx), joined(n, ny)
    m, n, qkv = together(m, n, qkv)
    my, nx = exchange(m, Y), exchange(n, X)
    mc, nc = exchange(m, C), exchange(n, C)
    mixed, x1, branch, n2, dm, stats, gb2 = attend(
        me, windows, qkv, tokens, cotangent, key_ids, query_ids, small, att
    )
    m, n, my, nx, mc, nc, n2 = together(m, n, my, nx, mc, nc, n2)
    myc, nxc = exchange(my, C), exchange(nx, C)
    mlp = (m, my, mc, myc, n, nx, nc, nxc)

    u, dz, gb1, *gmlp = feed_forward(me, n2, dm, small, mlp)

    mc, nc = exchange(gmlp[1], C), exchange(gmlp[3], C)
    output, dx1, others = feed_forward_out(me, u, dz, x1, cotangent, small, mlp)
    mc, nc, dx1 = together(mc, nc, dx1)
    m, n = [gmlp[0], mc], [gmlp[2], nc]
    mx, ny, dx1 = together(sent(m), sent(n), dx1)
    mx, ny = exchange(mx, X), exchange(ny, Y)
    da, gwo0, gwo1, small_proj = split(me, dx1, branch, mixed, small, att)
    dqkv0 = attend_back(0, windows, qkv, da, stats, key_ids, query_ids)
    mx, ny, dqkv0 = together(mx, ny, dqkv0)
    m, n = kept(m) + [mx], kept(n) + [ny]
    my, nx, dqkv0, da = together(sent(m), sent(n), dqkv0, da)
    my, nx = exchange(my, Y), exchange(nx, X)
    gatt0 = weight_grad(me, n1, dqkv0, gwo0)
    my, nx, *gatt0 = together(my, nx, *gatt0)
    m, n = kept(m) + [my], kept(n) + [nx]
    z1, z2, z3 = [z_part(m, n, k).astype(BF16) for k in range(1, 4)]
    z1, z2, z3, da, *gatt0 = together(z1, z2, z3, da, *gatt0)
    ac, bc = exchange(gatt0[1], C), exchange(gatt0[3], C)
    z1, z2 = exchange(z1, Z0), exchange(z2, 2 * Z0)
    dqkv1 = attend_back(1, windows, qkv, da, stats, key_ids, query_ids)
    ac, bc, z1, z2, dqkv1 = together(ac, bc, z1, z2, dqkv1)
    a, b = [gatt0[0], ac], [gatt0[2], bc]
    ax, by, z3, dqkv1 = together(sent(a), sent(b), z3, dqkv1)
    ax, by = exchange(ax, X), exchange(by, Y)
    z3 = exchange(z3, 3 * Z0)
    small_mlp = jnp.concatenate([others[:12], gb1, gb2, others[12:]])
    grad_input, *gatt1 = qkv_back(
        me, tokens, n1, dx1, dqkv0, dqkv1, small, small_proj, small_mlp, gwo1, att
    )
    ax, by, z3, *gatt1 = together(ax, by, z3, *gatt1)
    a, b = kept(a) + [ax], kept(b) + [by]
    ay, bx, c1, d1 = together(sent(a), sent(b), gatt1[1], gatt1[3])
    ay, bx = exchange(ay, Y), exchange(bx, X)
    c1, d1 = exchange(c1, C), exchange(d1, C)
    m_own = sum_terms([z_part(m, n, 0), z1, z2, z3])
    a, b = kept(a) + [ay], kept(b) + [bx]
    c, d = [gatt1[0], c1], [gatt1[2], d1]
    sends = [z_part(a, b, k).astype(BF16) for k in range(1, 4)]
    cx, dy, m_own, *sends = together(sent(c), sent(d), m_own, *sends)
    cx, dy = exchange(cx, X), exchange(dy, Y)
    got = [exchange(part, (k + 1) * Z0) for k, part in enumerate(sends)]
    c, d = kept(c) + [cx], kept(d) + [dy]
    cy, dx, *got = together(sent(c), sent(d), *got)
    group0 = sum_terms([z_part(a, b, 0)] + got)
    cy, dx = exchange(cy, Y), exchange(dx, X)
    c, d = kept(c) + [cy], kept(d) + [dx]
    sends = [z_part(c, d, k).astype(BF16) for k in range(1, 4)]
    group0, *sends = together(group0, *sends)
    got = [exchange(part, (k + 1) * Z0) for k, part in enumerate(sends)]
    group1 = sum_terms([z_part(c, d, 0)] + got)
    mine, to_before, to_after = spread(me, group0, group1, m_own, att_rows, mlp_rows, scale)
    grad_params = close(mine, shifted(to_after, 1), shifted(to_before, -1), att_rows)
    return output, grad_input, grad_params


def solution(mesh):
    return jax.shard_map(
        local,
        mesh=mesh,
        in_specs=(
            P(AXES, None),
            P(AXES, None),
            P(AXES),
            P(AXES),
            P(AXES),
            P(AXES, None),
        ),
        out_specs=(P(AXES, None), P(AXES, None), P(AXES, None)),
        check_vma=False,
    )
```

```python
import math
from functools import partial

import jax
import jax.numpy as jnp
from jax import lax
from jax.experimental import pallas as pl
from jax.experimental.pallas import tpu as pltpu
from jax.sharding import PartitionSpec as P

FF = 3072
HEADS = 12
EPSILON = 1e-06
NEGATIVE = -1e30
AXES = ("wide", "narrow")
LANES = 128
SUB = 16
QB = 128
MEGA = 1 << 20
GRANT = 58 * MEGA
F32 = jnp.float32
BF16 = jnp.bfloat16

BLOCKS = 32
QKV_BLOCKS, QKV_RT, QKV_CT = 24, 2, 18
WO_BLOCKS, WO_RT, WO_CT = 8, 6, 6
W1_BLOCKS, W1_RT, W1_CT = 16, 3, 24
W2_BLOCKS, W2_RT, W2_CT = 16, 12, 6
ATT_HALF, MLP_HALF = 18, 36
ATT_SENT = ATT_HALF + 1
ATT_PART = 9
HALF_BLOCKS = BLOCKS // 2
CHUNK = 768
CHUNKS = FF // CHUNK

G1, C1, BQ, BV, BO, S1 = 0, 6, 12, 18, 24, 30
G2, C2, B1, B2, S2 = 36, 42, 48, 72, 78
SMALL = 88

NT = (((1,), (1,)), ((), ()))
NN = (((1,), (0,)), ((), ()))
TN = (((0,), (0,)), ((), ()))


def mm(lhs, rhs, dims):
    return lax.dot_general(lhs, rhs, dims, preferred_element_type=F32)


def row_of(ref, first, count):
    return jnp.concatenate([ref[first + k : first + k + 1, :] for k in range(count)], axis=1)


def put_row(ref, first, values):
    for k in range(values.shape[1] // LANES):
        ref[first + k : first + k + 1, :] = values[:, k * LANES : (k + 1) * LANES]


def fold8(values):
    rows, columns = values.shape
    return jnp.sum(values.reshape(rows // 8, 8, columns), axis=0)


def total(values):
    return jnp.sum(values, axis=0, keepdims=True)


def vmem():
    return pl.BlockSpec(memory_space=pltpu.VMEM)


def smem():
    return pl.BlockSpec(memory_space=pltpu.SMEM)


def hbm():
    return pl.BlockSpec(memory_space=pltpu.HBM)


def shape(dims, kind):
    return jax.ShapeDtypeStruct(dims, kind)


def cost(flops, moved, exps=0):
    return pl.CostEstimate(flops=int(flops), transcendentals=int(exps), bytes_accessed=int(moved))


def normalized(values):
    center = values - jnp.mean(values, axis=-1, keepdims=True)
    inverse = lax.rsqrt(jnp.mean(center * center, axis=-1, keepdims=True) + EPSILON)
    return center * inverse, inverse


def norm_pullback(unit, inverse, grad, gain):
    scaled = grad * gain
    first = jnp.mean(scaled, axis=-1, keepdims=True)
    second = jnp.mean(scaled * unit, axis=-1, keepdims=True)
    return inverse * (scaled - first - unit * second)


def gelu_pair(z):
    magnitude = jnp.abs(z)
    t = 1.0 / (1.0 + (0.3275911 * math.sqrt(0.5)) * magnitude)
    density = jnp.exp(z * z * -0.5)
    tail = 0.5 * 1.061405429
    tail = tail * t + 0.5 * -1.453152027
    tail = tail * t + 0.5 * 1.421413741
    tail = tail * t + 0.5 * -0.284496736
    tail = tail * t + 0.5 * 0.254829592
    tail = tail * t * density
    cumulative = jnp.where(z < 0, tail, 1.0 - tail)
    return z * cumulative, cumulative + z * density * (1.0 / math.sqrt(2.0 * math.pi))


def fetch(copies):
    for copy in copies:
        copy.start()


def settle(copies):
    for copy in copies:
        copy.wait()


ATT_BEFORE, ATT_AFTER = 64, 32
MLP_BEFORE, MLP_AFTER = 64, 40


def window_offsets(me, att_rows, mlp_rows):
    att = ATT_BEFORE + 12 + me * (576 - att_rows) + jnp.where(me < QKV_BLOCKS, 0, 12)
    mlp = MLP_BEFORE + 12 + me * (1152 - mlp_rows) + jnp.where(me < W1_BLOCKS, 0, 24)
    return att, mlp


def each_tile(me, act):
    for name, blocks, rt_count, ct_count, mine in (
        ("qkv", QKV_BLOCKS, QKV_RT, QKV_CT, me < QKV_BLOCKS),
        ("wo", WO_BLOCKS, WO_RT, WO_CT, me >= QKV_BLOCKS),
        ("w1", W1_BLOCKS, W1_RT, W1_CT, me < W1_BLOCKS),
        ("w2", W2_BLOCKS, W2_RT, W2_CT, me >= W1_BLOCKS),
    ):

        @pl.when(mine)
        def _(name=name, rt_count=rt_count, ct_count=ct_count):
            for ct in range(ct_count):
                for rt in range(rt_count):
                    act(name, rt, ct, rt * SUB * ct_count + ct, ct_count)


def half_place(name, rt, ct):
    if name == "qkv":
        return ct // 9, ct % 9 * QKV_RT + rt
    if name == "wo":
        return rt // 3, rt % 3 * WO_CT + ct
    if name == "w1":
        return ct // 12, ct % 12 * W1_RT + rt
    return rt // 6, rt % 6 * W2_CT + ct


def part_place(name, rt, ct):
    if name == "qkv":
        return ct % 6 // 3, rt, ct // 6 * 3 + ct % 3
    place = rt * WO_CT + ct
    return place // 18, place // ATT_PART % 2, place % ATT_PART


def qkv_group(g):
    return [6 * third + 3 * g + i for third in range(3) for i in range(3)]


def small_rows(me, act):
    @pl.when(me == 0)
    def _():
        act("att", True, 12, G1)
        act("mlp", True, 12, G2)

    @pl.when(me == QKV_BLOCKS - 1)
    def _():
        act("att", False, 12, BQ)

    @pl.when(me == W1_BLOCKS - 1)
    def _():
        act("mlp", False, 24, B1)

    @pl.when(me == BLOCKS - 1)
    def _():
        act("att", False, 12, BO)
        act("mlp", False, 12, B2)


OWNERS = (0, W1_BLOCKS - 1, QKV_BLOCKS - 1, BLOCKS - 1)


def sent_rows(kind, first):
    return 12 if kind == "mlp" and first in (G2, B2) else 0


def pack_kernel(att_rows, me_ref, own, tails, heads, att, mlp, win_a, win_m, table):
    me = me_ref[0]
    mlp_rows = own.shape[0] - att_rows
    win_a[0:ATT_BEFORE, :] = tails[0:ATT_BEFORE, :]
    win_a[ATT_BEFORE : ATT_BEFORE + att_rows, :] = own[0:att_rows, :]
    win_a[ATT_BEFORE + att_rows :, :] = heads[0:ATT_AFTER, :]
    win_m[0:MLP_BEFORE, :] = tails[ATT_BEFORE:, :]
    win_m[MLP_BEFORE : MLP_BEFORE + mlp_rows, :] = own[att_rows:, :]
    win_m[MLP_BEFORE + mlp_rows :, :] = heads[ATT_AFTER:, :]
    att_off, mlp_off = window_offsets(me, att_rows, mlp_rows)

    def tile(name, rt, ct, first, stride):
        attention = name in ("qkv", "wo")
        window, out, off = (win_a, att, att_off) if attention else (win_m, mlp, mlp_off)
        values = window[pl.ds(off + first, SUB, stride=stride), :]
        out[half_place(name, rt, ct)] = values.astype(BF16)

    each_tile(me, tile)
    table[...] = jnp.zeros_like(table)

    def vector(kind, before, rows, first):
        window, off, size = (win_a, att_off, 576) if kind == "att" else (win_m, mlp_off, 1152)
        start = off - 12 if before else off + size
        place = sent_rows(kind, first)
        table[place : place + rows, :] = window[pl.ds(start, rows), :]

    small_rows(me, vector)
    att[0, ATT_HALF] = table[0:SUB, :].astype(BF16)
    att[1, ATT_HALF] = table[SUB : 2 * SUB, :].astype(BF16)


def pack(me, own, tails, heads, att_rows):
    mlp_rows = own.shape[0] - att_rows
    return pl.pallas_call(
        partial(pack_kernel, att_rows),
        out_shape=(
            shape((2, ATT_SENT, SUB, LANES), BF16),
            shape((2, MLP_HALF, SUB, LANES), BF16),
        ),
        in_specs=[smem(), vmem(), vmem(), vmem()],
        out_specs=(vmem(), vmem()),
        scratch_shapes=[
            pltpu.VMEM((ATT_BEFORE + att_rows + ATT_AFTER, LANES), F32),
            pltpu.VMEM((MLP_BEFORE + mlp_rows + MLP_AFTER, LANES), F32),
            pltpu.VMEM((2 * SUB, LANES), F32),
        ],
        name="pack",
    )(me, own, tails, heads)


def spread_kernel(
    att_rows, scale, me_ref, group0, group1, mlp, mine, to_before, to_after, win_a, win_m, table
):
    me = me_ref[0]
    mlp_rows = mine.shape[0] - att_rows
    att_off, mlp_off = window_offsets(me, att_rows, mlp_rows)
    win_a[...] = jnp.zeros_like(win_a)
    win_m[...] = jnp.zeros_like(win_m)

    def tile(name, rt, ct, first, stride):
        if name in ("qkv", "wo"):
            g, half, index = part_place(name, rt, ct)
            values = (group0, group1)[g][half, index]
            win_a[pl.ds(att_off + first, SUB, stride=stride), :] = values * scale
        else:
            values = mlp[half_place(name, rt, ct)]
            win_m[pl.ds(mlp_off + first, SUB, stride=stride), :] = values * scale

    each_tile(me, tile)
    for h in range(2):
        table[SUB * h : SUB * h + SUB, :] = group1[h, ATT_PART] * scale

    def vector(kind, before, rows, first):
        window, off, size = (win_a, att_off, 576) if kind == "att" else (win_m, mlp_off, 1152)
        start = off - 12 if before else off + size
        place = sent_rows(kind, first)
        window[pl.ds(start, rows), :] = table[place : place + rows, :]

    small_rows(me, vector)
    mine[0:att_rows, :] = win_a[ATT_BEFORE : ATT_BEFORE + att_rows, :]
    mine[att_rows:, :] = win_m[MLP_BEFORE : MLP_BEFORE + mlp_rows, :]
    to_before[0:ATT_BEFORE, :] = win_a[0:ATT_BEFORE, :]
    to_before[ATT_BEFORE:, :] = win_m[0:MLP_BEFORE, :]
    to_after[0:ATT_AFTER, :] = win_a[ATT_BEFORE + att_rows :, :]
    to_after[ATT_AFTER:, :] = win_m[MLP_BEFORE + mlp_rows :, :]


def spread(me, group0, group1, mlp, att_rows, mlp_rows, scale):
    return pl.pallas_call(
        partial(spread_kernel, att_rows, scale),
        out_shape=(
            shape((att_rows + mlp_rows, LANES), F32),
            shape((ATT_BEFORE + MLP_BEFORE, LANES), F32),
            shape((ATT_AFTER + MLP_AFTER, LANES), F32),
        ),
        in_specs=[smem(), vmem(), vmem(), vmem()],
        out_specs=(vmem(), vmem(), vmem()),
        scratch_shapes=[
            pltpu.VMEM((ATT_BEFORE + att_rows + ATT_AFTER, LANES), F32),
            pltpu.VMEM((MLP_BEFORE + mlp_rows + MLP_AFTER, LANES), F32),
            pltpu.VMEM((2 * SUB, LANES), F32),
        ],
        name="spread",
    )(me, group0, group1, mlp)


def close_kernel(att_rows, mine, below, above, out):
    rows = mine.shape[0]
    out[...] = mine[...]
    out[0:ATT_AFTER, :] += below[0:ATT_AFTER, :]
    out[att_rows : att_rows + MLP_AFTER, :] += below[ATT_AFTER:, :]
    out[att_rows - ATT_BEFORE : att_rows, :] += above[0:ATT_BEFORE, :]
    out[rows - MLP_BEFORE : rows, :] += above[ATT_BEFORE:, :]


def close(mine, below, above, att_rows):
    return pl.pallas_call(
        partial(close_kernel, att_rows),
        out_shape=shape(mine.shape, F32),
        in_specs=[vmem()] * 3,
        out_specs=vmem(),
        name="close",
    )(mine, below, above)


def spot(h, d):
    x, c, z, y = d >> 4, (d >> 3) & 1, (d >> 1) & 3, d & 1
    return c * 16 + (y * 8 + x * 4 if h == 0 else x * 8 + y * 4) + z


SLOTS = [sorted(range(BLOCKS), key=partial(spot, h)) for h in range(2)]


def fill_spots(me, spots):
    for h in range(2):
        mine = spot(h, me)
        for d in range(BLOCKS):
            spots[h, d] = jnp.bitwise_xor(mine, spot(h, d))


def slots_scratch(tiles):
    return pltpu.VMEM((2, BLOCKS, tiles, SUB, LANES), BF16)


def spots_scratch():
    return pltpu.SMEM((2, BLOCKS), jnp.int32)


def arriving_slots(buffers, w, sems):
    return [
        pltpu.make_async_copy(buffers[i], w.at[i // 4, pl.ds(i % 4 * 8, 8)], sems.at[i])
        for i in range(8)
    ]


def leaving_slots(buffers, w, sems):
    return [
        pltpu.make_async_copy(w.at[i // 2, pl.ds(i % 2 * 16, 16)], buffers[i], sems.at[i])
        for i in range(4)
    ]


def qkv_column(w, spots, ct):
    h, place = ct // 9, ct % 9 * QKV_RT
    tiles = [w[h, spots[h, d], place + rt] for d in range(QKV_BLOCKS) for rt in range(QKV_RT)]
    return jnp.concatenate(tiles, axis=0)


def wo_matrix(w, spots):
    columns = []
    for ct in range(WO_CT):
        tiles = [
            w[rt // 3, spots[rt // 3, QKV_BLOCKS + i] & 7, rt % 3 * WO_CT + ct]
            for i in range(WO_BLOCKS)
            for rt in range(WO_RT)
        ]
        columns.append(jnp.concatenate(tiles, axis=0))
    return jnp.concatenate(columns, axis=1)


def dma(count):
    return pltpu.SemaphoreType.DMA((count,))


def norm_rows(rows, gain, shift, source, target, step=256):
    def one(i, carry):
        at = pl.ds(pl.multiple_of(i * step, step), step)
        unit, _ = normalized(source[at, :].astype(F32))
        target[at, :] = (unit * gain + shift).astype(BF16)
        return carry

    lax.fori_loop(0, rows // step, one, 0)


def qkv_kernel(me_ref, tokens, *refs):
    buffers, (n1, qkv, small, w, spots, x, unit, triple, sems, own) = refs[:8], refs[8:]
    coming = pltpu.make_async_copy(tokens, x, own.at[0])
    coming.start()
    weights = arriving_slots(buffers, w, sems)
    fetch(weights)
    fill_spots(me_ref[0], spots)
    settle(weights)
    tables = [
        jnp.concatenate([w[h, spots[h, d], ATT_HALF] for h in range(2)], axis=0).astype(F32)
        for d in OWNERS
    ]
    small[G1 : G1 + 12, :] = tables[0][0:12]
    small[G2 : G2 + 12, :] = tables[0][12:24]
    small[B1 : B1 + 24, :] = tables[1][0:24]
    small[BQ : BQ + 12, :] = tables[2][0:12]
    small[BO : BO + 12, :] = tables[3][0:12]
    small[B2 : B2 + 12, :] = tables[3][12:24]
    small[SMALL - 4 :, :] = jnp.zeros((4, LANES), F32)
    coming.wait()
    norm_rows(x.shape[0], row_of(small, G1, 6), row_of(small, C1, 6), x, unit)
    going = [pltpu.make_async_copy(unit, n1, own.at[0])]
    going[0].start()
    bias = jnp.concatenate(
        [row_of(small, BQ, 6), jnp.zeros((1, 768), F32), row_of(small, BV, 6)], axis=1
    )
    for c in range(QKV_CT // 2):
        weight = jnp.concatenate([qkv_column(w, spots, 2 * c + i) for i in range(2)], axis=1)
        lanes = slice(256 * c, 256 * c + 256)
        triple[:, lanes] = (mm(unit[...], weight, NN) + bias[:, lanes]).astype(BF16)
        going.append(
            pltpu.make_async_copy(triple.at[:, lanes], qkv.at[:, lanes], own.at[1 + c])
        )
        going[-1].start()
    settle(going)


def project_qkv(me, tokens, att):
    rows, width = tokens.shape
    return pl.pallas_call(
        qkv_kernel,
        out_shape=(
            shape((rows, width), BF16),
            shape((rows, 3 * width), BF16),
            shape((SMALL, LANES), F32),
        ),
        in_specs=[smem(), hbm()] + [hbm()] * 8,
        out_specs=(hbm(), hbm(), vmem()),
        scratch_shapes=[
            slots_scratch(ATT_SENT),
            spots_scratch(),
            pltpu.VMEM((rows, width), BF16),
            pltpu.VMEM((rows, width), BF16),
            pltpu.VMEM((rows, 3 * width), BF16),
            dma(8),
            dma(1 + QKV_CT // 2),
        ],
        compiler_params=pltpu.CompilerParams(vmem_limit_bytes=GRANT),
        cost_estimate=cost(6 * rows * width * width, 12 * rows * width),
        name="qkv_forward",
    )(me, tokens, *att)


CLASSES = (128, 256, 384, 512, 768)


def head_masked(block):
    lane = lax.broadcasted_iota(jnp.int32, block.shape, 1)
    zero = jnp.zeros_like(block)
    return jnp.concatenate(
        [jnp.where(lane < 64, block, zero), jnp.where(lane >= 64, block, zero)], axis=0
    )


def pick_heads(both):
    return jnp.concatenate([both[0:64, 0:QB], both[64:128, QB : 2 * QB]], axis=0)


def mask_bias(start, width, b, key_ids, query_ids, bias):
    for j in range(width // QB):
        at = pl.ds(pl.multiple_of(start + j * QB, SUB), QB)
        same = key_ids[at, :] == query_ids[pl.ds(b, 1), :]
        bias[j * QB : (j + 1) * QB, :] = jnp.where(same, 0.0, NEGATIVE)


PAIRS = HEADS // 2


def attend_block(b, start, width, qkv, mixed, stats, bias, scores):
    rows = pl.ds(pl.multiple_of(b * QB, QB), QB)
    pieces = [slice(j * QB, (j + 1) * QB) for j in range(width // QB)]
    for p in range(PAIRS):
        lanes, key_lanes, value_lanes = [
            slice(LANES * (PAIRS * third + p), LANES * (PAIRS * third + p + 1))
            for third in range(3)
        ]
        queries = head_masked(qkv[rows, lanes] * 0.125)
        highest = jnp.full((8, 2 * QB), NEGATIVE, F32)
        for piece in pieces:
            at = pl.ds(pl.multiple_of(start + piece.start, SUB), QB)
            part = mm(qkv[at, key_lanes], queries, NT)
            part = part + jnp.concatenate([bias[piece, :]] * 2, axis=1)
            scores[p, piece, :] = part
            highest = jnp.maximum(highest, jnp.max(part.reshape(QB // 8, 8, 2 * QB), axis=0))
        highest = jnp.max(highest, axis=0, keepdims=True)
        summed = jnp.zeros((8, 2 * QB), F32)
        both = jnp.zeros((LANES, 2 * QB), F32)
        for piece in pieces:
            at = pl.ds(pl.multiple_of(start + piece.start, SUB), QB)
            raised = jnp.exp(scores[p, piece, :] - highest)
            summed = summed + fold8(raised)
            both = both + mm(qkv[at, value_lanes], raised.astype(BF16), TN)
        inverse = 1.0 / total(summed)
        mixed[rows, lanes] = pick_heads(both * inverse).T.astype(BF16)
        stats[b * PAIRS + p, 0:1, :] = highest
        stats[b * PAIRS + p, 1:2, :] = inverse


def wo_scratch():
    return pltpu.VMEM((2, WO_BLOCKS, ATT_SENT, SUB, LANES), BF16)


def wo_copies(buffers, w, sems, core, x):
    copies = []
    for y in range(2):
        source = buffers[2 * core + y].at[pl.ds(4 * x, 4)]
        copies.append(pltpu.make_async_copy(source, w.at[0, pl.ds(4 * y, 4)], sems.at[y]))
    copies.append(pltpu.make_async_copy(buffers[4 + 2 * core + x], w.at[1], sems.at[2]))
    return copies


def fetch_wo(me, buffers, w, spots, sems):
    fill_spots(me, spots)
    for h in range(2):
        for i in range(WO_BLOCKS):
            place = spot(h, jnp.bitwise_xor(me, QKV_BLOCKS + i) & 7)
            spots[h, QKV_BLOCKS + i] = (place >> (1 if h == 0 else 0)) & 4 | place & 3
    far = jnp.bitwise_xor(me, QKV_BLOCKS)
    for core in range(2):
        for x in range(2):

            @pl.when((far >> 3) == 2 * x + core)
            def _(core=core, x=x):
                fetch(wo_copies(buffers, w, sems, core, x))


def wait_wo(buffers, w, sems):
    settle(wo_copies(buffers, w, sems, 0, 0))


def attend_kernel(me_ref, windows, qkv, tokens, cot, key_ids, query_ids, small, *refs):
    buffers, refs = refs[:8], refs[8:]
    mixed, x1, branch, n2, dm, stats, gb2 = refs[:7]
    triple, x, g, mix, mid, out, unit, scaled, bias, scores, w, spots, sems, own, chunk_sems = refs[7:]
    rows = tokens.shape[0]
    blocks = rows // QB

    def chunk(i):
        at = pl.ds(pl.multiple_of(i * QB, QB), QB)
        return pltpu.make_async_copy(qkv.at[at, :], triple.at[at, :], chunk_sems.at[i])

    for i in range(blocks):
        chunk(i).start()
    coming = [
        pltpu.make_async_copy(tokens, x, own.at[0]),
        pltpu.make_async_copy(cot, g, own.at[1]),
    ]
    fetch(coming)
    fetch_wo(me_ref[0], buffers, w, spots, sems)

    def one_block(b, loaded):
        start = pl.multiple_of(windows[0, b], SUB)
        needed = jnp.maximum(windows[2, b], loaded)

        def arrived(i, carry):
            chunk(i).wait()
            return carry

        lax.fori_loop(loaded, needed, arrived, 0)
        for index, width in enumerate(CLASSES):

            @pl.when(windows[1, b] == index)
            def _(width=width):
                mask_bias(start, width, b, key_ids, query_ids, bias)
                attend_block(b, start, width, triple, mix, stats, bias, scores)

        return needed

    loaded = lax.fori_loop(0, blocks, one_block, jnp.int32(0))

    def arrived(i, carry):
        chunk(i).wait()
        return carry

    lax.fori_loop(loaded, blocks, arrived, 0)
    going = [pltpu.make_async_copy(mix, mixed, own.at[2])]
    going[0].start()
    wait_wo(buffers, w, sems)
    settle(coming)
    bo, s1 = row_of(small, BO, 6), row_of(small, S1, 6)
    gain, shift = row_of(small, G2, 6), row_of(small, C2, 6)
    s2 = row_of(small, S2, 6)
    weight = wo_matrix(w, spots)
    step = 256
    sums = jnp.zeros((8, 768), F32)
    for i in range(rows // step):
        at = slice(i * step, (i + 1) * step)
        made = mm(mix[at, :], weight, NN) + bo
        out[at, :] = made.astype(BF16)
        values = x[at, :].astype(F32) + s1 * made
        mid[at, :] = values
        normal, _ = normalized(values)
        unit[at, :] = (normal * gain + shift).astype(BF16)
        rounded = (g[at, :].astype(F32) * s2).astype(BF16)
        scaled[at, :] = rounded
        sums = sums + fold8(rounded.astype(F32))
        for k, (source, target) in enumerate(
            ((out, branch), (mid, x1), (unit, n2), (scaled, dm))
        ):
            sem = own.at[3 + 4 * i + k]
            going.append(pltpu.make_async_copy(source.at[at, :], target.at[at, :], sem))
            going[-1].start()
    put_row(gb2, 0, total(sums))
    settle(going)


def attend(me, windows, qkv, tokens, cot, key_ids, query_ids, small, att):
    rows, width = tokens.shape
    row = lambda kind: pltpu.VMEM((rows, width), kind)
    return pl.pallas_call(
        attend_kernel,
        out_shape=(
            shape((rows, width), BF16),
            shape((rows, width), F32),
            shape((rows, width), BF16),
            shape((rows, width), BF16),
            shape((rows, width), BF16),
            shape((rows // QB * PAIRS, 2, 2 * QB), F32),
            shape((6, LANES), F32),
        ),
        in_specs=[smem(), smem(), hbm(), hbm(), hbm(), vmem(), vmem(), vmem()] + [hbm()] * 8,
        out_specs=(hbm(),) * 5 + (vmem(), vmem()),
        scratch_shapes=[
            pltpu.VMEM((rows, 3 * width), BF16),
            row(BF16),
            row(BF16),
            row(BF16),
            row(F32),
            row(BF16),
            row(BF16),
            row(BF16),
            pltpu.VMEM((CLASSES[-1], QB), F32),
            pltpu.VMEM((PAIRS, CLASSES[-1], 2 * QB), F32),
            wo_scratch(),
            spots_scratch(),
            dma(3),
            dma(3 + 4 * rows // 256),
            dma(rows // QB),
        ],
        compiler_params=pltpu.CompilerParams(vmem_limit_bytes=GRANT),
        cost_estimate=cost(2 * rows * rows * width, 20 * rows * width, 4 * rows * rows),
        name="attend_forward",
    )(me, windows, qkv, tokens, cot, key_ids, query_ids, small, *att)


def lay_matrix(w, spots, name, blocks, first, rt_count, columns, out):
    def one_block(d, carry):
        places = [spots[h, first + d] for h in range(2)]
        base = pl.multiple_of(d * rt_count * SUB, SUB)
        for rt in range(rt_count):
            for column, ct in enumerate(columns):
                h, index = half_place(name, rt, ct)
                at = pl.ds(pl.multiple_of(base + rt * SUB, SUB), SUB)
                out[at, LANES * column : LANES * (column + 1)] = w[h, places[h], index]
        return carry

    lax.fori_loop(0, blocks, one_block, 0)


def lay_w1(w, spots, out):
    lay_matrix(w, spots, "w1", W1_BLOCKS, 0, W1_RT, range(W1_CT), out)


def lay_w2(w, spots, out):
    lay_matrix(w, spots, "w2", W2_BLOCKS, W1_BLOCKS, W2_RT, range(W2_CT), out)


def w2_place(spots, f, row, ct):
    rt = row % W2_RT
    h = rt // 6
    return h, spots[h, W1_BLOCKS + 4 * f + row // W2_RT], rt % 6 * W2_CT + ct


TALL = 256
PARTS = CHUNK // 256


def mlp_kernel(me_ref, n2_in, dm_in, small, *refs):
    arriving, refs = refs[:8], refs[8:]
    u_out, dz_out, vectors, *leaving = refs[:7]
    w, first, second, spots, n2, dm, u, dz, zs, dus, bias_sums, b1_lines, sems, own = refs[7:]
    rows, width = n2.shape
    tiles = rows // TALL
    coming = [
        pltpu.make_async_copy(n2_in, n2, own.at[0]),
        pltpu.make_async_copy(dm_in, dm, own.at[1]),
    ]
    fetch(coming)
    weights = arriving_slots(arriving, w, sems)
    fetch(weights)
    fill_spots(me_ref[0], spots)
    bias_sums[...] = jnp.zeros_like(bias_sums)
    for f in range(CHUNKS):
        b1_lines[f : f + 1, :] = row_of(small, B1 + 6 * f, 6)
    settle(coming + weights)
    lay_w1(w, spots, first)
    lay_w2(w, spots, second)

    units = [(t, c) for c in range(PARTS) for t in range(tiles)]

    def lanes_of(f, c):
        return pl.ds(pl.multiple_of(CHUNK * f + 256 * c, 256), 256)

    def outward(f):
        chunk = pl.ds(pl.multiple_of(CHUNK * f, CHUNK), CHUNK)
        return [
            pltpu.make_async_copy(u.at[:, chunk], u_out.at[:, chunk], own.at[2 * f]),
            pltpu.make_async_copy(dz.at[:, chunk], dz_out.at[:, chunk], own.at[2 * f + 1]),
        ]

    def one_chunk(f, carry):
        def multiply(unit, slot):
            t, c = unit
            at = slice(TALL * t, TALL * t + TALL)
            zs[slot] = mm(n2[at, :], first[:, lanes_of(f, c)], NN)
            dus[slot] = mm(dm[at, :], second[lanes_of(f, c), :], NT)

        def activate(unit, slot):
            t, c = unit
            lanes = slice(256 * c, 256 * c + 256)
            bias = b1_lines[pl.ds(f, 1), lanes]
            folded = jnp.zeros((8, 256), F32)
            for r in range(TALL // 32):
                part = slice(32 * r, 32 * r + 32)
                place = slice(TALL * t + 32 * r, TALL * t + 32 * r + 32)
                value, slope = gelu_pair(zs[slot, part, :] + bias)
                u[place, lanes_of(f, c)] = value.astype(BF16)
                rounded = (dus[slot, part, :] * slope).astype(BF16)
                dz[place, lanes_of(f, c)] = rounded
                folded = folded + fold8(rounded.astype(F32))
            bias_sums[:, lanes_of(f, c)] += folded

        multiply(units[0], 0)
        for i, unit in enumerate(units):
            if i + 1 < len(units):
                multiply(units[i + 1], (i + 1) % 2)
            activate(unit, i % 2)
        fetch(outward(f))
        return carry

    lax.fori_loop(0, CHUNKS, one_chunk, 0)
    put_row(vectors, 0, total(bias_sums[...]))

    def one_grad(f, carry):
        for c in range(PARTS):
            grad = mm(u[:, lanes_of(f, c)], dm[...], TN)
            for r in range(SUB):
                for ct in range(W2_CT):
                    tile = grad[SUB * r : SUB * r + SUB, LANES * ct : LANES * ct + LANES]
                    w[w2_place(spots, f, SUB * c + r, ct)] = tile.astype(BF16)
        h, base = f >> 1, MLP_HALF // 2 * (f & 1)
        chunk = pl.ds(pl.multiple_of(CHUNK * f, CHUNK), CHUNK)
        for c in range(PARTS):
            lanes = slice(256 * c, 256 * c + 256)
            grad = mm(n2[:, lanes], dz[:, chunk], TN)
            for r in range(SUB):
                d, rt = (SUB * c + r) // W1_RT, (SUB * c + r) % W1_RT
                for ct in range(6):
                    tile = grad[SUB * r : SUB * r + SUB, LANES * ct : LANES * ct + LANES]
                    w[h, spots[h, d], base + ct * W1_RT + rt] = tile.astype(BF16)
        return carry

    lax.fori_loop(0, CHUNKS, one_grad, 0)
    copies = leaving_slots(leaving, w, sems)
    fetch(copies)
    for f in range(CHUNKS):
        settle(outward(f))
    settle(copies)


def feed_forward(me, n2, dm, small, mlp):
    rows, width = n2.shape
    half = shape((HALF_BLOCKS, MLP_HALF, SUB, LANES), BF16)
    return pl.pallas_call(
        mlp_kernel,
        out_shape=(
            shape((rows, FF), BF16),
            shape((rows, FF), BF16),
            shape((24, LANES), F32),
            half,
            half,
            half,
            half,
        ),
        in_specs=[smem(), hbm(), hbm(), vmem()] + [hbm()] * 8,
        out_specs=(hbm(), hbm(), vmem()) + (hbm(),) * 4,
        scratch_shapes=[
            slots_scratch(MLP_HALF),
            pltpu.VMEM((width, FF), BF16),
            pltpu.VMEM((FF, width), BF16),
            spots_scratch(),
            pltpu.VMEM((rows, width), BF16),
            pltpu.VMEM((rows, width), BF16),
            pltpu.VMEM((rows, FF), BF16),
            pltpu.VMEM((rows, FF), BF16),
            pltpu.VMEM((2, TALL, 256), F32),
            pltpu.VMEM((2, TALL, 256), F32),
            pltpu.VMEM((8, FF), F32),
            pltpu.VMEM((CHUNKS, CHUNK), F32),
            dma(8),
            dma(2 * CHUNKS),
        ],
        compiler_params=pltpu.CompilerParams(vmem_limit_bytes=GRANT),
        cost_estimate=cost(8 * rows * width * FF, 40 * MEGA),
        name="feed_forward",
    )(me, n2, dm, small, *mlp)


def matrix_copies(buffers, w, sems, x):
    copies = []
    for i in range(4):
        source = buffers[i].at[pl.ds(4 * x, 4)]
        copies.append(pltpu.make_async_copy(source, w.at[0, pl.ds(4 * i, 4)], sems.at[i]))
    for c in range(2):
        source = buffers[4 + 2 * c + x]
        copies.append(pltpu.make_async_copy(source, w.at[1, pl.ds(8 * c, 8)], sems.at[4 + c]))
    return copies


def fetch_matrix(me, buffers, w, spots, sems, first):
    def place(d):
        return ((d >> 3) & 1) * 8 + (d & 1) * 4 + ((d >> 1) & 3)

    for x in range(2):

        @pl.when((me >> 4) == (x ^ (first >> 4)))
        def _(x=x):
            fetch(matrix_copies(buffers, w, sems, x))

    mine = place(me)
    for d in range(W1_BLOCKS):
        for h in range(2):
            spots[h, first + d] = jnp.bitwise_xor(mine, place(d))


def wait_matrix(buffers, w, sems):
    settle(matrix_copies(buffers, w, sems, 0))


def matrix_scratch():
    return pltpu.VMEM((2, W1_BLOCKS, MLP_HALF, SUB, LANES), BF16)


def mlp_out_kernel(me_ref, u_in, x1_in, cot_in, small, *refs):
    arriving, refs = refs[:8], refs[8:]
    out, vectors, w, second, spots, u, x1, cot, macc, done, sums, sems, own = refs
    rows, width = x1.shape
    tiles = rows // TALL

    def tile_copy(source, target, t, k):
        at = pl.ds(pl.multiple_of(TALL * t, TALL), TALL)
        return pltpu.make_async_copy(source.at[at, :], target.at[at, :], own.at[k, t])

    fetch_matrix(me_ref[0], arriving, w, spots, sems, W1_BLOCKS)
    for t in range(tiles):
        tile_copy(u_in, u, t, 0).start()
    for t in range(tiles):
        tile_copy(x1_in, x1, t, 1).start()
        tile_copy(cot_in, cot, t, 2).start()
    bias, scale = row_of(small, B2, 6), row_of(small, S2, 6)
    sums[...] = jnp.zeros_like(sums)
    wait_matrix(arriving, w, sems)
    lay_w2(w, spots, second)

    def contract(t):
        at = pl.ds(pl.multiple_of(TALL * t, TALL), TALL)
        tile_copy(u_in, u, t, 0).wait()
        macc[at, :] = mm(u[at, :], second[...], NN)

    def finish(t):
        tile_copy(x1_in, x1, t, 1).wait()
        tile_copy(cot_in, cot, t, 2).wait()
        for part in range(TALL // 64):
            at = pl.ds(pl.multiple_of(TALL * t + 64 * part, 64), 64)
            contracted = macc[at, :] + bias
            done[at, :] = (x1[at, :] + scale * contracted).astype(BF16)
            sums[...] += fold8(cot[at, :].astype(F32) * contracted)
        tile_copy(done, out, t, 3).start()

    def one_tile(t, carry):
        contract(t)
        finish(t - 1)
        return carry

    contract(0)
    lax.fori_loop(1, tiles, one_tile, 0)
    finish(tiles - 1)
    put_row(vectors, 0, total(sums[...]))
    for t in range(tiles):
        tile_copy(done, out, t, 3).wait()


def feed_forward_out(me, u, x1, cot, small, mlp):
    rows, width = x1.shape
    row = lambda kind: pltpu.VMEM((rows, width), kind)
    return pl.pallas_call(
        mlp_out_kernel,
        out_shape=(shape((rows, width), BF16), shape((6, LANES), F32)),
        in_specs=[smem()] + [hbm()] * 3 + [vmem()] + [hbm()] * 8,
        out_specs=(hbm(), vmem()),
        scratch_shapes=[
            matrix_scratch(),
            pltpu.VMEM((FF, width), BF16),
            spots_scratch(),
            pltpu.VMEM((rows, FF), BF16),
            row(F32),
            row(BF16),
            row(F32),
            row(BF16),
            pltpu.VMEM((8, width), F32),
            dma(6),
            pltpu.SemaphoreType.DMA((4, rows // TALL)),
        ],
        compiler_params=pltpu.CompilerParams(vmem_limit_bytes=GRANT),
        cost_estimate=cost(2 * rows * width * FF, 20 * MEGA),
        name="feed_forward_out",
    )(me, u, x1, cot, small, *mlp)


def split_kernel(me_ref, dz_in, x1_in, cot_in, branch_in, mixed_in, small, *refs):
    buffers, att_buffers, refs = refs[:8], refs[8:16], refs[16:]
    dx1_out, da_out, gwo0, gwo1, vectors = refs[:5]
    w, first, spots, wo, wo_spots, dz, x1, cot, dnacc, dx1, branch, mixed, db, da = refs[5:19]
    parts, sums, sems, wo_sems, own = refs[19:]
    me = me_ref[0]
    rows, width = x1.shape
    tiles = rows // TALL

    def tile_copy(source, target, t, k):
        at = pl.ds(pl.multiple_of(TALL * t, TALL), TALL)
        return pltpu.make_async_copy(source.at[at, :], target.at[at, :], own.at[k, t])

    fetch_matrix(me, buffers, w, spots, sems, 0)
    for t in range(tiles):
        tile_copy(dz_in, dz, t, 0).start()
    for t in range(tiles):
        tile_copy(x1_in, x1, t, 1).start()
        tile_copy(cot_in, cot, t, 2).start()
        tile_copy(branch_in, branch, t, 3).start()
    fetch_wo(me, att_buffers, wo, wo_spots, wo_sems)
    late = pltpu.make_async_copy(mixed_in, mixed, own.at[4, 0])
    late.start()
    gain, scale = row_of(small, G2, 6), row_of(small, S1, 6)
    sums[...] = jnp.zeros_like(sums)
    wait_matrix(buffers, w, sems)
    lay_w1(w, spots, first)

    def contract(t):
        at = pl.ds(pl.multiple_of(TALL * t, TALL), TALL)
        tile_copy(dz_in, dz, t, 0).wait()
        dnacc[at, :] = mm(dz[at, :], first[...], NT)

    def finish(t):
        tile_copy(x1_in, x1, t, 1).wait()
        tile_copy(cot_in, cot, t, 2).wait()
        tile_copy(branch_in, branch, t, 3).wait()
        for half in range(2):
            at = pl.ds(pl.multiple_of(TALL * t + TALL // 2 * half, TALL // 2), TALL // 2)
            unit, inverse = normalized(x1[at, :])
            grad = dnacc[at, :]
            middle = cot[at, :].astype(F32) + norm_pullback(unit, inverse, grad, gain)
            dx1[at, :] = middle
            rounded = (middle * scale).astype(BF16)
            db[at, :] = rounded
            sums[0:8, :] += fold8(grad * unit)
            sums[8:16, :] += fold8(grad)
            sums[16:24, :] += fold8(rounded.astype(F32))
            sums[24:32, :] += fold8(middle * branch[at, :].astype(F32))
        tile_copy(dx1, dx1_out, t, 1).start()

    def one_tile(t, carry):
        contract(t)
        finish(t - 1)
        return carry

    contract(0)
    lax.fori_loop(1, tiles, one_tile, 0)
    finish(tiles - 1)
    for k in range(4):
        put_row(vectors, 6 * k, total(sums[8 * k : 8 * k + 8, :]))
    wait_wo(att_buffers, wo, wo_sems)
    weight = wo_matrix(wo, wo_spots)
    going = []
    for c in range(3):
        lanes = slice(256 * c, 256 * c + 256)
        da[:, lanes] = mm(db[...], weight[lanes, :], NT).astype(BF16)
        going.append(pltpu.make_async_copy(da.at[:, lanes], da_out.at[:, lanes], own.at[0, c]))
        going[-1].start()
    late.wait()
    for c in range(3):
        grad = mm(mixed[:, 256 * c : 256 * c + 256], db[...], TN)
        for r in range(SUB):
            i, rt = (SUB * c + r) // WO_RT, (SUB * c + r) % WO_RT
            for ct in range(WO_CT):
                tile = grad[SUB * r : SUB * r + SUB, LANES * ct : LANES * ct + LANES]
                g, half, index = part_place("wo", rt, ct)
                parts[g, half, i, index] = tile.astype(BF16)
    for g, target in enumerate((gwo0, gwo1)):
        going.append(pltpu.make_async_copy(parts.at[g], target, own.at[4, g]))
        going[-1].start()
    settle(going)
    for t in range(tiles):
        tile_copy(dx1, dx1_out, t, 1).wait()


def split(me, dz, x1, cot, branch, mixed, small, mlp, att):
    rows, width = x1.shape
    part = (2, WO_BLOCKS, ATT_PART, SUB, LANES)
    row = lambda kind: pltpu.VMEM((rows, width), kind)
    return pl.pallas_call(
        split_kernel,
        out_shape=(
            shape((rows, width), F32),
            shape((rows, width), BF16),
            shape(part, BF16),
            shape(part, BF16),
            shape((24, LANES), F32),
        ),
        in_specs=[smem()] + [hbm()] * 5 + [vmem()] + [hbm()] * 16,
        out_specs=(hbm(),) * 4 + (vmem(),),
        scratch_shapes=[
            matrix_scratch(),
            pltpu.VMEM((width, FF), BF16),
            spots_scratch(),
            wo_scratch(),
            spots_scratch(),
            pltpu.VMEM((rows, FF), BF16),
            row(F32),
            row(BF16),
            row(F32),
            row(F32),
            row(BF16),
            row(BF16),
            row(BF16),
            row(BF16),
            pltpu.VMEM((2,) + part, BF16),
            pltpu.VMEM((32, width), F32),
            dma(6),
            dma(3),
            pltpu.SemaphoreType.DMA((5, rows // TALL)),
        ],
        compiler_params=pltpu.CompilerParams(vmem_limit_bytes=GRANT),
        cost_estimate=cost(2 * rows * width * FF + 4 * rows * width * width, 40 * MEGA),
        name="feed_forward_in",
    )(me, dz, x1, cot, branch, mixed, small, *mlp, *att)


GROUP = PAIRS // 2
GROUP_LANES = GROUP * LANES


def attend_back_block(b, start, width, group, refs):
    q, k, v, da, stats, dq, dkeys, dvalues, bias = refs
    rows = pl.ds(pl.multiple_of(b * QB, QB), QB)
    at = pl.ds(start, width)
    mask = jnp.concatenate([bias[0:width, :]] * 2, axis=1)
    for p in range(GROUP):
        lanes = slice(LANES * p, LANES * p + LANES)
        place = b * PAIRS + GROUP * group + p
        queries = head_masked(q[rows, lanes] * 0.125)
        grads = head_masked(da[rows, lanes])
        highest = stats[place, 0:1, :]
        inverse = stats[place, 1:2, :]
        keys, values = k[at, lanes], v[at, lanes]
        weight = jnp.exp(mm(keys, queries, NT) + mask - highest) * inverse
        dweight = mm(values, grads, NT)
        inner_sum = total(fold8(weight * dweight))
        dvalues[at, lanes] += mm(weight.astype(BF16), grads, NN)
        dscore = (weight * (dweight - inner_sum)).astype(BF16)
        dkeys[at, lanes] += mm(dscore, queries, NN)
        both = mm(keys, dscore, TN)
        dq[rows, lanes] = (pick_heads(both) * 0.125).T.astype(BF16)


def attend_back_kernel(group, windows, qkv, da_in, stats, key_ids, query_ids, dqkv, *refs):
    q, k, v, da, out, dkeys, dvalues, bias, own = refs
    rows = q.shape[0]
    blocks = rows // QB
    lanes = slice(GROUP_LANES * group, GROUP_LANES * group + GROUP_LANES)
    coming = [pltpu.make_async_copy(da_in.at[:, lanes], da, own.at[3])]
    for third, target in enumerate((q, k, v)):
        first = LANES * PAIRS * third + GROUP_LANES * group
        source = qkv.at[:, first : first + GROUP_LANES]
        coming.append(pltpu.make_async_copy(source, target, own.at[third]))
    fetch(coming)
    dkeys[...] = jnp.zeros_like(dkeys)
    dvalues[...] = jnp.zeros_like(dvalues)
    settle(coming)
    dq = out.at[:, 0:GROUP_LANES]

    def one_block(b, carry):
        start = pl.multiple_of(windows[0, b], SUB)
        for index, width in enumerate(CLASSES):

            @pl.when(windows[1, b] == index)
            def _(width=width):
                mask_bias(start, width, b, key_ids, query_ids, bias)
                parts = (q, k, v, da, stats, dq, dkeys, dvalues, bias)
                attend_back_block(b, start, width, group, parts)

        return carry

    lax.fori_loop(0, blocks, one_block, 0)
    going = []
    for i in range(rows // 256):
        at = slice(256 * i, 256 * i + 256)
        out[at, GROUP_LANES : 2 * GROUP_LANES] = dkeys[at, :].astype(BF16)
        out[at, 2 * GROUP_LANES :] = dvalues[at, :].astype(BF16)
        going.append(pltpu.make_async_copy(out.at[at, :], dqkv.at[at, :], own.at[i]))
        going[-1].start()
    settle(going)


def attend_back(group, windows, qkv, da, stats, key_ids, query_ids):
    rows = qkv.shape[0]
    part = lambda kind: pltpu.VMEM((rows, GROUP_LANES), kind)
    return pl.pallas_call(
        partial(attend_back_kernel, group),
        out_shape=shape((rows, 3 * GROUP_LANES), BF16),
        in_specs=[smem(), hbm(), hbm(), vmem(), vmem(), vmem()],
        out_specs=hbm(),
        scratch_shapes=[
            part(BF16),
            part(BF16),
            part(BF16),
            part(BF16),
            pltpu.VMEM((rows, 3 * GROUP_LANES), BF16),
            part(F32),
            part(F32),
            pltpu.VMEM((CLASSES[-1], QB), F32),
            dma(4),
        ],
        compiler_params=pltpu.CompilerParams(vmem_limit_bytes=GRANT),
        cost_estimate=cost(3 * rows * rows * rows, 14 * rows * rows, 4 * rows * rows),
        name="attend_backward",
    )(windows, qkv, da, stats, key_ids, query_ids)


def put_qkv_grad(n1, dqkv, w, spots):
    for c in range(3):
        grad = mm(n1[:, 256 * c : 256 * c + 256], dqkv[...], TN)
        for r in range(SUB):
            d, rt = (SUB * c + r) // QKV_RT, (SUB * c + r) % QKV_RT
            place = spots[rt, d]
            for index in range(ATT_PART):
                tile = grad[SUB * r : SUB * r + SUB, LANES * index : LANES * index + LANES]
                w[rt, place, index] = tile.astype(BF16)


def put_wo_grad(gwo, w, spots):
    for h in range(2):
        for i in range(WO_BLOCKS):
            w[h, spots[h, QKV_BLOCKS + i], 0:ATT_PART] = gwo[h, i]


def weight_grad_kernel(me_ref, n1_in, dqkv_in, gwo_in, *refs):
    leaving, (w, spots, n1, dqkv, gwo, sems, own) = refs[:4], refs[4:]
    coming = [
        pltpu.make_async_copy(n1_in, n1, own.at[0]),
        pltpu.make_async_copy(dqkv_in, dqkv, own.at[1]),
        pltpu.make_async_copy(gwo_in, gwo, own.at[2]),
    ]
    fetch(coming)
    fill_spots(me_ref[0], spots)
    settle(coming)
    put_wo_grad(gwo, w, spots)
    put_qkv_grad(n1, dqkv, w, spots)
    copies = leaving_slots(leaving, w, sems)
    fetch(copies)
    settle(copies)


def weight_grad(me, n1, dqkv, gwo):
    rows, width = n1.shape
    half = shape((HALF_BLOCKS, ATT_PART, SUB, LANES), BF16)
    return pl.pallas_call(
        weight_grad_kernel,
        out_shape=(half,) * 4,
        in_specs=[smem()] + [hbm()] * 3,
        out_specs=(hbm(),) * 4,
        scratch_shapes=[
            slots_scratch(ATT_PART),
            spots_scratch(),
            pltpu.VMEM((rows, width), BF16),
            pltpu.VMEM(dqkv.shape, BF16),
            pltpu.VMEM(gwo.shape, BF16),
            dma(4),
            dma(3),
        ],
        compiler_params=pltpu.CompilerParams(vmem_limit_bytes=GRANT),
        cost_estimate=cost(3 * rows * width * width, 10 * rows * width),
        name="qkv_weight_grad",
    )(me, n1, dqkv, gwo)


def qkv_back_kernel(
    me_ref, tokens_in, n1_in, dx1_in, dqkv0_in, dqkv1_in, small, proj, mlp, gwo_in, *refs
):
    arriving, refs = refs[:8], refs[8:]
    dx_out, *leaving = refs[:5]
    w, gw, weight, spots, gwo, tokens, n1, dx1, dqkv0, dqkv1, dn, dx, sums, table = refs[5:19]
    sems, out_sems, own = refs[19:]
    rows = tokens.shape[0]
    tiles = rows // TALL

    def tile_copy(source, target, t, k):
        at = pl.ds(pl.multiple_of(TALL * t, TALL), TALL)
        return pltpu.make_async_copy(source.at[at, :], target.at[at, :], own.at[k, t])

    for t in range(tiles):
        tile_copy(dqkv0_in, dqkv0, t, 0).start()
        tile_copy(dqkv1_in, dqkv1, t, 1).start()
    weights = arriving_slots(arriving, w, sems)
    fetch(weights)
    for t in range(tiles):
        tile_copy(tokens_in, tokens, t, 2).start()
        tile_copy(dx1_in, dx1, t, 3).start()
    late = [
        pltpu.make_async_copy(n1_in, n1, own.at[4, 0]),
        pltpu.make_async_copy(gwo_in, gwo, own.at[4, 1]),
    ]
    fetch(late)
    sums[...] = jnp.zeros_like(sums)
    gain = row_of(small, G1, 6)
    fill_spots(me_ref[0], spots)
    settle(weights)
    columns = qkv_group(0) + qkv_group(1)
    lay_matrix(w, spots, "qkv", QKV_BLOCKS, 0, QKV_RT, columns, weight)

    def contract(t):
        at = pl.ds(pl.multiple_of(TALL * t, TALL), TALL)
        for g, (source, part) in enumerate(((dqkv0_in, dqkv0), (dqkv1_in, dqkv1))):
            tile_copy(source, part, t, g).wait()
            lanes = slice(384 * g, 384 * g + 384)
            sums[16:24, lanes] += fold8(part[at, 0:384].astype(F32))
            sums[24:32, lanes] += fold8(part[at, 768:1152].astype(F32))
        both = jnp.concatenate([dqkv0[at, :], dqkv1[at, :]], axis=1)
        dn[at, :] = mm(both, weight[...], NT)

    def finish(t):
        tile_copy(tokens_in, tokens, t, 2).wait()
        tile_copy(dx1_in, dx1, t, 3).wait()
        for half in range(2):
            at = pl.ds(pl.multiple_of(TALL * t + TALL // 2 * half, TALL // 2), TALL // 2)
            unit, inverse = normalized(tokens[at, :].astype(F32))
            grad = dn[at, :]
            dx[at, :] = dx1[at, :] + norm_pullback(unit, inverse, grad, gain)
            sums[0:8, :] += fold8(grad * unit)
            sums[8:16, :] += fold8(grad)
        tile_copy(dx, dx_out, t, 3).start()

    def one_tile(t, carry):
        contract(t)
        finish(t - 1)
        return carry

    contract(0)
    lax.fori_loop(1, tiles, one_tile, 0)
    finish(tiles - 1)

    def put_table(owner, *places):
        table[...] = jnp.zeros_like(table)
        for place, values in places:
            if values.shape[1] == LANES:
                table[place : place + values.shape[0], :] = values
            else:
                put_row(table, place, values)
        for h in range(2):
            gw[h, spots[h, owner], ATT_PART] = table[SUB * h : SUB * h + SUB, :].astype(BF16)

    put_table(
        OWNERS[0], (0, total(sums[0:8, :])), (6, total(sums[8:16, :])), (12, mlp[0:12, :])
    )
    put_table(OWNERS[1], (0, mlp[12:36, :]))
    put_table(OWNERS[2], (0, total(sums[16:24, :])), (6, total(sums[24:32, :])))
    put_table(OWNERS[3], (0, proj[...]), (12, mlp[36:48, :]))
    settle(late)
    put_wo_grad(gwo, gw, spots)
    put_qkv_grad(n1, dqkv1, gw, spots)
    copies = leaving_slots(leaving, gw, out_sems)
    fetch(copies)
    for t in range(tiles):
        tile_copy(dx, dx_out, t, 3).wait()
    settle(copies)


def qkv_back(me, tokens, n1, dx1, dqkv0, dqkv1, small, proj, mlp, gwo, att):
    rows, width = tokens.shape
    tiles = ATT_PART + 1
    half = shape((HALF_BLOCKS, tiles, SUB, LANES), BF16)
    row = lambda kind: pltpu.VMEM((rows, width), kind)
    return pl.pallas_call(
        qkv_back_kernel,
        out_shape=(shape((rows, width), F32), half, half, half, half),
        in_specs=[smem()] + [hbm()] * 5 + [vmem()] * 3 + [hbm()] * 9,
        out_specs=(hbm(),) * 5,
        scratch_shapes=[
            slots_scratch(ATT_SENT),
            slots_scratch(tiles),
            pltpu.VMEM((width, 3 * width), BF16),
            spots_scratch(),
            pltpu.VMEM(gwo.shape, BF16),
            row(BF16),
            row(BF16),
            row(F32),
            pltpu.VMEM(dqkv0.shape, BF16),
            pltpu.VMEM(dqkv1.shape, BF16),
            row(F32),
            row(F32),
            pltpu.VMEM((32, width), F32),
            pltpu.VMEM((2 * SUB, LANES), F32),
            dma(8),
            dma(4),
            pltpu.SemaphoreType.DMA((5, rows // TALL)),
        ],
        compiler_params=pltpu.CompilerParams(vmem_limit_bytes=GRANT),
        cost_estimate=cost(9 * rows * width * width, 30 * rows * width),
        name="qkv_backward",
    )(me, tokens, n1, dx1, dqkv0, dqkv1, small, proj, mlp, gwo, *att)


X, C, Z1, Z0, Y = 16, 8, 4, 2, 1


def exchange(values, bit):
    return lax.ppermute(values, AXES, [(d, d ^ bit) for d in range(BLOCKS)])


def shifted(values, by):
    pairs = [(d, d + by) for d in range(BLOCKS) if 0 <= d + by < BLOCKS]
    return lax.ppermute(values, AXES, pairs)


def together(*values):
    return lax.optimization_barrier(values)


def along_z(first, second, received):
    return (
        jnp.stack([first] + [r[0] for r in received]),
        jnp.stack([second] + [r[1] for r in received]),
    )


def joined(own, received):
    return jnp.concatenate([own, received])


def sum_terms(terms):
    summed = terms[0].astype(F32)
    for term in terms[1:]:
        summed = summed + term.astype(F32)
    return summed


def kept(terms):
    return [t[: t.shape[0] // 2] for t in terms]


def z_part(first, second, k):
    return jnp.stack([sum_terms([t[k] for t in terms]) for terms in (first, second)])


def sent(terms):
    return sum_terms([t[t.shape[0] // 2 :] for t in terms]).astype(BF16)


def attention_amounts(width):
    return [width, width, 3 * width * width, width, width, width * width, width, width]


def feedforward_amounts(width):
    return [width, width, width * FF, FF, FF * width, width, width]


def pieces_of(vector, amounts):
    out, offset = [], 0
    for amount in amounts:
        out.append(vector[offset : offset + amount])
        offset += amount
    return out


def tiles_by_column(matrix, blocks, rt):
    ct = matrix.shape[1] // LANES
    return matrix.reshape(blocks, rt, SUB, ct, LANES).transpose(0, 3, 1, 2, 4)


def tiles_by_row(matrix, blocks, rt):
    ct = matrix.shape[1] // LANES
    return matrix.reshape(blocks, rt, SUB, ct, LANES).transpose(0, 1, 3, 2, 4)


def gather_plainly(params, att_rows, width):
    rounded = params.astype(BF16)
    att = lax.all_gather(rounded[:att_rows], AXES, axis=0, tiled=True).reshape(-1)
    mlp = lax.all_gather(rounded[att_rows:], AXES, axis=0, tiled=True).reshape(-1)
    g1, c1, wqkv, bq, bv, wo, bo, s1 = pieces_of(att, attention_amounts(width))
    g2, c2, w1, b1, w2, b2, s2 = pieces_of(mlp, feedforward_amounts(width))
    tile = (SUB, LANES)
    att = jnp.concatenate(
        [
            tiles_by_column(wqkv.reshape(width, -1), QKV_BLOCKS, QKV_RT).reshape((-1, 36) + tile),
            tiles_by_row(wo.reshape(width, -1), WO_BLOCKS, WO_RT).reshape((-1, 36) + tile),
        ]
    )
    mlp = jnp.concatenate(
        [
            tiles_by_column(w1.reshape(width, -1), W1_BLOCKS, W1_RT).reshape((-1, 72) + tile),
            tiles_by_row(w2.reshape(FF, -1), W2_BLOCKS, W2_RT).reshape((-1, 72) + tile),
        ]
    )
    vectors = jnp.concatenate([g1, c1, bq, bv, bo, s1, g2, c2, b1, b2, s2]).astype(F32)
    lines = vectors.reshape(-1, LANES)
    sent = jnp.zeros((BLOCKS, 2 * SUB, LANES), F32)
    for owner, place, first, count in (
        (OWNERS[0], 0, G1, 12),
        (OWNERS[0], 12, G2, 12),
        (OWNERS[1], 0, B1, 24),
        (OWNERS[2], 0, BQ, 12),
        (OWNERS[3], 0, BO, 12),
        (OWNERS[3], 12, B2, 12),
    ):
        sent = sent.at[owner, place : place + count].set(lines[first : first + count])
    sent = sent.astype(BF16).reshape((BLOCKS, 2, 1) + tile)
    att = [jnp.concatenate([att[:, 18 * h : 18 * h + 18], sent[:, h]], axis=1) for h in range(2)]
    return by_slot(*att), by_slot(mlp[:, :36], mlp[:, 36:])


def by_slot(first, second):
    halves = (first, second)
    return [
        jnp.stack([halves[i // 4][slot] for slot in SLOTS[i // 4][i % 4 * 8 : i % 4 * 8 + 8]])
        for i in range(8)
    ]


def from_slots(buffers):
    halves = []
    for h in range(2):
        slots = jnp.concatenate(buffers[2 * h : 2 * h + 2])
        halves.append(jnp.stack([slots[spot(h, d)] for d in range(BLOCKS)]))
    return halves


def reduce_plainly(gatt0, gatt1, gmlp, att_rows, mlp_rows, width, devices):
    groups = [from_slots(gatt0), from_slots(gatt1)]
    vectors = jnp.concatenate([groups[1][h][:, ATT_PART:] for h in range(2)], axis=1)
    vectors = vectors.astype(F32).reshape(BLOCKS, 2 * SUB, LANES)

    def matrix(name, first, last, rt_count, ct_count):
        rows = []
        for rt in range(rt_count):
            places = [part_place(name, rt, ct) for ct in range(ct_count)]
            rows.append(jnp.stack([groups[g][h][first:last, i] for g, h, i in places], axis=2))
        return jnp.stack(rows, axis=1).astype(F32).reshape(-1)

    wqkv = matrix("qkv", 0, QKV_BLOCKS, QKV_RT, QKV_CT)
    wo = matrix("wo", QKV_BLOCKS, BLOCKS, WO_RT, WO_CT)
    mlp = jnp.concatenate(from_slots(gmlp), axis=1).astype(F32)
    five = lambda v, dims: v.reshape((v.shape[0],) + dims + (SUB, LANES))
    w1 = five(mlp[:W1_BLOCKS], (W1_CT, W1_RT)).transpose(0, 2, 3, 1, 4).reshape(-1)
    w2 = five(mlp[W1_BLOCKS:], (W2_RT, W2_CT)).transpose(0, 1, 3, 2, 4).reshape(-1)
    line = lambda owner, first, count: vectors[owner, first : first + count].reshape(-1)
    att = [line(OWNERS[0], 0, 12), wqkv, line(OWNERS[2], 0, 12), wo, line(OWNERS[3], 0, 12)]
    mlp = [line(OWNERS[0], 12, 12), w1, line(OWNERS[1], 0, 24), w2, line(OWNERS[3], 12, 12)]

    def lay(parts, rows):
        vector = jnp.concatenate(parts)
        vector = jnp.pad(vector, (0, devices * rows * LANES - vector.shape[0]))
        return vector.reshape(devices, rows, LANES)

    whole = jnp.concatenate([lay(att, att_rows), lay(mlp, mlp_rows)], axis=1)
    return lax.psum_scatter(whole.reshape(-1, LANES), AXES, scatter_dimension=0, tiled=True)


def key_windows(segments, real):
    length = segments.shape[0]
    position = jnp.arange(length, dtype=jnp.int32)
    ids = jnp.where(real, segments, length + position)
    first = segments[0::QB]
    final = segments[QB - 1 :: QB]
    begin = jnp.sum((segments[None, :] < first[:, None]).astype(jnp.int32), axis=1)
    begin = jnp.where(real[0::QB], begin, position[0::QB])
    end = jnp.sum(((segments[None, :] <= final[:, None]) & real[None, :]).astype(jnp.int32), axis=1)
    end = jnp.where(real[QB - 1 :: QB], end, position[QB - 1 :: QB] + 1)
    begin = begin // SUB * SUB
    need = end - begin
    kind = sum((need > width).astype(jnp.int32) for width in CLASSES[:-1])
    widths = sum(
        jnp.where(kind == i, width, 0) for i, width in enumerate(CLASSES)
    )
    begin = jnp.minimum(begin, length - widths)
    chunks = (begin + widths + QB - 1) // QB
    return ids, jnp.stack([begin, kind, chunks]).astype(jnp.int32)


def local(tokens, cotangent, segment_ids, pad_mask, lengths, params):
    rows, width = tokens.shape
    wide, narrow = lax.axis_size("wide"), lax.axis_size("narrow")
    devices = wide * narrow
    att_count = 4 * width * width + 6 * width
    att_rows = (att_count // LANES + devices - 1) // devices
    mlp_rows = params.shape[0] - att_rows
    paired = (wide, narrow) == (4, 8)
    scale = 1.0 / math.sqrt(rows * devices)

    position = jnp.arange(rows, dtype=jnp.int32)
    real = (pad_mask > 0) & (position < lengths[0])
    ids, windows = key_windows(segment_ids, real)
    key_ids = ids.reshape(rows, 1)
    query_ids = ids.reshape(rows // QB, QB)

    if not paired:
        me = jnp.zeros((1,), jnp.int32)
        att, mlp = gather_plainly(params, att_rows, width)
        n1, qkv, small = project_qkv(me, tokens, att)
        mixed, x1, branch, n2, dm, stats, gb2 = attend(
            me, windows, qkv, tokens, cotangent, key_ids, query_ids, small, att
        )
        u, dz, gb1, *gmlp = feed_forward(me, n2, dm, small, mlp)
        output, gs2 = feed_forward_out(me, u, x1, cotangent, small, mlp)
        dx1, da, gwo0, gwo1, others = split(
            me, dz, x1, cotangent, branch, mixed, small, mlp, att
        )
        small_mlp = jnp.concatenate([others[:12], gb1, gb2, gs2])
        small_proj = others[12:]
        dqkv0 = attend_back(0, windows, qkv, da, stats, key_ids, query_ids)
        dqkv1 = attend_back(1, windows, qkv, da, stats, key_ids, query_ids)
        gatt0 = weight_grad(me, n1, dqkv0, gwo0)
        grad_input, *gatt1 = qkv_back(
            me, tokens, n1, dx1, dqkv0, dqkv1, small, small_proj, small_mlp, gwo1, att
        )
        owned = reduce_plainly(gatt0, gatt1, gmlp, att_rows, mlp_rows, width, devices)
        return output, grad_input, owned * scale

    me = lax.axis_index(AXES).astype(jnp.int32).reshape(1)
    tails = jnp.concatenate([params[att_rows - ATT_BEFORE : att_rows], params[-MLP_BEFORE:]])
    heads = jnp.concatenate([params[:ATT_AFTER], params[att_rows : att_rows + MLP_AFTER]])
    tails, heads = shifted(tails, 1), shifted(heads, -1)
    att_own, mlp_own = pack(me, params, tails, heads, att_rows)

    got = [exchange(att_own, k * Z0) for k in range(1, 4)]
    a, b = along_z(att_own[0], att_own[1], got)
    a, b, mlp_own, windows, key_ids, query_ids = together(
        a, b, mlp_own, windows, key_ids, query_ids
    )
    ax, by = exchange(a, X), exchange(b, Y)
    z1, z3 = exchange(mlp_own, Z0), exchange(mlp_own, 3 * Z0)
    a, b = joined(a, ax), joined(b, by)
    a, b, z1, z3, mlp_own = together(a, b, z1, z3, mlp_own)
    ay, bx = exchange(a, Y), exchange(b, X)
    ac, bc = exchange(a, C), exchange(b, C)
    z2 = exchange(mlp_own, 2 * Z0)
    m, n = along_z(mlp_own[0], mlp_own[1], [z1, z2, z3])
    ay, bx, ac, bc, m, n = together(ay, bx, ac, bc, m, n)
    ayc, bxc = exchange(ay, C), exchange(bx, C)
    att = together(a, ay, ac, ayc, b, bx, bc, bxc, m, n, tokens)
    *att, m, n, tokens_now = att
    mx, ny = exchange(m, X), exchange(n, Y)
    n1, qkv, small = project_qkv(me, tokens_now, att)
    m, n = joined(m, mx), joined(n, ny)
    m, n, qkv = together(m, n, qkv)
    my, nx = exchange(m, Y), exchange(n, X)
    mc, nc = exchange(m, C), exchange(n, C)
    mixed, x1, branch, n2, dm, stats, gb2 = attend(
        me, windows, qkv, tokens, cotangent, key_ids, query_ids, small, att
    )
    m, n, my, nx, mc, nc, n2 = together(m, n, my, nx, mc, nc, n2)
    myc, nxc = exchange(my, C), exchange(nx, C)
    mlp = (m, my, mc, myc, n, nx, nc, nxc)

    u, dz, gb1, *gmlp = feed_forward(me, n2, dm, small, mlp)

    mc, nc = exchange(gmlp[1], C), exchange(gmlp[3], C)
    output, gs2 = feed_forward_out(me, u, x1, cotangent, small, mlp)
    mc, nc, dz, gs2 = together(mc, nc, dz, gs2)
    m, n = [gmlp[0], mc], [gmlp[2], nc]
    my, nx, dz = together(sent(m), sent(n), dz)
    my, nx = exchange(my, Y), exchange(nx, X)
    dx1, da, gwo0, gwo1, others = split(
        me, dz, x1, cotangent, branch, mixed, small, mlp, att
    )
    dqkv0 = attend_back(0, windows, qkv, da, stats, key_ids, query_ids)
    my, nx, dqkv0, da = together(my, nx, dqkv0, da)
    m, n = kept(m) + [my], kept(n) + [nx]
    mx, ny, dqkv0, da = together(sent(m), sent(n), dqkv0, da)
    mx, ny = exchange(mx, X), exchange(ny, Y)
    gatt0 = weight_grad(me, n1, dqkv0, gwo0)
    dqkv1 = attend_back(1, windows, qkv, da, stats, key_ids, query_ids)
    mx, ny, dqkv1, *gatt0 = together(mx, ny, dqkv1, *gatt0)
    m, n = kept(m) + [mx], kept(n) + [ny]
    z1, z2, z3 = [z_part(m, n, k).astype(BF16) for k in range(1, 4)]
    z1, z2, z3, dqkv1, *gatt0 = together(z1, z2, z3, dqkv1, *gatt0)
    ac, bc = exchange(gatt0[1], C), exchange(gatt0[3], C)
    z1, z2 = exchange(z1, Z0), exchange(z2, 2 * Z0)
    small_mlp = jnp.concatenate([others[:12], gb1, gb2, gs2])
    grad_input, *gatt1 = qkv_back(
        me, tokens, n1, dx1, dqkv0, dqkv1, small, others[12:], small_mlp, gwo1, att
    )
    ac, bc, z1, z2, *gatt1 = together(ac, bc, z1, z2, *gatt1)
    a, b = [gatt0[0], ac], [gatt0[2], bc]
    ay, bx, c1, d1, z3 = together(sent(a), sent(b), gatt1[1], gatt1[3], z3)
    ay, bx = exchange(ay, Y), exchange(bx, X)
    c1, d1 = exchange(c1, C), exchange(d1, C)
    z3a = exchange(z3[0], 3 * Z0)
    a, b = kept(a) + [ay], kept(b) + [bx]
    c, d = [gatt1[0], c1], [gatt1[2], d1]
    ax, by, cy, dx, z3a, z3 = together(sent(a), sent(b), sent(c), sent(d), z3a, z3)
    ax, by = exchange(ax, X), exchange(by, Y)
    cy, dx = exchange(cy, Y), exchange(dx, X)
    z3b = exchange(z3[1], 3 * Z0)
    a, b = kept(a) + [ax], kept(b) + [by]
    c, d = kept(c) + [cy], kept(d) + [dx]
    sends = [z_part(a, b, k).astype(BF16) for k in range(1, 4)]
    cx, dy, z3b, *sends = together(sent(c), sent(d), z3b, *sends)
    m_own = sum_terms([z_part(m, n, 0), z1, z2, jnp.stack([z3a, z3b])])
    cx, dy = exchange(cx, X), exchange(dy, Y)
    got = [exchange(part, (k + 1) * Z0) for k, part in enumerate(sends)]
    c, d = kept(c) + [cx], kept(d) + [dy]
    group0 = sum_terms([z_part(a, b, 0)] + got)
    sends = [z_part(c, d, k).astype(BF16) for k in range(1, 4)]
    group0, m_own, *sends = together(group0, m_own, *sends)
    got = [exchange(part, (k + 1) * Z0) for k, part in enumerate(sends)]
    group1 = sum_terms([z_part(c, d, 0)] + got)
    mine, to_before, to_after = spread(me, group0, group1, m_own, att_rows, mlp_rows, scale)
    grad_params = close(mine, shifted(to_after, 1), shifted(to_before, -1), att_rows)
    return output, grad_input, grad_params


def solution(mesh):
    return jax.shard_map(
        local,
        mesh=mesh,
        in_specs=(
            P(AXES, None),
            P(AXES, None),
            P(AXES),
            P(AXES),
            P(AXES),
            P(AXES, None),
        ),
        out_specs=(P(AXES, None), P(AXES, None), P(AXES, None)),
        check_vma=False,
    )
```

```python
import math
from functools import partial

import jax
import jax.numpy as jnp
from jax import lax
from jax.experimental import pallas as pl
from jax.experimental.pallas import tpu as pltpu
from jax.sharding import PartitionSpec as P

FF = 3072
HEADS = 12
EPSILON = 1e-06
NEGATIVE = -1e30
AXES = ("wide", "narrow")
LANES = 128
SUB = 16
QB = 128
MEGA = 1 << 20
GRANT = 58 * MEGA
F32 = jnp.float32
BF16 = jnp.bfloat16

BLOCKS = 32
QKV_BLOCKS, QKV_RT, QKV_CT = 24, 2, 18
WO_BLOCKS, WO_RT, WO_CT = 8, 6, 6
W1_BLOCKS, W1_RT, W1_CT = 16, 3, 24
W2_BLOCKS, W2_RT, W2_CT = 16, 12, 6
ATT_HALF, MLP_HALF = 18, 36
ATT_SENT = ATT_HALF + 1
ATT_PART = 9
HALF_BLOCKS = BLOCKS // 2
CHUNK = 768
CHUNKS = FF // CHUNK

G1, C1, BQ, BV, BO, S1 = 0, 6, 12, 18, 24, 30
G2, C2, B1, B2, S2 = 36, 42, 48, 72, 78
SMALL = 88

NT = (((1,), (1,)), ((), ()))
NN = (((1,), (0,)), ((), ()))
TN = (((0,), (0,)), ((), ()))


def mm(lhs, rhs, dims):
    return lax.dot_general(lhs, rhs, dims, preferred_element_type=F32)


def row_of(ref, first, count):
    return jnp.concatenate([ref[first + k : first + k + 1, :] for k in range(count)], axis=1)


def put_row(ref, first, values):
    for k in range(values.shape[1] // LANES):
        ref[first + k : first + k + 1, :] = values[:, k * LANES : (k + 1) * LANES]


def fold8(values):
    rows, columns = values.shape
    return jnp.sum(values.reshape(rows // 8, 8, columns), axis=0)


def total(values):
    return jnp.sum(values, axis=0, keepdims=True)


def vmem():
    return pl.BlockSpec(memory_space=pltpu.VMEM)


def smem():
    return pl.BlockSpec(memory_space=pltpu.SMEM)


def hbm():
    return pl.BlockSpec(memory_space=pltpu.HBM)


def shape(dims, kind):
    return jax.ShapeDtypeStruct(dims, kind)


def cost(flops, moved, exps=0):
    return pl.CostEstimate(flops=int(flops), transcendentals=int(exps), bytes_accessed=int(moved))


def normalized(values):
    center = values - jnp.mean(values, axis=-1, keepdims=True)
    inverse = lax.rsqrt(jnp.mean(center * center, axis=-1, keepdims=True) + EPSILON)
    return center * inverse, inverse


def norm_pullback(unit, inverse, grad, gain):
    scaled = grad * gain
    first = jnp.mean(scaled, axis=-1, keepdims=True)
    second = jnp.mean(scaled * unit, axis=-1, keepdims=True)
    return inverse * (scaled - first - unit * second)


def gelu_pair(z):
    magnitude = jnp.abs(z)
    t = 1.0 / (1.0 + (0.3275911 * math.sqrt(0.5)) * magnitude)
    density = jnp.exp(z * z * -0.5)
    tail = 0.5 * 1.061405429
    tail = tail * t + 0.5 * -1.453152027
    tail = tail * t + 0.5 * 1.421413741
    tail = tail * t + 0.5 * -0.284496736
    tail = tail * t + 0.5 * 0.254829592
    tail = tail * t * density
    cumulative = jnp.where(z < 0, tail, 1.0 - tail)
    return z * cumulative, cumulative + z * density * (1.0 / math.sqrt(2.0 * math.pi))


def fetch(copies):
    for copy in copies:
        copy.start()


def settle(copies):
    for copy in copies:
        copy.wait()


ATT_BEFORE, ATT_AFTER = 64, 32
MLP_BEFORE, MLP_AFTER = 64, 40


def window_offsets(me, att_rows, mlp_rows):
    att = ATT_BEFORE + 12 + me * (576 - att_rows) + jnp.where(me < QKV_BLOCKS, 0, 12)
    mlp = MLP_BEFORE + 12 + me * (1152 - mlp_rows) + jnp.where(me < W1_BLOCKS, 0, 24)
    return att, mlp


def each_tile(me, act):
    for name, blocks, rt_count, ct_count, mine in (
        ("qkv", QKV_BLOCKS, QKV_RT, QKV_CT, me < QKV_BLOCKS),
        ("wo", WO_BLOCKS, WO_RT, WO_CT, me >= QKV_BLOCKS),
        ("w1", W1_BLOCKS, W1_RT, W1_CT, me < W1_BLOCKS),
        ("w2", W2_BLOCKS, W2_RT, W2_CT, me >= W1_BLOCKS),
    ):

        @pl.when(mine)
        def _(name=name, rt_count=rt_count, ct_count=ct_count):
            for ct in range(ct_count):
                for rt in range(rt_count):
                    act(name, rt, ct, rt * SUB * ct_count + ct, ct_count)


def half_place(name, rt, ct):
    if name == "qkv":
        return ct // 9, ct % 9 * QKV_RT + rt
    if name == "wo":
        return rt // 3, rt % 3 * WO_CT + ct
    if name == "w1":
        return ct // 12, ct % 12 * W1_RT + rt
    return rt // 6, rt % 6 * W2_CT + ct


def part_place(name, rt, ct):
    if name == "qkv":
        return ct % 6 // 3, rt, ct // 6 * 3 + ct % 3
    place = rt * WO_CT + ct
    return place // 18, place // ATT_PART % 2, place % ATT_PART


def qkv_group(g):
    return [6 * third + 3 * g + i for third in range(3) for i in range(3)]


def small_rows(me, act):
    @pl.when(me == 0)
    def _():
        act("att", True, 12, G1)
        act("mlp", True, 12, G2)

    @pl.when(me == QKV_BLOCKS - 1)
    def _():
        act("att", False, 12, BQ)

    @pl.when(me == W1_BLOCKS - 1)
    def _():
        act("mlp", False, 24, B1)

    @pl.when(me == BLOCKS - 1)
    def _():
        act("att", False, 12, BO)
        act("mlp", False, 12, B2)


OWNERS = (0, W1_BLOCKS - 1, QKV_BLOCKS - 1, BLOCKS - 1)


def sent_rows(kind, first):
    return 12 if kind == "mlp" and first in (G2, B2) else 0


def pack_kernel(att_rows, me_ref, own, tails, heads, att, mlp, win_a, win_m, table):
    me = me_ref[0]
    mlp_rows = own.shape[0] - att_rows
    win_a[0:ATT_BEFORE, :] = tails[0:ATT_BEFORE, :]
    win_a[ATT_BEFORE : ATT_BEFORE + att_rows, :] = own[0:att_rows, :]
    win_a[ATT_BEFORE + att_rows :, :] = heads[0:ATT_AFTER, :]
    win_m[0:MLP_BEFORE, :] = tails[ATT_BEFORE:, :]
    win_m[MLP_BEFORE : MLP_BEFORE + mlp_rows, :] = own[att_rows:, :]
    win_m[MLP_BEFORE + mlp_rows :, :] = heads[ATT_AFTER:, :]
    att_off, mlp_off = window_offsets(me, att_rows, mlp_rows)

    def tile(name, rt, ct, first, stride):
        attention = name in ("qkv", "wo")
        window, out, off = (win_a, att, att_off) if attention else (win_m, mlp, mlp_off)
        values = window[pl.ds(off + first, SUB, stride=stride), :]
        out[half_place(name, rt, ct)] = values.astype(BF16)

    each_tile(me, tile)
    table[...] = jnp.zeros_like(table)

    def vector(kind, before, rows, first):
        window, off, size = (win_a, att_off, 576) if kind == "att" else (win_m, mlp_off, 1152)
        start = off - 12 if before else off + size
        place = sent_rows(kind, first)
        table[place : place + rows, :] = window[pl.ds(start, rows), :]

    small_rows(me, vector)
    att[0, ATT_HALF] = table[0:SUB, :].astype(BF16)
    att[1, ATT_HALF] = table[SUB : 2 * SUB, :].astype(BF16)


def pack(me, own, tails, heads, att_rows):
    mlp_rows = own.shape[0] - att_rows
    return pl.pallas_call(
        partial(pack_kernel, att_rows),
        out_shape=(
            shape((2, ATT_SENT, SUB, LANES), BF16),
            shape((2, MLP_HALF, SUB, LANES), BF16),
        ),
        in_specs=[smem(), vmem(), vmem(), vmem()],
        out_specs=(vmem(), vmem()),
        scratch_shapes=[
            pltpu.VMEM((ATT_BEFORE + att_rows + ATT_AFTER, LANES), F32),
            pltpu.VMEM((MLP_BEFORE + mlp_rows + MLP_AFTER, LANES), F32),
            pltpu.VMEM((2 * SUB, LANES), F32),
        ],
        name="pack",
    )(me, own, tails, heads)


def spread_kernel(
    att_rows, scale, me_ref, group0, group1, mlp, mine, to_before, to_after, win_a, win_m, table
):
    me = me_ref[0]
    mlp_rows = mine.shape[0] - att_rows
    att_off, mlp_off = window_offsets(me, att_rows, mlp_rows)
    win_a[...] = jnp.zeros_like(win_a)
    win_m[...] = jnp.zeros_like(win_m)

    def tile(name, rt, ct, first, stride):
        if name in ("qkv", "wo"):
            g, half, index = part_place(name, rt, ct)
            values = (group0, group1)[g][half, index]
            win_a[pl.ds(att_off + first, SUB, stride=stride), :] = values * scale
        else:
            values = mlp[half_place(name, rt, ct)]
            win_m[pl.ds(mlp_off + first, SUB, stride=stride), :] = values * scale

    each_tile(me, tile)
    for h in range(2):
        table[SUB * h : SUB * h + SUB, :] = group1[h, ATT_PART] * scale

    def vector(kind, before, rows, first):
        window, off, size = (win_a, att_off, 576) if kind == "att" else (win_m, mlp_off, 1152)
        start = off - 12 if before else off + size
        place = sent_rows(kind, first)
        window[pl.ds(start, rows), :] = table[place : place + rows, :]

    small_rows(me, vector)
    mine[0:att_rows, :] = win_a[ATT_BEFORE : ATT_BEFORE + att_rows, :]
    mine[att_rows:, :] = win_m[MLP_BEFORE : MLP_BEFORE + mlp_rows, :]
    to_before[0:ATT_BEFORE, :] = win_a[0:ATT_BEFORE, :]
    to_before[ATT_BEFORE:, :] = win_m[0:MLP_BEFORE, :]
    to_after[0:ATT_AFTER, :] = win_a[ATT_BEFORE + att_rows :, :]
    to_after[ATT_AFTER:, :] = win_m[MLP_BEFORE + mlp_rows :, :]


def spread(me, group0, group1, mlp, att_rows, mlp_rows, scale):
    return pl.pallas_call(
        partial(spread_kernel, att_rows, scale),
        out_shape=(
            shape((att_rows + mlp_rows, LANES), F32),
            shape((ATT_BEFORE + MLP_BEFORE, LANES), F32),
            shape((ATT_AFTER + MLP_AFTER, LANES), F32),
        ),
        in_specs=[smem(), vmem(), vmem(), vmem()],
        out_specs=(vmem(), vmem(), vmem()),
        scratch_shapes=[
            pltpu.VMEM((ATT_BEFORE + att_rows + ATT_AFTER, LANES), F32),
            pltpu.VMEM((MLP_BEFORE + mlp_rows + MLP_AFTER, LANES), F32),
            pltpu.VMEM((2 * SUB, LANES), F32),
        ],
        name="spread",
    )(me, group0, group1, mlp)


def close_kernel(att_rows, mine, below, above, out):
    rows = mine.shape[0]
    out[...] = mine[...]
    out[0:ATT_AFTER, :] += below[0:ATT_AFTER, :]
    out[att_rows : att_rows + MLP_AFTER, :] += below[ATT_AFTER:, :]
    out[att_rows - ATT_BEFORE : att_rows, :] += above[0:ATT_BEFORE, :]
    out[rows - MLP_BEFORE : rows, :] += above[ATT_BEFORE:, :]


def close(mine, below, above, att_rows):
    return pl.pallas_call(
        partial(close_kernel, att_rows),
        out_shape=shape(mine.shape, F32),
        in_specs=[vmem()] * 3,
        out_specs=vmem(),
        name="close",
    )(mine, below, above)


def spot(h, d):
    x, c, z, y = d >> 4, (d >> 3) & 1, (d >> 1) & 3, d & 1
    return c * 16 + (y * 8 + x * 4 if h == 0 else x * 8 + y * 4) + z


SLOTS = [sorted(range(BLOCKS), key=partial(spot, h)) for h in range(2)]


def fill_spots(me, spots):
    for h in range(2):
        mine = spot(h, me)
        for d in range(BLOCKS):
            spots[h, d] = jnp.bitwise_xor(mine, spot(h, d))


def slots_scratch(tiles):
    return pltpu.VMEM((2, BLOCKS, tiles, SUB, LANES), BF16)


def spots_scratch():
    return pltpu.SMEM((2, BLOCKS), jnp.int32)


def arriving_slots(buffers, w, sems):
    return [
        pltpu.make_async_copy(buffers[i], w.at[i // 4, pl.ds(i % 4 * 8, 8)], sems.at[i])
        for i in range(8)
    ]


def leaving_slots(buffers, w, sems):
    return [
        pltpu.make_async_copy(w.at[i // 2, pl.ds(i % 2 * 16, 16)], buffers[i], sems.at[i])
        for i in range(4)
    ]


def qkv_column(w, spots, ct):
    h, place = ct // 9, ct % 9 * QKV_RT
    tiles = [w[h, spots[h, d], place + rt] for d in range(QKV_BLOCKS) for rt in range(QKV_RT)]
    return jnp.concatenate(tiles, axis=0)


def wo_matrix(w, spots):
    columns = []
    for ct in range(WO_CT):
        tiles = [
            w[rt // 3, spots[rt // 3, QKV_BLOCKS + i] & 7, rt % 3 * WO_CT + ct]
            for i in range(WO_BLOCKS)
            for rt in range(WO_RT)
        ]
        columns.append(jnp.concatenate(tiles, axis=0))
    return jnp.concatenate(columns, axis=1)


def dma(count):
    return pltpu.SemaphoreType.DMA((count,))


def norm_rows(rows, gain, shift, source, target, step=256):
    def one(i, carry):
        at = pl.ds(pl.multiple_of(i * step, step), step)
        unit, _ = normalized(source[at, :].astype(F32))
        target[at, :] = (unit * gain + shift).astype(BF16)
        return carry

    lax.fori_loop(0, rows // step, one, 0)


def qkv_kernel(me_ref, tokens, *refs):
    buffers, (n1, qkv, small, w, spots, x, unit, triple, sems, own) = refs[:8], refs[8:]
    coming = pltpu.make_async_copy(tokens, x, own.at[0])
    coming.start()
    weights = arriving_slots(buffers, w, sems)
    fetch(weights)
    fill_spots(me_ref[0], spots)
    settle(weights)
    tables = [
        jnp.concatenate([w[h, spots[h, d], ATT_HALF] for h in range(2)], axis=0).astype(F32)
        for d in OWNERS
    ]
    small[G1 : G1 + 12, :] = tables[0][0:12]
    small[G2 : G2 + 12, :] = tables[0][12:24]
    small[B1 : B1 + 24, :] = tables[1][0:24]
    small[BQ : BQ + 12, :] = tables[2][0:12]
    small[BO : BO + 12, :] = tables[3][0:12]
    small[B2 : B2 + 12, :] = tables[3][12:24]
    small[SMALL - 4 :, :] = jnp.zeros((4, LANES), F32)
    coming.wait()
    norm_rows(x.shape[0], row_of(small, G1, 6), row_of(small, C1, 6), x, unit)
    going = [pltpu.make_async_copy(unit, n1, own.at[0])]
    going[0].start()
    bias = jnp.concatenate(
        [row_of(small, BQ, 6), jnp.zeros((1, 768), F32), row_of(small, BV, 6)], axis=1
    )
    for c in range(QKV_CT // 2):
        weight = jnp.concatenate([qkv_column(w, spots, 2 * c + i) for i in range(2)], axis=1)
        lanes = slice(256 * c, 256 * c + 256)
        triple[:, lanes] = (mm(unit[...], weight, NN) + bias[:, lanes]).astype(BF16)
        going.append(
            pltpu.make_async_copy(triple.at[:, lanes], qkv.at[:, lanes], own.at[1 + c])
        )
        going[-1].start()
    settle(going)


def project_qkv(me, tokens, att):
    rows, width = tokens.shape
    return pl.pallas_call(
        qkv_kernel,
        out_shape=(
            shape((rows, width), BF16),
            shape((rows, 3 * width), BF16),
            shape((SMALL, LANES), F32),
        ),
        in_specs=[smem(), hbm()] + [hbm()] * 8,
        out_specs=(hbm(), hbm(), vmem()),
        scratch_shapes=[
            slots_scratch(ATT_SENT),
            spots_scratch(),
            pltpu.VMEM((rows, width), BF16),
            pltpu.VMEM((rows, width), BF16),
            pltpu.VMEM((rows, 3 * width), BF16),
            dma(8),
            dma(1 + QKV_CT // 2),
        ],
        compiler_params=pltpu.CompilerParams(vmem_limit_bytes=GRANT),
        cost_estimate=cost(6 * rows * width * width, 12 * rows * width),
        name="qkv_forward",
    )(me, tokens, *att)


CLASSES = (128, 256, 384, 512, 768)


def head_masked(block):
    lane = lax.broadcasted_iota(jnp.int32, block.shape, 1)
    zero = jnp.zeros_like(block)
    return jnp.concatenate(
        [jnp.where(lane < 64, block, zero), jnp.where(lane >= 64, block, zero)], axis=0
    )


def pick_heads(both):
    return jnp.concatenate([both[0:64, 0:QB], both[64:128, QB : 2 * QB]], axis=0)


def mask_bias(start, width, b, key_ids, query_ids, bias):
    for j in range(width // QB):
        at = pl.ds(pl.multiple_of(start + j * QB, SUB), QB)
        same = key_ids[at, :] == query_ids[pl.ds(b, 1), :]
        bias[j * QB : (j + 1) * QB, :] = jnp.where(same, 0.0, NEGATIVE)


PAIRS = HEADS // 2


def attend_block(b, start, width, qkv, mixed, stats, bias, scores):
    rows = pl.ds(pl.multiple_of(b * QB, QB), QB)
    pieces = [slice(j * QB, (j + 1) * QB) for j in range(width // QB)]
    for p in range(PAIRS):
        lanes, key_lanes, value_lanes = [
            slice(LANES * (PAIRS * third + p), LANES * (PAIRS * third + p + 1))
            for third in range(3)
        ]
        queries = head_masked(qkv[rows, lanes] * 0.125)
        highest = jnp.full((8, 2 * QB), NEGATIVE, F32)
        for piece in pieces:
            at = pl.ds(pl.multiple_of(start + piece.start, SUB), QB)
            part = mm(qkv[at, key_lanes], queries, NT)
            part = part + jnp.concatenate([bias[piece, :]] * 2, axis=1)
            scores[p, piece, :] = part
            highest = jnp.maximum(highest, jnp.max(part.reshape(QB // 8, 8, 2 * QB), axis=0))
        highest = jnp.max(highest, axis=0, keepdims=True)
        summed = jnp.zeros((8, 2 * QB), F32)
        both = jnp.zeros((LANES, 2 * QB), F32)
        for piece in pieces:
            at = pl.ds(pl.multiple_of(start + piece.start, SUB), QB)
            raised = jnp.exp(scores[p, piece, :] - highest)
            summed = summed + fold8(raised)
            both = both + mm(qkv[at, value_lanes], raised.astype(BF16), TN)
        inverse = 1.0 / total(summed)
        mixed[rows, lanes] = pick_heads(both * inverse).T.astype(BF16)
        stats[b * PAIRS + p, 0:1, :] = highest
        stats[b * PAIRS + p, 1:2, :] = inverse


def wo_scratch():
    return pltpu.VMEM((2, WO_BLOCKS, ATT_SENT, SUB, LANES), BF16)


def wo_copies(buffers, w, sems, core, x):
    copies = []
    for y in range(2):
        source = buffers[2 * core + y].at[pl.ds(4 * x, 4)]
        copies.append(pltpu.make_async_copy(source, w.at[0, pl.ds(4 * y, 4)], sems.at[y]))
    copies.append(pltpu.make_async_copy(buffers[4 + 2 * core + x], w.at[1], sems.at[2]))
    return copies


def fetch_wo(me, buffers, w, spots, sems):
    fill_spots(me, spots)
    for h in range(2):
        for i in range(WO_BLOCKS):
            place = spot(h, jnp.bitwise_xor(me, QKV_BLOCKS + i) & 7)
            spots[h, QKV_BLOCKS + i] = (place >> (1 if h == 0 else 0)) & 4 | place & 3
    far = jnp.bitwise_xor(me, QKV_BLOCKS)
    for core in range(2):
        for x in range(2):

            @pl.when((far >> 3) == 2 * x + core)
            def _(core=core, x=x):
                fetch(wo_copies(buffers, w, sems, core, x))


def wait_wo(buffers, w, sems):
    settle(wo_copies(buffers, w, sems, 0, 0))


def attend_kernel(me_ref, windows, qkv, tokens, cot, key_ids, query_ids, small, *refs):
    buffers, refs = refs[:8], refs[8:]
    mixed, x1, branch, n2, dm, stats, gb2 = refs[:7]
    triple, x, g, mix, mid, out, unit, scaled, bias, scores, w, spots, sems, own, chunk_sems = refs[7:]
    rows = tokens.shape[0]
    blocks = rows // QB

    def chunk(i):
        at = pl.ds(pl.multiple_of(i * QB, QB), QB)
        return pltpu.make_async_copy(qkv.at[at, :], triple.at[at, :], chunk_sems.at[i])

    for i in range(blocks):
        chunk(i).start()
    coming = [
        pltpu.make_async_copy(tokens, x, own.at[0]),
        pltpu.make_async_copy(cot, g, own.at[1]),
    ]
    fetch(coming)
    fetch_wo(me_ref[0], buffers, w, spots, sems)

    def one_block(b, loaded):
        start = pl.multiple_of(windows[0, b], SUB)
        needed = jnp.maximum(windows[2, b], loaded)

        def arrived(i, carry):
            chunk(i).wait()
            return carry

        lax.fori_loop(loaded, needed, arrived, 0)
        for index, width in enumerate(CLASSES):

            @pl.when(windows[1, b] == index)
            def _(width=width):
                mask_bias(start, width, b, key_ids, query_ids, bias)
                attend_block(b, start, width, triple, mix, stats, bias, scores)

        return needed

    loaded = lax.fori_loop(0, blocks, one_block, jnp.int32(0))

    def arrived(i, carry):
        chunk(i).wait()
        return carry

    lax.fori_loop(loaded, blocks, arrived, 0)
    going = [pltpu.make_async_copy(mix, mixed, own.at[2])]
    going[0].start()
    wait_wo(buffers, w, sems)
    settle(coming)
    bo, s1 = row_of(small, BO, 6), row_of(small, S1, 6)
    gain, shift = row_of(small, G2, 6), row_of(small, C2, 6)
    s2 = row_of(small, S2, 6)
    weight = wo_matrix(w, spots)
    step = 256
    sums = jnp.zeros((8, 768), F32)
    for i in range(rows // step):
        at = slice(i * step, (i + 1) * step)
        made = mm(mix[at, :], weight, NN) + bo
        out[at, :] = made.astype(BF16)
        values = x[at, :].astype(F32) + s1 * made
        mid[at, :] = values
        normal, _ = normalized(values)
        unit[at, :] = (normal * gain + shift).astype(BF16)
        rounded = (g[at, :].astype(F32) * s2).astype(BF16)
        scaled[at, :] = rounded
        sums = sums + fold8(rounded.astype(F32))
        for k, (source, target) in enumerate(
            ((out, branch), (mid, x1), (unit, n2), (scaled, dm))
        ):
            sem = own.at[3 + 4 * i + k]
            going.append(pltpu.make_async_copy(source.at[at, :], target.at[at, :], sem))
            going[-1].start()
    put_row(gb2, 0, total(sums))
    settle(going)


def attend(me, windows, qkv, tokens, cot, key_ids, query_ids, small, att):
    rows, width = tokens.shape
    row = lambda kind: pltpu.VMEM((rows, width), kind)
    return pl.pallas_call(
        attend_kernel,
        out_shape=(
            shape((rows, width), BF16),
            shape((rows, width), F32),
            shape((rows, width), BF16),
            shape((rows, width), BF16),
            shape((rows, width), BF16),
            shape((rows // QB * PAIRS, 2, 2 * QB), F32),
            shape((6, LANES), F32),
        ),
        in_specs=[smem(), smem(), hbm(), hbm(), hbm(), vmem(), vmem(), vmem()] + [hbm()] * 8,
        out_specs=(hbm(),) * 5 + (vmem(), vmem()),
        scratch_shapes=[
            pltpu.VMEM((rows, 3 * width), BF16),
            row(BF16),
            row(BF16),
            row(BF16),
            row(F32),
            row(BF16),
            row(BF16),
            row(BF16),
            pltpu.VMEM((CLASSES[-1], QB), F32),
            pltpu.VMEM((PAIRS, CLASSES[-1], 2 * QB), F32),
            wo_scratch(),
            spots_scratch(),
            dma(3),
            dma(3 + 4 * rows // 256),
            dma(rows // QB),
        ],
        compiler_params=pltpu.CompilerParams(vmem_limit_bytes=GRANT),
        cost_estimate=cost(2 * rows * rows * width, 20 * rows * width, 4 * rows * rows),
        name="attend_forward",
    )(me, windows, qkv, tokens, cot, key_ids, query_ids, small, *att)


def lay_matrix(w, spots, name, blocks, first, rt_count, columns, out):
    def one_block(d, carry):
        places = [spots[h, first + d] for h in range(2)]
        base = pl.multiple_of(d * rt_count * SUB, SUB)
        for rt in range(rt_count):
            for column, ct in enumerate(columns):
                h, index = half_place(name, rt, ct)
                at = pl.ds(pl.multiple_of(base + rt * SUB, SUB), SUB)
                out[at, LANES * column : LANES * (column + 1)] = w[h, places[h], index]
        return carry

    lax.fori_loop(0, blocks, one_block, 0)


def lay_w1(w, spots, out):
    lay_matrix(w, spots, "w1", W1_BLOCKS, 0, W1_RT, range(W1_CT), out)


def lay_w2(w, spots, out):
    lay_matrix(w, spots, "w2", W2_BLOCKS, W1_BLOCKS, W2_RT, range(W2_CT), out)


def w2_place(spots, f, row, ct):
    rt = row % W2_RT
    h = rt // 6
    return h, spots[h, W1_BLOCKS + 4 * f + row // W2_RT], rt % 6 * W2_CT + ct


TALL = 256
PARTS = CHUNK // 256


def mlp_kernel(me_ref, n2_in, dm_in, small, *refs):
    arriving, refs = refs[:8], refs[8:]
    u_out, dz_out, vectors, *leaving = refs[:7]
    w, first, second, spots, n2, dm, u, dz, zs, dus, bias_sums, b1_lines, sems, own = refs[7:]
    rows, width = n2.shape
    tiles = rows // TALL
    coming = [
        pltpu.make_async_copy(n2_in, n2, own.at[0]),
        pltpu.make_async_copy(dm_in, dm, own.at[1]),
    ]
    fetch(coming)
    weights = arriving_slots(arriving, w, sems)
    fetch(weights)
    fill_spots(me_ref[0], spots)
    bias_sums[...] = jnp.zeros_like(bias_sums)
    for f in range(CHUNKS):
        b1_lines[f : f + 1, :] = row_of(small, B1 + 6 * f, 6)
    settle(coming + weights)

    def lay_chunk(f, side):
        h, base = f >> 1, MLP_HALF // 2 * (f & 1)
        for d in range(W1_BLOCKS):
            place = spots[h, d]
            for rt in range(W1_RT):
                at = slice((d * W1_RT + rt) * SUB, (d * W1_RT + rt + 1) * SUB)
                for ct in range(6):
                    lanes = slice(LANES * ct, LANES * ct + LANES)
                    first[side, at, lanes] = w[h, place, base + ct * W1_RT + rt]
        for k in range(4):
            places = [spots[i, W1_BLOCKS + 4 * f + k] for i in range(2)]
            for rt in range(W2_RT):
                at = slice((k * W2_RT + rt) * SUB, (k * W2_RT + rt + 1) * SUB)
                for ct in range(W2_CT):
                    lanes = slice(LANES * ct, LANES * ct + LANES)
                    i, index = half_place("w2", rt, ct)
                    second[side, at, lanes] = w[i, places[i], index]

    lay_chunk(jnp.int32(0), jnp.int32(0))

    units = [(t, c) for c in range(PARTS) for t in range(tiles)]

    def lanes_of(f, c):
        return pl.ds(pl.multiple_of(CHUNK * f + 256 * c, 256), 256)

    def outward(f):
        chunk = pl.ds(pl.multiple_of(CHUNK * f, CHUNK), CHUNK)
        return [
            pltpu.make_async_copy(u.at[:, chunk], u_out.at[:, chunk], own.at[2 * f]),
            pltpu.make_async_copy(dz.at[:, chunk], dz_out.at[:, chunk], own.at[2 * f + 1]),
        ]

    def one_chunk(f, carry):
        side = f & 1
        lay_chunk(jnp.minimum(f + 1, CHUNKS - 1), 1 - side)

        def multiply(unit, slot):
            t, c = unit
            at = slice(TALL * t, TALL * t + TALL)
            zs[slot] = mm(n2[at, :], first[side, :, 256 * c : 256 * c + 256], NN)
            dus[slot] = mm(dm[at, :], second[side, 256 * c : 256 * c + 256, :], NT)

        def activate(unit, slot):
            t, c = unit
            lanes = slice(256 * c, 256 * c + 256)
            bias = b1_lines[pl.ds(f, 1), lanes]
            folded = jnp.zeros((8, 256), F32)
            for r in range(TALL // 32):
                part = slice(32 * r, 32 * r + 32)
                place = slice(TALL * t + 32 * r, TALL * t + 32 * r + 32)
                value, slope = gelu_pair(zs[slot, part, :] + bias)
                u[place, lanes_of(f, c)] = value.astype(BF16)
                rounded = (dus[slot, part, :] * slope).astype(BF16)
                dz[place, lanes_of(f, c)] = rounded
                folded = folded + fold8(rounded.astype(F32))
            bias_sums[:, lanes_of(f, c)] += folded

        multiply(units[0], 0)
        for i, unit in enumerate(units):
            if i + 1 < len(units):
                multiply(units[i + 1], (i + 1) % 2)
            activate(unit, i % 2)
        fetch(outward(f))
        return carry

    lax.fori_loop(0, CHUNKS, one_chunk, 0)
    put_row(vectors, 0, total(bias_sums[...]))

    def one_grad(f, carry):
        for c in range(PARTS):
            grad = mm(u[:, lanes_of(f, c)], dm[...], TN)
            for r in range(SUB):
                for ct in range(W2_CT):
                    tile = grad[SUB * r : SUB * r + SUB, LANES * ct : LANES * ct + LANES]
                    w[w2_place(spots, f, SUB * c + r, ct)] = tile.astype(BF16)
        h, base = f >> 1, MLP_HALF // 2 * (f & 1)
        chunk = pl.ds(pl.multiple_of(CHUNK * f, CHUNK), CHUNK)
        for c in range(PARTS):
            lanes = slice(256 * c, 256 * c + 256)
            grad = mm(n2[:, lanes], dz[:, chunk], TN)
            for r in range(SUB):
                d, rt = (SUB * c + r) // W1_RT, (SUB * c + r) % W1_RT
                for ct in range(6):
                    tile = grad[SUB * r : SUB * r + SUB, LANES * ct : LANES * ct + LANES]
                    w[h, spots[h, d], base + ct * W1_RT + rt] = tile.astype(BF16)
        return carry

    lax.fori_loop(0, CHUNKS, one_grad, 0)
    copies = leaving_slots(leaving, w, sems)
    fetch(copies)
    for f in range(CHUNKS):
        settle(outward(f))
    settle(copies)


def feed_forward(me, n2, dm, small, mlp):
    rows, width = n2.shape
    half = shape((HALF_BLOCKS, MLP_HALF, SUB, LANES), BF16)
    return pl.pallas_call(
        mlp_kernel,
        out_shape=(
            shape((rows, FF), BF16),
            shape((rows, FF), BF16),
            shape((24, LANES), F32),
            half,
            half,
            half,
            half,
        ),
        in_specs=[smem(), hbm(), hbm(), vmem()] + [hbm()] * 8,
        out_specs=(hbm(), hbm(), vmem()) + (hbm(),) * 4,
        scratch_shapes=[
            slots_scratch(MLP_HALF),
            pltpu.VMEM((2, width, CHUNK), BF16),
            pltpu.VMEM((2, CHUNK, width), BF16),
            spots_scratch(),
            pltpu.VMEM((rows, width), BF16),
            pltpu.VMEM((rows, width), BF16),
            pltpu.VMEM((rows, FF), BF16),
            pltpu.VMEM((rows, FF), BF16),
            pltpu.VMEM((2, TALL, 256), F32),
            pltpu.VMEM((2, TALL, 256), F32),
            pltpu.VMEM((8, FF), F32),
            pltpu.VMEM((CHUNKS, CHUNK), F32),
            dma(8),
            dma(2 * CHUNKS),
        ],
        compiler_params=pltpu.CompilerParams(vmem_limit_bytes=42 * MEGA),
        cost_estimate=cost(8 * rows * width * FF, 40 * MEGA),
        name="feed_forward",
    )(me, n2, dm, small, *mlp)


def matrix_copies(buffers, w, sems, x):
    copies = []
    for i in range(4):
        source = buffers[i].at[pl.ds(4 * x, 4)]
        copies.append(pltpu.make_async_copy(source, w.at[0, pl.ds(4 * i, 4)], sems.at[i]))
    for c in range(2):
        source = buffers[4 + 2 * c + x]
        copies.append(pltpu.make_async_copy(source, w.at[1, pl.ds(8 * c, 8)], sems.at[4 + c]))
    return copies


def fetch_matrix(me, buffers, w, spots, sems, first):
    def place(d):
        return ((d >> 3) & 1) * 8 + (d & 1) * 4 + ((d >> 1) & 3)

    for x in range(2):

        @pl.when((me >> 4) == (x ^ (first >> 4)))
        def _(x=x):
            fetch(matrix_copies(buffers, w, sems, x))

    mine = place(me)
    for d in range(W1_BLOCKS):
        for h in range(2):
            spots[h, first + d] = jnp.bitwise_xor(mine, place(d))


def wait_matrix(buffers, w, sems):
    settle(matrix_copies(buffers, w, sems, 0))


def matrix_scratch():
    return pltpu.VMEM((2, W1_BLOCKS, MLP_HALF, SUB, LANES), BF16)


def mlp_out_kernel(me_ref, u_in, x1_in, cot_in, small, *refs):
    arriving, refs = refs[:8], refs[8:]
    out, vectors, w, second, spots, u, x1, cot, macc, done, sums, sems, own = refs
    rows, width = x1.shape
    tiles = rows // TALL

    def tile_copy(source, target, t, k):
        at = pl.ds(pl.multiple_of(TALL * t, TALL), TALL)
        return pltpu.make_async_copy(source.at[at, :], target.at[at, :], own.at[k, t])

    fetch_matrix(me_ref[0], arriving, w, spots, sems, W1_BLOCKS)
    for t in range(tiles):
        tile_copy(u_in, u, t, 0).start()
    for t in range(tiles):
        tile_copy(x1_in, x1, t, 1).start()
        tile_copy(cot_in, cot, t, 2).start()
    bias, scale = row_of(small, B2, 6), row_of(small, S2, 6)
    sums[...] = jnp.zeros_like(sums)
    wait_matrix(arriving, w, sems)
    lay_w2(w, spots, second)

    def contract(t):
        at = pl.ds(pl.multiple_of(TALL * t, TALL), TALL)
        tile_copy(u_in, u, t, 0).wait()
        macc[at, :] = mm(u[at, :], second[...], NN)

    def finish(t):
        tile_copy(x1_in, x1, t, 1).wait()
        tile_copy(cot_in, cot, t, 2).wait()
        for part in range(TALL // 64):
            at = pl.ds(pl.multiple_of(TALL * t + 64 * part, 64), 64)
            contracted = macc[at, :] + bias
            done[at, :] = (x1[at, :] + scale * contracted).astype(BF16)
            sums[...] += fold8(cot[at, :].astype(F32) * contracted)
        tile_copy(done, out, t, 3).start()

    def one_tile(t, carry):
        contract(t)
        finish(t - 1)
        return carry

    contract(0)
    lax.fori_loop(1, tiles, one_tile, 0)
    finish(tiles - 1)
    put_row(vectors, 0, total(sums[...]))
    for t in range(tiles):
        tile_copy(done, out, t, 3).wait()


def feed_forward_out(me, u, x1, cot, small, mlp):
    rows, width = x1.shape
    row = lambda kind: pltpu.VMEM((rows, width), kind)
    return pl.pallas_call(
        mlp_out_kernel,
        out_shape=(shape((rows, width), BF16), shape((6, LANES), F32)),
        in_specs=[smem()] + [hbm()] * 3 + [vmem()] + [hbm()] * 8,
        out_specs=(hbm(), vmem()),
        scratch_shapes=[
            matrix_scratch(),
            pltpu.VMEM((FF, width), BF16),
            spots_scratch(),
            pltpu.VMEM((rows, FF), BF16),
            row(F32),
            row(BF16),
            row(F32),
            row(BF16),
            pltpu.VMEM((8, width), F32),
            dma(6),
            pltpu.SemaphoreType.DMA((4, rows // TALL)),
        ],
        compiler_params=pltpu.CompilerParams(vmem_limit_bytes=32 * MEGA),
        cost_estimate=cost(2 * rows * width * FF, 20 * MEGA),
        name="feed_forward_out",
    )(me, u, x1, cot, small, *mlp)


def split_kernel(me_ref, dz_in, x1_in, cot_in, branch_in, mixed_in, small, *refs):
    buffers, att_buffers, refs = refs[:8], refs[8:16], refs[16:]
    dx1_out, da_out, gwo0, gwo1, vectors = refs[:5]
    w, first, spots, wo, wo_spots, dz, x1, cot, dnacc, dx1, branch, mixed, db, da = refs[5:19]
    parts, sums, sems, wo_sems, own = refs[19:]
    me = me_ref[0]
    rows, width = x1.shape
    tiles = rows // TALL

    def tile_copy(source, target, t, k):
        at = pl.ds(pl.multiple_of(TALL * t, TALL), TALL)
        return pltpu.make_async_copy(source.at[at, :], target.at[at, :], own.at[k, t])

    fetch_matrix(me, buffers, w, spots, sems, 0)
    for t in range(tiles):
        tile_copy(dz_in, dz, t, 0).start()
    for t in range(tiles):
        tile_copy(x1_in, x1, t, 1).start()
        tile_copy(cot_in, cot, t, 2).start()
        tile_copy(branch_in, branch, t, 3).start()
    fetch_wo(me, att_buffers, wo, wo_spots, wo_sems)
    late = pltpu.make_async_copy(mixed_in, mixed, own.at[4, 0])
    late.start()
    gain, scale = row_of(small, G2, 6), row_of(small, S1, 6)
    sums[...] = jnp.zeros_like(sums)
    wait_matrix(buffers, w, sems)
    lay_w1(w, spots, first)

    def contract(t):
        at = pl.ds(pl.multiple_of(TALL * t, TALL), TALL)
        tile_copy(dz_in, dz, t, 0).wait()
        dnacc[at, :] = mm(dz[at, :], first[...], NT)

    def finish(t):
        tile_copy(x1_in, x1, t, 1).wait()
        tile_copy(cot_in, cot, t, 2).wait()
        tile_copy(branch_in, branch, t, 3).wait()
        for half in range(2):
            at = pl.ds(pl.multiple_of(TALL * t + TALL // 2 * half, TALL // 2), TALL // 2)
            unit, inverse = normalized(x1[at, :])
            grad = dnacc[at, :]
            middle = cot[at, :].astype(F32) + norm_pullback(unit, inverse, grad, gain)
            dx1[at, :] = middle
            rounded = (middle * scale).astype(BF16)
            db[at, :] = rounded
            sums[0:8, :] += fold8(grad * unit)
            sums[8:16, :] += fold8(grad)
            sums[16:24, :] += fold8(rounded.astype(F32))
            sums[24:32, :] += fold8(middle * branch[at, :].astype(F32))
        tile_copy(dx1, dx1_out, t, 1).start()

    def one_tile(t, carry):
        contract(t)
        finish(t - 1)
        return carry

    contract(0)
    lax.fori_loop(1, tiles, one_tile, 0)
    finish(tiles - 1)
    for k in range(4):
        put_row(vectors, 6 * k, total(sums[8 * k : 8 * k + 8, :]))
    wait_wo(att_buffers, wo, wo_sems)
    weight = wo_matrix(wo, wo_spots)
    going = []
    for c in range(3):
        lanes = slice(256 * c, 256 * c + 256)
        da[:, lanes] = mm(db[...], weight[lanes, :], NT).astype(BF16)
        going.append(pltpu.make_async_copy(da.at[:, lanes], da_out.at[:, lanes], own.at[0, c]))
        going[-1].start()
    late.wait()
    for c in range(3):
        grad = mm(mixed[:, 256 * c : 256 * c + 256], db[...], TN)
        for r in range(SUB):
            i, rt = (SUB * c + r) // WO_RT, (SUB * c + r) % WO_RT
            for ct in range(WO_CT):
                tile = grad[SUB * r : SUB * r + SUB, LANES * ct : LANES * ct + LANES]
                g, half, index = part_place("wo", rt, ct)
                parts[g, half, i, index] = tile.astype(BF16)
    for g, target in enumerate((gwo0, gwo1)):
        going.append(pltpu.make_async_copy(parts.at[g], target, own.at[4, g]))
        going[-1].start()
    settle(going)
    for t in range(tiles):
        tile_copy(dx1, dx1_out, t, 1).wait()


def split(me, dz, x1, cot, branch, mixed, small, mlp, att):
    rows, width = x1.shape
    part = (2, WO_BLOCKS, ATT_PART, SUB, LANES)
    row = lambda kind: pltpu.VMEM((rows, width), kind)
    return pl.pallas_call(
        split_kernel,
        out_shape=(
            shape((rows, width), F32),
            shape((rows, width), BF16),
            shape(part, BF16),
            shape(part, BF16),
            shape((24, LANES), F32),
        ),
        in_specs=[smem()] + [hbm()] * 5 + [vmem()] + [hbm()] * 16,
        out_specs=(hbm(),) * 4 + (vmem(),),
        scratch_shapes=[
            matrix_scratch(),
            pltpu.VMEM((width, FF), BF16),
            spots_scratch(),
            wo_scratch(),
            spots_scratch(),
            pltpu.VMEM((rows, FF), BF16),
            row(F32),
            row(BF16),
            row(F32),
            row(F32),
            row(BF16),
            row(BF16),
            row(BF16),
            row(BF16),
            pltpu.VMEM((2,) + part, BF16),
            pltpu.VMEM((32, width), F32),
            dma(6),
            dma(3),
            pltpu.SemaphoreType.DMA((5, rows // TALL)),
        ],
        compiler_params=pltpu.CompilerParams(vmem_limit_bytes=44 * MEGA),
        cost_estimate=cost(2 * rows * width * FF + 4 * rows * width * width, 40 * MEGA),
        name="feed_forward_in",
    )(me, dz, x1, cot, branch, mixed, small, *mlp, *att)


GROUP = PAIRS // 2
GROUP_LANES = GROUP * LANES


def attend_back_block(b, start, width, group, refs):
    q, k, v, da, stats, dq, dkeys, dvalues, bias = refs
    rows = pl.ds(pl.multiple_of(b * QB, QB), QB)
    at = pl.ds(start, width)
    mask = jnp.concatenate([bias[0:width, :]] * 2, axis=1)
    for p in range(GROUP):
        lanes = slice(LANES * p, LANES * p + LANES)
        place = b * PAIRS + GROUP * group + p
        queries = head_masked(q[rows, lanes] * 0.125)
        grads = head_masked(da[rows, lanes])
        highest = stats[place, 0:1, :]
        inverse = stats[place, 1:2, :]
        keys, values = k[at, lanes], v[at, lanes]
        weight = jnp.exp(mm(keys, queries, NT) + mask - highest) * inverse
        dweight = mm(values, grads, NT)
        inner_sum = total(fold8(weight * dweight))
        dvalues[at, lanes] += mm(weight.astype(BF16), grads, NN)
        dscore = (weight * (dweight - inner_sum)).astype(BF16)
        dkeys[at, lanes] += mm(dscore, queries, NN)
        both = mm(keys, dscore, TN)
        dq[rows, lanes] = (pick_heads(both) * 0.125).T.astype(BF16)


def attend_back_kernel(group, windows, qkv, da_in, stats, key_ids, query_ids, dqkv, *refs):
    q, k, v, da, out, dkeys, dvalues, bias, own = refs
    rows = q.shape[0]
    blocks = rows // QB
    lanes = slice(GROUP_LANES * group, GROUP_LANES * group + GROUP_LANES)
    coming = [pltpu.make_async_copy(da_in.at[:, lanes], da, own.at[3])]
    for third, target in enumerate((q, k, v)):
        first = LANES * PAIRS * third + GROUP_LANES * group
        source = qkv.at[:, first : first + GROUP_LANES]
        coming.append(pltpu.make_async_copy(source, target, own.at[third]))
    fetch(coming)
    dkeys[...] = jnp.zeros_like(dkeys)
    dvalues[...] = jnp.zeros_like(dvalues)
    settle(coming)
    dq = out.at[:, 0:GROUP_LANES]

    def one_block(b, carry):
        start = pl.multiple_of(windows[0, b], SUB)
        for index, width in enumerate(CLASSES):

            @pl.when(windows[1, b] == index)
            def _(width=width):
                mask_bias(start, width, b, key_ids, query_ids, bias)
                parts = (q, k, v, da, stats, dq, dkeys, dvalues, bias)
                attend_back_block(b, start, width, group, parts)

        return carry

    lax.fori_loop(0, blocks, one_block, 0)
    going = []
    for i in range(rows // 256):
        at = slice(256 * i, 256 * i + 256)
        out[at, GROUP_LANES : 2 * GROUP_LANES] = dkeys[at, :].astype(BF16)
        out[at, 2 * GROUP_LANES :] = dvalues[at, :].astype(BF16)
        going.append(pltpu.make_async_copy(out.at[at, :], dqkv.at[at, :], own.at[i]))
        going[-1].start()
    settle(going)


def attend_back(group, windows, qkv, da, stats, key_ids, query_ids):
    rows = qkv.shape[0]
    part = lambda kind: pltpu.VMEM((rows, GROUP_LANES), kind)
    return pl.pallas_call(
        partial(attend_back_kernel, group),
        out_shape=shape((rows, 3 * GROUP_LANES), BF16),
        in_specs=[smem(), hbm(), hbm(), vmem(), vmem(), vmem()],
        out_specs=hbm(),
        scratch_shapes=[
            part(BF16),
            part(BF16),
            part(BF16),
            part(BF16),
            pltpu.VMEM((rows, 3 * GROUP_LANES), BF16),
            part(F32),
            part(F32),
            pltpu.VMEM((CLASSES[-1], QB), F32),
            dma(4),
        ],
        compiler_params=pltpu.CompilerParams(vmem_limit_bytes=32 * MEGA),
        cost_estimate=cost(3 * rows * rows * rows, 14 * rows * rows, 4 * rows * rows),
        name="attend_backward",
    )(windows, qkv, da, stats, key_ids, query_ids)


def put_qkv_grad(n1, dqkv, w, spots):
    for c in range(3):
        grad = mm(n1[:, 256 * c : 256 * c + 256], dqkv[...], TN)
        for r in range(SUB):
            d, rt = (SUB * c + r) // QKV_RT, (SUB * c + r) % QKV_RT
            place = spots[rt, d]
            for index in range(ATT_PART):
                tile = grad[SUB * r : SUB * r + SUB, LANES * index : LANES * index + LANES]
                w[rt, place, index] = tile.astype(BF16)


def put_wo_grad(gwo, w, spots):
    for h in range(2):
        for i in range(WO_BLOCKS):
            w[h, spots[h, QKV_BLOCKS + i], 0:ATT_PART] = gwo[h, i]


def weight_grad_kernel(me_ref, n1_in, dqkv_in, gwo_in, *refs):
    leaving, (w, spots, n1, dqkv, gwo, sems, own) = refs[:4], refs[4:]
    coming = [
        pltpu.make_async_copy(n1_in, n1, own.at[0]),
        pltpu.make_async_copy(dqkv_in, dqkv, own.at[1]),
        pltpu.make_async_copy(gwo_in, gwo, own.at[2]),
    ]
    fetch(coming)
    fill_spots(me_ref[0], spots)
    settle(coming)
    put_wo_grad(gwo, w, spots)
    put_qkv_grad(n1, dqkv, w, spots)
    copies = leaving_slots(leaving, w, sems)
    fetch(copies)
    settle(copies)


def weight_grad(me, n1, dqkv, gwo):
    rows, width = n1.shape
    half = shape((HALF_BLOCKS, ATT_PART, SUB, LANES), BF16)
    return pl.pallas_call(
        weight_grad_kernel,
        out_shape=(half,) * 4,
        in_specs=[smem()] + [hbm()] * 3,
        out_specs=(hbm(),) * 4,
        scratch_shapes=[
            slots_scratch(ATT_PART),
            spots_scratch(),
            pltpu.VMEM((rows, width), BF16),
            pltpu.VMEM(dqkv.shape, BF16),
            pltpu.VMEM(gwo.shape, BF16),
            dma(4),
            dma(3),
        ],
        compiler_params=pltpu.CompilerParams(vmem_limit_bytes=20 * MEGA),
        cost_estimate=cost(3 * rows * width * width, 10 * rows * width),
        name="qkv_weight_grad",
    )(me, n1, dqkv, gwo)


def qkv_back_kernel(
    me_ref, tokens_in, n1_in, dx1_in, dqkv0_in, dqkv1_in, small, proj, mlp, gwo_in, *refs
):
    arriving, refs = refs[:8], refs[8:]
    dx_out, *leaving = refs[:5]
    w, gw, weight, spots, gwo, tokens, n1, dx1, dqkv0, dqkv1, dn, dx, sums, table = refs[5:19]
    sems, out_sems, own = refs[19:]
    rows = tokens.shape[0]
    tiles = rows // TALL

    def tile_copy(source, target, t, k):
        at = pl.ds(pl.multiple_of(TALL * t, TALL), TALL)
        return pltpu.make_async_copy(source.at[at, :], target.at[at, :], own.at[k, t])

    for t in range(tiles):
        tile_copy(dqkv0_in, dqkv0, t, 0).start()
        tile_copy(dqkv1_in, dqkv1, t, 1).start()
    weights = arriving_slots(arriving, w, sems)
    fetch(weights)
    for t in range(tiles):
        tile_copy(tokens_in, tokens, t, 2).start()
        tile_copy(dx1_in, dx1, t, 3).start()
    late = [
        pltpu.make_async_copy(n1_in, n1, own.at[4, 0]),
        pltpu.make_async_copy(gwo_in, gwo, own.at[4, 1]),
    ]
    fetch(late)
    sums[...] = jnp.zeros_like(sums)
    gain = row_of(small, G1, 6)
    fill_spots(me_ref[0], spots)
    settle(weights)
    columns = qkv_group(0) + qkv_group(1)
    lay_matrix(w, spots, "qkv", QKV_BLOCKS, 0, QKV_RT, columns, weight)

    def contract(t):
        at = pl.ds(pl.multiple_of(TALL * t, TALL), TALL)
        for g, (source, part) in enumerate(((dqkv0_in, dqkv0), (dqkv1_in, dqkv1))):
            tile_copy(source, part, t, g).wait()
            lanes = slice(384 * g, 384 * g + 384)
            sums[16:24, lanes] += fold8(part[at, 0:384].astype(F32))
            sums[24:32, lanes] += fold8(part[at, 768:1152].astype(F32))
        both = jnp.concatenate([dqkv0[at, :], dqkv1[at, :]], axis=1)
        dn[at, :] = mm(both, weight[...], NT)

    def finish(t):
        tile_copy(tokens_in, tokens, t, 2).wait()
        tile_copy(dx1_in, dx1, t, 3).wait()
        for half in range(2):
            at = pl.ds(pl.multiple_of(TALL * t + TALL // 2 * half, TALL // 2), TALL // 2)
            unit, inverse = normalized(tokens[at, :].astype(F32))
            grad = dn[at, :]
            dx[at, :] = dx1[at, :] + norm_pullback(unit, inverse, grad, gain)
            sums[0:8, :] += fold8(grad * unit)
            sums[8:16, :] += fold8(grad)
        tile_copy(dx, dx_out, t, 3).start()

    def one_tile(t, carry):
        contract(t)
        finish(t - 1)
        return carry

    contract(0)
    lax.fori_loop(1, tiles, one_tile, 0)
    finish(tiles - 1)

    def put_table(owner, *places):
        table[...] = jnp.zeros_like(table)
        for place, values in places:
            if values.shape[1] == LANES:
                table[place : place + values.shape[0], :] = values
            else:
                put_row(table, place, values)
        for h in range(2):
            gw[h, spots[h, owner], ATT_PART] = table[SUB * h : SUB * h + SUB, :].astype(BF16)

    put_table(
        OWNERS[0], (0, total(sums[0:8, :])), (6, total(sums[8:16, :])), (12, mlp[0:12, :])
    )
    put_table(OWNERS[1], (0, mlp[12:36, :]))
    put_table(OWNERS[2], (0, total(sums[16:24, :])), (6, total(sums[24:32, :])))
    put_table(OWNERS[3], (0, proj[...]), (12, mlp[36:48, :]))
    settle(late)
    put_wo_grad(gwo, gw, spots)
    put_qkv_grad(n1, dqkv1, gw, spots)
    copies = leaving_slots(leaving, gw, out_sems)
    fetch(copies)
    for t in range(tiles):
        tile_copy(dx, dx_out, t, 3).wait()
    settle(copies)


def qkv_back(me, tokens, n1, dx1, dqkv0, dqkv1, small, proj, mlp, gwo, att):
    rows, width = tokens.shape
    tiles = ATT_PART + 1
    half = shape((HALF_BLOCKS, tiles, SUB, LANES), BF16)
    row = lambda kind: pltpu.VMEM((rows, width), kind)
    return pl.pallas_call(
        qkv_back_kernel,
        out_shape=(shape((rows, width), F32), half, half, half, half),
        in_specs=[smem()] + [hbm()] * 5 + [vmem()] * 3 + [hbm()] * 9,
        out_specs=(hbm(),) * 5,
        scratch_shapes=[
            slots_scratch(ATT_SENT),
            slots_scratch(tiles),
            pltpu.VMEM((width, 3 * width), BF16),
            spots_scratch(),
            pltpu.VMEM(gwo.shape, BF16),
            row(BF16),
            row(BF16),
            row(F32),
            pltpu.VMEM(dqkv0.shape, BF16),
            pltpu.VMEM(dqkv1.shape, BF16),
            row(F32),
            row(F32),
            pltpu.VMEM((32, width), F32),
            pltpu.VMEM((2 * SUB, LANES), F32),
            dma(8),
            dma(4),
            pltpu.SemaphoreType.DMA((5, rows // TALL)),
        ],
        compiler_params=pltpu.CompilerParams(vmem_limit_bytes=46 * MEGA),
        cost_estimate=cost(9 * rows * width * width, 30 * rows * width),
        name="qkv_backward",
    )(me, tokens, n1, dx1, dqkv0, dqkv1, small, proj, mlp, gwo, *att)


X, C, Z1, Z0, Y = 16, 8, 4, 2, 1


def exchange(values, bit):
    return lax.ppermute(values, AXES, [(d, d ^ bit) for d in range(BLOCKS)])


def shifted(values, by):
    pairs = [(d, d + by) for d in range(BLOCKS) if 0 <= d + by < BLOCKS]
    return lax.ppermute(values, AXES, pairs)


def together(*values):
    return lax.optimization_barrier(values)


def along_z(first, second, received):
    return (
        jnp.stack([first] + [r[0] for r in received]),
        jnp.stack([second] + [r[1] for r in received]),
    )


def joined(own, received):
    return jnp.concatenate([own, received])


def sum_terms(terms):
    summed = terms[0].astype(F32)
    for term in terms[1:]:
        summed = summed + term.astype(F32)
    return summed


def kept(terms):
    return [t[: t.shape[0] // 2] for t in terms]


def z_part(first, second, k):
    return jnp.stack([sum_terms([t[k] for t in terms]) for terms in (first, second)])


def sent(terms):
    return sum_terms([t[t.shape[0] // 2 :] for t in terms]).astype(BF16)


def attention_amounts(width):
    return [width, width, 3 * width * width, width, width, width * width, width, width]


def feedforward_amounts(width):
    return [width, width, width * FF, FF, FF * width, width, width]


def pieces_of(vector, amounts):
    out, offset = [], 0
    for amount in amounts:
        out.append(vector[offset : offset + amount])
        offset += amount
    return out


def tiles_by_column(matrix, blocks, rt):
    ct = matrix.shape[1] // LANES
    return matrix.reshape(blocks, rt, SUB, ct, LANES).transpose(0, 3, 1, 2, 4)


def tiles_by_row(matrix, blocks, rt):
    ct = matrix.shape[1] // LANES
    return matrix.reshape(blocks, rt, SUB, ct, LANES).transpose(0, 1, 3, 2, 4)


def gather_plainly(params, att_rows, width):
    rounded = params.astype(BF16)
    att = lax.all_gather(rounded[:att_rows], AXES, axis=0, tiled=True).reshape(-1)
    mlp = lax.all_gather(rounded[att_rows:], AXES, axis=0, tiled=True).reshape(-1)
    g1, c1, wqkv, bq, bv, wo, bo, s1 = pieces_of(att, attention_amounts(width))
    g2, c2, w1, b1, w2, b2, s2 = pieces_of(mlp, feedforward_amounts(width))
    tile = (SUB, LANES)
    att = jnp.concatenate(
        [
            tiles_by_column(wqkv.reshape(width, -1), QKV_BLOCKS, QKV_RT).reshape((-1, 36) + tile),
            tiles_by_row(wo.reshape(width, -1), WO_BLOCKS, WO_RT).reshape((-1, 36) + tile),
        ]
    )
    mlp = jnp.concatenate(
        [
            tiles_by_column(w1.reshape(width, -1), W1_BLOCKS, W1_RT).reshape((-1, 72) + tile),
            tiles_by_row(w2.reshape(FF, -1), W2_BLOCKS, W2_RT).reshape((-1, 72) + tile),
        ]
    )
    vectors = jnp.concatenate([g1, c1, bq, bv, bo, s1, g2, c2, b1, b2, s2]).astype(F32)
    lines = vectors.reshape(-1, LANES)
    sent = jnp.zeros((BLOCKS, 2 * SUB, LANES), F32)
    for owner, place, first, count in (
        (OWNERS[0], 0, G1, 12),
        (OWNERS[0], 12, G2, 12),
        (OWNERS[1], 0, B1, 24),
        (OWNERS[2], 0, BQ, 12),
        (OWNERS[3], 0, BO, 12),
        (OWNERS[3], 12, B2, 12),
    ):
        sent = sent.at[owner, place : place + count].set(lines[first : first + count])
    sent = sent.astype(BF16).reshape((BLOCKS, 2, 1) + tile)
    att = [jnp.concatenate([att[:, 18 * h : 18 * h + 18], sent[:, h]], axis=1) for h in range(2)]
    return by_slot(*att), by_slot(mlp[:, :36], mlp[:, 36:])


def by_slot(first, second):
    halves = (first, second)
    return [
        jnp.stack([halves[i // 4][slot] for slot in SLOTS[i // 4][i % 4 * 8 : i % 4 * 8 + 8]])
        for i in range(8)
    ]


def from_slots(buffers):
    halves = []
    for h in range(2):
        slots = jnp.concatenate(buffers[2 * h : 2 * h + 2])
        halves.append(jnp.stack([slots[spot(h, d)] for d in range(BLOCKS)]))
    return halves


def reduce_plainly(gatt0, gatt1, gmlp, att_rows, mlp_rows, width, devices):
    groups = [from_slots(gatt0), from_slots(gatt1)]
    vectors = jnp.concatenate([groups[1][h][:, ATT_PART:] for h in range(2)], axis=1)
    vectors = vectors.astype(F32).reshape(BLOCKS, 2 * SUB, LANES)

    def matrix(name, first, last, rt_count, ct_count):
        rows = []
        for rt in range(rt_count):
            places = [part_place(name, rt, ct) for ct in range(ct_count)]
            rows.append(jnp.stack([groups[g][h][first:last, i] for g, h, i in places], axis=2))
        return jnp.stack(rows, axis=1).astype(F32).reshape(-1)

    wqkv = matrix("qkv", 0, QKV_BLOCKS, QKV_RT, QKV_CT)
    wo = matrix("wo", QKV_BLOCKS, BLOCKS, WO_RT, WO_CT)
    mlp = jnp.concatenate(from_slots(gmlp), axis=1).astype(F32)
    five = lambda v, dims: v.reshape((v.shape[0],) + dims + (SUB, LANES))
    w1 = five(mlp[:W1_BLOCKS], (W1_CT, W1_RT)).transpose(0, 2, 3, 1, 4).reshape(-1)
    w2 = five(mlp[W1_BLOCKS:], (W2_RT, W2_CT)).transpose(0, 1, 3, 2, 4).reshape(-1)
    line = lambda owner, first, count: vectors[owner, first : first + count].reshape(-1)
    att = [line(OWNERS[0], 0, 12), wqkv, line(OWNERS[2], 0, 12), wo, line(OWNERS[3], 0, 12)]
    mlp = [line(OWNERS[0], 12, 12), w1, line(OWNERS[1], 0, 24), w2, line(OWNERS[3], 12, 12)]

    def lay(parts, rows):
        vector = jnp.concatenate(parts)
        vector = jnp.pad(vector, (0, devices * rows * LANES - vector.shape[0]))
        return vector.reshape(devices, rows, LANES)

    whole = jnp.concatenate([lay(att, att_rows), lay(mlp, mlp_rows)], axis=1)
    return lax.psum_scatter(whole.reshape(-1, LANES), AXES, scatter_dimension=0, tiled=True)


def key_windows(segments, real):
    length = segments.shape[0]
    position = jnp.arange(length, dtype=jnp.int32)
    ids = jnp.where(real, segments, length + position)
    first = segments[0::QB]
    final = segments[QB - 1 :: QB]
    begin = jnp.sum((segments[None, :] < first[:, None]).astype(jnp.int32), axis=1)
    begin = jnp.where(real[0::QB], begin, position[0::QB])
    end = jnp.sum(((segments[None, :] <= final[:, None]) & real[None, :]).astype(jnp.int32), axis=1)
    end = jnp.where(real[QB - 1 :: QB], end, position[QB - 1 :: QB] + 1)
    begin = begin // SUB * SUB
    need = end - begin
    kind = sum((need > width).astype(jnp.int32) for width in CLASSES[:-1])
    widths = sum(
        jnp.where(kind == i, width, 0) for i, width in enumerate(CLASSES)
    )
    begin = jnp.minimum(begin, length - widths)
    chunks = (begin + widths + QB - 1) // QB
    return ids, jnp.stack([begin, kind, chunks]).astype(jnp.int32)


def local(tokens, cotangent, segment_ids, pad_mask, lengths, params):
    rows, width = tokens.shape
    wide, narrow = lax.axis_size("wide"), lax.axis_size("narrow")
    devices = wide * narrow
    att_count = 4 * width * width + 6 * width
    att_rows = (att_count // LANES + devices - 1) // devices
    mlp_rows = params.shape[0] - att_rows
    paired = (wide, narrow) == (4, 8)
    scale = 1.0 / math.sqrt(rows * devices)

    position = jnp.arange(rows, dtype=jnp.int32)
    real = (pad_mask > 0) & (position < lengths[0])
    ids, windows = key_windows(segment_ids, real)
    key_ids = ids.reshape(rows, 1)
    query_ids = ids.reshape(rows // QB, QB)

    if not paired:
        me = jnp.zeros((1,), jnp.int32)
        att, mlp = gather_plainly(params, att_rows, width)
        n1, qkv, small = project_qkv(me, tokens, att)
        mixed, x1, branch, n2, dm, stats, gb2 = attend(
            me, windows, qkv, tokens, cotangent, key_ids, query_ids, small, att
        )
        u, dz, gb1, *gmlp = feed_forward(me, n2, dm, small, mlp)
        output, gs2 = feed_forward_out(me, u, x1, cotangent, small, mlp)
        dx1, da, gwo0, gwo1, others = split(
            me, dz, x1, cotangent, branch, mixed, small, mlp, att
        )
        small_mlp = jnp.concatenate([others[:12], gb1, gb2, gs2])
        small_proj = others[12:]
        dqkv0 = attend_back(0, windows, qkv, da, stats, key_ids, query_ids)
        dqkv1 = attend_back(1, windows, qkv, da, stats, key_ids, query_ids)
        gatt0 = weight_grad(me, n1, dqkv0, gwo0)
        grad_input, *gatt1 = qkv_back(
            me, tokens, n1, dx1, dqkv0, dqkv1, small, small_proj, small_mlp, gwo1, att
        )
        owned = reduce_plainly(gatt0, gatt1, gmlp, att_rows, mlp_rows, width, devices)
        return output, grad_input, owned * scale

    me = lax.axis_index(AXES).astype(jnp.int32).reshape(1)
    tails = jnp.concatenate([params[att_rows - ATT_BEFORE : att_rows], params[-MLP_BEFORE:]])
    heads = jnp.concatenate([params[:ATT_AFTER], params[att_rows : att_rows + MLP_AFTER]])
    tails, heads = shifted(tails, 1), shifted(heads, -1)
    att_own, mlp_own = pack(me, params, tails, heads, att_rows)

    got = [exchange(att_own, k * Z0) for k in range(1, 4)]
    a, b = along_z(att_own[0], att_own[1], got)
    a, b, mlp_own, windows, key_ids, query_ids = together(
        a, b, mlp_own, windows, key_ids, query_ids
    )
    ax, by = exchange(a, X), exchange(b, Y)
    z1, z3 = exchange(mlp_own, Z0), exchange(mlp_own, 3 * Z0)
    a, b = joined(a, ax), joined(b, by)
    a, b, z1, z3, mlp_own = together(a, b, z1, z3, mlp_own)
    ay, bx = exchange(a, Y), exchange(b, X)
    ac, bc = exchange(a, C), exchange(b, C)
    z2 = exchange(mlp_own, 2 * Z0)
    m, n = along_z(mlp_own[0], mlp_own[1], [z1, z2, z3])
    ay, bx, ac, bc, m, n = together(ay, bx, ac, bc, m, n)
    ayc, bxc = exchange(ay, C), exchange(bx, C)
    att = together(a, ay, ac, ayc, b, bx, bc, bxc, m, n, tokens)
    *att, m, n, tokens_now = att
    mx, ny = exchange(m, X), exchange(n, Y)
    n1, qkv, small = project_qkv(me, tokens_now, att)
    m, n = joined(m, mx), joined(n, ny)
    m, n, qkv = together(m, n, qkv)
    my, nx = exchange(m, Y), exchange(n, X)
    mc, nc = exchange(m, C), exchange(n, C)
    mixed, x1, branch, n2, dm, stats, gb2 = attend(
        me, windows, qkv, tokens, cotangent, key_ids, query_ids, small, att
    )
    m, n, my, nx, mc, nc, n2 = together(m, n, my, nx, mc, nc, n2)
    myc, nxc = exchange(my, C), exchange(nx, C)
    mlp = (m, my, mc, myc, n, nx, nc, nxc)

    u, dz, gb1, *gmlp = feed_forward(me, n2, dm, small, mlp)

    mc, nc = exchange(gmlp[1], C), exchange(gmlp[3], C)
    output, gs2 = feed_forward_out(me, u, x1, cotangent, small, mlp)
    mc, nc, dz, gs2 = together(mc, nc, dz, gs2)
    m, n = [gmlp[0], mc], [gmlp[2], nc]
    my, nx, dz = together(sent(m), sent(n), dz)
    my, nx = exchange(my, Y), exchange(nx, X)
    dx1, da, gwo0, gwo1, others = split(
        me, dz, x1, cotangent, branch, mixed, small, mlp, att
    )
    dqkv0 = attend_back(0, windows, qkv, da, stats, key_ids, query_ids)
    gatt0 = weight_grad(me, n1, dqkv0, gwo0)
    my, nx, da, *gatt0 = together(my, nx, da, *gatt0)
    m, n = kept(m) + [my], kept(n) + [nx]
    mx, ny, da, *gatt0 = together(sent(m), sent(n), da, *gatt0)
    mx, ny = exchange(mx, X), exchange(ny, Y)
    ac, bc = exchange(gatt0[1], C), exchange(gatt0[3], C)
    dqkv1 = attend_back(1, windows, qkv, da, stats, key_ids, query_ids)
    mx, ny, ac, bc, dqkv1 = together(mx, ny, ac, bc, dqkv1)
    m, n = kept(m) + [mx], kept(n) + [ny]
    z1, z2, z3 = [z_part(m, n, k).astype(BF16) for k in range(1, 4)]
    a, b = [gatt0[0], ac], [gatt0[2], bc]
    ay, bx, z1, z2, z3, dqkv1 = together(sent(a), sent(b), z1, z2, z3, dqkv1)
    z1, z2 = exchange(z1, Z0), exchange(z2, 2 * Z0)
    ay, bx = exchange(ay, Y), exchange(bx, X)
    small_mlp = jnp.concatenate([others[:12], gb1, gb2, gs2])
    grad_input, *gatt1 = qkv_back(
        me, tokens, n1, dx1, dqkv0, dqkv1, small, others[12:], small_mlp, gwo1, att
    )
    ay, bx, z1, z2, *gatt1 = together(ay, bx, z1, z2, *gatt1)
    a, b = kept(a) + [ay], kept(b) + [bx]
    ax, by, c1, d1, z3 = together(sent(a), sent(b), gatt1[1], gatt1[3], z3)
    c1, d1 = exchange(c1, C), exchange(d1, C)
    ax, by = exchange(ax, X), exchange(by, Y)
    z3 = exchange(z3, 3 * Z0)
    c, d = [gatt1[0], c1], [gatt1[2], d1]
    a, b = kept(a) + [ax], kept(b) + [by]
    sends = [z_part(a, b, k).astype(BF16) for k in range(1, 4)]
    cy, dx, *sends = together(sent(c), sent(d), *sends)
    cy, dx = exchange(cy, Y), exchange(dx, X)
    got = [exchange(part, (k + 1) * Z0) for k, part in enumerate(sends)]
    c, d = kept(c) + [cy], kept(d) + [dx]
    cx, dy, z3, *got = together(sent(c), sent(d), z3, *got)
    group0 = sum_terms([z_part(a, b, 0)] + got)
    m_own = sum_terms([z_part(m, n, 0), z1, z2, z3])
    cx, dy = exchange(cx, X), exchange(dy, Y)
    c, d = kept(c) + [cx], kept(d) + [dy]
    sends = [z_part(c, d, k).astype(BF16) for k in range(1, 4)]
    group0, m_own, *sends = together(group0, m_own, *sends)
    got = [exchange(part, (k + 1) * Z0) for k, part in enumerate(sends)]
    group1 = sum_terms([z_part(c, d, 0)] + got)
    mine, to_before, to_after = spread(me, group0, group1, m_own, att_rows, mlp_rows, scale)
    grad_params = close(mine, shifted(to_after, 1), shifted(to_before, -1), att_rows)
    return output, grad_input, grad_params


def solution(mesh):
    return jax.shard_map(
        local,
        mesh=mesh,
        in_specs=(
            P(AXES, None),
            P(AXES, None),
            P(AXES),
            P(AXES),
            P(AXES),
            P(AXES, None),
        ),
        out_specs=(P(AXES, None), P(AXES, None), P(AXES, None)),
        check_vma=False,
    )
```

```python
import math
from functools import partial

import jax
import jax.numpy as jnp
from jax import lax
from jax.experimental import pallas as pl
from jax.experimental.pallas import tpu as pltpu
from jax.sharding import PartitionSpec as P

FF = 3072
HEADS = 12
EPSILON = 1e-06
NEGATIVE = -1e30
AXES = ("wide", "narrow")
LANES = 128
SUB = 16
QB = 128
MEGA = 1 << 20
GRANT = 58 * MEGA
F32 = jnp.float32
BF16 = jnp.bfloat16

BLOCKS = 32
QKV_BLOCKS, QKV_RT, QKV_CT = 24, 2, 18
WO_BLOCKS, WO_RT, WO_CT = 8, 6, 6
W1_BLOCKS, W1_RT, W1_CT = 16, 3, 24
W2_BLOCKS, W2_RT, W2_CT = 16, 12, 6
ATT_HALF, MLP_HALF = 18, 36
ATT_SENT = ATT_HALF + 1
ATT_PART = 9
HALF_BLOCKS = BLOCKS // 2
CHUNK = 768
CHUNKS = FF // CHUNK

G1, C1, BQ, BV, BO, S1 = 0, 6, 12, 18, 24, 30
G2, C2, B1, B2, S2 = 36, 42, 48, 72, 78
SMALL = 88

NT = (((1,), (1,)), ((), ()))
NN = (((1,), (0,)), ((), ()))
TN = (((0,), (0,)), ((), ()))


def mm(lhs, rhs, dims):
    return lax.dot_general(lhs, rhs, dims, preferred_element_type=F32)


def row_of(ref, first, count):
    return jnp.concatenate([ref[first + k : first + k + 1, :] for k in range(count)], axis=1)


def put_row(ref, first, values):
    for k in range(values.shape[1] // LANES):
        ref[first + k : first + k + 1, :] = values[:, k * LANES : (k + 1) * LANES]


def fold8(values):
    rows, columns = values.shape
    return jnp.sum(values.reshape(rows // 8, 8, columns), axis=0)


def total(values):
    return jnp.sum(values, axis=0, keepdims=True)


def vmem():
    return pl.BlockSpec(memory_space=pltpu.VMEM)


def smem():
    return pl.BlockSpec(memory_space=pltpu.SMEM)


def hbm():
    return pl.BlockSpec(memory_space=pltpu.HBM)


def shape(dims, kind):
    return jax.ShapeDtypeStruct(dims, kind)


def cost(flops, moved, exps=0):
    return pl.CostEstimate(flops=int(flops), transcendentals=int(exps), bytes_accessed=int(moved))


def normalized(values):
    center = values - jnp.mean(values, axis=-1, keepdims=True)
    inverse = lax.rsqrt(jnp.mean(center * center, axis=-1, keepdims=True) + EPSILON)
    return center * inverse, inverse


def norm_pullback(unit, inverse, grad, gain):
    scaled = grad * gain
    first = jnp.mean(scaled, axis=-1, keepdims=True)
    second = jnp.mean(scaled * unit, axis=-1, keepdims=True)
    return inverse * (scaled - first - unit * second)


def gelu_pair(z):
    magnitude = jnp.abs(z)
    t = 1.0 / (1.0 + (0.3275911 * math.sqrt(0.5)) * magnitude)
    density = jnp.exp(z * z * -0.5)
    tail = 0.5 * 1.061405429
    tail = tail * t + 0.5 * -1.453152027
    tail = tail * t + 0.5 * 1.421413741
    tail = tail * t + 0.5 * -0.284496736
    tail = tail * t + 0.5 * 0.254829592
    tail = tail * t * density
    cumulative = jnp.where(z < 0, tail, 1.0 - tail)
    return z * cumulative, cumulative + z * density * (1.0 / math.sqrt(2.0 * math.pi))


def fetch(copies):
    for copy in copies:
        copy.start()


def settle(copies):
    for copy in copies:
        copy.wait()


ATT_BEFORE, ATT_AFTER = 64, 32
MLP_BEFORE, MLP_AFTER = 64, 40


def window_offsets(me, att_rows, mlp_rows):
    att = ATT_BEFORE + 12 + me * (576 - att_rows) + jnp.where(me < QKV_BLOCKS, 0, 12)
    mlp = MLP_BEFORE + 12 + me * (1152 - mlp_rows) + jnp.where(me < W1_BLOCKS, 0, 24)
    return att, mlp


def each_tile(me, act):
    for name, blocks, rt_count, ct_count, mine in (
        ("qkv", QKV_BLOCKS, QKV_RT, QKV_CT, me < QKV_BLOCKS),
        ("wo", WO_BLOCKS, WO_RT, WO_CT, me >= QKV_BLOCKS),
        ("w1", W1_BLOCKS, W1_RT, W1_CT, me < W1_BLOCKS),
        ("w2", W2_BLOCKS, W2_RT, W2_CT, me >= W1_BLOCKS),
    ):

        @pl.when(mine)
        def _(name=name, rt_count=rt_count, ct_count=ct_count):
            for ct in range(ct_count):
                for rt in range(rt_count):
                    act(name, rt, ct, rt * SUB * ct_count + ct, ct_count)


def half_place(name, rt, ct):
    if name == "qkv":
        return ct // 9, ct % 9 * QKV_RT + rt
    if name == "wo":
        return rt // 3, rt % 3 * WO_CT + ct
    if name == "w1":
        return ct // 12, ct % 12 * W1_RT + rt
    return rt // 6, rt % 6 * W2_CT + ct


def part_place(name, rt, ct):
    if name == "qkv":
        return ct % 6 // 3, rt, ct // 6 * 3 + ct % 3
    place = rt * WO_CT + ct
    return place // 18, place // ATT_PART % 2, place % ATT_PART


def qkv_group(g):
    return [6 * third + 3 * g + i for third in range(3) for i in range(3)]


def small_rows(me, act):
    @pl.when(me == 0)
    def _():
        act("att", True, 12, G1)
        act("mlp", True, 12, G2)

    @pl.when(me == QKV_BLOCKS - 1)
    def _():
        act("att", False, 12, BQ)

    @pl.when(me == W1_BLOCKS - 1)
    def _():
        act("mlp", False, 24, B1)

    @pl.when(me == BLOCKS - 1)
    def _():
        act("att", False, 12, BO)
        act("mlp", False, 12, B2)


OWNERS = (0, W1_BLOCKS - 1, QKV_BLOCKS - 1, BLOCKS - 1)


def sent_rows(kind, first):
    return 12 if kind == "mlp" and first in (G2, B2) else 0


def pack_kernel(att_rows, me_ref, own, tails, heads, att, mlp, win_a, win_m, table):
    me = me_ref[0]
    mlp_rows = own.shape[0] - att_rows
    win_a[0:ATT_BEFORE, :] = tails[0:ATT_BEFORE, :]
    win_a[ATT_BEFORE : ATT_BEFORE + att_rows, :] = own[0:att_rows, :]
    win_a[ATT_BEFORE + att_rows :, :] = heads[0:ATT_AFTER, :]
    win_m[0:MLP_BEFORE, :] = tails[ATT_BEFORE:, :]
    win_m[MLP_BEFORE : MLP_BEFORE + mlp_rows, :] = own[att_rows:, :]
    win_m[MLP_BEFORE + mlp_rows :, :] = heads[ATT_AFTER:, :]
    att_off, mlp_off = window_offsets(me, att_rows, mlp_rows)

    def tile(name, rt, ct, first, stride):
        attention = name in ("qkv", "wo")
        window, out, off = (win_a, att, att_off) if attention else (win_m, mlp, mlp_off)
        values = window[pl.ds(off + first, SUB, stride=stride), :]
        out[half_place(name, rt, ct)] = values.astype(BF16)

    each_tile(me, tile)
    table[...] = jnp.zeros_like(table)

    def vector(kind, before, rows, first):
        window, off, size = (win_a, att_off, 576) if kind == "att" else (win_m, mlp_off, 1152)
        start = off - 12 if before else off + size
        place = sent_rows(kind, first)
        table[place : place + rows, :] = window[pl.ds(start, rows), :]

    small_rows(me, vector)
    att[0, ATT_HALF] = table[0:SUB, :].astype(BF16)
    att[1, ATT_HALF] = table[SUB : 2 * SUB, :].astype(BF16)


def pack(me, own, tails, heads, att_rows):
    mlp_rows = own.shape[0] - att_rows
    return pl.pallas_call(
        partial(pack_kernel, att_rows),
        out_shape=(
            shape((2, ATT_SENT, SUB, LANES), BF16),
            shape((2, MLP_HALF, SUB, LANES), BF16),
        ),
        in_specs=[smem(), vmem(), vmem(), vmem()],
        out_specs=(vmem(), vmem()),
        scratch_shapes=[
            pltpu.VMEM((ATT_BEFORE + att_rows + ATT_AFTER, LANES), F32),
            pltpu.VMEM((MLP_BEFORE + mlp_rows + MLP_AFTER, LANES), F32),
            pltpu.VMEM((2 * SUB, LANES), F32),
        ],
        name="pack",
    )(me, own, tails, heads)


def spread_kernel(
    att_rows, scale, me_ref, group0, group1, mlp, mine, to_before, to_after, win_a, win_m, table
):
    me = me_ref[0]
    mlp_rows = mine.shape[0] - att_rows
    att_off, mlp_off = window_offsets(me, att_rows, mlp_rows)
    win_a[...] = jnp.zeros_like(win_a)
    win_m[...] = jnp.zeros_like(win_m)

    def tile(name, rt, ct, first, stride):
        if name in ("qkv", "wo"):
            g, half, index = part_place(name, rt, ct)
            values = (group0, group1)[g][half, index]
            win_a[pl.ds(att_off + first, SUB, stride=stride), :] = values * scale
        else:
            values = mlp[half_place(name, rt, ct)]
            win_m[pl.ds(mlp_off + first, SUB, stride=stride), :] = values * scale

    each_tile(me, tile)
    for h in range(2):
        table[SUB * h : SUB * h + SUB, :] = group1[h, ATT_PART] * scale

    def vector(kind, before, rows, first):
        window, off, size = (win_a, att_off, 576) if kind == "att" else (win_m, mlp_off, 1152)
        start = off - 12 if before else off + size
        place = sent_rows(kind, first)
        window[pl.ds(start, rows), :] = table[place : place + rows, :]

    small_rows(me, vector)
    mine[0:att_rows, :] = win_a[ATT_BEFORE : ATT_BEFORE + att_rows, :]
    mine[att_rows:, :] = win_m[MLP_BEFORE : MLP_BEFORE + mlp_rows, :]
    to_before[0:ATT_BEFORE, :] = win_a[0:ATT_BEFORE, :]
    to_before[ATT_BEFORE:, :] = win_m[0:MLP_BEFORE, :]
    to_after[0:ATT_AFTER, :] = win_a[ATT_BEFORE + att_rows :, :]
    to_after[ATT_AFTER:, :] = win_m[MLP_BEFORE + mlp_rows :, :]


def spread(me, group0, group1, mlp, att_rows, mlp_rows, scale):
    return pl.pallas_call(
        partial(spread_kernel, att_rows, scale),
        out_shape=(
            shape((att_rows + mlp_rows, LANES), F32),
            shape((ATT_BEFORE + MLP_BEFORE, LANES), F32),
            shape((ATT_AFTER + MLP_AFTER, LANES), F32),
        ),
        in_specs=[smem(), vmem(), vmem(), vmem()],
        out_specs=(vmem(), vmem(), vmem()),
        scratch_shapes=[
            pltpu.VMEM((ATT_BEFORE + att_rows + ATT_AFTER, LANES), F32),
            pltpu.VMEM((MLP_BEFORE + mlp_rows + MLP_AFTER, LANES), F32),
            pltpu.VMEM((2 * SUB, LANES), F32),
        ],
        name="spread",
    )(me, group0, group1, mlp)


def close_kernel(att_rows, mine, below, above, out):
    rows = mine.shape[0]
    out[...] = mine[...]
    out[0:ATT_AFTER, :] += below[0:ATT_AFTER, :]
    out[att_rows : att_rows + MLP_AFTER, :] += below[ATT_AFTER:, :]
    out[att_rows - ATT_BEFORE : att_rows, :] += above[0:ATT_BEFORE, :]
    out[rows - MLP_BEFORE : rows, :] += above[ATT_BEFORE:, :]


def close(mine, below, above, att_rows):
    return pl.pallas_call(
        partial(close_kernel, att_rows),
        out_shape=shape(mine.shape, F32),
        in_specs=[vmem()] * 3,
        out_specs=vmem(),
        name="close",
    )(mine, below, above)


def spot(h, d):
    x, c, z, y = d >> 4, (d >> 3) & 1, (d >> 1) & 3, d & 1
    return c * 16 + (y * 8 + x * 4 if h == 0 else x * 8 + y * 4) + z


SLOTS = [sorted(range(BLOCKS), key=partial(spot, h)) for h in range(2)]


def fill_spots(me, spots):
    for h in range(2):
        mine = spot(h, me)
        for d in range(BLOCKS):
            spots[h, d] = jnp.bitwise_xor(mine, spot(h, d))


def slots_scratch(tiles):
    return pltpu.VMEM((2, BLOCKS, tiles, SUB, LANES), BF16)


def spots_scratch():
    return pltpu.SMEM((2, BLOCKS), jnp.int32)


def arriving_slots(buffers, w, sems):
    return [
        pltpu.make_async_copy(buffers[i], w.at[i // 4, pl.ds(i % 4 * 8, 8)], sems.at[i])
        for i in range(8)
    ]


def leaving_slots(buffers, w, sems):
    return [
        pltpu.make_async_copy(w.at[i // 2, pl.ds(i % 2 * 16, 16)], buffers[i], sems.at[i])
        for i in range(4)
    ]


def qkv_column(w, spots, ct):
    h, place = ct // 9, ct % 9 * QKV_RT
    tiles = [w[h, spots[h, d], place + rt] for d in range(QKV_BLOCKS) for rt in range(QKV_RT)]
    return jnp.concatenate(tiles, axis=0)


def wo_matrix(w, spots):
    columns = []
    for ct in range(WO_CT):
        tiles = [
            w[rt // 3, spots[rt // 3, QKV_BLOCKS + i] & 7, rt % 3 * WO_CT + ct]
            for i in range(WO_BLOCKS)
            for rt in range(WO_RT)
        ]
        columns.append(jnp.concatenate(tiles, axis=0))
    return jnp.concatenate(columns, axis=1)


def dma(count):
    return pltpu.SemaphoreType.DMA((count,))


def norm_rows(rows, gain, shift, source, target, step=256):
    def one(i, carry):
        at = pl.ds(pl.multiple_of(i * step, step), step)
        unit, _ = normalized(source[at, :].astype(F32))
        target[at, :] = (unit * gain + shift).astype(BF16)
        return carry

    lax.fori_loop(0, rows // step, one, 0)


def qkv_kernel(me_ref, tokens, *refs):
    buffers, (n1, qkv, small, w, spots, x, unit, triple, sems, own) = refs[:8], refs[8:]
    coming = pltpu.make_async_copy(tokens, x, own.at[0])
    coming.start()
    weights = arriving_slots(buffers, w, sems)
    fetch(weights)
    fill_spots(me_ref[0], spots)
    settle(weights)
    tables = [
        jnp.concatenate([w[h, spots[h, d], ATT_HALF] for h in range(2)], axis=0).astype(F32)
        for d in OWNERS
    ]
    small[G1 : G1 + 12, :] = tables[0][0:12]
    small[G2 : G2 + 12, :] = tables[0][12:24]
    small[B1 : B1 + 24, :] = tables[1][0:24]
    small[BQ : BQ + 12, :] = tables[2][0:12]
    small[BO : BO + 12, :] = tables[3][0:12]
    small[B2 : B2 + 12, :] = tables[3][12:24]
    small[SMALL - 4 :, :] = jnp.zeros((4, LANES), F32)
    coming.wait()
    norm_rows(x.shape[0], row_of(small, G1, 6), row_of(small, C1, 6), x, unit)
    going = [pltpu.make_async_copy(unit, n1, own.at[0])]
    going[0].start()
    bias = jnp.concatenate(
        [row_of(small, BQ, 6), jnp.zeros((1, 768), F32), row_of(small, BV, 6)], axis=1
    )
    for c in range(QKV_CT // 2):
        weight = jnp.concatenate([qkv_column(w, spots, 2 * c + i) for i in range(2)], axis=1)
        lanes = slice(256 * c, 256 * c + 256)
        triple[:, lanes] = (mm(unit[...], weight, NN) + bias[:, lanes]).astype(BF16)
        going.append(
            pltpu.make_async_copy(triple.at[:, lanes], qkv.at[:, lanes], own.at[1 + c])
        )
        going[-1].start()
    settle(going)


def project_qkv(me, tokens, att):
    rows, width = tokens.shape
    return pl.pallas_call(
        qkv_kernel,
        out_shape=(
            shape((rows, width), BF16),
            shape((rows, 3 * width), BF16),
            shape((SMALL, LANES), F32),
        ),
        in_specs=[smem(), hbm()] + [hbm()] * 8,
        out_specs=(hbm(), hbm(), vmem()),
        scratch_shapes=[
            slots_scratch(ATT_SENT),
            spots_scratch(),
            pltpu.VMEM((rows, width), BF16),
            pltpu.VMEM((rows, width), BF16),
            pltpu.VMEM((rows, 3 * width), BF16),
            dma(8),
            dma(1 + QKV_CT // 2),
        ],
        compiler_params=pltpu.CompilerParams(vmem_limit_bytes=GRANT),
        cost_estimate=cost(6 * rows * width * width, 12 * rows * width),
        name="qkv_forward",
    )(me, tokens, *att)


CLASSES = (128, 256, 320, 384, 448, 512, 768)


def head_masked(block):
    lane = lax.broadcasted_iota(jnp.int32, block.shape, 1)
    zero = jnp.zeros_like(block)
    return jnp.concatenate(
        [jnp.where(lane < 64, block, zero), jnp.where(lane >= 64, block, zero)], axis=0
    )


def pick_heads(both):
    return jnp.concatenate([both[0:64, 0:QB], both[64:128, QB : 2 * QB]], axis=0)


def pieces_of_window(width):
    return [slice(first, min(first + QB, width)) for first in range(0, width, QB)]


def spread_ids(query_ids, key_ids):
    for b in range(query_ids.shape[0]):
        row = jnp.broadcast_to(query_ids[b : b + 1, :], (QB, QB))
        key_ids[b * QB : (b + 1) * QB, :] = row.T


def mask_bias(start, width, b, key_ids, query_ids, bias):
    for piece in pieces_of_window(width):
        size = piece.stop - piece.start
        at = pl.ds(pl.multiple_of(start + piece.start, SUB), size)
        same = key_ids[at, :] == query_ids[pl.ds(b, 1), :]
        bias[piece, :] = jnp.where(same, 0.0, NEGATIVE)


PAIRS = HEADS // 2


def attend_block(b, start, width, qkv, mixed, stats, bias, scores):
    rows = pl.ds(pl.multiple_of(b * QB, QB), QB)
    pieces = pieces_of_window(width)
    for p in range(PAIRS):
        lanes, key_lanes, value_lanes = [
            slice(LANES * (PAIRS * third + p), LANES * (PAIRS * third + p + 1))
            for third in range(3)
        ]
        queries = head_masked(qkv[rows, lanes] * 0.125)
        highest = jnp.full((8, 2 * QB), NEGATIVE, F32)
        for piece in pieces:
            size = piece.stop - piece.start
            at = pl.ds(pl.multiple_of(start + piece.start, SUB), size)
            part = mm(qkv[at, key_lanes], queries, NT)
            part = part + jnp.concatenate([bias[piece, :]] * 2, axis=1)
            scores[p, piece, :] = part
            highest = jnp.maximum(highest, jnp.max(part.reshape(size // 8, 8, 2 * QB), axis=0))
        highest = jnp.max(highest, axis=0, keepdims=True)
        summed = jnp.zeros((8, 2 * QB), F32)
        both = jnp.zeros((LANES, 2 * QB), F32)
        for piece in pieces:
            size = piece.stop - piece.start
            at = pl.ds(pl.multiple_of(start + piece.start, SUB), size)
            raised = jnp.exp(scores[p, piece, :] - highest)
            summed = summed + fold8(raised)
            both = both + mm(qkv[at, value_lanes], raised.astype(BF16), TN)
        inverse = 1.0 / total(summed)
        mixed[rows, lanes] = pick_heads(both * inverse).T.astype(BF16)
        stats[b * PAIRS + p, 0:1, :] = highest
        stats[b * PAIRS + p, 1:2, :] = inverse


def wo_scratch():
    return pltpu.VMEM((2, WO_BLOCKS, ATT_SENT, SUB, LANES), BF16)


def wo_copies(buffers, w, sems, core, x):
    copies = []
    for y in range(2):
        source = buffers[2 * core + y].at[pl.ds(4 * x, 4)]
        copies.append(pltpu.make_async_copy(source, w.at[0, pl.ds(4 * y, 4)], sems.at[y]))
    copies.append(pltpu.make_async_copy(buffers[4 + 2 * core + x], w.at[1], sems.at[2]))
    return copies


def fetch_wo(me, buffers, w, spots, sems):
    fill_spots(me, spots)
    for h in range(2):
        for i in range(WO_BLOCKS):
            place = spot(h, jnp.bitwise_xor(me, QKV_BLOCKS + i) & 7)
            spots[h, QKV_BLOCKS + i] = (place >> (1 if h == 0 else 0)) & 4 | place & 3
    far = jnp.bitwise_xor(me, QKV_BLOCKS)
    for core in range(2):
        for x in range(2):

            @pl.when((far >> 3) == 2 * x + core)
            def _(core=core, x=x):
                fetch(wo_copies(buffers, w, sems, core, x))


def wait_wo(buffers, w, sems):
    settle(wo_copies(buffers, w, sems, 0, 0))


def attend_kernel(me_ref, windows, qkv, tokens, cot, query_ids, small, *refs):
    buffers, refs = refs[:8], refs[8:]
    mixed, x1, branch, n2, dm, stats, gb2 = refs[:7]
    key_ids, triple, x, g, mix, mid, out, unit, scaled, bias, scores, w, spots = refs[7:20]
    sems, own, chunk_sems = refs[20:]
    rows = tokens.shape[0]
    blocks = rows // QB

    def chunk(i):
        at = pl.ds(pl.multiple_of(i * QB, QB), QB)
        return pltpu.make_async_copy(qkv.at[at, :], triple.at[at, :], chunk_sems.at[i])

    for i in range(blocks):
        chunk(i).start()
    coming = [
        pltpu.make_async_copy(tokens, x, own.at[0]),
        pltpu.make_async_copy(cot, g, own.at[1]),
    ]
    fetch(coming)
    fetch_wo(me_ref[0], buffers, w, spots, sems)
    spread_ids(query_ids, key_ids)

    def one_block(b, loaded):
        start = pl.multiple_of(windows[0, b], SUB)
        needed = jnp.maximum(windows[2, b], loaded)

        def arrived(i, carry):
            chunk(i).wait()
            return carry

        lax.fori_loop(loaded, needed, arrived, 0)
        for index, width in enumerate(CLASSES):

            @pl.when(windows[1, b] == index)
            def _(width=width):
                mask_bias(start, width, b, key_ids, query_ids, bias)
                attend_block(b, start, width, triple, mix, stats, bias, scores)

        return needed

    loaded = lax.fori_loop(0, blocks, one_block, jnp.int32(0))

    def arrived(i, carry):
        chunk(i).wait()
        return carry

    lax.fori_loop(loaded, blocks, arrived, 0)
    going = [pltpu.make_async_copy(mix, mixed, own.at[2])]
    going[0].start()
    wait_wo(buffers, w, sems)
    settle(coming)
    bo, s1 = row_of(small, BO, 6), row_of(small, S1, 6)
    gain, shift = row_of(small, G2, 6), row_of(small, C2, 6)
    s2 = row_of(small, S2, 6)
    weight = wo_matrix(w, spots)
    step = 256
    sums = jnp.zeros((8, 768), F32)
    for i in range(rows // step):
        at = slice(i * step, (i + 1) * step)
        made = mm(mix[at, :], weight, NN) + bo
        out[at, :] = made.astype(BF16)
        values = x[at, :].astype(F32) + s1 * made
        mid[at, :] = values
        normal, _ = normalized(values)
        unit[at, :] = (normal * gain + shift).astype(BF16)
        rounded = (g[at, :].astype(F32) * s2).astype(BF16)
        scaled[at, :] = rounded
        sums = sums + fold8(rounded.astype(F32))
        for k, (source, target) in enumerate(
            ((out, branch), (mid, x1), (unit, n2), (scaled, dm))
        ):
            sem = own.at[3 + 4 * i + k]
            going.append(pltpu.make_async_copy(source.at[at, :], target.at[at, :], sem))
            going[-1].start()
    put_row(gb2, 0, total(sums))
    settle(going)


def attend(me, windows, qkv, tokens, cot, query_ids, small, att):
    rows, width = tokens.shape
    row = lambda kind: pltpu.VMEM((rows, width), kind)
    return pl.pallas_call(
        attend_kernel,
        out_shape=(
            shape((rows, width), BF16),
            shape((rows, width), F32),
            shape((rows, width), BF16),
            shape((rows, width), BF16),
            shape((rows, width), BF16),
            shape((rows // QB * PAIRS, 2, 2 * QB), F32),
            shape((6, LANES), F32),
        ),
        in_specs=[smem(), smem(), hbm(), hbm(), hbm(), vmem(), vmem()] + [hbm()] * 8,
        out_specs=(hbm(),) * 5 + (vmem(), vmem()),
        scratch_shapes=[
            pltpu.VMEM((rows, QB), F32),
            pltpu.VMEM((rows, 3 * width), BF16),
            row(BF16),
            row(BF16),
            row(BF16),
            row(F32),
            row(BF16),
            row(BF16),
            row(BF16),
            pltpu.VMEM((CLASSES[-1], QB), F32),
            pltpu.VMEM((PAIRS, CLASSES[-1], 2 * QB), F32),
            wo_scratch(),
            spots_scratch(),
            dma(3),
            dma(3 + 4 * rows // 256),
            dma(rows // QB),
        ],
        compiler_params=pltpu.CompilerParams(vmem_limit_bytes=GRANT),
        cost_estimate=cost(2 * rows * rows * width, 20 * rows * width, 4 * rows * rows),
        name="attend_forward",
    )(me, windows, qkv, tokens, cot, query_ids, small, *att)


def lay_matrix(w, spots, name, blocks, first, rt_count, columns, out):
    def one_block(d, carry):
        places = [spots[h, first + d] for h in range(2)]
        base = pl.multiple_of(d * rt_count * SUB, SUB)
        for rt in range(rt_count):
            for column, ct in enumerate(columns):
                h, index = half_place(name, rt, ct)
                at = pl.ds(pl.multiple_of(base + rt * SUB, SUB), SUB)
                out[at, LANES * column : LANES * (column + 1)] = w[h, places[h], index]
        return carry

    lax.fori_loop(0, blocks, one_block, 0)


def lay_w1(w, spots, out):
    lay_matrix(w, spots, "w1", W1_BLOCKS, 0, W1_RT, range(W1_CT), out)


def lay_w2(w, spots, out):
    lay_matrix(w, spots, "w2", W2_BLOCKS, W1_BLOCKS, W2_RT, range(W2_CT), out)


def w2_place(spots, f, row, ct):
    rt = row % W2_RT
    h = rt // 6
    return h, spots[h, W1_BLOCKS + 4 * f + row // W2_RT], rt % 6 * W2_CT + ct


TALL = 256
PARTS = CHUNK // 256


def device_of(x, c, z, y):
    return x * 16 + c * 8 + z * 2 + y


W1_RUNS = [
    [(0, device_of(0, c, 0, y), 4) for c in range(2) for y in range(2)],
    [(1, device_of(0, c, 0, 0), 8) for c in range(2)],
]
W2_RUNS = [
    [(h, device_of(1, f >> 1, 2 * (f & 1), y), 2) for h in range(2) for y in range(2)]
    for f in range(CHUNKS)
]
RUN_ORDER = W1_RUNS[0] + W2_RUNS[0] + W2_RUNS[1] + W1_RUNS[1] + W2_RUNS[2] + W2_RUNS[3]


class Runs:
    def __init__(self, buffers, w, spots, sems, out=False):
        self.buffers, self.w, self.spots, self.sems, self.out = buffers, w, spots, sems, out
        self.each = len(buffers) // 2

    def copy(self, run, which, index, place):
        h, first, size = run
        outer = self.buffers[self.each * h + which].at[pl.ds(index, size)]
        inner = self.w.at[h, pl.ds(place, size)]
        sem = self.sems.at[RUN_ORDER.index(run)]
        ends = (inner, outer) if self.out else (outer, inner)
        return pltpu.make_async_copy(*ends, sem)

    def start(self, runs):
        length = BLOCKS // self.each
        for run in runs:
            h, first, size = run
            place = self.spots[h, first] & (BLOCKS - size)
            for which in range(self.each):

                @pl.when(place // length == which)
                def _(run=run, which=which, place=place):
                    self.copy(run, which, place & (length - 1), place).start()

    def wait(self, runs):
        for run in runs:
            self.copy(run, 0, 0, 0).wait()


def mlp_kernel(me_ref, n2_in, dm_in, small, *refs):
    arriving, refs = refs[:8], refs[8:]
    u_out, dz_out, vectors, *leaving = refs[:7]
    w, first, second, spots, n2, dm, u, dz, zs, dus, bias_sums, b1_lines, sems, own = refs[7:]
    rows, width = n2.shape
    tiles = rows // TALL
    coming = [
        pltpu.make_async_copy(n2_in, n2, own.at[0]),
        pltpu.make_async_copy(dm_in, dm, own.at[1]),
    ]
    fetch(coming)
    fill_spots(me_ref[0], spots)
    incoming = Runs(arriving, w, spots, sems)
    incoming.start(RUN_ORDER)
    bias_sums[...] = jnp.zeros_like(bias_sums)
    for f in range(CHUNKS):
        b1_lines[f : f + 1, :] = row_of(small, B1 + 6 * f, 6)
    def lay_chunk(f, side):
        h, base = f >> 1, MLP_HALF // 2 * (f & 1)
        for d in range(W1_BLOCKS):
            place = spots[h, d]
            for rt in range(W1_RT):
                at = slice((d * W1_RT + rt) * SUB, (d * W1_RT + rt + 1) * SUB)
                for ct in range(6):
                    lanes = slice(LANES * ct, LANES * ct + LANES)
                    first[side, at, lanes] = w[h, place, base + ct * W1_RT + rt]
        for k in range(4):
            places = [spots[i, W1_BLOCKS + 4 * f + k] for i in range(2)]
            for rt in range(W2_RT):
                at = slice((k * W2_RT + rt) * SUB, (k * W2_RT + rt + 1) * SUB)
                for ct in range(W2_CT):
                    lanes = slice(LANES * ct, LANES * ct + LANES)
                    i, index = half_place("w2", rt, ct)
                    second[side, at, lanes] = w[i, places[i], index]

    incoming.wait(W1_RUNS[0] + W2_RUNS[0])
    lay_chunk(jnp.int32(0), jnp.int32(0))
    settle(coming)

    units = [(t, c) for c in range(PARTS) for t in range(tiles)]

    def lanes_of(f, c):
        return pl.ds(pl.multiple_of(CHUNK * f + 256 * c, 256), 256)

    def outward(f):
        chunk = pl.ds(pl.multiple_of(CHUNK * f, CHUNK), CHUNK)
        return [
            pltpu.make_async_copy(u.at[:, chunk], u_out.at[:, chunk], own.at[2 * f]),
            pltpu.make_async_copy(dz.at[:, chunk], dz_out.at[:, chunk], own.at[2 * f + 1]),
        ]

    def one_chunk(f, carry):
        for index in range(CHUNKS - 1):

            @pl.when(f == index)
            def _(index=index):
                incoming.wait(W2_RUNS[index + 1] + (W1_RUNS[1] if index == 1 else []))

        side = f & 1
        lay_chunk(jnp.minimum(f + 1, CHUNKS - 1), 1 - side)

        def multiply(unit, slot):
            t, c = unit
            at = slice(TALL * t, TALL * t + TALL)
            zs[slot] = mm(n2[at, :], first[side, :, 256 * c : 256 * c + 256], NN)
            dus[slot] = mm(dm[at, :], second[side, 256 * c : 256 * c + 256, :], NT)

        def activate(unit, slot):
            t, c = unit
            lanes = slice(256 * c, 256 * c + 256)
            bias = b1_lines[pl.ds(f, 1), lanes]
            folded = jnp.zeros((8, 256), F32)
            for r in range(TALL // 32):
                part = slice(32 * r, 32 * r + 32)
                place = slice(TALL * t + 32 * r, TALL * t + 32 * r + 32)
                value, slope = gelu_pair(zs[slot, part, :] + bias)
                u[place, lanes_of(f, c)] = value.astype(BF16)
                rounded = (dus[slot, part, :] * slope).astype(BF16)
                dz[place, lanes_of(f, c)] = rounded
                folded = folded + fold8(rounded.astype(F32))
            bias_sums[:, lanes_of(f, c)] += folded

        multiply(units[0], 0)
        for i, unit in enumerate(units):
            if i + 1 < len(units):
                multiply(units[i + 1], (i + 1) % 2)
            activate(unit, i % 2)
        fetch(outward(f))
        return carry

    lax.fori_loop(0, CHUNKS, one_chunk, 0)
    put_row(vectors, 0, total(bias_sums[...]))

    outgoing = Runs(leaving, w, spots, sems, out=True)

    def one_grad(f, carry):
        h, base = f >> 1, MLP_HALF // 2 * (f & 1)
        chunk = pl.ds(pl.multiple_of(CHUNK * f, CHUNK), CHUNK)
        for c in range(PARTS):
            lanes = slice(256 * c, 256 * c + 256)
            grad = mm(n2[:, lanes], dz[:, chunk], TN)
            for r in range(SUB):
                d, rt = (SUB * c + r) // W1_RT, (SUB * c + r) % W1_RT
                for ct in range(6):
                    tile = grad[SUB * r : SUB * r + SUB, LANES * ct : LANES * ct + LANES]
                    w[h, spots[h, d], base + ct * W1_RT + rt] = tile.astype(BF16)
        for side in range(2):

            @pl.when(f == 2 * side + 1)
            def _(side=side):
                outgoing.start(W1_RUNS[side])

        for c in range(PARTS):
            grad = mm(u[:, lanes_of(f, c)], dm[...], TN)
            for r in range(SUB):
                for ct in range(W2_CT):
                    tile = grad[SUB * r : SUB * r + SUB, LANES * ct : LANES * ct + LANES]
                    w[w2_place(spots, f, SUB * c + r, ct)] = tile.astype(BF16)
        for index in range(CHUNKS):

            @pl.when(f == index)
            def _(index=index):
                outgoing.start(W2_RUNS[index])

        return carry

    lax.fori_loop(0, CHUNKS, one_grad, 0)
    for f in range(CHUNKS):
        settle(outward(f))
    outgoing.wait(RUN_ORDER)


def feed_forward(me, n2, dm, small, mlp):
    rows, width = n2.shape
    half = shape((HALF_BLOCKS, MLP_HALF, SUB, LANES), BF16)
    return pl.pallas_call(
        mlp_kernel,
        out_shape=(
            shape((rows, FF), BF16),
            shape((rows, FF), BF16),
            shape((24, LANES), F32),
            half,
            half,
            half,
            half,
        ),
        in_specs=[smem(), hbm(), hbm(), vmem()] + [hbm()] * 8,
        out_specs=(hbm(), hbm(), vmem()) + (hbm(),) * 4,
        scratch_shapes=[
            slots_scratch(MLP_HALF),
            pltpu.VMEM((2, width, CHUNK), BF16),
            pltpu.VMEM((2, CHUNK, width), BF16),
            spots_scratch(),
            pltpu.VMEM((rows, width), BF16),
            pltpu.VMEM((rows, width), BF16),
            pltpu.VMEM((rows, FF), BF16),
            pltpu.VMEM((rows, FF), BF16),
            pltpu.VMEM((2, TALL, 256), F32),
            pltpu.VMEM((2, TALL, 256), F32),
            pltpu.VMEM((8, FF), F32),
            pltpu.VMEM((CHUNKS, CHUNK), F32),
            dma(len(RUN_ORDER)),
            dma(2 * CHUNKS),
        ],
        compiler_params=pltpu.CompilerParams(vmem_limit_bytes=42 * MEGA),
        cost_estimate=cost(8 * rows * width * FF, 40 * MEGA),
        name="feed_forward",
    )(me, n2, dm, small, *mlp)


def matrix_copies(buffers, w, sems, x):
    copies = []
    for i in range(4):
        source = buffers[i].at[pl.ds(4 * x, 4)]
        copies.append(pltpu.make_async_copy(source, w.at[0, pl.ds(4 * i, 4)], sems.at[i]))
    for c in range(2):
        source = buffers[4 + 2 * c + x]
        copies.append(pltpu.make_async_copy(source, w.at[1, pl.ds(8 * c, 8)], sems.at[4 + c]))
    return copies


def fetch_matrix(me, buffers, w, spots, sems, first):
    def place(d):
        return ((d >> 3) & 1) * 8 + (d & 1) * 4 + ((d >> 1) & 3)

    for x in range(2):

        @pl.when((me >> 4) == (x ^ (first >> 4)))
        def _(x=x):
            fetch(matrix_copies(buffers, w, sems, x))

    mine = place(me)
    for d in range(W1_BLOCKS):
        for h in range(2):
            spots[h, first + d] = jnp.bitwise_xor(mine, place(d))


def wait_matrix(buffers, w, sems):
    settle(matrix_copies(buffers, w, sems, 0))


def matrix_scratch():
    return pltpu.VMEM((2, W1_BLOCKS, MLP_HALF, SUB, LANES), BF16)


def mlp_out_kernel(me_ref, u_in, x1_in, cot_in, small, *refs):
    arriving, refs = refs[:8], refs[8:]
    out, vectors, w, second, spots, u, x1, cot, macc, done, sums, sems, own = refs
    rows, width = x1.shape
    tiles = rows // TALL

    def tile_copy(source, target, t, k):
        at = pl.ds(pl.multiple_of(TALL * t, TALL), TALL)
        return pltpu.make_async_copy(source.at[at, :], target.at[at, :], own.at[k, t])

    fetch_matrix(me_ref[0], arriving, w, spots, sems, W1_BLOCKS)
    for t in range(tiles):
        tile_copy(u_in, u, t, 0).start()
    for t in range(tiles):
        tile_copy(x1_in, x1, t, 1).start()
        tile_copy(cot_in, cot, t, 2).start()
    bias, scale = row_of(small, B2, 6), row_of(small, S2, 6)
    sums[...] = jnp.zeros_like(sums)
    wait_matrix(arriving, w, sems)
    lay_w2(w, spots, second)

    def contract(t):
        at = pl.ds(pl.multiple_of(TALL * t, TALL), TALL)
        tile_copy(u_in, u, t, 0).wait()
        macc[at, :] = mm(u[at, :], second[...], NN)

    def finish(t):
        tile_copy(x1_in, x1, t, 1).wait()
        tile_copy(cot_in, cot, t, 2).wait()
        for part in range(TALL // 64):
            at = pl.ds(pl.multiple_of(TALL * t + 64 * part, 64), 64)
            contracted = macc[at, :] + bias
            done[at, :] = (x1[at, :] + scale * contracted).astype(BF16)
            sums[...] += fold8(cot[at, :].astype(F32) * contracted)
        tile_copy(done, out, t, 3).start()

    def one_tile(t, carry):
        contract(t)
        finish(t - 1)
        return carry

    contract(0)
    lax.fori_loop(1, tiles, one_tile, 0)
    finish(tiles - 1)
    put_row(vectors, 0, total(sums[...]))
    for t in range(tiles):
        tile_copy(done, out, t, 3).wait()


def feed_forward_out(me, u, x1, cot, small, mlp):
    rows, width = x1.shape
    row = lambda kind: pltpu.VMEM((rows, width), kind)
    return pl.pallas_call(
        mlp_out_kernel,
        out_shape=(shape((rows, width), BF16), shape((6, LANES), F32)),
        in_specs=[smem()] + [hbm()] * 3 + [vmem()] + [hbm()] * 8,
        out_specs=(hbm(), vmem()),
        scratch_shapes=[
            matrix_scratch(),
            pltpu.VMEM((FF, width), BF16),
            spots_scratch(),
            pltpu.VMEM((rows, FF), BF16),
            row(F32),
            row(BF16),
            row(F32),
            row(BF16),
            pltpu.VMEM((8, width), F32),
            dma(6),
            pltpu.SemaphoreType.DMA((4, rows // TALL)),
        ],
        compiler_params=pltpu.CompilerParams(vmem_limit_bytes=32 * MEGA),
        cost_estimate=cost(2 * rows * width * FF, 20 * MEGA),
        name="feed_forward_out",
    )(me, u, x1, cot, small, *mlp)


def split_kernel(me_ref, dz_in, x1_in, cot_in, branch_in, mixed_in, small, *refs):
    buffers, att_buffers, refs = refs[:8], refs[8:16], refs[16:]
    dx1_out, da_out, gwo0, gwo1, vectors = refs[:5]
    w, first, spots, wo, wo_spots, dz, x1, cot, dnacc, dx1, branch, mixed, db, da = refs[5:19]
    parts, sums, sems, wo_sems, own = refs[19:]
    me = me_ref[0]
    rows, width = x1.shape
    tiles = rows // TALL

    def tile_copy(source, target, t, k):
        at = pl.ds(pl.multiple_of(TALL * t, TALL), TALL)
        return pltpu.make_async_copy(source.at[at, :], target.at[at, :], own.at[k, t])

    fetch_matrix(me, buffers, w, spots, sems, 0)
    for t in range(tiles):
        tile_copy(dz_in, dz, t, 0).start()
    for t in range(tiles):
        tile_copy(x1_in, x1, t, 1).start()
        tile_copy(cot_in, cot, t, 2).start()
        tile_copy(branch_in, branch, t, 3).start()
    fetch_wo(me, att_buffers, wo, wo_spots, wo_sems)
    late = pltpu.make_async_copy(mixed_in, mixed, own.at[4, 0])
    late.start()
    gain, scale = row_of(small, G2, 6), row_of(small, S1, 6)
    sums[...] = jnp.zeros_like(sums)
    wait_matrix(buffers, w, sems)
    lay_w1(w, spots, first)

    def contract(t):
        at = pl.ds(pl.multiple_of(TALL * t, TALL), TALL)
        tile_copy(dz_in, dz, t, 0).wait()
        dnacc[at, :] = mm(dz[at, :], first[...], NT)

    def finish(t):
        tile_copy(x1_in, x1, t, 1).wait()
        tile_copy(cot_in, cot, t, 2).wait()
        tile_copy(branch_in, branch, t, 3).wait()
        for half in range(2):
            at = pl.ds(pl.multiple_of(TALL * t + TALL // 2 * half, TALL // 2), TALL // 2)
            unit, inverse = normalized(x1[at, :])
            grad = dnacc[at, :]
            middle = cot[at, :].astype(F32) + norm_pullback(unit, inverse, grad, gain)
            dx1[at, :] = middle
            rounded = (middle * scale).astype(BF16)
            db[at, :] = rounded
            sums[0:8, :] += fold8(grad * unit)
            sums[8:16, :] += fold8(grad)
            sums[16:24, :] += fold8(rounded.astype(F32))
            sums[24:32, :] += fold8(middle * branch[at, :].astype(F32))
        tile_copy(dx1, dx1_out, t, 1).start()

    def one_tile(t, carry):
        contract(t)
        finish(t - 1)
        return carry

    contract(0)
    lax.fori_loop(1, tiles, one_tile, 0)
    finish(tiles - 1)
    for k in range(4):
        put_row(vectors, 6 * k, total(sums[8 * k : 8 * k + 8, :]))
    wait_wo(att_buffers, wo, wo_sems)
    weight = wo_matrix(wo, wo_spots)
    going = []
    for c in range(3):
        lanes = slice(256 * c, 256 * c + 256)
        da[:, lanes] = mm(db[...], weight[lanes, :], NT).astype(BF16)
        going.append(pltpu.make_async_copy(da.at[:, lanes], da_out.at[:, lanes], own.at[0, c]))
        going[-1].start()
    late.wait()
    for c in range(3):
        grad = mm(mixed[:, 256 * c : 256 * c + 256], db[...], TN)
        for r in range(SUB):
            i, rt = (SUB * c + r) // WO_RT, (SUB * c + r) % WO_RT
            for ct in range(WO_CT):
                tile = grad[SUB * r : SUB * r + SUB, LANES * ct : LANES * ct + LANES]
                g, half, index = part_place("wo", rt, ct)
                parts[g, half, i, index] = tile.astype(BF16)
    for g, target in enumerate((gwo0, gwo1)):
        going.append(pltpu.make_async_copy(parts.at[g], target, own.at[4, g]))
        going[-1].start()
    settle(going)
    for t in range(tiles):
        tile_copy(dx1, dx1_out, t, 1).wait()


def split(me, dz, x1, cot, branch, mixed, small, mlp, att):
    rows, width = x1.shape
    part = (2, WO_BLOCKS, ATT_PART, SUB, LANES)
    row = lambda kind: pltpu.VMEM((rows, width), kind)
    return pl.pallas_call(
        split_kernel,
        out_shape=(
            shape((rows, width), F32),
            shape((rows, width), BF16),
            shape(part, BF16),
            shape(part, BF16),
            shape((24, LANES), F32),
        ),
        in_specs=[smem()] + [hbm()] * 5 + [vmem()] + [hbm()] * 16,
        out_specs=(hbm(),) * 4 + (vmem(),),
        scratch_shapes=[
            matrix_scratch(),
            pltpu.VMEM((width, FF), BF16),
            spots_scratch(),
            wo_scratch(),
            spots_scratch(),
            pltpu.VMEM((rows, FF), BF16),
            row(F32),
            row(BF16),
            row(F32),
            row(F32),
            row(BF16),
            row(BF16),
            row(BF16),
            row(BF16),
            pltpu.VMEM((2,) + part, BF16),
            pltpu.VMEM((32, width), F32),
            dma(6),
            dma(3),
            pltpu.SemaphoreType.DMA((5, rows // TALL)),
        ],
        compiler_params=pltpu.CompilerParams(vmem_limit_bytes=44 * MEGA),
        cost_estimate=cost(2 * rows * width * FF + 4 * rows * width * width, 40 * MEGA),
        name="feed_forward_in",
    )(me, dz, x1, cot, branch, mixed, small, *mlp, *att)


GROUP = PAIRS // 2
GROUP_LANES = GROUP * LANES


def attend_back_block(b, start, width, group, refs):
    q, k, v, da, stats, dq, dkeys, dvalues, bias = refs
    rows = pl.ds(pl.multiple_of(b * QB, QB), QB)
    at = pl.ds(start, width)
    mask = jnp.concatenate([bias[0:width, :]] * 2, axis=1)
    for p in range(GROUP):
        lanes = slice(LANES * p, LANES * p + LANES)
        place = b * PAIRS + GROUP * group + p
        queries = head_masked(q[rows, lanes] * 0.125)
        grads = head_masked(da[rows, lanes])
        highest = stats[place, 0:1, :]
        inverse = stats[place, 1:2, :]
        keys, values = k[at, lanes], v[at, lanes]
        weight = jnp.exp(mm(keys, queries, NT) + mask - highest) * inverse
        dweight = mm(values, grads, NT)
        inner_sum = total(fold8(weight * dweight))
        dvalues[at, lanes] += mm(weight.astype(BF16), grads, NN)
        dscore = (weight * (dweight - inner_sum)).astype(BF16)
        dkeys[at, lanes] += mm(dscore, queries, NN)
        both = mm(keys, dscore, TN)
        dq[rows, lanes] = (pick_heads(both) * 0.125).T.astype(BF16)


def attend_back_kernel(group, windows, qkv, da_in, stats, query_ids, dqkv, *refs):
    q, k, v, da, out, dkeys, dvalues, bias, key_ids, own = refs
    rows = q.shape[0]
    blocks = rows // QB
    lanes = slice(GROUP_LANES * group, GROUP_LANES * group + GROUP_LANES)
    coming = [pltpu.make_async_copy(da_in.at[:, lanes], da, own.at[3])]
    for third, target in enumerate((q, k, v)):
        first = LANES * PAIRS * third + GROUP_LANES * group
        source = qkv.at[:, first : first + GROUP_LANES]
        coming.append(pltpu.make_async_copy(source, target, own.at[third]))
    fetch(coming)
    dkeys[...] = jnp.zeros_like(dkeys)
    dvalues[...] = jnp.zeros_like(dvalues)
    spread_ids(query_ids, key_ids)
    settle(coming)
    dq = out.at[:, 0:GROUP_LANES]

    def one_block(b, carry):
        start = pl.multiple_of(windows[0, b], SUB)
        for index, width in enumerate(CLASSES):

            @pl.when(windows[1, b] == index)
            def _(width=width):
                mask_bias(start, width, b, key_ids, query_ids, bias)
                parts = (q, k, v, da, stats, dq, dkeys, dvalues, bias)
                attend_back_block(b, start, width, group, parts)

        return carry

    lax.fori_loop(0, blocks, one_block, 0)
    going = []
    for i in range(rows // 256):
        at = slice(256 * i, 256 * i + 256)
        out[at, GROUP_LANES : 2 * GROUP_LANES] = dkeys[at, :].astype(BF16)
        out[at, 2 * GROUP_LANES :] = dvalues[at, :].astype(BF16)
        going.append(pltpu.make_async_copy(out.at[at, :], dqkv.at[at, :], own.at[i]))
        going[-1].start()
    settle(going)


def attend_back(group, windows, qkv, da, stats, query_ids):
    rows = qkv.shape[0]
    part = lambda kind: pltpu.VMEM((rows, GROUP_LANES), kind)
    return pl.pallas_call(
        partial(attend_back_kernel, group),
        out_shape=shape((rows, 3 * GROUP_LANES), BF16),
        in_specs=[smem(), hbm(), hbm(), vmem(), vmem()],
        out_specs=hbm(),
        scratch_shapes=[
            part(BF16),
            part(BF16),
            part(BF16),
            part(BF16),
            pltpu.VMEM((rows, 3 * GROUP_LANES), BF16),
            part(F32),
            part(F32),
            pltpu.VMEM((CLASSES[-1], QB), F32),
            pltpu.VMEM((rows, QB), F32),
            dma(4),
        ],
        compiler_params=pltpu.CompilerParams(vmem_limit_bytes=32 * MEGA),
        cost_estimate=cost(3 * rows * rows * rows, 14 * rows * rows, 4 * rows * rows),
        name="attend_backward",
    )(windows, qkv, da, stats, query_ids)


def put_qkv_grad(n1, dqkv, w, spots):
    for c in range(3):
        grad = mm(n1[:, 256 * c : 256 * c + 256], dqkv[...], TN)
        for r in range(SUB):
            d, rt = (SUB * c + r) // QKV_RT, (SUB * c + r) % QKV_RT
            place = spots[rt, d]
            for index in range(ATT_PART):
                tile = grad[SUB * r : SUB * r + SUB, LANES * index : LANES * index + LANES]
                w[rt, place, index] = tile.astype(BF16)


def put_wo_grad(gwo, w, spots):
    for h in range(2):
        for i in range(WO_BLOCKS):
            w[h, spots[h, QKV_BLOCKS + i], 0:ATT_PART] = gwo[h, i]


def weight_grad_kernel(me_ref, n1_in, dqkv_in, gwo_in, *refs):
    leaving, (w, spots, n1, dqkv, gwo, sems, own) = refs[:4], refs[4:]
    coming = [
        pltpu.make_async_copy(n1_in, n1, own.at[0]),
        pltpu.make_async_copy(dqkv_in, dqkv, own.at[1]),
        pltpu.make_async_copy(gwo_in, gwo, own.at[2]),
    ]
    fetch(coming)
    fill_spots(me_ref[0], spots)
    settle(coming)
    put_wo_grad(gwo, w, spots)
    put_qkv_grad(n1, dqkv, w, spots)
    copies = leaving_slots(leaving, w, sems)
    fetch(copies)
    settle(copies)


def weight_grad(me, n1, dqkv, gwo):
    rows, width = n1.shape
    half = shape((HALF_BLOCKS, ATT_PART, SUB, LANES), BF16)
    return pl.pallas_call(
        weight_grad_kernel,
        out_shape=(half,) * 4,
        in_specs=[smem()] + [hbm()] * 3,
        out_specs=(hbm(),) * 4,
        scratch_shapes=[
            slots_scratch(ATT_PART),
            spots_scratch(),
            pltpu.VMEM((rows, width), BF16),
            pltpu.VMEM(dqkv.shape, BF16),
            pltpu.VMEM(gwo.shape, BF16),
            dma(4),
            dma(3),
        ],
        compiler_params=pltpu.CompilerParams(vmem_limit_bytes=20 * MEGA),
        cost_estimate=cost(3 * rows * width * width, 10 * rows * width),
        name="qkv_weight_grad",
    )(me, n1, dqkv, gwo)


def qkv_back_kernel(
    me_ref, tokens_in, n1_in, dx1_in, dqkv0_in, dqkv1_in, small, proj, mlp, gwo_in, *refs
):
    arriving, refs = refs[:8], refs[8:]
    dx_out, *leaving = refs[:5]
    w, gw, weight, spots, gwo, tokens, n1, dx1, dqkv0, dqkv1, dn, dx, sums, table = refs[5:19]
    sems, out_sems, own = refs[19:]
    rows = tokens.shape[0]
    tiles = rows // TALL

    def tile_copy(source, target, t, k):
        at = pl.ds(pl.multiple_of(TALL * t, TALL), TALL)
        return pltpu.make_async_copy(source.at[at, :], target.at[at, :], own.at[k, t])

    for t in range(tiles):
        tile_copy(dqkv0_in, dqkv0, t, 0).start()
        tile_copy(dqkv1_in, dqkv1, t, 1).start()
    weights = arriving_slots(arriving, w, sems)
    fetch(weights)
    for t in range(tiles):
        tile_copy(tokens_in, tokens, t, 2).start()
        tile_copy(dx1_in, dx1, t, 3).start()
    late = [
        pltpu.make_async_copy(n1_in, n1, own.at[4, 0]),
        pltpu.make_async_copy(gwo_in, gwo, own.at[4, 1]),
    ]
    fetch(late)
    sums[...] = jnp.zeros_like(sums)
    gain = row_of(small, G1, 6)
    fill_spots(me_ref[0], spots)
    settle(weights)
    columns = qkv_group(0) + qkv_group(1)
    lay_matrix(w, spots, "qkv", QKV_BLOCKS, 0, QKV_RT, columns, weight)

    def contract(t):
        at = pl.ds(pl.multiple_of(TALL * t, TALL), TALL)
        for g, (source, part) in enumerate(((dqkv0_in, dqkv0), (dqkv1_in, dqkv1))):
            tile_copy(source, part, t, g).wait()
            lanes = slice(384 * g, 384 * g + 384)
            sums[16:24, lanes] += fold8(part[at, 0:384].astype(F32))
            sums[24:32, lanes] += fold8(part[at, 768:1152].astype(F32))
        both = jnp.concatenate([dqkv0[at, :], dqkv1[at, :]], axis=1)
        dn[at, :] = mm(both, weight[...], NT)

    def finish(t):
        tile_copy(tokens_in, tokens, t, 2).wait()
        tile_copy(dx1_in, dx1, t, 3).wait()
        for half in range(2):
            at = pl.ds(pl.multiple_of(TALL * t + TALL // 2 * half, TALL // 2), TALL // 2)
            unit, inverse = normalized(tokens[at, :].astype(F32))
            grad = dn[at, :]
            dx[at, :] = dx1[at, :] + norm_pullback(unit, inverse, grad, gain)
            sums[0:8, :] += fold8(grad * unit)
            sums[8:16, :] += fold8(grad)
        tile_copy(dx, dx_out, t, 3).start()

    def one_tile(t, carry):
        contract(t)
        finish(t - 1)
        return carry

    contract(0)
    lax.fori_loop(1, tiles, one_tile, 0)
    finish(tiles - 1)

    def put_table(owner, *places):
        table[...] = jnp.zeros_like(table)
        for place, values in places:
            if values.shape[1] == LANES:
                table[place : place + values.shape[0], :] = values
            else:
                put_row(table, place, values)
        for h in range(2):
            gw[h, spots[h, owner], ATT_PART] = table[SUB * h : SUB * h + SUB, :].astype(BF16)

    put_table(
        OWNERS[0], (0, total(sums[0:8, :])), (6, total(sums[8:16, :])), (12, mlp[0:12, :])
    )
    put_table(OWNERS[1], (0, mlp[12:36, :]))
    put_table(OWNERS[2], (0, total(sums[16:24, :])), (6, total(sums[24:32, :])))
    put_table(OWNERS[3], (0, proj[...]), (12, mlp[36:48, :]))
    settle(late)
    put_wo_grad(gwo, gw, spots)
    put_qkv_grad(n1, dqkv1, gw, spots)
    copies = leaving_slots(leaving, gw, out_sems)
    fetch(copies)
    for t in range(tiles):
        tile_copy(dx, dx_out, t, 3).wait()
    settle(copies)


def qkv_back(me, tokens, n1, dx1, dqkv0, dqkv1, small, proj, mlp, gwo, att):
    rows, width = tokens.shape
    tiles = ATT_PART + 1
    half = shape((HALF_BLOCKS, tiles, SUB, LANES), BF16)
    row = lambda kind: pltpu.VMEM((rows, width), kind)
    return pl.pallas_call(
        qkv_back_kernel,
        out_shape=(shape((rows, width), F32), half, half, half, half),
        in_specs=[smem()] + [hbm()] * 5 + [vmem()] * 3 + [hbm()] * 9,
        out_specs=(hbm(),) * 5,
        scratch_shapes=[
            slots_scratch(ATT_SENT),
            slots_scratch(tiles),
            pltpu.VMEM((width, 3 * width), BF16),
            spots_scratch(),
            pltpu.VMEM(gwo.shape, BF16),
            row(BF16),
            row(BF16),
            row(F32),
            pltpu.VMEM(dqkv0.shape, BF16),
            pltpu.VMEM(dqkv1.shape, BF16),
            row(F32),
            row(F32),
            pltpu.VMEM((32, width), F32),
            pltpu.VMEM((2 * SUB, LANES), F32),
            dma(8),
            dma(4),
            pltpu.SemaphoreType.DMA((5, rows // TALL)),
        ],
        compiler_params=pltpu.CompilerParams(vmem_limit_bytes=46 * MEGA),
        cost_estimate=cost(9 * rows * width * width, 30 * rows * width),
        name="qkv_backward",
    )(me, tokens, n1, dx1, dqkv0, dqkv1, small, proj, mlp, gwo, *att)


X, C, Z1, Z0, Y = 16, 8, 4, 2, 1


def exchange(values, bit):
    return lax.ppermute(values, AXES, [(d, d ^ bit) for d in range(BLOCKS)])


def shifted(values, by):
    pairs = [(d, d + by) for d in range(BLOCKS) if 0 <= d + by < BLOCKS]
    return lax.ppermute(values, AXES, pairs)


def together(*values):
    return lax.optimization_barrier(values)


def along_z(first, second, received):
    return (
        jnp.stack([first] + [r[0] for r in received]),
        jnp.stack([second] + [r[1] for r in received]),
    )


def joined(own, received):
    return jnp.concatenate([own, received])


def sum_terms(terms):
    summed = terms[0].astype(F32)
    for term in terms[1:]:
        summed = summed + term.astype(F32)
    return summed


def kept(terms):
    return [t[: t.shape[0] // 2] for t in terms]


def z_part(first, second, k):
    return jnp.stack([sum_terms([t[k] for t in terms]) for terms in (first, second)])


def sent(terms):
    return sum_terms([t[t.shape[0] // 2 :] for t in terms]).astype(BF16)


def attention_amounts(width):
    return [width, width, 3 * width * width, width, width, width * width, width, width]


def feedforward_amounts(width):
    return [width, width, width * FF, FF, FF * width, width, width]


def pieces_of(vector, amounts):
    out, offset = [], 0
    for amount in amounts:
        out.append(vector[offset : offset + amount])
        offset += amount
    return out


def tiles_by_column(matrix, blocks, rt):
    ct = matrix.shape[1] // LANES
    return matrix.reshape(blocks, rt, SUB, ct, LANES).transpose(0, 3, 1, 2, 4)


def tiles_by_row(matrix, blocks, rt):
    ct = matrix.shape[1] // LANES
    return matrix.reshape(blocks, rt, SUB, ct, LANES).transpose(0, 1, 3, 2, 4)


def gather_plainly(params, att_rows, width):
    rounded = params.astype(BF16)
    att = lax.all_gather(rounded[:att_rows], AXES, axis=0, tiled=True).reshape(-1)
    mlp = lax.all_gather(rounded[att_rows:], AXES, axis=0, tiled=True).reshape(-1)
    g1, c1, wqkv, bq, bv, wo, bo, s1 = pieces_of(att, attention_amounts(width))
    g2, c2, w1, b1, w2, b2, s2 = pieces_of(mlp, feedforward_amounts(width))
    tile = (SUB, LANES)
    att = jnp.concatenate(
        [
            tiles_by_column(wqkv.reshape(width, -1), QKV_BLOCKS, QKV_RT).reshape((-1, 36) + tile),
            tiles_by_row(wo.reshape(width, -1), WO_BLOCKS, WO_RT).reshape((-1, 36) + tile),
        ]
    )
    mlp = jnp.concatenate(
        [
            tiles_by_column(w1.reshape(width, -1), W1_BLOCKS, W1_RT).reshape((-1, 72) + tile),
            tiles_by_row(w2.reshape(FF, -1), W2_BLOCKS, W2_RT).reshape((-1, 72) + tile),
        ]
    )
    vectors = jnp.concatenate([g1, c1, bq, bv, bo, s1, g2, c2, b1, b2, s2]).astype(F32)
    lines = vectors.reshape(-1, LANES)
    sent = jnp.zeros((BLOCKS, 2 * SUB, LANES), F32)
    for owner, place, first, count in (
        (OWNERS[0], 0, G1, 12),
        (OWNERS[0], 12, G2, 12),
        (OWNERS[1], 0, B1, 24),
        (OWNERS[2], 0, BQ, 12),
        (OWNERS[3], 0, BO, 12),
        (OWNERS[3], 12, B2, 12),
    ):
        sent = sent.at[owner, place : place + count].set(lines[first : first + count])
    sent = sent.astype(BF16).reshape((BLOCKS, 2, 1) + tile)
    att = [jnp.concatenate([att[:, 18 * h : 18 * h + 18], sent[:, h]], axis=1) for h in range(2)]
    return by_slot(*att), by_slot(mlp[:, :36], mlp[:, 36:])


def by_slot(first, second):
    halves = (first, second)
    return [
        jnp.stack([halves[i // 4][slot] for slot in SLOTS[i // 4][i % 4 * 8 : i % 4 * 8 + 8]])
        for i in range(8)
    ]


def from_slots(buffers):
    halves = []
    for h in range(2):
        slots = jnp.concatenate(buffers[2 * h : 2 * h + 2])
        halves.append(jnp.stack([slots[spot(h, d)] for d in range(BLOCKS)]))
    return halves


def reduce_plainly(gatt0, gatt1, gmlp, att_rows, mlp_rows, width, devices):
    groups = [from_slots(gatt0), from_slots(gatt1)]
    vectors = jnp.concatenate([groups[1][h][:, ATT_PART:] for h in range(2)], axis=1)
    vectors = vectors.astype(F32).reshape(BLOCKS, 2 * SUB, LANES)

    def matrix(name, first, last, rt_count, ct_count):
        rows = []
        for rt in range(rt_count):
            places = [part_place(name, rt, ct) for ct in range(ct_count)]
            rows.append(jnp.stack([groups[g][h][first:last, i] for g, h, i in places], axis=2))
        return jnp.stack(rows, axis=1).astype(F32).reshape(-1)

    wqkv = matrix("qkv", 0, QKV_BLOCKS, QKV_RT, QKV_CT)
    wo = matrix("wo", QKV_BLOCKS, BLOCKS, WO_RT, WO_CT)
    mlp = jnp.concatenate(from_slots(gmlp), axis=1).astype(F32)
    five = lambda v, dims: v.reshape((v.shape[0],) + dims + (SUB, LANES))
    w1 = five(mlp[:W1_BLOCKS], (W1_CT, W1_RT)).transpose(0, 2, 3, 1, 4).reshape(-1)
    w2 = five(mlp[W1_BLOCKS:], (W2_RT, W2_CT)).transpose(0, 1, 3, 2, 4).reshape(-1)
    line = lambda owner, first, count: vectors[owner, first : first + count].reshape(-1)
    att = [line(OWNERS[0], 0, 12), wqkv, line(OWNERS[2], 0, 12), wo, line(OWNERS[3], 0, 12)]
    mlp = [line(OWNERS[0], 12, 12), w1, line(OWNERS[1], 0, 24), w2, line(OWNERS[3], 12, 12)]

    def lay(parts, rows):
        vector = jnp.concatenate(parts)
        vector = jnp.pad(vector, (0, devices * rows * LANES - vector.shape[0]))
        return vector.reshape(devices, rows, LANES)

    whole = jnp.concatenate([lay(att, att_rows), lay(mlp, mlp_rows)], axis=1)
    return lax.psum_scatter(whole.reshape(-1, LANES), AXES, scatter_dimension=0, tiled=True)


def key_windows(segments, real):
    length = segments.shape[0]
    position = jnp.arange(length, dtype=jnp.int32)
    ids = jnp.where(real, segments, length + position)
    first = segments[0::QB]
    final = segments[QB - 1 :: QB]
    begin = jnp.sum((segments[None, :] < first[:, None]).astype(jnp.int32), axis=1)
    begin = jnp.where(real[0::QB], begin, position[0::QB])
    end = jnp.sum(((segments[None, :] <= final[:, None]) & real[None, :]).astype(jnp.int32), axis=1)
    end = jnp.where(real[QB - 1 :: QB], end, position[QB - 1 :: QB] + 1)
    begin = begin // SUB * SUB
    need = end - begin
    kind = sum((need > width).astype(jnp.int32) for width in CLASSES[:-1])
    widths = sum(
        jnp.where(kind == i, width, 0) for i, width in enumerate(CLASSES)
    )
    begin = jnp.minimum(begin, length - widths)
    chunks = (begin + widths + QB - 1) // QB
    return ids, jnp.stack([begin, kind, chunks]).astype(jnp.int32)


def local(tokens, cotangent, segment_ids, pad_mask, lengths, params):
    rows, width = tokens.shape
    wide, narrow = lax.axis_size("wide"), lax.axis_size("narrow")
    devices = wide * narrow
    att_count = 4 * width * width + 6 * width
    att_rows = (att_count // LANES + devices - 1) // devices
    mlp_rows = params.shape[0] - att_rows
    paired = (wide, narrow) == (4, 8)
    scale = 1.0 / math.sqrt(rows * devices)

    position = jnp.arange(rows, dtype=jnp.int32)
    real = (pad_mask > 0) & (position < lengths[0])
    ids, windows = key_windows(segment_ids, real)
    query_ids = ids.astype(F32).reshape(rows // QB, QB)

    if not paired:
        me = jnp.zeros((1,), jnp.int32)
        att, mlp = gather_plainly(params, att_rows, width)
        n1, qkv, small = project_qkv(me, tokens, att)
        mixed, x1, branch, n2, dm, stats, gb2 = attend(
            me, windows, qkv, tokens, cotangent, query_ids, small, att
        )
        u, dz, gb1, *gmlp = feed_forward(me, n2, dm, small, mlp)
        output, gs2 = feed_forward_out(me, u, x1, cotangent, small, mlp)
        dx1, da, gwo0, gwo1, others = split(
            me, dz, x1, cotangent, branch, mixed, small, mlp, att
        )
        small_mlp = jnp.concatenate([others[:12], gb1, gb2, gs2])
        small_proj = others[12:]
        dqkv0 = attend_back(0, windows, qkv, da, stats, query_ids)
        dqkv1 = attend_back(1, windows, qkv, da, stats, query_ids)
        gatt0 = weight_grad(me, n1, dqkv0, gwo0)
        grad_input, *gatt1 = qkv_back(
            me, tokens, n1, dx1, dqkv0, dqkv1, small, small_proj, small_mlp, gwo1, att
        )
        owned = reduce_plainly(gatt0, gatt1, gmlp, att_rows, mlp_rows, width, devices)
        return output, grad_input, owned * scale

    me = lax.axis_index(AXES).astype(jnp.int32).reshape(1)
    tails = jnp.concatenate([params[att_rows - ATT_BEFORE : att_rows], params[-MLP_BEFORE:]])
    heads = jnp.concatenate([params[:ATT_AFTER], params[att_rows : att_rows + MLP_AFTER]])
    tails, heads = shifted(tails, 1), shifted(heads, -1)
    att_own, mlp_own = pack(me, params, tails, heads, att_rows)

    got = [exchange(att_own, k * Z0) for k in range(1, 4)]
    a, b = along_z(att_own[0], att_own[1], got)
    a, b, mlp_own, windows, query_ids = together(a, b, mlp_own, windows, query_ids)
    ax, by = exchange(a, X), exchange(b, Y)
    z1, z3 = exchange(mlp_own, Z0), exchange(mlp_own, 3 * Z0)
    a, b = joined(a, ax), joined(b, by)
    a, b, z1, z3, mlp_own = together(a, b, z1, z3, mlp_own)
    ay, bx = exchange(a, Y), exchange(b, X)
    ac, bc = exchange(a, C), exchange(b, C)
    z2 = exchange(mlp_own, 2 * Z0)
    m, n = along_z(mlp_own[0], mlp_own[1], [z1, z2, z3])
    ay, bx, ac, bc, m, n = together(ay, bx, ac, bc, m, n)
    ayc, bxc = exchange(ay, C), exchange(bx, C)
    att = together(a, ay, ac, ayc, b, bx, bc, bxc, m, n, tokens)
    *att, m, n, tokens_now = att
    mx, ny = exchange(m, X), exchange(n, Y)
    n1, qkv, small = project_qkv(me, tokens_now, att)
    m, n = joined(m, mx), joined(n, ny)
    m, n, qkv = together(m, n, qkv)
    my, nx = exchange(m, Y), exchange(n, X)
    mc, nc = exchange(m, C), exchange(n, C)
    mixed, x1, branch, n2, dm, stats, gb2 = attend(
        me, windows, qkv, tokens, cotangent, query_ids, small, att
    )
    m, n, my, nx, mc, nc, n2 = together(m, n, my, nx, mc, nc, n2)
    myc, nxc = exchange(my, C), exchange(nx, C)
    mlp = (m, my, mc, myc, n, nx, nc, nxc)

    u, dz, gb1, *gmlp = feed_forward(me, n2, dm, small, mlp)

    mc, nc = exchange(gmlp[1], C), exchange(gmlp[3], C)
    output, gs2 = feed_forward_out(me, u, x1, cotangent, small, mlp)
    mc, nc, dz, gs2 = together(mc, nc, dz, gs2)
    m, n = [gmlp[0], mc], [gmlp[2], nc]
    my, nx, dz = together(sent(m), sent(n), dz)
    my, nx = exchange(my, Y), exchange(nx, X)
    dx1, da, gwo0, gwo1, others = split(
        me, dz, x1, cotangent, branch, mixed, small, mlp, att
    )
    dqkv0 = attend_back(0, windows, qkv, da, stats, query_ids)
    gatt0 = weight_grad(me, n1, dqkv0, gwo0)
    my, nx, da, *gatt0 = together(my, nx, da, *gatt0)
    m, n = kept(m) + [my], kept(n) + [nx]
    mx, ny, da, *gatt0 = together(sent(m), sent(n), da, *gatt0)
    mx, ny = exchange(mx, X), exchange(ny, Y)
    ac, bc = exchange(gatt0[1], C), exchange(gatt0[3], C)
    dqkv1 = attend_back(1, windows, qkv, da, stats, query_ids)
    mx, ny, ac, bc, dqkv1 = together(mx, ny, ac, bc, dqkv1)
    m, n = kept(m) + [mx], kept(n) + [ny]
    z1, z2, z3 = [z_part(m, n, k).astype(BF16) for k in range(1, 4)]
    a, b = [gatt0[0], ac], [gatt0[2], bc]
    ay, bx, z1, z2, z3, dqkv1 = together(sent(a), sent(b), z1, z2, z3, dqkv1)
    z1, z2 = exchange(z1, Z0), exchange(z2, 2 * Z0)
    ay, bx = exchange(ay, Y), exchange(bx, X)
    small_mlp = jnp.concatenate([others[:12], gb1, gb2, gs2])
    grad_input, *gatt1 = qkv_back(
        me, tokens, n1, dx1, dqkv0, dqkv1, small, others[12:], small_mlp, gwo1, att
    )
    ay, bx, z1, z2, *gatt1 = together(ay, bx, z1, z2, *gatt1)
    a, b = kept(a) + [ay], kept(b) + [bx]
    ax, by, c1, d1, z3 = together(sent(a), sent(b), gatt1[1], gatt1[3], z3)
    c1, d1 = exchange(c1, C), exchange(d1, C)
    ax, by = exchange(ax, X), exchange(by, Y)
    z3a = exchange(z3[0], 3 * Z0)
    c, d = [gatt1[0], c1], [gatt1[2], d1]
    a, b = kept(a) + [ax], kept(b) + [by]
    sends = [z_part(a, b, k).astype(BF16) for k in range(1, 4)]
    cy, dx, z3a, z3, *sends = together(sent(c), sent(d), z3a, z3, *sends)
    cy, dx = exchange(cy, Y), exchange(dx, X)
    got = [exchange(part, (k + 1) * Z0) for k, part in enumerate(sends)]
    c, d = kept(c) + [cy], kept(d) + [dx]
    cx, dy, z3, *got = together(sent(c), sent(d), z3, *got)
    z3b = exchange(z3[1], 3 * Z0)
    group0 = sum_terms([z_part(a, b, 0)] + got)
    cx, dy = exchange(cx, X), exchange(dy, Y)
    c, d = kept(c) + [cx], kept(d) + [dy]
    m_own = sum_terms([z_part(m, n, 0), z1, z2, jnp.stack([z3a, z3b])])
    sends = [z_part(c, d, k).astype(BF16) for k in range(1, 4)]
    group0, m_own, *sends = together(group0, m_own, *sends)
    got = [exchange(part, (k + 1) * Z0) for k, part in enumerate(sends)]
    group1 = sum_terms([z_part(c, d, 0)] + got)
    mine, to_before, to_after = spread(me, group0, group1, m_own, att_rows, mlp_rows, scale)
    grad_params = close(mine, shifted(to_after, 1), shifted(to_before, -1), att_rows)
    return output, grad_input, grad_params


def solution(mesh):
    return jax.shard_map(
        local,
        mesh=mesh,
        in_specs=(
            P(AXES, None),
            P(AXES, None),
            P(AXES),
            P(AXES),
            P(AXES),
            P(AXES, None),
        ),
        out_specs=(P(AXES, None), P(AXES, None), P(AXES, None)),
        check_vma=False,
    )
```

```python
import math
from functools import partial

import jax
import jax.numpy as jnp
from jax import lax
from jax.experimental import pallas as pl
from jax.experimental.pallas import tpu as pltpu
from jax.sharding import PartitionSpec as P

FF = 3072
HEADS = 12
EPSILON = 1e-06
NEGATIVE = -1e30
AXES = ("wide", "narrow")
LANES = 128
SUB = 16
QB = 128
MEGA = 1 << 20
GRANT = 58 * MEGA
F32 = jnp.float32
BF16 = jnp.bfloat16

BLOCKS = 32
QKV_BLOCKS, QKV_RT, QKV_CT = 24, 2, 18
WO_BLOCKS, WO_RT, WO_CT = 8, 6, 6
W1_BLOCKS, W1_RT, W1_CT = 16, 3, 24
W2_BLOCKS, W2_RT, W2_CT = 16, 12, 6
ATT_HALF, MLP_HALF = 18, 36
ATT_SENT = ATT_HALF + 1
ATT_PART = 9
HALF_BLOCKS = BLOCKS // 2
CHUNK = 768
CHUNKS = FF // CHUNK

G1, C1, BQ, BV, BO, S1 = 0, 6, 12, 18, 24, 30
G2, C2, B1, B2, S2 = 36, 42, 48, 72, 78
SMALL = 88

NT = (((1,), (1,)), ((), ()))
NN = (((1,), (0,)), ((), ()))
TN = (((0,), (0,)), ((), ()))


def mm(lhs, rhs, dims):
    return lax.dot_general(lhs, rhs, dims, preferred_element_type=F32)


def row_of(ref, first, count):
    return jnp.concatenate([ref[first + k : first + k + 1, :] for k in range(count)], axis=1)


def put_row(ref, first, values):
    for k in range(values.shape[1] // LANES):
        ref[first + k : first + k + 1, :] = values[:, k * LANES : (k + 1) * LANES]


def fold8(values):
    rows, columns = values.shape
    return jnp.sum(values.reshape(rows // 8, 8, columns), axis=0)


def total(values):
    return jnp.sum(values, axis=0, keepdims=True)


def vmem():
    return pl.BlockSpec(memory_space=pltpu.VMEM)


def smem():
    return pl.BlockSpec(memory_space=pltpu.SMEM)


def hbm():
    return pl.BlockSpec(memory_space=pltpu.HBM)


def shape(dims, kind):
    return jax.ShapeDtypeStruct(dims, kind)


def cost(flops, moved, exps=0):
    return pl.CostEstimate(flops=int(flops), transcendentals=int(exps), bytes_accessed=int(moved))


def normalized(values):
    center = values - jnp.mean(values, axis=-1, keepdims=True)
    inverse = lax.rsqrt(jnp.mean(center * center, axis=-1, keepdims=True) + EPSILON)
    return center * inverse, inverse


def norm_pullback(unit, inverse, grad, gain):
    scaled = grad * gain
    first = jnp.mean(scaled, axis=-1, keepdims=True)
    second = jnp.mean(scaled * unit, axis=-1, keepdims=True)
    return inverse * (scaled - first - unit * second)


def gelu_pair(z):
    magnitude = jnp.abs(z)
    t = 1.0 / (1.0 + (0.3275911 * math.sqrt(0.5)) * magnitude)
    density = jnp.exp(z * z * -0.5)
    tail = 0.5 * 1.061405429
    tail = tail * t + 0.5 * -1.453152027
    tail = tail * t + 0.5 * 1.421413741
    tail = tail * t + 0.5 * -0.284496736
    tail = tail * t + 0.5 * 0.254829592
    tail = tail * t * density
    cumulative = jnp.where(z < 0, tail, 1.0 - tail)
    return z * cumulative, cumulative + z * density * (1.0 / math.sqrt(2.0 * math.pi))


def fetch(copies):
    for copy in copies:
        copy.start()


def settle(copies):
    for copy in copies:
        copy.wait()


ATT_BEFORE, ATT_AFTER = 64, 32
MLP_BEFORE, MLP_AFTER = 64, 40


def window_offsets(me, att_rows, mlp_rows):
    att = ATT_BEFORE + 12 + me * (576 - att_rows) + jnp.where(me < QKV_BLOCKS, 0, 12)
    mlp = MLP_BEFORE + 12 + me * (1152 - mlp_rows) + jnp.where(me < W1_BLOCKS, 0, 24)
    return att, mlp


def each_tile(me, act):
    for name, blocks, rt_count, ct_count, mine in (
        ("qkv", QKV_BLOCKS, QKV_RT, QKV_CT, me < QKV_BLOCKS),
        ("wo", WO_BLOCKS, WO_RT, WO_CT, me >= QKV_BLOCKS),
        ("w1", W1_BLOCKS, W1_RT, W1_CT, me < W1_BLOCKS),
        ("w2", W2_BLOCKS, W2_RT, W2_CT, me >= W1_BLOCKS),
    ):

        @pl.when(mine)
        def _(name=name, rt_count=rt_count, ct_count=ct_count):
            for ct in range(ct_count):
                for rt in range(rt_count):
                    act(name, rt, ct, rt * SUB * ct_count + ct, ct_count)


def half_place(name, rt, ct):
    if name == "qkv":
        return ct // 9, ct % 9 * QKV_RT + rt
    if name == "wo":
        return rt // 3, rt % 3 * WO_CT + ct
    if name == "w1":
        return ct // 12, ct % 12 * W1_RT + rt
    return rt // 6, rt % 6 * W2_CT + ct


def part_place(name, rt, ct):
    if name == "qkv":
        return ct % 6 // 3, rt, ct // 6 * 3 + ct % 3
    place = rt * WO_CT + ct
    return place // 18, place // ATT_PART % 2, place % ATT_PART


def qkv_group(g):
    return [6 * third + 3 * g + i for third in range(3) for i in range(3)]


def small_rows(me, act):
    @pl.when(me == 0)
    def _():
        act("att", True, 12, G1)
        act("mlp", True, 12, G2)

    @pl.when(me == QKV_BLOCKS - 1)
    def _():
        act("att", False, 12, BQ)

    @pl.when(me == W1_BLOCKS - 1)
    def _():
        act("mlp", False, 24, B1)

    @pl.when(me == BLOCKS - 1)
    def _():
        act("att", False, 12, BO)
        act("mlp", False, 12, B2)


OWNERS = (0, W1_BLOCKS - 1, QKV_BLOCKS - 1, BLOCKS - 1)


def sent_rows(kind, first):
    return 12 if kind == "mlp" and first in (G2, B2) else 0


def pack_kernel(att_rows, me_ref, own, tails, heads, att, mlp, win_a, win_m, table):
    me = me_ref[0]
    mlp_rows = own.shape[0] - att_rows
    win_a[0:ATT_BEFORE, :] = tails[0:ATT_BEFORE, :].astype(F32)
    win_a[ATT_BEFORE : ATT_BEFORE + att_rows, :] = own[0:att_rows, :]
    win_a[ATT_BEFORE + att_rows :, :] = heads[0:ATT_AFTER, :].astype(F32)
    win_m[0:MLP_BEFORE, :] = tails[ATT_BEFORE:, :].astype(F32)
    win_m[MLP_BEFORE : MLP_BEFORE + mlp_rows, :] = own[att_rows:, :]
    win_m[MLP_BEFORE + mlp_rows :, :] = heads[ATT_AFTER:, :].astype(F32)
    att_off, mlp_off = window_offsets(me, att_rows, mlp_rows)

    def tile(name, rt, ct, first, stride):
        attention = name in ("qkv", "wo")
        window, out, off = (win_a, att, att_off) if attention else (win_m, mlp, mlp_off)
        values = window[pl.ds(off + first, SUB, stride=stride), :]
        out[half_place(name, rt, ct)] = values.astype(BF16)

    each_tile(me, tile)
    table[...] = jnp.zeros_like(table)

    def vector(kind, before, rows, first):
        window, off, size = (win_a, att_off, 576) if kind == "att" else (win_m, mlp_off, 1152)
        start = off - 12 if before else off + size
        place = sent_rows(kind, first)
        table[place : place + rows, :] = window[pl.ds(start, rows), :]

    small_rows(me, vector)
    att[0, ATT_HALF] = table[0:SUB, :].astype(BF16)
    att[1, ATT_HALF] = table[SUB : 2 * SUB, :].astype(BF16)


def pack(me, own, tails, heads, att_rows):
    mlp_rows = own.shape[0] - att_rows
    return pl.pallas_call(
        partial(pack_kernel, att_rows),
        out_shape=(
            shape((2, ATT_SENT, SUB, LANES), BF16),
            shape((2, MLP_HALF, SUB, LANES), BF16),
        ),
        in_specs=[smem(), vmem(), vmem(), vmem()],
        out_specs=(vmem(), vmem()),
        scratch_shapes=[
            pltpu.VMEM((ATT_BEFORE + att_rows + ATT_AFTER, LANES), F32),
            pltpu.VMEM((MLP_BEFORE + mlp_rows + MLP_AFTER, LANES), F32),
            pltpu.VMEM((2 * SUB, LANES), F32),
        ],
        name="pack",
    )(me, own, tails, heads)


def spread_kernel(
    att_rows, scale, me_ref, group0, group1, mlp, mine, to_before, to_after, win_a, win_m, table
):
    me = me_ref[0]
    mlp_rows = mine.shape[0] - att_rows
    att_off, mlp_off = window_offsets(me, att_rows, mlp_rows)
    win_a[...] = jnp.zeros_like(win_a)
    win_m[...] = jnp.zeros_like(win_m)

    def tile(name, rt, ct, first, stride):
        if name in ("qkv", "wo"):
            g, half, index = part_place(name, rt, ct)
            values = (group0, group1)[g][half, index]
            win_a[pl.ds(att_off + first, SUB, stride=stride), :] = values * scale
        else:
            values = mlp[half_place(name, rt, ct)]
            win_m[pl.ds(mlp_off + first, SUB, stride=stride), :] = values * scale

    each_tile(me, tile)
    for h in range(2):
        table[SUB * h : SUB * h + SUB, :] = group1[h, ATT_PART] * scale

    def vector(kind, before, rows, first):
        window, off, size = (win_a, att_off, 576) if kind == "att" else (win_m, mlp_off, 1152)
        start = off - 12 if before else off + size
        place = sent_rows(kind, first)
        window[pl.ds(start, rows), :] = table[place : place + rows, :]

    small_rows(me, vector)
    mine[0:att_rows, :] = win_a[ATT_BEFORE : ATT_BEFORE + att_rows, :]
    mine[att_rows:, :] = win_m[MLP_BEFORE : MLP_BEFORE + mlp_rows, :]
    to_before[0:ATT_BEFORE, :] = win_a[0:ATT_BEFORE, :]
    to_before[ATT_BEFORE:, :] = win_m[0:MLP_BEFORE, :]
    to_after[0:ATT_AFTER, :] = win_a[ATT_BEFORE + att_rows :, :]
    to_after[ATT_AFTER:, :] = win_m[MLP_BEFORE + mlp_rows :, :]


def spread(me, group0, group1, mlp, att_rows, mlp_rows, scale):
    return pl.pallas_call(
        partial(spread_kernel, att_rows, scale),
        out_shape=(
            shape((att_rows + mlp_rows, LANES), F32),
            shape((ATT_BEFORE + MLP_BEFORE, LANES), F32),
            shape((ATT_AFTER + MLP_AFTER, LANES), F32),
        ),
        in_specs=[smem(), vmem(), vmem(), vmem()],
        out_specs=(vmem(), vmem(), vmem()),
        scratch_shapes=[
            pltpu.VMEM((ATT_BEFORE + att_rows + ATT_AFTER, LANES), F32),
            pltpu.VMEM((MLP_BEFORE + mlp_rows + MLP_AFTER, LANES), F32),
            pltpu.VMEM((2 * SUB, LANES), F32),
        ],
        name="spread",
    )(me, group0, group1, mlp)


def close_kernel(att_rows, mine, below, above, out):
    rows = mine.shape[0]
    out[...] = mine[...]
    out[0:ATT_AFTER, :] += below[0:ATT_AFTER, :]
    out[att_rows : att_rows + MLP_AFTER, :] += below[ATT_AFTER:, :]
    out[att_rows - ATT_BEFORE : att_rows, :] += above[0:ATT_BEFORE, :]
    out[rows - MLP_BEFORE : rows, :] += above[ATT_BEFORE:, :]


def close(mine, below, above, att_rows):
    return pl.pallas_call(
        partial(close_kernel, att_rows),
        out_shape=shape(mine.shape, F32),
        in_specs=[vmem()] * 3,
        out_specs=vmem(),
        name="close",
    )(mine, below, above)


def spot(h, d):
    x, c, z, y = d >> 4, (d >> 3) & 1, (d >> 1) & 3, d & 1
    return c * 16 + (y * 8 + x * 4 if h == 0 else x * 8 + y * 4) + z


SLOTS = [sorted(range(BLOCKS), key=partial(spot, h)) for h in range(2)]


def fill_spots(me, spots):
    for h in range(2):
        mine = spot(h, me)
        for d in range(BLOCKS):
            spots[h, d] = jnp.bitwise_xor(mine, spot(h, d))


def slots_scratch(tiles):
    return pltpu.VMEM((2, BLOCKS, tiles, SUB, LANES), BF16)


def spots_scratch():
    return pltpu.SMEM((2, BLOCKS), jnp.int32)


def arriving_slots(buffers, w, sems):
    return [
        pltpu.make_async_copy(buffers[i], w.at[i // 4, pl.ds(i % 4 * 8, 8)], sems.at[i])
        for i in range(8)
    ]


def leaving_slots(buffers, w, sems):
    return [
        pltpu.make_async_copy(w.at[i // 2, pl.ds(i % 2 * 16, 16)], buffers[i], sems.at[i])
        for i in range(4)
    ]


def qkv_column(w, spots, ct):
    h, place = ct // 9, ct % 9 * QKV_RT
    tiles = [w[h, spots[h, d], place + rt] for d in range(QKV_BLOCKS) for rt in range(QKV_RT)]
    return jnp.concatenate(tiles, axis=0)


def wo_matrix(w, spots):
    columns = []
    for ct in range(WO_CT):
        tiles = [
            w[rt // 3, spots[rt // 3, QKV_BLOCKS + i] & 7, rt % 3 * WO_CT + ct]
            for i in range(WO_BLOCKS)
            for rt in range(WO_RT)
        ]
        columns.append(jnp.concatenate(tiles, axis=0))
    return jnp.concatenate(columns, axis=1)


def dma(count):
    return pltpu.SemaphoreType.DMA((count,))


def norm_rows(rows, gain, shift, source, target, step=256):
    def one(i, carry):
        at = pl.ds(pl.multiple_of(i * step, step), step)
        unit, _ = normalized(source[at, :].astype(F32))
        target[at, :] = (unit * gain + shift).astype(BF16)
        return carry

    lax.fori_loop(0, rows // step, one, 0)


def qkv_kernel(me_ref, tokens, *refs):
    buffers, (n1, qkv, small, w, spots, x, unit, triple, sems, own) = refs[:8], refs[8:]
    coming = pltpu.make_async_copy(tokens, x, own.at[0])
    coming.start()
    weights = arriving_slots(buffers, w, sems)
    fetch(weights)
    fill_spots(me_ref[0], spots)
    settle(weights)
    tables = [
        jnp.concatenate([w[h, spots[h, d], ATT_HALF] for h in range(2)], axis=0).astype(F32)
        for d in OWNERS
    ]
    small[G1 : G1 + 12, :] = tables[0][0:12]
    small[G2 : G2 + 12, :] = tables[0][12:24]
    small[B1 : B1 + 24, :] = tables[1][0:24]
    small[BQ : BQ + 12, :] = tables[2][0:12]
    small[BO : BO + 12, :] = tables[3][0:12]
    small[B2 : B2 + 12, :] = tables[3][12:24]
    small[SMALL - 4 :, :] = jnp.zeros((4, LANES), F32)
    coming.wait()
    norm_rows(x.shape[0], row_of(small, G1, 6), row_of(small, C1, 6), x, unit)
    going = [pltpu.make_async_copy(unit, n1, own.at[0])]
    going[0].start()
    bias = jnp.concatenate(
        [row_of(small, BQ, 6), jnp.zeros((1, 768), F32), row_of(small, BV, 6)], axis=1
    )
    for c in range(QKV_CT // 2):
        weight = jnp.concatenate([qkv_column(w, spots, 2 * c + i) for i in range(2)], axis=1)
        lanes = slice(256 * c, 256 * c + 256)
        triple[:, lanes] = (mm(unit[...], weight, NN) + bias[:, lanes]).astype(BF16)
        going.append(
            pltpu.make_async_copy(triple.at[:, lanes], qkv.at[:, lanes], own.at[1 + c])
        )
        going[-1].start()
    settle(going)


def project_qkv(me, tokens, att):
    rows, width = tokens.shape
    return pl.pallas_call(
        qkv_kernel,
        out_shape=(
            shape((rows, width), BF16),
            shape((rows, 3 * width), BF16),
            shape((SMALL, LANES), F32),
        ),
        in_specs=[smem(), hbm()] + [hbm()] * 8,
        out_specs=(hbm(), hbm(), vmem()),
        scratch_shapes=[
            slots_scratch(ATT_SENT),
            spots_scratch(),
            pltpu.VMEM((rows, width), BF16),
            pltpu.VMEM((rows, width), BF16),
            pltpu.VMEM((rows, 3 * width), BF16),
            dma(8),
            dma(1 + QKV_CT // 2),
        ],
        compiler_params=pltpu.CompilerParams(vmem_limit_bytes=GRANT),
        cost_estimate=cost(6 * rows * width * width, 12 * rows * width),
        name="qkv_forward",
    )(me, tokens, *att)


CLASSES = (128, 256, 320, 384, 448, 512, 768)


def head_masked(block):
    lane = lax.broadcasted_iota(jnp.int32, block.shape, 1)
    zero = jnp.zeros_like(block)
    return jnp.concatenate(
        [jnp.where(lane < 64, block, zero), jnp.where(lane >= 64, block, zero)], axis=0
    )


def pick_heads(both):
    return jnp.concatenate([both[0:64, 0:QB], both[64:128, QB : 2 * QB]], axis=0)


def pieces_of_window(width):
    return [slice(first, min(first + QB, width)) for first in range(0, width, QB)]


def spread_ids(query_ids, key_ids):
    for b in range(query_ids.shape[0]):
        row = jnp.broadcast_to(query_ids[b : b + 1, :], (QB, QB))
        key_ids[b * QB : (b + 1) * QB, :] = row.T


def mask_bias(start, width, b, key_ids, query_ids, bias):
    for piece in pieces_of_window(width):
        size = piece.stop - piece.start
        at = pl.ds(pl.multiple_of(start + piece.start, SUB), size)
        same = key_ids[at, :] == query_ids[pl.ds(b, 1), :]
        bias[piece, :] = jnp.where(same, 0.0, NEGATIVE)


PAIRS = HEADS // 2


def attend_block(b, start, width, qkv, mixed, stats, bias, scores):
    rows = pl.ds(pl.multiple_of(b * QB, QB), QB)
    pieces = pieces_of_window(width)
    for p in range(PAIRS):
        lanes, key_lanes, value_lanes = [
            slice(LANES * (PAIRS * third + p), LANES * (PAIRS * third + p + 1))
            for third in range(3)
        ]
        queries = head_masked(qkv[rows, lanes] * 0.125)
        highest = jnp.full((8, 2 * QB), NEGATIVE, F32)
        for piece in pieces:
            size = piece.stop - piece.start
            at = pl.ds(pl.multiple_of(start + piece.start, SUB), size)
            part = mm(qkv[at, key_lanes], queries, NT)
            part = part + jnp.concatenate([bias[piece, :]] * 2, axis=1)
            scores[p, piece, :] = part
            highest = jnp.maximum(highest, jnp.max(part.reshape(size // 8, 8, 2 * QB), axis=0))
        highest = jnp.max(highest, axis=0, keepdims=True)
        summed = jnp.zeros((8, 2 * QB), F32)
        both = jnp.zeros((LANES, 2 * QB), F32)
        for piece in pieces:
            size = piece.stop - piece.start
            at = pl.ds(pl.multiple_of(start + piece.start, SUB), size)
            raised = jnp.exp(scores[p, piece, :] - highest)
            summed = summed + fold8(raised)
            both = both + mm(qkv[at, value_lanes], raised.astype(BF16), TN)
        inverse = 1.0 / total(summed)
        mixed[rows, lanes] = pick_heads(both * inverse).T.astype(BF16)
        stats[b * PAIRS + p, 0:1, :] = highest
        stats[b * PAIRS + p, 1:2, :] = inverse


def wo_scratch():
    return pltpu.VMEM((2, WO_BLOCKS, ATT_SENT, SUB, LANES), BF16)


def wo_copies(buffers, w, sems, core, x):
    copies = []
    for y in range(2):
        source = buffers[2 * core + y].at[pl.ds(4 * x, 4)]
        copies.append(pltpu.make_async_copy(source, w.at[0, pl.ds(4 * y, 4)], sems.at[y]))
    copies.append(pltpu.make_async_copy(buffers[4 + 2 * core + x], w.at[1], sems.at[2]))
    return copies


def fetch_wo(me, buffers, w, spots, sems):
    fill_spots(me, spots)
    for h in range(2):
        for i in range(WO_BLOCKS):
            place = spot(h, jnp.bitwise_xor(me, QKV_BLOCKS + i) & 7)
            spots[h, QKV_BLOCKS + i] = (place >> (1 if h == 0 else 0)) & 4 | place & 3
    far = jnp.bitwise_xor(me, QKV_BLOCKS)
    for core in range(2):
        for x in range(2):

            @pl.when((far >> 3) == 2 * x + core)
            def _(core=core, x=x):
                fetch(wo_copies(buffers, w, sems, core, x))


def wait_wo(buffers, w, sems):
    settle(wo_copies(buffers, w, sems, 0, 0))


def attend_kernel(me_ref, windows, qkv, tokens, cot, query_ids, small, *refs):
    buffers, refs = refs[:8], refs[8:]
    mixed, x1, branch, n2, dm, stats, gb2 = refs[:7]
    key_ids, triple, x, g, mix, mid, out, unit, scaled, bias, scores, w, spots = refs[7:20]
    sems, own, chunk_sems = refs[20:]
    rows = tokens.shape[0]
    blocks = rows // QB

    def chunk(i):
        at = pl.ds(pl.multiple_of(i * QB, QB), QB)
        return pltpu.make_async_copy(qkv.at[at, :], triple.at[at, :], chunk_sems.at[i])

    for i in range(blocks):
        chunk(i).start()
    coming = [
        pltpu.make_async_copy(tokens, x, own.at[0]),
        pltpu.make_async_copy(cot, g, own.at[1]),
    ]
    fetch(coming)
    fetch_wo(me_ref[0], buffers, w, spots, sems)
    spread_ids(query_ids, key_ids)

    def one_block(b, loaded):
        start = pl.multiple_of(windows[0, b], SUB)
        needed = jnp.maximum(windows[2, b], loaded)

        def arrived(i, carry):
            chunk(i).wait()
            return carry

        lax.fori_loop(loaded, needed, arrived, 0)
        for index, width in enumerate(CLASSES):

            @pl.when(windows[1, b] == index)
            def _(width=width):
                mask_bias(start, width, b, key_ids, query_ids, bias)
                attend_block(b, start, width, triple, mix, stats, bias, scores)

        return needed

    loaded = lax.fori_loop(0, blocks, one_block, jnp.int32(0))

    def arrived(i, carry):
        chunk(i).wait()
        return carry

    lax.fori_loop(loaded, blocks, arrived, 0)
    going = [pltpu.make_async_copy(mix, mixed, own.at[2])]
    going[0].start()
    wait_wo(buffers, w, sems)
    settle(coming)
    bo, s1 = row_of(small, BO, 6), row_of(small, S1, 6)
    gain, shift = row_of(small, G2, 6), row_of(small, C2, 6)
    s2 = row_of(small, S2, 6)
    weight = wo_matrix(w, spots)
    step = 256
    sums = jnp.zeros((8, 768), F32)
    for i in range(rows // step):
        at = slice(i * step, (i + 1) * step)
        made = mm(mix[at, :], weight, NN) + bo
        out[at, :] = made.astype(BF16)
        values = x[at, :].astype(F32) + s1 * made
        mid[at, :] = values
        normal, _ = normalized(values)
        unit[at, :] = (normal * gain + shift).astype(BF16)
        rounded = (g[at, :].astype(F32) * s2).astype(BF16)
        scaled[at, :] = rounded
        sums = sums + fold8(rounded.astype(F32))
        for k, (source, target) in enumerate(
            ((out, branch), (mid, x1), (unit, n2), (scaled, dm))
        ):
            sem = own.at[3 + 4 * i + k]
            going.append(pltpu.make_async_copy(source.at[at, :], target.at[at, :], sem))
            going[-1].start()
    put_row(gb2, 0, total(sums))
    settle(going)


def attend(me, windows, qkv, tokens, cot, query_ids, small, att):
    rows, width = tokens.shape
    row = lambda kind: pltpu.VMEM((rows, width), kind)
    return pl.pallas_call(
        attend_kernel,
        out_shape=(
            shape((rows, width), BF16),
            shape((rows, width), F32),
            shape((rows, width), BF16),
            shape((rows, width), BF16),
            shape((rows, width), BF16),
            shape((rows // QB * PAIRS, 2, 2 * QB), F32),
            shape((6, LANES), F32),
        ),
        in_specs=[smem(), smem(), hbm(), hbm(), hbm(), vmem(), vmem()] + [hbm()] * 8,
        out_specs=(hbm(),) * 5 + (vmem(), vmem()),
        scratch_shapes=[
            pltpu.VMEM((rows, QB), F32),
            pltpu.VMEM((rows, 3 * width), BF16),
            row(BF16),
            row(BF16),
            row(BF16),
            row(F32),
            row(BF16),
            row(BF16),
            row(BF16),
            pltpu.VMEM((CLASSES[-1], QB), F32),
            pltpu.VMEM((PAIRS, CLASSES[-1], 2 * QB), F32),
            wo_scratch(),
            spots_scratch(),
            dma(3),
            dma(3 + 4 * rows // 256),
            dma(rows // QB),
        ],
        compiler_params=pltpu.CompilerParams(vmem_limit_bytes=GRANT),
        cost_estimate=cost(2 * rows * rows * width, 20 * rows * width, 4 * rows * rows),
        name="attend_forward",
    )(me, windows, qkv, tokens, cot, query_ids, small, *att)


def lay_matrix(w, spots, name, blocks, first, rt_count, columns, out):
    def one_block(d, carry):
        places = [spots[h, first + d] for h in range(2)]
        base = pl.multiple_of(d * rt_count * SUB, SUB)
        for rt in range(rt_count):
            for column, ct in enumerate(columns):
                h, index = half_place(name, rt, ct)
                at = pl.ds(pl.multiple_of(base + rt * SUB, SUB), SUB)
                out[at, LANES * column : LANES * (column + 1)] = w[h, places[h], index]
        return carry

    lax.fori_loop(0, blocks, one_block, 0)


def lay_w1(w, spots, out):
    lay_matrix(w, spots, "w1", W1_BLOCKS, 0, W1_RT, range(W1_CT), out)


def lay_w2(w, spots, out):
    lay_matrix(w, spots, "w2", W2_BLOCKS, W1_BLOCKS, W2_RT, range(W2_CT), out)


def w2_place(spots, f, row, ct):
    rt = row % W2_RT
    h = rt // 6
    return h, spots[h, W1_BLOCKS + 4 * f + row // W2_RT], rt % 6 * W2_CT + ct


TALL = 256
PARTS = CHUNK // 256


def device_of(x, c, z, y):
    return x * 16 + c * 8 + z * 2 + y


W1_RUNS = [
    [(0, device_of(0, c, 0, y), 4) for c in range(2) for y in range(2)],
    [(1, device_of(0, c, 0, 0), 8) for c in range(2)],
]
W2_RUNS = [
    [(h, device_of(1, f >> 1, 2 * (f & 1), y), 2) for h in range(2) for y in range(2)]
    for f in range(CHUNKS)
]
RUN_ORDER = W1_RUNS[0] + W2_RUNS[0] + W2_RUNS[1] + W1_RUNS[1] + W2_RUNS[2] + W2_RUNS[3]


class Runs:
    def __init__(self, buffers, w, spots, sems, out=False):
        self.buffers, self.w, self.spots, self.sems, self.out = buffers, w, spots, sems, out
        self.each = len(buffers) // 2

    def copy(self, run, which, index, place):
        h, first, size = run
        outer = self.buffers[self.each * h + which].at[pl.ds(index, size)]
        inner = self.w.at[h, pl.ds(place, size)]
        sem = self.sems.at[RUN_ORDER.index(run)]
        ends = (inner, outer) if self.out else (outer, inner)
        return pltpu.make_async_copy(*ends, sem)

    def start(self, runs):
        length = BLOCKS // self.each
        for run in runs:
            h, first, size = run
            place = self.spots[h, first] & (BLOCKS - size)
            for which in range(self.each):

                @pl.when(place // length == which)
                def _(run=run, which=which, place=place):
                    self.copy(run, which, place & (length - 1), place).start()

    def wait(self, runs):
        for run in runs:
            self.copy(run, 0, 0, 0).wait()


def mlp_kernel(me_ref, n2_in, dm_in, small, *refs):
    arriving, refs = refs[:8], refs[8:]
    u_out, dz_out, vectors, *leaving = refs[:7]
    w, first, second, spots, n2, dm, u, dz, zs, dus, bias_sums, b1_lines, sems, own = refs[7:]
    rows, width = n2.shape
    tiles = rows // TALL
    coming = [
        pltpu.make_async_copy(n2_in, n2, own.at[0]),
        pltpu.make_async_copy(dm_in, dm, own.at[1]),
    ]
    fetch(coming)
    fill_spots(me_ref[0], spots)
    incoming = Runs(arriving, w, spots, sems)
    incoming.start(RUN_ORDER)
    bias_sums[...] = jnp.zeros_like(bias_sums)
    for f in range(CHUNKS):
        b1_lines[f : f + 1, :] = row_of(small, B1 + 6 * f, 6)
    def lay_chunk(f, side):
        h, base = f >> 1, MLP_HALF // 2 * (f & 1)
        for d in range(W1_BLOCKS):
            place = spots[h, d]
            for rt in range(W1_RT):
                at = slice((d * W1_RT + rt) * SUB, (d * W1_RT + rt + 1) * SUB)
                for ct in range(6):
                    lanes = slice(LANES * ct, LANES * ct + LANES)
                    first[side, at, lanes] = w[h, place, base + ct * W1_RT + rt]
        for k in range(4):
            places = [spots[i, W1_BLOCKS + 4 * f + k] for i in range(2)]
            for rt in range(W2_RT):
                at = slice((k * W2_RT + rt) * SUB, (k * W2_RT + rt + 1) * SUB)
                for ct in range(W2_CT):
                    lanes = slice(LANES * ct, LANES * ct + LANES)
                    i, index = half_place("w2", rt, ct)
                    second[side, at, lanes] = w[i, places[i], index]

    incoming.wait(W1_RUNS[0] + W2_RUNS[0])
    lay_chunk(jnp.int32(0), jnp.int32(0))
    settle(coming)

    units = [(t, c) for c in range(PARTS) for t in range(tiles)]

    def lanes_of(f, c):
        return pl.ds(pl.multiple_of(CHUNK * f + 256 * c, 256), 256)

    def outward(f):
        chunk = pl.ds(pl.multiple_of(CHUNK * f, CHUNK), CHUNK)
        return [
            pltpu.make_async_copy(u.at[:, chunk], u_out.at[:, chunk], own.at[2 * f]),
            pltpu.make_async_copy(dz.at[:, chunk], dz_out.at[:, chunk], own.at[2 * f + 1]),
        ]

    def one_chunk(f, carry):
        for index in range(CHUNKS - 1):

            @pl.when(f == index)
            def _(index=index):
                incoming.wait(W2_RUNS[index + 1] + (W1_RUNS[1] if index == 1 else []))

        side = f & 1
        lay_chunk(jnp.minimum(f + 1, CHUNKS - 1), 1 - side)

        def multiply(unit, slot):
            t, c = unit
            at = slice(TALL * t, TALL * t + TALL)
            zs[slot] = mm(n2[at, :], first[side, :, 256 * c : 256 * c + 256], NN)
            dus[slot] = mm(dm[at, :], second[side, 256 * c : 256 * c + 256, :], NT)

        def activate(unit, slot):
            t, c = unit
            lanes = slice(256 * c, 256 * c + 256)
            bias = b1_lines[pl.ds(f, 1), lanes]
            folded = jnp.zeros((8, 256), F32)
            for r in range(TALL // 32):
                part = slice(32 * r, 32 * r + 32)
                place = slice(TALL * t + 32 * r, TALL * t + 32 * r + 32)
                value, slope = gelu_pair(zs[slot, part, :] + bias)
                u[place, lanes_of(f, c)] = value.astype(BF16)
                rounded = (dus[slot, part, :] * slope).astype(BF16)
                dz[place, lanes_of(f, c)] = rounded
                folded = folded + fold8(rounded.astype(F32))
            bias_sums[:, lanes_of(f, c)] += folded

        multiply(units[0], 0)
        for i, unit in enumerate(units):
            if i + 1 < len(units):
                multiply(units[i + 1], (i + 1) % 2)
            activate(unit, i % 2)
        fetch(outward(f))
        return carry

    lax.fori_loop(0, CHUNKS, one_chunk, 0)
    put_row(vectors, 0, total(bias_sums[...]))

    outgoing = Runs(leaving, w, spots, sems, out=True)

    def one_grad(f, carry):
        h, base = f >> 1, MLP_HALF // 2 * (f & 1)
        chunk = pl.ds(pl.multiple_of(CHUNK * f, CHUNK), CHUNK)
        for c in range(PARTS):
            lanes = slice(256 * c, 256 * c + 256)
            grad = mm(n2[:, lanes], dz[:, chunk], TN)
            for r in range(SUB):
                d, rt = (SUB * c + r) // W1_RT, (SUB * c + r) % W1_RT
                for ct in range(6):
                    tile = grad[SUB * r : SUB * r + SUB, LANES * ct : LANES * ct + LANES]
                    w[h, spots[h, d], base + ct * W1_RT + rt] = tile.astype(BF16)
        for side in range(2):

            @pl.when(f == 2 * side + 1)
            def _(side=side):
                outgoing.start(W1_RUNS[side])

        for c in range(PARTS):
            grad = mm(u[:, lanes_of(f, c)], dm[...], TN)
            for r in range(SUB):
                for ct in range(W2_CT):
                    tile = grad[SUB * r : SUB * r + SUB, LANES * ct : LANES * ct + LANES]
                    w[w2_place(spots, f, SUB * c + r, ct)] = tile.astype(BF16)
        for index in range(CHUNKS):

            @pl.when(f == index)
            def _(index=index):
                outgoing.start(W2_RUNS[index])

        return carry

    lax.fori_loop(0, CHUNKS, one_grad, 0)
    for f in range(CHUNKS):
        settle(outward(f))
    outgoing.wait(RUN_ORDER)


def feed_forward(me, n2, dm, small, mlp):
    rows, width = n2.shape
    half = shape((HALF_BLOCKS, MLP_HALF, SUB, LANES), BF16)
    return pl.pallas_call(
        mlp_kernel,
        out_shape=(
            shape((rows, FF), BF16),
            shape((rows, FF), BF16),
            shape((24, LANES), F32),
            half,
            half,
            half,
            half,
        ),
        in_specs=[smem(), hbm(), hbm(), vmem()] + [hbm()] * 8,
        out_specs=(hbm(), hbm(), vmem()) + (hbm(),) * 4,
        scratch_shapes=[
            slots_scratch(MLP_HALF),
            pltpu.VMEM((2, width, CHUNK), BF16),
            pltpu.VMEM((2, CHUNK, width), BF16),
            spots_scratch(),
            pltpu.VMEM((rows, width), BF16),
            pltpu.VMEM((rows, width), BF16),
            pltpu.VMEM((rows, FF), BF16),
            pltpu.VMEM((rows, FF), BF16),
            pltpu.VMEM((2, TALL, 256), F32),
            pltpu.VMEM((2, TALL, 256), F32),
            pltpu.VMEM((8, FF), F32),
            pltpu.VMEM((CHUNKS, CHUNK), F32),
            dma(len(RUN_ORDER)),
            dma(2 * CHUNKS),
        ],
        compiler_params=pltpu.CompilerParams(vmem_limit_bytes=42 * MEGA),
        cost_estimate=cost(8 * rows * width * FF, 40 * MEGA),
        name="feed_forward",
    )(me, n2, dm, small, *mlp)


def matrix_copies(buffers, w, sems, x):
    copies = []
    for i in range(4):
        source = buffers[i].at[pl.ds(4 * x, 4)]
        copies.append(pltpu.make_async_copy(source, w.at[0, pl.ds(4 * i, 4)], sems.at[i]))
    for c in range(2):
        source = buffers[4 + 2 * c + x]
        copies.append(pltpu.make_async_copy(source, w.at[1, pl.ds(8 * c, 8)], sems.at[4 + c]))
    return copies


def fetch_matrix(me, buffers, w, spots, sems, first):
    def place(d):
        return ((d >> 3) & 1) * 8 + (d & 1) * 4 + ((d >> 1) & 3)

    for x in range(2):

        @pl.when((me >> 4) == (x ^ (first >> 4)))
        def _(x=x):
            fetch(matrix_copies(buffers, w, sems, x))

    mine = place(me)
    for d in range(W1_BLOCKS):
        for h in range(2):
            spots[h, first + d] = jnp.bitwise_xor(mine, place(d))


def wait_matrix(buffers, w, sems):
    settle(matrix_copies(buffers, w, sems, 0))


def matrix_scratch():
    return pltpu.VMEM((2, W1_BLOCKS, MLP_HALF, SUB, LANES), BF16)


def mlp_out_kernel(me_ref, u_in, x1_in, cot_in, small, *refs):
    arriving, refs = refs[:8], refs[8:]
    out, vectors, w, second, spots, u, x1, cot, macc, done, sums, sems, own = refs
    rows, width = x1.shape
    tiles = rows // TALL

    def tile_copy(source, target, t, k):
        at = pl.ds(pl.multiple_of(TALL * t, TALL), TALL)
        return pltpu.make_async_copy(source.at[at, :], target.at[at, :], own.at[k, t])

    fetch_matrix(me_ref[0], arriving, w, spots, sems, W1_BLOCKS)
    for t in range(tiles):
        tile_copy(u_in, u, t, 0).start()
    for t in range(tiles):
        tile_copy(x1_in, x1, t, 1).start()
        tile_copy(cot_in, cot, t, 2).start()
    bias, scale = row_of(small, B2, 6), row_of(small, S2, 6)
    sums[...] = jnp.zeros_like(sums)
    wait_matrix(arriving, w, sems)
    lay_w2(w, spots, second)

    def contract(t):
        at = pl.ds(pl.multiple_of(TALL * t, TALL), TALL)
        tile_copy(u_in, u, t, 0).wait()
        macc[at, :] = mm(u[at, :], second[...], NN)

    def finish(t):
        tile_copy(x1_in, x1, t, 1).wait()
        tile_copy(cot_in, cot, t, 2).wait()
        for part in range(TALL // 64):
            at = pl.ds(pl.multiple_of(TALL * t + 64 * part, 64), 64)
            contracted = macc[at, :] + bias
            done[at, :] = (x1[at, :] + scale * contracted).astype(BF16)
            sums[...] += fold8(cot[at, :].astype(F32) * contracted)
        tile_copy(done, out, t, 3).start()

    def one_tile(t, carry):
        contract(t)
        finish(t - 1)
        return carry

    contract(0)
    lax.fori_loop(1, tiles, one_tile, 0)
    finish(tiles - 1)
    put_row(vectors, 0, total(sums[...]))
    for t in range(tiles):
        tile_copy(done, out, t, 3).wait()


def feed_forward_out(me, u, x1, cot, small, mlp):
    rows, width = x1.shape
    row = lambda kind: pltpu.VMEM((rows, width), kind)
    return pl.pallas_call(
        mlp_out_kernel,
        out_shape=(shape((rows, width), BF16), shape((6, LANES), F32)),
        in_specs=[smem()] + [hbm()] * 3 + [vmem()] + [hbm()] * 8,
        out_specs=(hbm(), vmem()),
        scratch_shapes=[
            matrix_scratch(),
            pltpu.VMEM((FF, width), BF16),
            spots_scratch(),
            pltpu.VMEM((rows, FF), BF16),
            row(F32),
            row(BF16),
            row(F32),
            row(BF16),
            pltpu.VMEM((8, width), F32),
            dma(6),
            pltpu.SemaphoreType.DMA((4, rows // TALL)),
        ],
        compiler_params=pltpu.CompilerParams(vmem_limit_bytes=32 * MEGA),
        cost_estimate=cost(2 * rows * width * FF, 20 * MEGA),
        name="feed_forward_out",
    )(me, u, x1, cot, small, *mlp)


def split_kernel(me_ref, dz_in, x1_in, cot_in, branch_in, mixed_in, small, *refs):
    buffers, att_buffers, refs = refs[:8], refs[8:16], refs[16:]
    dx1_out, da_out, gwo0, gwo1, vectors = refs[:5]
    w, first, spots, wo, wo_spots, dz, x1, cot, dnacc, dx1, branch, mixed, db, da = refs[5:19]
    parts, sums, sems, wo_sems, own = refs[19:]
    me = me_ref[0]
    rows, width = x1.shape
    tiles = rows // TALL

    def tile_copy(source, target, t, k):
        at = pl.ds(pl.multiple_of(TALL * t, TALL), TALL)
        return pltpu.make_async_copy(source.at[at, :], target.at[at, :], own.at[k, t])

    fetch_matrix(me, buffers, w, spots, sems, 0)
    for t in range(tiles):
        tile_copy(dz_in, dz, t, 0).start()
    for t in range(tiles):
        tile_copy(x1_in, x1, t, 1).start()
        tile_copy(cot_in, cot, t, 2).start()
        tile_copy(branch_in, branch, t, 3).start()
    fetch_wo(me, att_buffers, wo, wo_spots, wo_sems)
    late = pltpu.make_async_copy(mixed_in, mixed, own.at[4, 0])
    late.start()
    gain, scale = row_of(small, G2, 6), row_of(small, S1, 6)
    sums[...] = jnp.zeros_like(sums)
    wait_matrix(buffers, w, sems)
    lay_w1(w, spots, first)

    def contract(t):
        at = pl.ds(pl.multiple_of(TALL * t, TALL), TALL)
        tile_copy(dz_in, dz, t, 0).wait()
        dnacc[at, :] = mm(dz[at, :], first[...], NT)

    def finish(t):
        tile_copy(x1_in, x1, t, 1).wait()
        tile_copy(cot_in, cot, t, 2).wait()
        tile_copy(branch_in, branch, t, 3).wait()
        for half in range(2):
            at = pl.ds(pl.multiple_of(TALL * t + TALL // 2 * half, TALL // 2), TALL // 2)
            unit, inverse = normalized(x1[at, :])
            grad = dnacc[at, :]
            middle = cot[at, :].astype(F32) + norm_pullback(unit, inverse, grad, gain)
            dx1[at, :] = middle
            rounded = (middle * scale).astype(BF16)
            db[at, :] = rounded
            sums[0:8, :] += fold8(grad * unit)
            sums[8:16, :] += fold8(grad)
            sums[16:24, :] += fold8(rounded.astype(F32))
            sums[24:32, :] += fold8(middle * branch[at, :].astype(F32))
        tile_copy(dx1, dx1_out, t, 1).start()

    def one_tile(t, carry):
        contract(t)
        finish(t - 1)
        return carry

    contract(0)
    lax.fori_loop(1, tiles, one_tile, 0)
    finish(tiles - 1)
    for k in range(4):
        put_row(vectors, 6 * k, total(sums[8 * k : 8 * k + 8, :]))
    wait_wo(att_buffers, wo, wo_sems)
    weight = wo_matrix(wo, wo_spots)
    going = []
    for c in range(3):
        lanes = slice(256 * c, 256 * c + 256)
        da[:, lanes] = mm(db[...], weight[lanes, :], NT).astype(BF16)
        going.append(pltpu.make_async_copy(da.at[:, lanes], da_out.at[:, lanes], own.at[0, c]))
        going[-1].start()
    late.wait()
    for c in range(3):
        grad = mm(mixed[:, 256 * c : 256 * c + 256], db[...], TN)
        for r in range(SUB):
            i, rt = (SUB * c + r) // WO_RT, (SUB * c + r) % WO_RT
            for ct in range(WO_CT):
                tile = grad[SUB * r : SUB * r + SUB, LANES * ct : LANES * ct + LANES]
                g, half, index = part_place("wo", rt, ct)
                parts[g, half, i, index] = tile.astype(BF16)
    for g, target in enumerate((gwo0, gwo1)):
        going.append(pltpu.make_async_copy(parts.at[g], target, own.at[4, g]))
        going[-1].start()
    settle(going)
    for t in range(tiles):
        tile_copy(dx1, dx1_out, t, 1).wait()


def split(me, dz, x1, cot, branch, mixed, small, mlp, att):
    rows, width = x1.shape
    part = (2, WO_BLOCKS, ATT_PART, SUB, LANES)
    row = lambda kind: pltpu.VMEM((rows, width), kind)
    return pl.pallas_call(
        split_kernel,
        out_shape=(
            shape((rows, width), F32),
            shape((rows, width), BF16),
            shape(part, BF16),
            shape(part, BF16),
            shape((24, LANES), F32),
        ),
        in_specs=[smem()] + [hbm()] * 5 + [vmem()] + [hbm()] * 16,
        out_specs=(hbm(),) * 4 + (vmem(),),
        scratch_shapes=[
            matrix_scratch(),
            pltpu.VMEM((width, FF), BF16),
            spots_scratch(),
            wo_scratch(),
            spots_scratch(),
            pltpu.VMEM((rows, FF), BF16),
            row(F32),
            row(BF16),
            row(F32),
            row(F32),
            row(BF16),
            row(BF16),
            row(BF16),
            row(BF16),
            pltpu.VMEM((2,) + part, BF16),
            pltpu.VMEM((32, width), F32),
            dma(6),
            dma(3),
            pltpu.SemaphoreType.DMA((5, rows // TALL)),
        ],
        compiler_params=pltpu.CompilerParams(vmem_limit_bytes=44 * MEGA),
        cost_estimate=cost(2 * rows * width * FF + 4 * rows * width * width, 40 * MEGA),
        name="feed_forward_in",
    )(me, dz, x1, cot, branch, mixed, small, *mlp, *att)


GROUP = PAIRS // 2
GROUP_LANES = GROUP * LANES


def attend_back_block(b, start, width, group, refs):
    q, k, v, da, stats, dq, dkeys, dvalues, bias = refs
    rows = pl.ds(pl.multiple_of(b * QB, QB), QB)
    at = pl.ds(start, width)
    mask = jnp.concatenate([bias[0:width, :]] * 2, axis=1)
    pairs = []
    for p in range(GROUP):
        lanes = slice(LANES * p, LANES * p + LANES)
        place = b * PAIRS + GROUP * group + p
        queries = head_masked(q[rows, lanes] * 0.125)
        grads = head_masked(da[rows, lanes])
        keys, values = k[at, lanes], v[at, lanes]
        scores = mm(keys, queries, NT)
        dweight = mm(values, grads, NT)
        pairs.append((lanes, place, queries, grads, keys, scores, dweight))
    later = []
    for lanes, place, queries, grads, keys, scores, dweight in pairs:
        highest = stats[place, 0:1, :]
        inverse = stats[place, 1:2, :]
        weight = jnp.exp(scores + mask - highest) * inverse
        inner_sum = total(fold8(weight * dweight))
        dvalues[at, lanes] += mm(weight.astype(BF16), grads, NN)
        dscore = (weight * (dweight - inner_sum)).astype(BF16)
        later.append((lanes, queries, keys, dscore))
    for lanes, queries, keys, dscore in later:
        dkeys[at, lanes] += mm(dscore, queries, NN)
        both = mm(keys, dscore, TN)
        dq[rows, lanes] = (pick_heads(both) * 0.125).T.astype(BF16)


def attend_back_kernel(group, windows, qkv, da_in, stats, query_ids, dqkv, *refs):
    q, k, v, da, out, dkeys, dvalues, bias, key_ids, own = refs
    rows = q.shape[0]
    blocks = rows // QB
    lanes = slice(GROUP_LANES * group, GROUP_LANES * group + GROUP_LANES)
    coming = [pltpu.make_async_copy(da_in.at[:, lanes], da, own.at[3])]
    for third, target in enumerate((q, k, v)):
        first = LANES * PAIRS * third + GROUP_LANES * group
        source = qkv.at[:, first : first + GROUP_LANES]
        coming.append(pltpu.make_async_copy(source, target, own.at[third]))
    fetch(coming)
    dkeys[...] = jnp.zeros_like(dkeys)
    dvalues[...] = jnp.zeros_like(dvalues)
    spread_ids(query_ids, key_ids)
    settle(coming)
    dq = out.at[:, 0:GROUP_LANES]

    def one_block(b, carry):
        start = pl.multiple_of(windows[0, b], SUB)
        for index, width in enumerate(CLASSES):

            @pl.when(windows[1, b] == index)
            def _(width=width):
                mask_bias(start, width, b, key_ids, query_ids, bias)
                parts = (q, k, v, da, stats, dq, dkeys, dvalues, bias)
                attend_back_block(b, start, width, group, parts)

        return carry

    lax.fori_loop(0, blocks, one_block, 0)
    going = []
    for i in range(rows // 256):
        at = slice(256 * i, 256 * i + 256)
        out[at, GROUP_LANES : 2 * GROUP_LANES] = dkeys[at, :].astype(BF16)
        out[at, 2 * GROUP_LANES :] = dvalues[at, :].astype(BF16)
        going.append(pltpu.make_async_copy(out.at[at, :], dqkv.at[at, :], own.at[i]))
        going[-1].start()
    settle(going)


def attend_back(group, windows, qkv, da, stats, query_ids):
    rows = qkv.shape[0]
    part = lambda kind: pltpu.VMEM((rows, GROUP_LANES), kind)
    return pl.pallas_call(
        partial(attend_back_kernel, group),
        out_shape=shape((rows, 3 * GROUP_LANES), BF16),
        in_specs=[smem(), hbm(), hbm(), vmem(), vmem()],
        out_specs=hbm(),
        scratch_shapes=[
            part(BF16),
            part(BF16),
            part(BF16),
            part(BF16),
            pltpu.VMEM((rows, 3 * GROUP_LANES), BF16),
            part(F32),
            part(F32),
            pltpu.VMEM((CLASSES[-1], QB), F32),
            pltpu.VMEM((rows, QB), F32),
            dma(4),
        ],
        compiler_params=pltpu.CompilerParams(vmem_limit_bytes=32 * MEGA),
        cost_estimate=cost(3 * rows * rows * rows, 14 * rows * rows, 4 * rows * rows),
        name="attend_backward",
    )(windows, qkv, da, stats, query_ids)


def put_qkv_grad(n1, dqkv, w, spots):
    for c in range(3):
        grad = mm(n1[:, 256 * c : 256 * c + 256], dqkv[...], TN)
        for r in range(SUB):
            d, rt = (SUB * c + r) // QKV_RT, (SUB * c + r) % QKV_RT
            place = spots[rt, d]
            for index in range(ATT_PART):
                tile = grad[SUB * r : SUB * r + SUB, LANES * index : LANES * index + LANES]
                w[rt, place, index] = tile.astype(BF16)


def put_wo_grad(gwo, w, spots):
    for h in range(2):
        for i in range(WO_BLOCKS):
            w[h, spots[h, QKV_BLOCKS + i], 0:ATT_PART] = gwo[h, i]


def weight_grad_kernel(me_ref, n1_in, dqkv_in, gwo_in, *refs):
    leaving, (w, spots, n1, dqkv, gwo, sems, own) = refs[:4], refs[4:]
    coming = [
        pltpu.make_async_copy(n1_in, n1, own.at[0]),
        pltpu.make_async_copy(dqkv_in, dqkv, own.at[1]),
        pltpu.make_async_copy(gwo_in, gwo, own.at[2]),
    ]
    fetch(coming)
    fill_spots(me_ref[0], spots)
    settle(coming)
    put_wo_grad(gwo, w, spots)
    put_qkv_grad(n1, dqkv, w, spots)
    copies = leaving_slots(leaving, w, sems)
    fetch(copies)
    settle(copies)


def weight_grad(me, n1, dqkv, gwo):
    rows, width = n1.shape
    half = shape((HALF_BLOCKS, ATT_PART, SUB, LANES), BF16)
    return pl.pallas_call(
        weight_grad_kernel,
        out_shape=(half,) * 4,
        in_specs=[smem()] + [hbm()] * 3,
        out_specs=(hbm(),) * 4,
        scratch_shapes=[
            slots_scratch(ATT_PART),
            spots_scratch(),
            pltpu.VMEM((rows, width), BF16),
            pltpu.VMEM(dqkv.shape, BF16),
            pltpu.VMEM(gwo.shape, BF16),
            dma(4),
            dma(3),
        ],
        compiler_params=pltpu.CompilerParams(vmem_limit_bytes=20 * MEGA),
        cost_estimate=cost(3 * rows * width * width, 10 * rows * width),
        name="qkv_weight_grad",
    )(me, n1, dqkv, gwo)


def qkv_back_kernel(
    me_ref, tokens_in, n1_in, dx1_in, dqkv0_in, dqkv1_in, small, proj, mlp, gwo_in, *refs
):
    arriving, refs = refs[:8], refs[8:]
    dx_out, *leaving = refs[:5]
    w, gw, weight, spots, gwo, tokens, n1, dx1, dqkv0, dqkv1, dn, dx, sums, table = refs[5:19]
    sems, out_sems, own = refs[19:]
    rows = tokens.shape[0]
    tiles = rows // TALL

    def tile_copy(source, target, t, k):
        at = pl.ds(pl.multiple_of(TALL * t, TALL), TALL)
        return pltpu.make_async_copy(source.at[at, :], target.at[at, :], own.at[k, t])

    for t in range(tiles):
        tile_copy(dqkv0_in, dqkv0, t, 0).start()
        tile_copy(dqkv1_in, dqkv1, t, 1).start()
    weights = arriving_slots(arriving, w, sems)
    fetch(weights)
    for t in range(tiles):
        tile_copy(tokens_in, tokens, t, 2).start()
        tile_copy(dx1_in, dx1, t, 3).start()
    late = [
        pltpu.make_async_copy(n1_in, n1, own.at[4, 0]),
        pltpu.make_async_copy(gwo_in, gwo, own.at[4, 1]),
    ]
    fetch(late)
    sums[...] = jnp.zeros_like(sums)
    gain = row_of(small, G1, 6)
    fill_spots(me_ref[0], spots)
    settle(weights)
    columns = qkv_group(0) + qkv_group(1)
    lay_matrix(w, spots, "qkv", QKV_BLOCKS, 0, QKV_RT, columns, weight)

    def contract(t):
        at = pl.ds(pl.multiple_of(TALL * t, TALL), TALL)
        for g, (source, part) in enumerate(((dqkv0_in, dqkv0), (dqkv1_in, dqkv1))):
            tile_copy(source, part, t, g).wait()
            lanes = slice(384 * g, 384 * g + 384)
            sums[16:24, lanes] += fold8(part[at, 0:384].astype(F32))
            sums[24:32, lanes] += fold8(part[at, 768:1152].astype(F32))
        both = jnp.concatenate([dqkv0[at, :], dqkv1[at, :]], axis=1)
        dn[at, :] = mm(both, weight[...], NT)

    def finish(t):
        tile_copy(tokens_in, tokens, t, 2).wait()
        tile_copy(dx1_in, dx1, t, 3).wait()
        for half in range(2):
            at = pl.ds(pl.multiple_of(TALL * t + TALL // 2 * half, TALL // 2), TALL // 2)
            unit, inverse = normalized(tokens[at, :].astype(F32))
            grad = dn[at, :]
            dx[at, :] = dx1[at, :] + norm_pullback(unit, inverse, grad, gain)
            sums[0:8, :] += fold8(grad * unit)
            sums[8:16, :] += fold8(grad)
        tile_copy(dx, dx_out, t, 3).start()

    def one_tile(t, carry):
        contract(t)
        finish(t - 1)
        return carry

    contract(0)
    lax.fori_loop(1, tiles, one_tile, 0)
    finish(tiles - 1)

    def put_table(owner, *places):
        table[...] = jnp.zeros_like(table)
        for place, values in places:
            if values.shape[1] == LANES:
                table[place : place + values.shape[0], :] = values
            else:
                put_row(table, place, values)
        for h in range(2):
            gw[h, spots[h, owner], ATT_PART] = table[SUB * h : SUB * h + SUB, :].astype(BF16)

    put_table(
        OWNERS[0], (0, total(sums[0:8, :])), (6, total(sums[8:16, :])), (12, mlp[0:12, :])
    )
    put_table(OWNERS[1], (0, mlp[12:36, :]))
    put_table(OWNERS[2], (0, total(sums[16:24, :])), (6, total(sums[24:32, :])))
    put_table(OWNERS[3], (0, proj[...]), (12, mlp[36:48, :]))
    settle(late)
    put_wo_grad(gwo, gw, spots)
    put_qkv_grad(n1, dqkv1, gw, spots)
    copies = leaving_slots(leaving, gw, out_sems)
    fetch(copies)
    for t in range(tiles):
        tile_copy(dx, dx_out, t, 3).wait()
    settle(copies)


def qkv_back(me, tokens, n1, dx1, dqkv0, dqkv1, small, proj, mlp, gwo, att):
    rows, width = tokens.shape
    tiles = ATT_PART + 1
    half = shape((HALF_BLOCKS, tiles, SUB, LANES), BF16)
    row = lambda kind: pltpu.VMEM((rows, width), kind)
    return pl.pallas_call(
        qkv_back_kernel,
        out_shape=(shape((rows, width), F32), half, half, half, half),
        in_specs=[smem()] + [hbm()] * 5 + [vmem()] * 3 + [hbm()] * 9,
        out_specs=(hbm(),) * 5,
        scratch_shapes=[
            slots_scratch(ATT_SENT),
            slots_scratch(tiles),
            pltpu.VMEM((width, 3 * width), BF16),
            spots_scratch(),
            pltpu.VMEM(gwo.shape, BF16),
            row(BF16),
            row(BF16),
            row(F32),
            pltpu.VMEM(dqkv0.shape, BF16),
            pltpu.VMEM(dqkv1.shape, BF16),
            row(F32),
            row(F32),
            pltpu.VMEM((32, width), F32),
            pltpu.VMEM((2 * SUB, LANES), F32),
            dma(8),
            dma(4),
            pltpu.SemaphoreType.DMA((5, rows // TALL)),
        ],
        compiler_params=pltpu.CompilerParams(vmem_limit_bytes=46 * MEGA),
        cost_estimate=cost(9 * rows * width * width, 30 * rows * width),
        name="qkv_backward",
    )(me, tokens, n1, dx1, dqkv0, dqkv1, small, proj, mlp, gwo, *att)


X, C, Z1, Z0, Y = 16, 8, 4, 2, 1


def exchange(values, bit):
    return lax.ppermute(values, AXES, [(d, d ^ bit) for d in range(BLOCKS)])


def shifted(values, by):
    pairs = [(d, d + by) for d in range(BLOCKS) if 0 <= d + by < BLOCKS]
    return lax.ppermute(values, AXES, pairs)


def together(*values):
    return lax.optimization_barrier(values)


def along_z(first, second, received):
    return (
        jnp.stack([first] + [r[0] for r in received]),
        jnp.stack([second] + [r[1] for r in received]),
    )


def joined(own, received):
    return jnp.concatenate([own, received])


def sum_terms(terms):
    summed = terms[0].astype(F32)
    for term in terms[1:]:
        summed = summed + term.astype(F32)
    return summed


def kept(terms):
    return [t[: t.shape[0] // 2] for t in terms]


def z_part(first, second, k):
    return jnp.stack([sum_terms([t[k] for t in terms]) for terms in (first, second)])


def sent(terms):
    return sum_terms([t[t.shape[0] // 2 :] for t in terms]).astype(BF16)


def attention_amounts(width):
    return [width, width, 3 * width * width, width, width, width * width, width, width]


def feedforward_amounts(width):
    return [width, width, width * FF, FF, FF * width, width, width]


def pieces_of(vector, amounts):
    out, offset = [], 0
    for amount in amounts:
        out.append(vector[offset : offset + amount])
        offset += amount
    return out


def tiles_by_column(matrix, blocks, rt):
    ct = matrix.shape[1] // LANES
    return matrix.reshape(blocks, rt, SUB, ct, LANES).transpose(0, 3, 1, 2, 4)


def tiles_by_row(matrix, blocks, rt):
    ct = matrix.shape[1] // LANES
    return matrix.reshape(blocks, rt, SUB, ct, LANES).transpose(0, 1, 3, 2, 4)


def gather_plainly(params, att_rows, width):
    rounded = params.astype(BF16)
    att = lax.all_gather(rounded[:att_rows], AXES, axis=0, tiled=True).reshape(-1)
    mlp = lax.all_gather(rounded[att_rows:], AXES, axis=0, tiled=True).reshape(-1)
    g1, c1, wqkv, bq, bv, wo, bo, s1 = pieces_of(att, attention_amounts(width))
    g2, c2, w1, b1, w2, b2, s2 = pieces_of(mlp, feedforward_amounts(width))
    tile = (SUB, LANES)
    att = jnp.concatenate(
        [
            tiles_by_column(wqkv.reshape(width, -1), QKV_BLOCKS, QKV_RT).reshape((-1, 36) + tile),
            tiles_by_row(wo.reshape(width, -1), WO_BLOCKS, WO_RT).reshape((-1, 36) + tile),
        ]
    )
    mlp = jnp.concatenate(
        [
            tiles_by_column(w1.reshape(width, -1), W1_BLOCKS, W1_RT).reshape((-1, 72) + tile),
            tiles_by_row(w2.reshape(FF, -1), W2_BLOCKS, W2_RT).reshape((-1, 72) + tile),
        ]
    )
    vectors = jnp.concatenate([g1, c1, bq, bv, bo, s1, g2, c2, b1, b2, s2]).astype(F32)
    lines = vectors.reshape(-1, LANES)
    sent = jnp.zeros((BLOCKS, 2 * SUB, LANES), F32)
    for owner, place, first, count in (
        (OWNERS[0], 0, G1, 12),
        (OWNERS[0], 12, G2, 12),
        (OWNERS[1], 0, B1, 24),
        (OWNERS[2], 0, BQ, 12),
        (OWNERS[3], 0, BO, 12),
        (OWNERS[3], 12, B2, 12),
    ):
        sent = sent.at[owner, place : place + count].set(lines[first : first + count])
    sent = sent.astype(BF16).reshape((BLOCKS, 2, 1) + tile)
    att = [jnp.concatenate([att[:, 18 * h : 18 * h + 18], sent[:, h]], axis=1) for h in range(2)]
    return by_slot(*att), by_slot(mlp[:, :36], mlp[:, 36:])


def by_slot(first, second):
    halves = (first, second)
    return [
        jnp.stack([halves[i // 4][slot] for slot in SLOTS[i // 4][i % 4 * 8 : i % 4 * 8 + 8]])
        for i in range(8)
    ]


def from_slots(buffers):
    halves = []
    for h in range(2):
        slots = jnp.concatenate(buffers[2 * h : 2 * h + 2])
        halves.append(jnp.stack([slots[spot(h, d)] for d in range(BLOCKS)]))
    return halves


def reduce_plainly(gatt0, gatt1, gmlp, att_rows, mlp_rows, width, devices):
    groups = [from_slots(gatt0), from_slots(gatt1)]
    vectors = jnp.concatenate([groups[1][h][:, ATT_PART:] for h in range(2)], axis=1)
    vectors = vectors.astype(F32).reshape(BLOCKS, 2 * SUB, LANES)

    def matrix(name, first, last, rt_count, ct_count):
        rows = []
        for rt in range(rt_count):
            places = [part_place(name, rt, ct) for ct in range(ct_count)]
            rows.append(jnp.stack([groups[g][h][first:last, i] for g, h, i in places], axis=2))
        return jnp.stack(rows, axis=1).astype(F32).reshape(-1)

    wqkv = matrix("qkv", 0, QKV_BLOCKS, QKV_RT, QKV_CT)
    wo = matrix("wo", QKV_BLOCKS, BLOCKS, WO_RT, WO_CT)
    mlp = jnp.concatenate(from_slots(gmlp), axis=1).astype(F32)
    five = lambda v, dims: v.reshape((v.shape[0],) + dims + (SUB, LANES))
    w1 = five(mlp[:W1_BLOCKS], (W1_CT, W1_RT)).transpose(0, 2, 3, 1, 4).reshape(-1)
    w2 = five(mlp[W1_BLOCKS:], (W2_RT, W2_CT)).transpose(0, 1, 3, 2, 4).reshape(-1)
    line = lambda owner, first, count: vectors[owner, first : first + count].reshape(-1)
    att = [line(OWNERS[0], 0, 12), wqkv, line(OWNERS[2], 0, 12), wo, line(OWNERS[3], 0, 12)]
    mlp = [line(OWNERS[0], 12, 12), w1, line(OWNERS[1], 0, 24), w2, line(OWNERS[3], 12, 12)]

    def lay(parts, rows):
        vector = jnp.concatenate(parts)
        vector = jnp.pad(vector, (0, devices * rows * LANES - vector.shape[0]))
        return vector.reshape(devices, rows, LANES)

    whole = jnp.concatenate([lay(att, att_rows), lay(mlp, mlp_rows)], axis=1)
    return lax.psum_scatter(whole.reshape(-1, LANES), AXES, scatter_dimension=0, tiled=True)


def key_windows(segments, real):
    length = segments.shape[0]
    position = jnp.arange(length, dtype=jnp.int32)
    ids = jnp.where(real, segments, length + position)
    first = segments[0::QB]
    final = segments[QB - 1 :: QB]
    begin = jnp.sum((segments[None, :] < first[:, None]).astype(jnp.int32), axis=1)
    begin = jnp.where(real[0::QB], begin, position[0::QB])
    end = jnp.sum(((segments[None, :] <= final[:, None]) & real[None, :]).astype(jnp.int32), axis=1)
    end = jnp.where(real[QB - 1 :: QB], end, position[QB - 1 :: QB] + 1)
    begin = begin // SUB * SUB
    need = end - begin
    kind = sum((need > width).astype(jnp.int32) for width in CLASSES[:-1])
    widths = sum(
        jnp.where(kind == i, width, 0) for i, width in enumerate(CLASSES)
    )
    begin = jnp.minimum(begin, length - widths)
    chunks = (begin + widths + QB - 1) // QB
    return ids, jnp.stack([begin, kind, chunks]).astype(jnp.int32)


def local(tokens, cotangent, segment_ids, pad_mask, lengths, params):
    rows, width = tokens.shape
    wide, narrow = lax.axis_size("wide"), lax.axis_size("narrow")
    devices = wide * narrow
    att_count = 4 * width * width + 6 * width
    att_rows = (att_count // LANES + devices - 1) // devices
    mlp_rows = params.shape[0] - att_rows
    paired = (wide, narrow) == (4, 8)
    scale = 1.0 / math.sqrt(rows * devices)

    position = jnp.arange(rows, dtype=jnp.int32)
    real = (pad_mask > 0) & (position < lengths[0])
    ids, windows = key_windows(segment_ids, real)
    query_ids = ids.astype(F32).reshape(rows // QB, QB)

    if not paired:
        me = jnp.zeros((1,), jnp.int32)
        att, mlp = gather_plainly(params, att_rows, width)
        n1, qkv, small = project_qkv(me, tokens, att)
        mixed, x1, branch, n2, dm, stats, gb2 = attend(
            me, windows, qkv, tokens, cotangent, query_ids, small, att
        )
        u, dz, gb1, *gmlp = feed_forward(me, n2, dm, small, mlp)
        output, gs2 = feed_forward_out(me, u, x1, cotangent, small, mlp)
        dx1, da, gwo0, gwo1, others = split(
            me, dz, x1, cotangent, branch, mixed, small, mlp, att
        )
        small_mlp = jnp.concatenate([others[:12], gb1, gb2, gs2])
        small_proj = others[12:]
        dqkv0 = attend_back(0, windows, qkv, da, stats, query_ids)
        dqkv1 = attend_back(1, windows, qkv, da, stats, query_ids)
        gatt0 = weight_grad(me, n1, dqkv0, gwo0)
        grad_input, *gatt1 = qkv_back(
            me, tokens, n1, dx1, dqkv0, dqkv1, small, small_proj, small_mlp, gwo1, att
        )
        owned = reduce_plainly(gatt0, gatt1, gmlp, att_rows, mlp_rows, width, devices)
        return output, grad_input, owned * scale

    me = lax.axis_index(AXES).astype(jnp.int32).reshape(1)
    tails = jnp.concatenate([params[att_rows - ATT_BEFORE : att_rows], params[-MLP_BEFORE:]])
    heads = jnp.concatenate([params[:ATT_AFTER], params[att_rows : att_rows + MLP_AFTER]])
    tails, heads = shifted(tails.astype(BF16), 1), shifted(heads.astype(BF16), -1)
    att_own, mlp_own = pack(me, params, tails, heads, att_rows)

    got = [exchange(att_own, k * Z0) for k in range(1, 4)]
    a, b = along_z(att_own[0], att_own[1], got)
    a, b, mlp_own, windows, query_ids = together(a, b, mlp_own, windows, query_ids)
    ax, by = exchange(a, X), exchange(b, Y)
    z1, z3 = exchange(mlp_own, Z0), exchange(mlp_own, 3 * Z0)
    a, b = joined(a, ax), joined(b, by)
    a, b, z1, z3, mlp_own = together(a, b, z1, z3, mlp_own)
    ay, bx = exchange(a, Y), exchange(b, X)
    ac, bc = exchange(a, C), exchange(b, C)
    z2 = exchange(mlp_own, 2 * Z0)
    m, n = along_z(mlp_own[0], mlp_own[1], [z1, z2, z3])
    ay, bx, ac, bc, m, n = together(ay, bx, ac, bc, m, n)
    ayc, bxc = exchange(ay, C), exchange(bx, C)
    att = together(a, ay, ac, ayc, b, bx, bc, bxc, m, n, tokens)
    *att, m, n, tokens_now = att
    mx, ny = exchange(m, X), exchange(n, Y)
    n1, qkv, small = project_qkv(me, tokens_now, att)
    m, n = joined(m, mx), joined(n, ny)
    m, n, qkv = together(m, n, qkv)
    my, nx = exchange(m, Y), exchange(n, X)
    mc, nc = exchange(m, C), exchange(n, C)
    mixed, x1, branch, n2, dm, stats, gb2 = attend(
        me, windows, qkv, tokens, cotangent, query_ids, small, att
    )
    m, n, my, nx, mc, nc, n2 = together(m, n, my, nx, mc, nc, n2)
    myc, nxc = exchange(my, C), exchange(nx, C)
    mlp = (m, my, mc, myc, n, nx, nc, nxc)

    u, dz, gb1, *gmlp = feed_forward(me, n2, dm, small, mlp)

    mc, nc = exchange(gmlp[1], C), exchange(gmlp[3], C)
    output, gs2 = feed_forward_out(me, u, x1, cotangent, small, mlp)
    mc, nc, dz, gs2 = together(mc, nc, dz, gs2)
    m, n = [gmlp[0], mc], [gmlp[2], nc]
    my, nx, dz = together(sent(m), sent(n), dz)
    my, nx = exchange(my, Y), exchange(nx, X)
    dx1, da, gwo0, gwo1, others = split(
        me, dz, x1, cotangent, branch, mixed, small, mlp, att
    )
    dqkv0 = attend_back(0, windows, qkv, da, stats, query_ids)
    gatt0 = weight_grad(me, n1, dqkv0, gwo0)
    my, nx, da, *gatt0 = together(my, nx, da, *gatt0)
    m, n = kept(m) + [my], kept(n) + [nx]
    mx, ny, da, *gatt0 = together(sent(m), sent(n), da, *gatt0)
    mx, ny = exchange(mx, X), exchange(ny, Y)
    ac, bc = exchange(gatt0[1], C), exchange(gatt0[3], C)
    dqkv1 = attend_back(1, windows, qkv, da, stats, query_ids)
    mx, ny, ac, bc, dqkv1 = together(mx, ny, ac, bc, dqkv1)
    m, n = kept(m) + [mx], kept(n) + [ny]
    z1, z2, z3 = [z_part(m, n, k).astype(BF16) for k in range(1, 4)]
    a, b = [gatt0[0], ac], [gatt0[2], bc]
    ay, bx, z1, z2, z3, dqkv1 = together(sent(a), sent(b), z1, z2, z3, dqkv1)
    z1, z2 = exchange(z1, Z0), exchange(z2, 2 * Z0)
    ay, bx = exchange(ay, Y), exchange(bx, X)
    small_mlp = jnp.concatenate([others[:12], gb1, gb2, gs2])
    grad_input, *gatt1 = qkv_back(
        me, tokens, n1, dx1, dqkv0, dqkv1, small, others[12:], small_mlp, gwo1, att
    )
    ay, bx, z1, z2, *gatt1 = together(ay, bx, z1, z2, *gatt1)
    a, b = kept(a) + [ay], kept(b) + [bx]
    ax, by, c1, d1, z3 = together(sent(a), sent(b), gatt1[1], gatt1[3], z3)
    c1, d1 = exchange(c1, C), exchange(d1, C)
    ax, by = exchange(ax, X), exchange(by, Y)
    z3a = exchange(z3[0], 3 * Z0)
    c, d = [gatt1[0], c1], [gatt1[2], d1]
    a, b = kept(a) + [ax], kept(b) + [by]
    sends = [z_part(a, b, k).astype(BF16) for k in range(1, 4)]
    cy, dx, z3a, z3, *sends = together(sent(c), sent(d), z3a, z3, *sends)
    cy, dx = exchange(cy, Y), exchange(dx, X)
    got = [exchange(part, (k + 1) * Z0) for k, part in enumerate(sends)]
    c, d = kept(c) + [cy], kept(d) + [dx]
    cx, dy, z3, *got = together(sent(c), sent(d), z3, *got)
    z3b = exchange(z3[1], 3 * Z0)
    group0 = sum_terms([z_part(a, b, 0)] + got)
    cx, dy = exchange(cx, X), exchange(dy, Y)
    c, d = kept(c) + [cx], kept(d) + [dy]
    m_own = sum_terms([z_part(m, n, 0), z1, z2, jnp.stack([z3a, z3b])])
    sends = [z_part(c, d, k).astype(BF16) for k in range(1, 4)]
    group0, m_own, *sends = together(group0, m_own, *sends)
    got = [exchange(part, (k + 1) * Z0) for k, part in enumerate(sends)]
    group1 = sum_terms([z_part(c, d, 0)] + got)
    mine, to_before, to_after = spread(me, group0, group1, m_own, att_rows, mlp_rows, scale)
    grad_params = close(mine, shifted(to_after, 1), shifted(to_before, -1), att_rows)
    return output, grad_input, grad_params


def solution(mesh):
    return jax.shard_map(
        local,
        mesh=mesh,
        in_specs=(
            P(AXES, None),
            P(AXES, None),
            P(AXES),
            P(AXES),
            P(AXES),
            P(AXES, None),
        ),
        out_specs=(P(AXES, None), P(AXES, None), P(AXES, None)),
        check_vma=False,
    )
```

```python
import math
from functools import partial

import jax
import jax.numpy as jnp
from jax import lax
from jax.experimental import pallas as pl
from jax.experimental.pallas import tpu as pltpu
from jax.sharding import PartitionSpec as P

FF = 3072
HEADS = 12
EPSILON = 1e-06
NEGATIVE = -1e30
AXES = ("wide", "narrow")
LANES = 128
SUB = 16
QB = 128
MEGA = 1 << 20
GRANT = 58 * MEGA
F32 = jnp.float32
BF16 = jnp.bfloat16

BLOCKS = 32
QKV_BLOCKS, QKV_RT, QKV_CT = 24, 2, 18
WO_BLOCKS, WO_RT, WO_CT = 8, 6, 6
W1_BLOCKS, W1_RT, W1_CT = 16, 3, 24
W2_BLOCKS, W2_RT, W2_CT = 16, 12, 6
ATT_HALF, MLP_HALF = 18, 36
ATT_SENT = ATT_HALF + 1
ATT_PART = 9
HALF_BLOCKS = BLOCKS // 2
CHUNK = 768
CHUNKS = FF // CHUNK

G1, C1, BQ, BV, BO, S1 = 0, 6, 12, 18, 24, 30
G2, C2, B1, B2, S2 = 36, 42, 48, 72, 78
SMALL = 88

NT = (((1,), (1,)), ((), ()))
NN = (((1,), (0,)), ((), ()))
TN = (((0,), (0,)), ((), ()))


def mm(lhs, rhs, dims):
    return lax.dot_general(lhs, rhs, dims, preferred_element_type=F32)


def row_of(ref, first, count):
    return jnp.concatenate([ref[first + k : first + k + 1, :] for k in range(count)], axis=1)


def put_row(ref, first, values):
    for k in range(values.shape[1] // LANES):
        ref[first + k : first + k + 1, :] = values[:, k * LANES : (k + 1) * LANES]


def fold8(values):
    rows, columns = values.shape
    return jnp.sum(values.reshape(rows // 8, 8, columns), axis=0)


def total(values):
    return jnp.sum(values, axis=0, keepdims=True)


def vmem():
    return pl.BlockSpec(memory_space=pltpu.VMEM)


def smem():
    return pl.BlockSpec(memory_space=pltpu.SMEM)


def hbm():
    return pl.BlockSpec(memory_space=pltpu.HBM)


def shape(dims, kind):
    return jax.ShapeDtypeStruct(dims, kind)


def cost(flops, moved, exps=0):
    return pl.CostEstimate(flops=int(flops), transcendentals=int(exps), bytes_accessed=int(moved))


def normalized(values):
    center = values - jnp.mean(values, axis=-1, keepdims=True)
    inverse = lax.rsqrt(jnp.mean(center * center, axis=-1, keepdims=True) + EPSILON)
    return center * inverse, inverse


def norm_pullback(unit, inverse, grad, gain):
    scaled = grad * gain
    first = jnp.mean(scaled, axis=-1, keepdims=True)
    second = jnp.mean(scaled * unit, axis=-1, keepdims=True)
    return inverse * (scaled - first - unit * second)


def gelu_pair(z):
    magnitude = jnp.abs(z)
    t = 1.0 / (1.0 + (0.3275911 * math.sqrt(0.5)) * magnitude)
    density = jnp.exp(z * z * -0.5)
    tail = 0.5 * 1.061405429
    tail = tail * t + 0.5 * -1.453152027
    tail = tail * t + 0.5 * 1.421413741
    tail = tail * t + 0.5 * -0.284496736
    tail = tail * t + 0.5 * 0.254829592
    tail = tail * t * density
    cumulative = jnp.where(z < 0, tail, 1.0 - tail)
    return z * cumulative, cumulative + z * density * (1.0 / math.sqrt(2.0 * math.pi))


def fetch(copies):
    for copy in copies:
        copy.start()


def settle(copies):
    for copy in copies:
        copy.wait()


ATT_BEFORE, ATT_AFTER = 64, 32
MLP_BEFORE, MLP_AFTER = 64, 40


def window_offsets(me, att_rows, mlp_rows):
    att = ATT_BEFORE + 12 + me * (576 - att_rows) + jnp.where(me < QKV_BLOCKS, 0, 12)
    mlp = MLP_BEFORE + 12 + me * (1152 - mlp_rows) + jnp.where(me < W1_BLOCKS, 0, 24)
    return att, mlp


def each_tile(me, act):
    for name, blocks, rt_count, ct_count, mine in (
        ("qkv", QKV_BLOCKS, QKV_RT, QKV_CT, me < QKV_BLOCKS),
        ("wo", WO_BLOCKS, WO_RT, WO_CT, me >= QKV_BLOCKS),
        ("w1", W1_BLOCKS, W1_RT, W1_CT, me < W1_BLOCKS),
        ("w2", W2_BLOCKS, W2_RT, W2_CT, me >= W1_BLOCKS),
    ):

        @pl.when(mine)
        def _(name=name, rt_count=rt_count, ct_count=ct_count):
            for ct in range(ct_count):
                for rt in range(rt_count):
                    act(name, rt, ct, rt * SUB * ct_count + ct, ct_count)


def half_place(name, rt, ct):
    if name == "qkv":
        return ct // 9, ct % 9 * QKV_RT + rt
    if name == "wo":
        return rt // 3, rt % 3 * WO_CT + ct
    if name == "w1":
        return ct // 12, ct % 12 * W1_RT + rt
    return rt // 6, rt % 6 * W2_CT + ct


def part_place(name, rt, ct):
    if name == "qkv":
        return ct % 6 // 3, rt, ct // 6 * 3 + ct % 3
    place = rt * WO_CT + ct
    return place // 18, place // ATT_PART % 2, place % ATT_PART


def qkv_group(g):
    return [6 * third + 3 * g + i for third in range(3) for i in range(3)]


def small_rows(me, act):
    @pl.when(me == 0)
    def _():
        act("att", True, 12, G1)
        act("mlp", True, 12, G2)

    @pl.when(me == QKV_BLOCKS - 1)
    def _():
        act("att", False, 12, BQ)

    @pl.when(me == W1_BLOCKS - 1)
    def _():
        act("mlp", False, 24, B1)

    @pl.when(me == BLOCKS - 1)
    def _():
        act("att", False, 12, BO)
        act("mlp", False, 12, B2)


OWNERS = (0, W1_BLOCKS - 1, QKV_BLOCKS - 1, BLOCKS - 1)


def sent_rows(kind, first):
    return 12 if kind == "mlp" and first in (G2, B2) else 0


def pack_kernel(att_rows, me_ref, own, tails, heads, att, mlp, win_a, win_m, table):
    me = me_ref[0]
    mlp_rows = own.shape[0] - att_rows
    win_a[0:ATT_BEFORE, :] = tails[0:ATT_BEFORE, :].astype(F32)
    win_a[ATT_BEFORE : ATT_BEFORE + att_rows, :] = own[0:att_rows, :]
    win_a[ATT_BEFORE + att_rows :, :] = heads[0:ATT_AFTER, :].astype(F32)
    win_m[0:MLP_BEFORE, :] = tails[ATT_BEFORE:, :].astype(F32)
    win_m[MLP_BEFORE : MLP_BEFORE + mlp_rows, :] = own[att_rows:, :]
    win_m[MLP_BEFORE + mlp_rows :, :] = heads[ATT_AFTER:, :].astype(F32)
    att_off, mlp_off = window_offsets(me, att_rows, mlp_rows)

    def tile(name, rt, ct, first, stride):
        attention = name in ("qkv", "wo")
        window, out, off = (win_a, att, att_off) if attention else (win_m, mlp, mlp_off)
        values = window[pl.ds(off + first, SUB, stride=stride), :]
        out[half_place(name, rt, ct)] = values.astype(BF16)

    each_tile(me, tile)
    table[...] = jnp.zeros_like(table)

    def vector(kind, before, rows, first):
        window, off, size = (win_a, att_off, 576) if kind == "att" else (win_m, mlp_off, 1152)
        start = off - 12 if before else off + size
        place = sent_rows(kind, first)
        table[place : place + rows, :] = window[pl.ds(start, rows), :]

    small_rows(me, vector)
    att[0, ATT_HALF] = table[0:SUB, :].astype(BF16)
    att[1, ATT_HALF] = table[SUB : 2 * SUB, :].astype(BF16)


def pack(me, own, tails, heads, att_rows):
    mlp_rows = own.shape[0] - att_rows
    return pl.pallas_call(
        partial(pack_kernel, att_rows),
        out_shape=(
            shape((2, ATT_SENT, SUB, LANES), BF16),
            shape((2, MLP_HALF, SUB, LANES), BF16),
        ),
        in_specs=[smem(), vmem(), vmem(), vmem()],
        out_specs=(vmem(), vmem()),
        scratch_shapes=[
            pltpu.VMEM((ATT_BEFORE + att_rows + ATT_AFTER, LANES), F32),
            pltpu.VMEM((MLP_BEFORE + mlp_rows + MLP_AFTER, LANES), F32),
            pltpu.VMEM((2 * SUB, LANES), F32),
        ],
        name="pack",
    )(me, own, tails, heads)


def spread_kernel(
    att_rows, scale, me_ref, group0, group1, mlp, mine, to_before, to_after, win_a, win_m, table
):
    me = me_ref[0]
    mlp_rows = mine.shape[0] - att_rows
    att_off, mlp_off = window_offsets(me, att_rows, mlp_rows)
    win_a[...] = jnp.zeros_like(win_a)
    win_m[...] = jnp.zeros_like(win_m)

    def tile(name, rt, ct, first, stride):
        if name in ("qkv", "wo"):
            g, half, index = part_place(name, rt, ct)
            values = (group0, group1)[g][half, index]
            win_a[pl.ds(att_off + first, SUB, stride=stride), :] = values * scale
        else:
            values = mlp[half_place(name, rt, ct)]
            win_m[pl.ds(mlp_off + first, SUB, stride=stride), :] = values * scale

    each_tile(me, tile)
    for h in range(2):
        table[SUB * h : SUB * h + SUB, :] = group1[h, ATT_PART] * scale

    def vector(kind, before, rows, first):
        window, off, size = (win_a, att_off, 576) if kind == "att" else (win_m, mlp_off, 1152)
        start = off - 12 if before else off + size
        place = sent_rows(kind, first)
        window[pl.ds(start, rows), :] = table[place : place + rows, :]

    small_rows(me, vector)
    mine[0:att_rows, :] = win_a[ATT_BEFORE : ATT_BEFORE + att_rows, :]
    mine[att_rows:, :] = win_m[MLP_BEFORE : MLP_BEFORE + mlp_rows, :]
    to_before[0:ATT_BEFORE, :] = win_a[0:ATT_BEFORE, :]
    to_before[ATT_BEFORE:, :] = win_m[0:MLP_BEFORE, :]
    to_after[0:ATT_AFTER, :] = win_a[ATT_BEFORE + att_rows :, :]
    to_after[ATT_AFTER:, :] = win_m[MLP_BEFORE + mlp_rows :, :]


def spread(me, group0, group1, mlp, att_rows, mlp_rows, scale):
    return pl.pallas_call(
        partial(spread_kernel, att_rows, scale),
        out_shape=(
            shape((att_rows + mlp_rows, LANES), F32),
            shape((ATT_BEFORE + MLP_BEFORE, LANES), F32),
            shape((ATT_AFTER + MLP_AFTER, LANES), F32),
        ),
        in_specs=[smem(), vmem(), vmem(), vmem()],
        out_specs=(vmem(), vmem(), vmem()),
        scratch_shapes=[
            pltpu.VMEM((ATT_BEFORE + att_rows + ATT_AFTER, LANES), F32),
            pltpu.VMEM((MLP_BEFORE + mlp_rows + MLP_AFTER, LANES), F32),
            pltpu.VMEM((2 * SUB, LANES), F32),
        ],
        name="spread",
    )(me, group0, group1, mlp)


def close_kernel(att_rows, mine, below, above, out):
    rows = mine.shape[0]
    out[...] = mine[...]
    out[0:ATT_AFTER, :] += below[0:ATT_AFTER, :]
    out[att_rows : att_rows + MLP_AFTER, :] += below[ATT_AFTER:, :]
    out[att_rows - ATT_BEFORE : att_rows, :] += above[0:ATT_BEFORE, :]
    out[rows - MLP_BEFORE : rows, :] += above[ATT_BEFORE:, :]


def close(mine, below, above, att_rows):
    return pl.pallas_call(
        partial(close_kernel, att_rows),
        out_shape=shape(mine.shape, F32),
        in_specs=[vmem()] * 3,
        out_specs=vmem(),
        name="close",
    )(mine, below, above)


def spot(h, d):
    x, c, z, y = d >> 4, (d >> 3) & 1, (d >> 1) & 3, d & 1
    return c * 16 + (y * 8 + x * 4 if h == 0 else x * 8 + y * 4) + z


SLOTS = [sorted(range(BLOCKS), key=partial(spot, h)) for h in range(2)]


def fill_spots(me, spots):
    for h in range(2):
        mine = spot(h, me)
        for d in range(BLOCKS):
            spots[h, d] = jnp.bitwise_xor(mine, spot(h, d))


def slots_scratch(tiles):
    return pltpu.VMEM((2, BLOCKS, tiles, SUB, LANES), BF16)


def spots_scratch():
    return pltpu.SMEM((2, BLOCKS), jnp.int32)


def arriving_slots(buffers, w, sems):
    return [
        pltpu.make_async_copy(buffers[i], w.at[i // 4, pl.ds(i % 4 * 8, 8)], sems.at[i])
        for i in range(8)
    ]


def leaving_slots(buffers, w, sems):
    return [
        pltpu.make_async_copy(w.at[i // 2, pl.ds(i % 2 * 16, 16)], buffers[i], sems.at[i])
        for i in range(4)
    ]


def qkv_column(w, spots, ct):
    h, place = ct // 9, ct % 9 * QKV_RT
    tiles = [w[h, spots[h, d], place + rt] for d in range(QKV_BLOCKS) for rt in range(QKV_RT)]
    return jnp.concatenate(tiles, axis=0)


def wo_matrix(w, spots):
    columns = []
    for ct in range(WO_CT):
        tiles = [
            w[rt // 3, spots[rt // 3, QKV_BLOCKS + i] & 7, rt % 3 * WO_CT + ct]
            for i in range(WO_BLOCKS)
            for rt in range(WO_RT)
        ]
        columns.append(jnp.concatenate(tiles, axis=0))
    return jnp.concatenate(columns, axis=1)


def dma(count):
    return pltpu.SemaphoreType.DMA((count,))


def norm_rows(rows, gain, shift, source, target, step=256):
    def one(i, carry):
        at = pl.ds(pl.multiple_of(i * step, step), step)
        unit, _ = normalized(source[at, :].astype(F32))
        target[at, :] = (unit * gain + shift).astype(BF16)
        return carry

    lax.fori_loop(0, rows // step, one, 0)


def qkv_kernel(me_ref, tokens, *refs):
    buffers, (n1, qkv, small, w, spots, x, unit, triple, sems, own) = refs[:8], refs[8:]
    coming = pltpu.make_async_copy(tokens, x, own.at[0])
    coming.start()
    weights = arriving_slots(buffers, w, sems)
    fetch(weights)
    fill_spots(me_ref[0], spots)
    settle(weights)
    tables = [
        jnp.concatenate([w[h, spots[h, d], ATT_HALF] for h in range(2)], axis=0).astype(F32)
        for d in OWNERS
    ]
    small[G1 : G1 + 12, :] = tables[0][0:12]
    small[G2 : G2 + 12, :] = tables[0][12:24]
    small[B1 : B1 + 24, :] = tables[1][0:24]
    small[BQ : BQ + 12, :] = tables[2][0:12]
    small[BO : BO + 12, :] = tables[3][0:12]
    small[B2 : B2 + 12, :] = tables[3][12:24]
    small[SMALL - 4 :, :] = jnp.zeros((4, LANES), F32)
    coming.wait()
    norm_rows(x.shape[0], row_of(small, G1, 6), row_of(small, C1, 6), x, unit)
    going = [pltpu.make_async_copy(unit, n1, own.at[0])]
    going[0].start()
    bias = jnp.concatenate(
        [row_of(small, BQ, 6), jnp.zeros((1, 768), F32), row_of(small, BV, 6)], axis=1
    )
    for c in range(QKV_CT // 2):
        weight = jnp.concatenate([qkv_column(w, spots, 2 * c + i) for i in range(2)], axis=1)
        lanes = slice(256 * c, 256 * c + 256)
        triple[:, lanes] = (mm(unit[...], weight, NN) + bias[:, lanes]).astype(BF16)
        going.append(
            pltpu.make_async_copy(triple.at[:, lanes], qkv.at[:, lanes], own.at[1 + c])
        )
        going[-1].start()
    settle(going)


def project_qkv(me, tokens, att):
    rows, width = tokens.shape
    return pl.pallas_call(
        qkv_kernel,
        out_shape=(
            shape((rows, width), BF16),
            shape((rows, 3 * width), BF16),
            shape((SMALL, LANES), F32),
        ),
        in_specs=[smem(), hbm()] + [hbm()] * 8,
        out_specs=(hbm(), hbm(), vmem()),
        scratch_shapes=[
            slots_scratch(ATT_SENT),
            spots_scratch(),
            pltpu.VMEM((rows, width), BF16),
            pltpu.VMEM((rows, width), BF16),
            pltpu.VMEM((rows, 3 * width), BF16),
            dma(8),
            dma(1 + QKV_CT // 2),
        ],
        compiler_params=pltpu.CompilerParams(vmem_limit_bytes=GRANT),
        cost_estimate=cost(6 * rows * width * width, 12 * rows * width),
        name="qkv_forward",
    )(me, tokens, *att)


CLASSES = (128, 256, 320, 384, 448, 512, 768)


def head_masked(block):
    lane = lax.broadcasted_iota(jnp.int32, block.shape, 1)
    zero = jnp.zeros_like(block)
    return jnp.concatenate(
        [jnp.where(lane < 64, block, zero), jnp.where(lane >= 64, block, zero)], axis=0
    )


def pick_heads(both):
    return jnp.concatenate([both[0:64, 0:QB], both[64:128, QB : 2 * QB]], axis=0)


def pieces_of_window(width):
    return [slice(first, min(first + QB, width)) for first in range(0, width, QB)]


def spread_ids(query_ids, key_ids):
    for b in range(query_ids.shape[0]):
        row = jnp.broadcast_to(query_ids[b : b + 1, :], (QB, QB))
        key_ids[b * QB : (b + 1) * QB, :] = row.T


def mask_bias(start, width, b, key_ids, query_ids, bias):
    for piece in pieces_of_window(width):
        size = piece.stop - piece.start
        at = pl.ds(pl.multiple_of(start + piece.start, SUB), size)
        same = key_ids[at, :] == query_ids[pl.ds(b, 1), :]
        bias[piece, :] = jnp.where(same, 0.0, NEGATIVE)


PAIRS = HEADS // 2


def attend_block(b, start, width, qkv, mixed, stats, bias, scores):
    rows = pl.ds(pl.multiple_of(b * QB, QB), QB)
    pieces = pieces_of_window(width)
    for p in range(PAIRS):
        lanes, key_lanes, value_lanes = [
            slice(LANES * (PAIRS * third + p), LANES * (PAIRS * third + p + 1))
            for third in range(3)
        ]
        queries = head_masked(qkv[rows, lanes] * 0.125)
        highest = jnp.full((8, 2 * QB), NEGATIVE, F32)
        for piece in pieces:
            size = piece.stop - piece.start
            at = pl.ds(pl.multiple_of(start + piece.start, SUB), size)
            part = mm(qkv[at, key_lanes], queries, NT)
            part = part + jnp.concatenate([bias[piece, :]] * 2, axis=1)
            scores[p, piece, :] = part
            highest = jnp.maximum(highest, jnp.max(part.reshape(size // 8, 8, 2 * QB), axis=0))
        highest = jnp.max(highest, axis=0, keepdims=True)
        summed = jnp.zeros((8, 2 * QB), F32)
        both = jnp.zeros((LANES, 2 * QB), F32)
        for piece in pieces:
            size = piece.stop - piece.start
            at = pl.ds(pl.multiple_of(start + piece.start, SUB), size)
            raised = jnp.exp(scores[p, piece, :] - highest)
            summed = summed + fold8(raised)
            both = both + mm(qkv[at, value_lanes], raised.astype(BF16), TN)
        inverse = 1.0 / total(summed)
        mixed[rows, lanes] = pick_heads(both * inverse).T.astype(BF16)
        stats[b * PAIRS + p, 0:1, :] = highest
        stats[b * PAIRS + p, 1:2, :] = inverse


def wo_scratch():
    return pltpu.VMEM((2, WO_BLOCKS, ATT_SENT, SUB, LANES), BF16)


def wo_copies(buffers, w, sems, core, x):
    copies = []
    for y in range(2):
        source = buffers[2 * core + y].at[pl.ds(4 * x, 4)]
        copies.append(pltpu.make_async_copy(source, w.at[0, pl.ds(4 * y, 4)], sems.at[y]))
    copies.append(pltpu.make_async_copy(buffers[4 + 2 * core + x], w.at[1], sems.at[2]))
    return copies


def fetch_wo(me, buffers, w, spots, sems):
    fill_spots(me, spots)
    for h in range(2):
        for i in range(WO_BLOCKS):
            place = spot(h, jnp.bitwise_xor(me, QKV_BLOCKS + i) & 7)
            spots[h, QKV_BLOCKS + i] = (place >> (1 if h == 0 else 0)) & 4 | place & 3
    far = jnp.bitwise_xor(me, QKV_BLOCKS)
    for core in range(2):
        for x in range(2):

            @pl.when((far >> 3) == 2 * x + core)
            def _(core=core, x=x):
                fetch(wo_copies(buffers, w, sems, core, x))


def wait_wo(buffers, w, sems):
    settle(wo_copies(buffers, w, sems, 0, 0))


def attend_kernel(me_ref, windows, qkv, tokens, cot, query_ids, small, *refs):
    buffers, refs = refs[:8], refs[8:]
    mixed, x1, branch, n2, dm, stats, gb2 = refs[:7]
    key_ids, triple, x, g, mix, mid, out, unit, scaled, bias, scores, w, spots = refs[7:20]
    sems, own, chunk_sems = refs[20:]
    rows = tokens.shape[0]
    blocks = rows // QB

    def chunk(i):
        at = pl.ds(pl.multiple_of(i * QB, QB), QB)
        return pltpu.make_async_copy(qkv.at[at, :], triple.at[at, :], chunk_sems.at[i])

    for i in range(blocks):
        chunk(i).start()
    coming = [
        pltpu.make_async_copy(tokens, x, own.at[0]),
        pltpu.make_async_copy(cot, g, own.at[1]),
    ]
    fetch(coming)
    fetch_wo(me_ref[0], buffers, w, spots, sems)
    spread_ids(query_ids, key_ids)

    def one_block(b, loaded):
        start = pl.multiple_of(windows[0, b], SUB)
        needed = jnp.maximum(windows[2, b], loaded)

        def arrived(i, carry):
            chunk(i).wait()
            return carry

        lax.fori_loop(loaded, needed, arrived, 0)
        for index, width in enumerate(CLASSES):

            @pl.when(windows[1, b] == index)
            def _(width=width):
                mask_bias(start, width, b, key_ids, query_ids, bias)
                attend_block(b, start, width, triple, mix, stats, bias, scores)

        return needed

    loaded = lax.fori_loop(0, blocks, one_block, jnp.int32(0))

    def arrived(i, carry):
        chunk(i).wait()
        return carry

    lax.fori_loop(loaded, blocks, arrived, 0)
    going = [pltpu.make_async_copy(mix, mixed, own.at[2])]
    going[0].start()
    wait_wo(buffers, w, sems)
    settle(coming)
    bo, s1 = row_of(small, BO, 6), row_of(small, S1, 6)
    gain, shift = row_of(small, G2, 6), row_of(small, C2, 6)
    s2 = row_of(small, S2, 6)
    weight = wo_matrix(w, spots)
    step = 256
    sums = jnp.zeros((8, 768), F32)
    for i in range(rows // step):
        at = slice(i * step, (i + 1) * step)
        made = mm(mix[at, :], weight, NN) + bo
        out[at, :] = made.astype(BF16)
        values = x[at, :].astype(F32) + s1 * made
        mid[at, :] = values
        normal, _ = normalized(values)
        unit[at, :] = (normal * gain + shift).astype(BF16)
        rounded = (g[at, :].astype(F32) * s2).astype(BF16)
        scaled[at, :] = rounded
        sums = sums + fold8(rounded.astype(F32))
        for k, (source, target) in enumerate(
            ((out, branch), (mid, x1), (unit, n2), (scaled, dm))
        ):
            sem = own.at[3 + 4 * i + k]
            going.append(pltpu.make_async_copy(source.at[at, :], target.at[at, :], sem))
            going[-1].start()
    put_row(gb2, 0, total(sums))
    settle(going)


def attend(me, windows, qkv, tokens, cot, query_ids, small, att):
    rows, width = tokens.shape
    row = lambda kind: pltpu.VMEM((rows, width), kind)
    return pl.pallas_call(
        attend_kernel,
        out_shape=(
            shape((rows, width), BF16),
            shape((rows, width), F32),
            shape((rows, width), BF16),
            shape((rows, width), BF16),
            shape((rows, width), BF16),
            shape((rows // QB * PAIRS, 2, 2 * QB), F32),
            shape((6, LANES), F32),
        ),
        in_specs=[smem(), smem(), hbm(), hbm(), hbm(), vmem(), vmem()] + [hbm()] * 8,
        out_specs=(hbm(),) * 5 + (vmem(), vmem()),
        scratch_shapes=[
            pltpu.VMEM((rows, QB), F32),
            pltpu.VMEM((rows, 3 * width), BF16),
            row(BF16),
            row(BF16),
            row(BF16),
            row(F32),
            row(BF16),
            row(BF16),
            row(BF16),
            pltpu.VMEM((CLASSES[-1], QB), F32),
            pltpu.VMEM((PAIRS, CLASSES[-1], 2 * QB), F32),
            wo_scratch(),
            spots_scratch(),
            dma(3),
            dma(3 + 4 * rows // 256),
            dma(rows // QB),
        ],
        compiler_params=pltpu.CompilerParams(vmem_limit_bytes=GRANT),
        cost_estimate=cost(2 * rows * rows * width, 20 * rows * width, 4 * rows * rows),
        name="attend_forward",
    )(me, windows, qkv, tokens, cot, query_ids, small, *att)


def lay_matrix(w, spots, name, blocks, first, rt_count, columns, out):
    def one_block(d, carry):
        places = [spots[h, first + d] for h in range(2)]
        base = pl.multiple_of(d * rt_count * SUB, SUB)
        for rt in range(rt_count):
            for column, ct in enumerate(columns):
                h, index = half_place(name, rt, ct)
                at = pl.ds(pl.multiple_of(base + rt * SUB, SUB), SUB)
                out[at, LANES * column : LANES * (column + 1)] = w[h, places[h], index]
        return carry

    lax.fori_loop(0, blocks, one_block, 0)


def lay_w1(w, spots, out):
    lay_matrix(w, spots, "w1", W1_BLOCKS, 0, W1_RT, range(W1_CT), out)


def lay_w2(w, spots, out):
    lay_matrix(w, spots, "w2", W2_BLOCKS, W1_BLOCKS, W2_RT, range(W2_CT), out)


def w2_place(spots, f, row, ct):
    rt = row % W2_RT
    h = rt // 6
    return h, spots[h, W1_BLOCKS + 4 * f + row // W2_RT], rt % 6 * W2_CT + ct


TALL = 256
PARTS = CHUNK // 256


def device_of(x, c, z, y):
    return x * 16 + c * 8 + z * 2 + y


W1_RUNS = [
    [(0, device_of(0, c, 0, y), 4) for c in range(2) for y in range(2)],
    [(1, device_of(0, c, 0, 0), 8) for c in range(2)],
]
W2_RUNS = [
    [(h, device_of(1, f >> 1, 2 * (f & 1), y), 2) for h in range(2) for y in range(2)]
    for f in range(CHUNKS)
]
RUN_ORDER = W1_RUNS[0] + W2_RUNS[0] + W2_RUNS[1] + W1_RUNS[1] + W2_RUNS[2] + W2_RUNS[3]


class Runs:
    def __init__(self, buffers, w, spots, sems, out=False):
        self.buffers, self.w, self.spots, self.sems, self.out = buffers, w, spots, sems, out
        self.each = len(buffers) // 2

    def copy(self, run, which, index, place):
        h, first, size = run
        outer = self.buffers[self.each * h + which].at[pl.ds(index, size)]
        inner = self.w.at[h, pl.ds(place, size)]
        sem = self.sems.at[RUN_ORDER.index(run)]
        ends = (inner, outer) if self.out else (outer, inner)
        return pltpu.make_async_copy(*ends, sem)

    def start(self, runs):
        length = BLOCKS // self.each
        for run in runs:
            h, first, size = run
            place = self.spots[h, first] & (BLOCKS - size)
            for which in range(self.each):

                @pl.when(place // length == which)
                def _(run=run, which=which, place=place):
                    self.copy(run, which, place & (length - 1), place).start()

    def wait(self, runs):
        for run in runs:
            self.copy(run, 0, 0, 0).wait()


def mlp_kernel(me_ref, n2_in, dm_in, small, *refs):
    arriving, refs = refs[:8], refs[8:]
    u_out, dz_out, vectors, *leaving = refs[:7]
    w, first, second, spots, n2, dm, u, dz, zs, dus, bias_sums, b1_lines, sems, own = refs[7:]
    rows, width = n2.shape
    tiles = rows // TALL
    coming = [
        pltpu.make_async_copy(n2_in, n2, own.at[0]),
        pltpu.make_async_copy(dm_in, dm, own.at[1]),
    ]
    fetch(coming)
    fill_spots(me_ref[0], spots)
    incoming = Runs(arriving, w, spots, sems)
    incoming.start(RUN_ORDER)
    bias_sums[...] = jnp.zeros_like(bias_sums)
    for f in range(CHUNKS):
        b1_lines[f : f + 1, :] = row_of(small, B1 + 6 * f, 6)
    def lay_chunk(f, side):
        h, base = f >> 1, MLP_HALF // 2 * (f & 1)
        for d in range(W1_BLOCKS):
            place = spots[h, d]
            for rt in range(W1_RT):
                at = slice((d * W1_RT + rt) * SUB, (d * W1_RT + rt + 1) * SUB)
                for ct in range(6):
                    lanes = slice(LANES * ct, LANES * ct + LANES)
                    first[side, at, lanes] = w[h, place, base + ct * W1_RT + rt]
        for k in range(4):
            places = [spots[i, W1_BLOCKS + 4 * f + k] for i in range(2)]
            for rt in range(W2_RT):
                at = slice((k * W2_RT + rt) * SUB, (k * W2_RT + rt + 1) * SUB)
                for ct in range(W2_CT):
                    lanes = slice(LANES * ct, LANES * ct + LANES)
                    i, index = half_place("w2", rt, ct)
                    second[side, at, lanes] = w[i, places[i], index]

    incoming.wait(W1_RUNS[0] + W2_RUNS[0])
    lay_chunk(jnp.int32(0), jnp.int32(0))
    settle(coming)

    units = [(t, c) for c in range(PARTS) for t in range(tiles)]

    def lanes_of(f, c):
        return pl.ds(pl.multiple_of(CHUNK * f + 256 * c, 256), 256)

    def outward(f):
        chunk = pl.ds(pl.multiple_of(CHUNK * f, CHUNK), CHUNK)
        return [
            pltpu.make_async_copy(u.at[:, chunk], u_out.at[:, chunk], own.at[2 * f]),
            pltpu.make_async_copy(dz.at[:, chunk], dz_out.at[:, chunk], own.at[2 * f + 1]),
        ]

    def one_chunk(f, carry):
        for index in range(CHUNKS - 1):

            @pl.when(f == index)
            def _(index=index):
                incoming.wait(W2_RUNS[index + 1] + (W1_RUNS[1] if index == 1 else []))

        side = f & 1
        lay_chunk(jnp.minimum(f + 1, CHUNKS - 1), 1 - side)

        def multiply(unit, slot):
            t, c = unit
            at = slice(TALL * t, TALL * t + TALL)
            zs[slot] = mm(n2[at, :], first[side, :, 256 * c : 256 * c + 256], NN)
            dus[slot] = mm(dm[at, :], second[side, 256 * c : 256 * c + 256, :], NT)

        def activate(unit, slot):
            t, c = unit
            lanes = slice(256 * c, 256 * c + 256)
            bias = b1_lines[pl.ds(f, 1), lanes]
            folded = jnp.zeros((8, 256), F32)
            for r in range(TALL // 32):
                part = slice(32 * r, 32 * r + 32)
                place = slice(TALL * t + 32 * r, TALL * t + 32 * r + 32)
                value, slope = gelu_pair(zs[slot, part, :] + bias)
                u[place, lanes_of(f, c)] = value.astype(BF16)
                rounded = (dus[slot, part, :] * slope).astype(BF16)
                dz[place, lanes_of(f, c)] = rounded
                folded = folded + fold8(rounded.astype(F32))
            bias_sums[:, lanes_of(f, c)] += folded

        multiply(units[0], 0)
        for i, unit in enumerate(units):
            if i + 1 < len(units):
                multiply(units[i + 1], (i + 1) % 2)
            activate(unit, i % 2)
        fetch(outward(f))
        return carry

    lax.fori_loop(0, CHUNKS, one_chunk, 0)
    put_row(vectors, 0, total(bias_sums[...]))

    outgoing = Runs(leaving, w, spots, sems, out=True)

    def one_grad(f, carry):
        h, base = f >> 1, MLP_HALF // 2 * (f & 1)
        chunk = pl.ds(pl.multiple_of(CHUNK * f, CHUNK), CHUNK)
        for c in range(PARTS):
            lanes = slice(256 * c, 256 * c + 256)
            grad = mm(n2[:, lanes], dz[:, chunk], TN)
            for r in range(SUB):
                d, rt = (SUB * c + r) // W1_RT, (SUB * c + r) % W1_RT
                for ct in range(6):
                    tile = grad[SUB * r : SUB * r + SUB, LANES * ct : LANES * ct + LANES]
                    w[h, spots[h, d], base + ct * W1_RT + rt] = tile.astype(BF16)
        for side in range(2):

            @pl.when(f == 2 * side + 1)
            def _(side=side):
                outgoing.start(W1_RUNS[side])

        for c in range(PARTS):
            grad = mm(u[:, lanes_of(f, c)], dm[...], TN)
            for r in range(SUB):
                for ct in range(W2_CT):
                    tile = grad[SUB * r : SUB * r + SUB, LANES * ct : LANES * ct + LANES]
                    w[w2_place(spots, f, SUB * c + r, ct)] = tile.astype(BF16)
        for index in range(CHUNKS):

            @pl.when(f == index)
            def _(index=index):
                outgoing.start(W2_RUNS[index])

        return carry

    lax.fori_loop(0, CHUNKS, one_grad, 0)
    for f in range(CHUNKS):
        settle(outward(f))
    outgoing.wait(RUN_ORDER)


def feed_forward(me, n2, dm, small, mlp):
    rows, width = n2.shape
    half = shape((HALF_BLOCKS, MLP_HALF, SUB, LANES), BF16)
    return pl.pallas_call(
        mlp_kernel,
        out_shape=(
            shape((rows, FF), BF16),
            shape((rows, FF), BF16),
            shape((24, LANES), F32),
            half,
            half,
            half,
            half,
        ),
        in_specs=[smem(), hbm(), hbm(), vmem()] + [hbm()] * 8,
        out_specs=(hbm(), hbm(), vmem()) + (hbm(),) * 4,
        scratch_shapes=[
            slots_scratch(MLP_HALF),
            pltpu.VMEM((2, width, CHUNK), BF16),
            pltpu.VMEM((2, CHUNK, width), BF16),
            spots_scratch(),
            pltpu.VMEM((rows, width), BF16),
            pltpu.VMEM((rows, width), BF16),
            pltpu.VMEM((rows, FF), BF16),
            pltpu.VMEM((rows, FF), BF16),
            pltpu.VMEM((2, TALL, 256), F32),
            pltpu.VMEM((2, TALL, 256), F32),
            pltpu.VMEM((8, FF), F32),
            pltpu.VMEM((CHUNKS, CHUNK), F32),
            dma(len(RUN_ORDER)),
            dma(2 * CHUNKS),
        ],
        compiler_params=pltpu.CompilerParams(vmem_limit_bytes=42 * MEGA),
        cost_estimate=cost(8 * rows * width * FF, 40 * MEGA),
        name="feed_forward",
    )(me, n2, dm, small, *mlp)


def matrix_copies(buffers, w, sems, x):
    copies = []
    for i in range(4):
        source = buffers[i].at[pl.ds(4 * x, 4)]
        copies.append(pltpu.make_async_copy(source, w.at[0, pl.ds(4 * i, 4)], sems.at[i]))
    for c in range(2):
        source = buffers[4 + 2 * c + x]
        copies.append(pltpu.make_async_copy(source, w.at[1, pl.ds(8 * c, 8)], sems.at[4 + c]))
    return copies


def fetch_matrix(me, buffers, w, spots, sems, first):
    def place(d):
        return ((d >> 3) & 1) * 8 + (d & 1) * 4 + ((d >> 1) & 3)

    for x in range(2):

        @pl.when((me >> 4) == (x ^ (first >> 4)))
        def _(x=x):
            fetch(matrix_copies(buffers, w, sems, x))

    mine = place(me)
    for d in range(W1_BLOCKS):
        for h in range(2):
            spots[h, first + d] = jnp.bitwise_xor(mine, place(d))


def wait_matrix(buffers, w, sems):
    settle(matrix_copies(buffers, w, sems, 0))


def matrix_scratch():
    return pltpu.VMEM((2, W1_BLOCKS, MLP_HALF, SUB, LANES), BF16)


def mlp_out_kernel(me_ref, u_in, x1_in, cot_in, small, *refs):
    arriving, refs = refs[:8], refs[8:]
    out, vectors, w, second, spots, u, x1, cot, macc, done, sums, sems, own = refs
    rows, width = x1.shape
    tiles = rows // TALL

    def tile_copy(source, target, t, k):
        at = pl.ds(pl.multiple_of(TALL * t, TALL), TALL)
        return pltpu.make_async_copy(source.at[at, :], target.at[at, :], own.at[k, t])

    fetch_matrix(me_ref[0], arriving, w, spots, sems, W1_BLOCKS)
    for t in range(tiles):
        tile_copy(u_in, u, t, 0).start()
    for t in range(tiles):
        tile_copy(x1_in, x1, t, 1).start()
        tile_copy(cot_in, cot, t, 2).start()
    bias, scale = row_of(small, B2, 6), row_of(small, S2, 6)
    sums[...] = jnp.zeros_like(sums)
    wait_matrix(arriving, w, sems)
    lay_w2(w, spots, second)

    def contract(t):
        at = pl.ds(pl.multiple_of(TALL * t, TALL), TALL)
        tile_copy(u_in, u, t, 0).wait()
        macc[at, :] = mm(u[at, :], second[...], NN)

    def finish(t):
        tile_copy(x1_in, x1, t, 1).wait()
        tile_copy(cot_in, cot, t, 2).wait()
        for part in range(TALL // 64):
            at = pl.ds(pl.multiple_of(TALL * t + 64 * part, 64), 64)
            contracted = macc[at, :] + bias
            done[at, :] = (x1[at, :] + scale * contracted).astype(BF16)
            sums[...] += fold8(cot[at, :].astype(F32) * contracted)
        tile_copy(done, out, t, 3).start()

    def one_tile(t, carry):
        contract(t)
        finish(t - 1)
        return carry

    contract(0)
    lax.fori_loop(1, tiles, one_tile, 0)
    finish(tiles - 1)
    put_row(vectors, 0, total(sums[...]))
    for t in range(tiles):
        tile_copy(done, out, t, 3).wait()


def feed_forward_out(me, u, x1, cot, small, mlp):
    rows, width = x1.shape
    row = lambda kind: pltpu.VMEM((rows, width), kind)
    return pl.pallas_call(
        mlp_out_kernel,
        out_shape=(shape((rows, width), BF16), shape((6, LANES), F32)),
        in_specs=[smem()] + [hbm()] * 3 + [vmem()] + [hbm()] * 8,
        out_specs=(hbm(), vmem()),
        scratch_shapes=[
            matrix_scratch(),
            pltpu.VMEM((FF, width), BF16),
            spots_scratch(),
            pltpu.VMEM((rows, FF), BF16),
            row(F32),
            row(BF16),
            row(F32),
            row(BF16),
            pltpu.VMEM((8, width), F32),
            dma(6),
            pltpu.SemaphoreType.DMA((4, rows // TALL)),
        ],
        compiler_params=pltpu.CompilerParams(vmem_limit_bytes=32 * MEGA),
        cost_estimate=cost(2 * rows * width * FF, 20 * MEGA),
        name="feed_forward_out",
    )(me, u, x1, cot, small, *mlp)


def split_kernel(me_ref, dz_in, x1_in, cot_in, branch_in, mixed_in, small, *refs):
    buffers, att_buffers, refs = refs[:8], refs[8:16], refs[16:]
    dx1_out, da_out, gwo0, gwo1, vectors = refs[:5]
    w, first, spots, wo, wo_spots, dz, x1, cot, dnacc, dx1, branch, mixed, db, da = refs[5:19]
    parts, sums, sems, wo_sems, own = refs[19:]
    me = me_ref[0]
    rows, width = x1.shape
    tiles = rows // TALL

    def tile_copy(source, target, t, k):
        at = pl.ds(pl.multiple_of(TALL * t, TALL), TALL)
        return pltpu.make_async_copy(source.at[at, :], target.at[at, :], own.at[k, t])

    fetch_matrix(me, buffers, w, spots, sems, 0)
    for t in range(tiles):
        tile_copy(dz_in, dz, t, 0).start()
    for t in range(tiles):
        tile_copy(x1_in, x1, t, 1).start()
        tile_copy(cot_in, cot, t, 2).start()
        tile_copy(branch_in, branch, t, 3).start()
    fetch_wo(me, att_buffers, wo, wo_spots, wo_sems)
    late = pltpu.make_async_copy(mixed_in, mixed, own.at[4, 0])
    late.start()
    gain, scale = row_of(small, G2, 6), row_of(small, S1, 6)
    sums[...] = jnp.zeros_like(sums)
    wait_matrix(buffers, w, sems)
    lay_w1(w, spots, first)

    def contract(t):
        at = pl.ds(pl.multiple_of(TALL * t, TALL), TALL)
        tile_copy(dz_in, dz, t, 0).wait()
        dnacc[at, :] = mm(dz[at, :], first[...], NT)

    def finish(t):
        tile_copy(x1_in, x1, t, 1).wait()
        tile_copy(cot_in, cot, t, 2).wait()
        tile_copy(branch_in, branch, t, 3).wait()
        for half in range(2):
            at = pl.ds(pl.multiple_of(TALL * t + TALL // 2 * half, TALL // 2), TALL // 2)
            unit, inverse = normalized(x1[at, :])
            grad = dnacc[at, :]
            middle = cot[at, :].astype(F32) + norm_pullback(unit, inverse, grad, gain)
            dx1[at, :] = middle
            rounded = (middle * scale).astype(BF16)
            db[at, :] = rounded
            sums[0:8, :] += fold8(grad * unit)
            sums[8:16, :] += fold8(grad)
            sums[16:24, :] += fold8(rounded.astype(F32))
            sums[24:32, :] += fold8(middle * branch[at, :].astype(F32))
        tile_copy(dx1, dx1_out, t, 1).start()

    def one_tile(t, carry):
        contract(t)
        finish(t - 1)
        return carry

    contract(0)
    lax.fori_loop(1, tiles, one_tile, 0)
    finish(tiles - 1)
    for k in range(4):
        put_row(vectors, 6 * k, total(sums[8 * k : 8 * k + 8, :]))
    wait_wo(att_buffers, wo, wo_sems)
    weight = wo_matrix(wo, wo_spots)
    going = []
    for c in range(3):
        lanes = slice(256 * c, 256 * c + 256)
        da[:, lanes] = mm(db[...], weight[lanes, :], NT).astype(BF16)
        going.append(pltpu.make_async_copy(da.at[:, lanes], da_out.at[:, lanes], own.at[0, c]))
        going[-1].start()
    late.wait()
    for c in range(3):
        grad = mm(mixed[:, 256 * c : 256 * c + 256], db[...], TN)
        for r in range(SUB):
            i, rt = (SUB * c + r) // WO_RT, (SUB * c + r) % WO_RT
            for ct in range(WO_CT):
                tile = grad[SUB * r : SUB * r + SUB, LANES * ct : LANES * ct + LANES]
                g, half, index = part_place("wo", rt, ct)
                parts[g, half, i, index] = tile.astype(BF16)
    for g, target in enumerate((gwo0, gwo1)):
        going.append(pltpu.make_async_copy(parts.at[g], target, own.at[4, g]))
        going[-1].start()
    settle(going)
    for t in range(tiles):
        tile_copy(dx1, dx1_out, t, 1).wait()


def split(me, dz, x1, cot, branch, mixed, small, mlp, att):
    rows, width = x1.shape
    part = (2, WO_BLOCKS, ATT_PART, SUB, LANES)
    row = lambda kind: pltpu.VMEM((rows, width), kind)
    return pl.pallas_call(
        split_kernel,
        out_shape=(
            shape((rows, width), F32),
            shape((rows, width), BF16),
            shape(part, BF16),
            shape(part, BF16),
            shape((24, LANES), F32),
        ),
        in_specs=[smem()] + [hbm()] * 5 + [vmem()] + [hbm()] * 16,
        out_specs=(hbm(),) * 4 + (vmem(),),
        scratch_shapes=[
            matrix_scratch(),
            pltpu.VMEM((width, FF), BF16),
            spots_scratch(),
            wo_scratch(),
            spots_scratch(),
            pltpu.VMEM((rows, FF), BF16),
            row(F32),
            row(BF16),
            row(F32),
            row(F32),
            row(BF16),
            row(BF16),
            row(BF16),
            row(BF16),
            pltpu.VMEM((2,) + part, BF16),
            pltpu.VMEM((32, width), F32),
            dma(6),
            dma(3),
            pltpu.SemaphoreType.DMA((5, rows // TALL)),
        ],
        compiler_params=pltpu.CompilerParams(vmem_limit_bytes=44 * MEGA),
        cost_estimate=cost(2 * rows * width * FF + 4 * rows * width * width, 40 * MEGA),
        name="feed_forward_in",
    )(me, dz, x1, cot, branch, mixed, small, *mlp, *att)


GROUP = PAIRS // 2
GROUP_LANES = GROUP * LANES


def attend_back_block(b, start, width, group, refs):
    q, k, v, da, stats, dq, dkeys, dvalues, bias = refs
    rows = pl.ds(pl.multiple_of(b * QB, QB), QB)
    at = pl.ds(start, width)
    mask = jnp.concatenate([bias[0:width, :]] * 2, axis=1)
    pairs = []
    for p in range(GROUP):
        lanes = slice(LANES * p, LANES * p + LANES)
        place = b * PAIRS + GROUP * group + p
        queries = head_masked(q[rows, lanes] * 0.125)
        grads = head_masked(da[rows, lanes])
        keys, values = k[at, lanes], v[at, lanes]
        scores = mm(keys, queries, NT)
        dweight = mm(values, grads, NT)
        pairs.append((lanes, place, queries, grads, keys, scores, dweight))
    later = []
    for lanes, place, queries, grads, keys, scores, dweight in pairs:
        highest = stats[place, 0:1, :]
        inverse = stats[place, 1:2, :]
        weight = jnp.exp(scores + mask - highest) * inverse
        inner_sum = total(fold8(weight * dweight))
        dvalues[at, lanes] += mm(weight.astype(BF16), grads, NN)
        dscore = (weight * (dweight - inner_sum)).astype(BF16)
        later.append((lanes, queries, keys, dscore))
    for lanes, queries, keys, dscore in later:
        dkeys[at, lanes] += mm(dscore, queries, NN)
        both = mm(keys, dscore, TN)
        dq[rows, lanes] = (pick_heads(both) * 0.125).T.astype(BF16)


def attend_back_kernel(group, windows, qkv, da_in, stats, query_ids, dqkv, *refs):
    q, k, v, da, out, dkeys, dvalues, bias, key_ids, own = refs
    rows = q.shape[0]
    blocks = rows // QB
    lanes = slice(GROUP_LANES * group, GROUP_LANES * group + GROUP_LANES)
    coming = [pltpu.make_async_copy(da_in.at[:, lanes], da, own.at[3])]
    for third, target in enumerate((q, k, v)):
        first = LANES * PAIRS * third + GROUP_LANES * group
        source = qkv.at[:, first : first + GROUP_LANES]
        coming.append(pltpu.make_async_copy(source, target, own.at[third]))
    fetch(coming)
    dkeys[...] = jnp.zeros_like(dkeys)
    dvalues[...] = jnp.zeros_like(dvalues)
    spread_ids(query_ids, key_ids)
    settle(coming)
    dq = out.at[:, 0:GROUP_LANES]

    def one_block(b, carry):
        start = pl.multiple_of(windows[0, b], SUB)
        for index, width in enumerate(CLASSES):

            @pl.when(windows[1, b] == index)
            def _(width=width):
                mask_bias(start, width, b, key_ids, query_ids, bias)
                parts = (q, k, v, da, stats, dq, dkeys, dvalues, bias)
                attend_back_block(b, start, width, group, parts)

        return carry

    lax.fori_loop(0, blocks, one_block, 0)
    going = []
    for i in range(rows // 256):
        at = slice(256 * i, 256 * i + 256)
        out[at, GROUP_LANES : 2 * GROUP_LANES] = dkeys[at, :].astype(BF16)
        out[at, 2 * GROUP_LANES :] = dvalues[at, :].astype(BF16)
        going.append(pltpu.make_async_copy(out.at[at, :], dqkv.at[at, :], own.at[i]))
        going[-1].start()
    settle(going)


def attend_back(group, windows, qkv, da, stats, query_ids):
    rows = qkv.shape[0]
    part = lambda kind: pltpu.VMEM((rows, GROUP_LANES), kind)
    return pl.pallas_call(
        partial(attend_back_kernel, group),
        out_shape=shape((rows, 3 * GROUP_LANES), BF16),
        in_specs=[smem(), hbm(), hbm(), vmem(), vmem()],
        out_specs=hbm(),
        scratch_shapes=[
            part(BF16),
            part(BF16),
            part(BF16),
            part(BF16),
            pltpu.VMEM((rows, 3 * GROUP_LANES), BF16),
            part(F32),
            part(F32),
            pltpu.VMEM((CLASSES[-1], QB), F32),
            pltpu.VMEM((rows, QB), F32),
            dma(4),
        ],
        compiler_params=pltpu.CompilerParams(vmem_limit_bytes=32 * MEGA),
        cost_estimate=cost(3 * rows * rows * rows, 14 * rows * rows, 4 * rows * rows),
        name="attend_backward",
    )(windows, qkv, da, stats, query_ids)


def put_qkv_grad(n1, dqkv, w, spots):
    for c in range(3):
        grad = mm(n1[:, 256 * c : 256 * c + 256], dqkv[...], TN)
        for r in range(SUB):
            d, rt = (SUB * c + r) // QKV_RT, (SUB * c + r) % QKV_RT
            place = spots[rt, d]
            for index in range(ATT_PART):
                tile = grad[SUB * r : SUB * r + SUB, LANES * index : LANES * index + LANES]
                w[rt, place, index] = tile.astype(BF16)


def put_wo_grad(gwo, w, spots):
    for h in range(2):
        for i in range(WO_BLOCKS):
            w[h, spots[h, QKV_BLOCKS + i], 0:ATT_PART] = gwo[h, i]


def weight_grad_kernel(me_ref, n1_in, dqkv_in, gwo_in, *refs):
    leaving, (w, spots, n1, dqkv, gwo, sems, own) = refs[:4], refs[4:]
    coming = [
        pltpu.make_async_copy(n1_in, n1, own.at[0]),
        pltpu.make_async_copy(dqkv_in, dqkv, own.at[1]),
        pltpu.make_async_copy(gwo_in, gwo, own.at[2]),
    ]
    fetch(coming)
    fill_spots(me_ref[0], spots)
    settle(coming)
    put_wo_grad(gwo, w, spots)
    put_qkv_grad(n1, dqkv, w, spots)
    copies = leaving_slots(leaving, w, sems)
    fetch(copies)
    settle(copies)


def weight_grad(me, n1, dqkv, gwo):
    rows, width = n1.shape
    half = shape((HALF_BLOCKS, ATT_PART, SUB, LANES), BF16)
    return pl.pallas_call(
        weight_grad_kernel,
        out_shape=(half,) * 4,
        in_specs=[smem()] + [hbm()] * 3,
        out_specs=(hbm(),) * 4,
        scratch_shapes=[
            slots_scratch(ATT_PART),
            spots_scratch(),
            pltpu.VMEM((rows, width), BF16),
            pltpu.VMEM(dqkv.shape, BF16),
            pltpu.VMEM(gwo.shape, BF16),
            dma(4),
            dma(3),
        ],
        compiler_params=pltpu.CompilerParams(vmem_limit_bytes=20 * MEGA),
        cost_estimate=cost(3 * rows * width * width, 10 * rows * width),
        name="qkv_weight_grad",
    )(me, n1, dqkv, gwo)


def qkv_back_kernel(
    me_ref, tokens_in, n1_in, dx1_in, dqkv0_in, dqkv1_in, small, proj, mlp, gwo_in, *refs
):
    arriving, refs = refs[:8], refs[8:]
    dx_out, *leaving = refs[:5]
    w, gw, weight, spots, gwo, tokens, n1, dx1, dqkv0, dqkv1, dn, dx, sums, table = refs[5:19]
    sems, out_sems, own = refs[19:]
    rows = tokens.shape[0]
    tiles = rows // TALL

    def tile_copy(source, target, t, k):
        at = pl.ds(pl.multiple_of(TALL * t, TALL), TALL)
        return pltpu.make_async_copy(source.at[at, :], target.at[at, :], own.at[k, t])

    for t in range(tiles):
        tile_copy(dqkv0_in, dqkv0, t, 0).start()
        tile_copy(dqkv1_in, dqkv1, t, 1).start()
    weights = arriving_slots(arriving, w, sems)
    fetch(weights)
    for t in range(tiles):
        tile_copy(tokens_in, tokens, t, 2).start()
        tile_copy(dx1_in, dx1, t, 3).start()
    late = [
        pltpu.make_async_copy(n1_in, n1, own.at[4, 0]),
        pltpu.make_async_copy(gwo_in, gwo, own.at[4, 1]),
    ]
    fetch(late)
    sums[...] = jnp.zeros_like(sums)
    gain = row_of(small, G1, 6)
    fill_spots(me_ref[0], spots)
    settle(weights)
    columns = qkv_group(0) + qkv_group(1)
    lay_matrix(w, spots, "qkv", QKV_BLOCKS, 0, QKV_RT, columns, weight)

    def contract(t):
        at = pl.ds(pl.multiple_of(TALL * t, TALL), TALL)
        for g, (source, part) in enumerate(((dqkv0_in, dqkv0), (dqkv1_in, dqkv1))):
            tile_copy(source, part, t, g).wait()
            lanes = slice(384 * g, 384 * g + 384)
            sums[16:24, lanes] += fold8(part[at, 0:384].astype(F32))
            sums[24:32, lanes] += fold8(part[at, 768:1152].astype(F32))
        both = jnp.concatenate([dqkv0[at, :], dqkv1[at, :]], axis=1)
        dn[at, :] = mm(both, weight[...], NT)

    def finish(t):
        tile_copy(tokens_in, tokens, t, 2).wait()
        tile_copy(dx1_in, dx1, t, 3).wait()
        for half in range(2):
            at = pl.ds(pl.multiple_of(TALL * t + TALL // 2 * half, TALL // 2), TALL // 2)
            unit, inverse = normalized(tokens[at, :].astype(F32))
            grad = dn[at, :]
            dx[at, :] = dx1[at, :] + norm_pullback(unit, inverse, grad, gain)
            sums[0:8, :] += fold8(grad * unit)
            sums[8:16, :] += fold8(grad)
        tile_copy(dx, dx_out, t, 3).start()

    def one_tile(t, carry):
        contract(t)
        finish(t - 1)
        return carry

    contract(0)
    lax.fori_loop(1, tiles, one_tile, 0)
    finish(tiles - 1)

    def put_table(owner, *places):
        table[...] = jnp.zeros_like(table)
        for place, values in places:
            if values.shape[1] == LANES:
                table[place : place + values.shape[0], :] = values
            else:
                put_row(table, place, values)
        for h in range(2):
            gw[h, spots[h, owner], ATT_PART] = table[SUB * h : SUB * h + SUB, :].astype(BF16)

    put_table(
        OWNERS[0], (0, total(sums[0:8, :])), (6, total(sums[8:16, :])), (12, mlp[0:12, :])
    )
    put_table(OWNERS[1], (0, mlp[12:36, :]))
    put_table(OWNERS[2], (0, total(sums[16:24, :])), (6, total(sums[24:32, :])))
    put_table(OWNERS[3], (0, proj[...]), (12, mlp[36:48, :]))
    settle(late)
    put_wo_grad(gwo, gw, spots)
    put_qkv_grad(n1, dqkv1, gw, spots)
    copies = leaving_slots(leaving, gw, out_sems)
    fetch(copies)
    for t in range(tiles):
        tile_copy(dx, dx_out, t, 3).wait()
    settle(copies)


def qkv_back(me, tokens, n1, dx1, dqkv0, dqkv1, small, proj, mlp, gwo, att):
    rows, width = tokens.shape
    tiles = ATT_PART + 1
    half = shape((HALF_BLOCKS, tiles, SUB, LANES), BF16)
    row = lambda kind: pltpu.VMEM((rows, width), kind)
    return pl.pallas_call(
        qkv_back_kernel,
        out_shape=(shape((rows, width), F32), half, half, half, half),
        in_specs=[smem()] + [hbm()] * 5 + [vmem()] * 3 + [hbm()] * 9,
        out_specs=(hbm(),) * 5,
        scratch_shapes=[
            slots_scratch(ATT_SENT),
            slots_scratch(tiles),
            pltpu.VMEM((width, 3 * width), BF16),
            spots_scratch(),
            pltpu.VMEM(gwo.shape, BF16),
            row(BF16),
            row(BF16),
            row(F32),
            pltpu.VMEM(dqkv0.shape, BF16),
            pltpu.VMEM(dqkv1.shape, BF16),
            row(F32),
            row(F32),
            pltpu.VMEM((32, width), F32),
            pltpu.VMEM((2 * SUB, LANES), F32),
            dma(8),
            dma(4),
            pltpu.SemaphoreType.DMA((5, rows // TALL)),
        ],
        compiler_params=pltpu.CompilerParams(vmem_limit_bytes=46 * MEGA),
        cost_estimate=cost(9 * rows * width * width, 30 * rows * width),
        name="qkv_backward",
    )(me, tokens, n1, dx1, dqkv0, dqkv1, small, proj, mlp, gwo, *att)


X, C, Z1, Z0, Y = 16, 8, 4, 2, 1


def exchange(values, bit):
    return lax.ppermute(values, AXES, [(d, d ^ bit) for d in range(BLOCKS)])


def overhangs(att_rows, mlp_rows):
    before, after = [], []
    for d in range(BLOCKS):
        att = 12 + d * (576 - att_rows) + (0 if d < QKV_BLOCKS else 12)
        mlp = 12 + d * (1152 - mlp_rows) + (0 if d < W1_BLOCKS else 24)
        ahead = 12 if d == 0 else 0
        att_end = att + 576 + (12 if d in (QKV_BLOCKS - 1, BLOCKS - 1) else 0)
        mlp_end = mlp + 1152 + (24 if d == W1_BLOCKS - 1 else 12 if d == BLOCKS - 1 else 0)
        if min(att, mlp) < ahead:
            before.append(d)
        if att_end > att_rows or mlp_end > mlp_rows:
            after.append(d)
    return before, after


def together(*values):
    return lax.optimization_barrier(values)


def along_z(first, second, received):
    return (
        jnp.stack([first] + [r[0] for r in received]),
        jnp.stack([second] + [r[1] for r in received]),
    )


def joined(own, received):
    return jnp.concatenate([own, received])


def sum_terms(terms):
    summed = terms[0].astype(F32)
    for term in terms[1:]:
        summed = summed + term.astype(F32)
    return summed


def kept(terms):
    return [t[: t.shape[0] // 2] for t in terms]


def z_part(first, second, k):
    return jnp.stack([sum_terms([t[k] for t in terms]) for terms in (first, second)])


def sent(terms):
    return sum_terms([t[t.shape[0] // 2 :] for t in terms]).astype(BF16)


def attention_amounts(width):
    return [width, width, 3 * width * width, width, width, width * width, width, width]


def feedforward_amounts(width):
    return [width, width, width * FF, FF, FF * width, width, width]


def pieces_of(vector, amounts):
    out, offset = [], 0
    for amount in amounts:
        out.append(vector[offset : offset + amount])
        offset += amount
    return out


def tiles_by_column(matrix, blocks, rt):
    ct = matrix.shape[1] // LANES
    return matrix.reshape(blocks, rt, SUB, ct, LANES).transpose(0, 3, 1, 2, 4)


def tiles_by_row(matrix, blocks, rt):
    ct = matrix.shape[1] // LANES
    return matrix.reshape(blocks, rt, SUB, ct, LANES).transpose(0, 1, 3, 2, 4)


def gather_plainly(params, att_rows, width):
    rounded = params.astype(BF16)
    att = lax.all_gather(rounded[:att_rows], AXES, axis=0, tiled=True).reshape(-1)
    mlp = lax.all_gather(rounded[att_rows:], AXES, axis=0, tiled=True).reshape(-1)
    g1, c1, wqkv, bq, bv, wo, bo, s1 = pieces_of(att, attention_amounts(width))
    g2, c2, w1, b1, w2, b2, s2 = pieces_of(mlp, feedforward_amounts(width))
    tile = (SUB, LANES)
    att = jnp.concatenate(
        [
            tiles_by_column(wqkv.reshape(width, -1), QKV_BLOCKS, QKV_RT).reshape((-1, 36) + tile),
            tiles_by_row(wo.reshape(width, -1), WO_BLOCKS, WO_RT).reshape((-1, 36) + tile),
        ]
    )
    mlp = jnp.concatenate(
        [
            tiles_by_column(w1.reshape(width, -1), W1_BLOCKS, W1_RT).reshape((-1, 72) + tile),
            tiles_by_row(w2.reshape(FF, -1), W2_BLOCKS, W2_RT).reshape((-1, 72) + tile),
        ]
    )
    vectors = jnp.concatenate([g1, c1, bq, bv, bo, s1, g2, c2, b1, b2, s2]).astype(F32)
    lines = vectors.reshape(-1, LANES)
    sent = jnp.zeros((BLOCKS, 2 * SUB, LANES), F32)
    for owner, place, first, count in (
        (OWNERS[0], 0, G1, 12),
        (OWNERS[0], 12, G2, 12),
        (OWNERS[1], 0, B1, 24),
        (OWNERS[2], 0, BQ, 12),
        (OWNERS[3], 0, BO, 12),
        (OWNERS[3], 12, B2, 12),
    ):
        sent = sent.at[owner, place : place + count].set(lines[first : first + count])
    sent = sent.astype(BF16).reshape((BLOCKS, 2, 1) + tile)
    att = [jnp.concatenate([att[:, 18 * h : 18 * h + 18], sent[:, h]], axis=1) for h in range(2)]
    return by_slot(*att), by_slot(mlp[:, :36], mlp[:, 36:])


def by_slot(first, second):
    halves = (first, second)
    return [
        jnp.stack([halves[i // 4][slot] for slot in SLOTS[i // 4][i % 4 * 8 : i % 4 * 8 + 8]])
        for i in range(8)
    ]


def from_slots(buffers):
    halves = []
    for h in range(2):
        slots = jnp.concatenate(buffers[2 * h : 2 * h + 2])
        halves.append(jnp.stack([slots[spot(h, d)] for d in range(BLOCKS)]))
    return halves


def reduce_plainly(gatt0, gatt1, gmlp, att_rows, mlp_rows, width, devices):
    groups = [from_slots(gatt0), from_slots(gatt1)]
    vectors = jnp.concatenate([groups[1][h][:, ATT_PART:] for h in range(2)], axis=1)
    vectors = vectors.astype(F32).reshape(BLOCKS, 2 * SUB, LANES)

    def matrix(name, first, last, rt_count, ct_count):
        rows = []
        for rt in range(rt_count):
            places = [part_place(name, rt, ct) for ct in range(ct_count)]
            rows.append(jnp.stack([groups[g][h][first:last, i] for g, h, i in places], axis=2))
        return jnp.stack(rows, axis=1).astype(F32).reshape(-1)

    wqkv = matrix("qkv", 0, QKV_BLOCKS, QKV_RT, QKV_CT)
    wo = matrix("wo", QKV_BLOCKS, BLOCKS, WO_RT, WO_CT)
    mlp = jnp.concatenate(from_slots(gmlp), axis=1).astype(F32)
    five = lambda v, dims: v.reshape((v.shape[0],) + dims + (SUB, LANES))
    w1 = five(mlp[:W1_BLOCKS], (W1_CT, W1_RT)).transpose(0, 2, 3, 1, 4).reshape(-1)
    w2 = five(mlp[W1_BLOCKS:], (W2_RT, W2_CT)).transpose(0, 1, 3, 2, 4).reshape(-1)
    line = lambda owner, first, count: vectors[owner, first : first + count].reshape(-1)
    att = [line(OWNERS[0], 0, 12), wqkv, line(OWNERS[2], 0, 12), wo, line(OWNERS[3], 0, 12)]
    mlp = [line(OWNERS[0], 12, 12), w1, line(OWNERS[1], 0, 24), w2, line(OWNERS[3], 12, 12)]

    def lay(parts, rows):
        vector = jnp.concatenate(parts)
        vector = jnp.pad(vector, (0, devices * rows * LANES - vector.shape[0]))
        return vector.reshape(devices, rows, LANES)

    whole = jnp.concatenate([lay(att, att_rows), lay(mlp, mlp_rows)], axis=1)
    return lax.psum_scatter(whole.reshape(-1, LANES), AXES, scatter_dimension=0, tiled=True)


def key_windows(segments, real):
    length = segments.shape[0]
    position = jnp.arange(length, dtype=jnp.int32)
    ids = jnp.where(real, segments, length + position)
    first = segments[0::QB]
    final = segments[QB - 1 :: QB]
    begin = jnp.sum((segments[None, :] < first[:, None]).astype(jnp.int32), axis=1)
    begin = jnp.where(real[0::QB], begin, position[0::QB])
    end = jnp.sum(((segments[None, :] <= final[:, None]) & real[None, :]).astype(jnp.int32), axis=1)
    end = jnp.where(real[QB - 1 :: QB], end, position[QB - 1 :: QB] + 1)
    begin = begin // SUB * SUB
    need = end - begin
    kind = sum((need > width).astype(jnp.int32) for width in CLASSES[:-1])
    widths = sum(
        jnp.where(kind == i, width, 0) for i, width in enumerate(CLASSES)
    )
    begin = jnp.minimum(begin, length - widths)
    chunks = (begin + widths + QB - 1) // QB
    return ids, jnp.stack([begin, kind, chunks]).astype(jnp.int32)


def local(tokens, cotangent, segment_ids, pad_mask, lengths, params):
    rows, width = tokens.shape
    wide, narrow = lax.axis_size("wide"), lax.axis_size("narrow")
    devices = wide * narrow
    att_count = 4 * width * width + 6 * width
    att_rows = (att_count // LANES + devices - 1) // devices
    mlp_rows = params.shape[0] - att_rows
    paired = (wide, narrow) == (4, 8)
    scale = 1.0 / math.sqrt(rows * devices)

    position = jnp.arange(rows, dtype=jnp.int32)
    real = (pad_mask > 0) & (position < lengths[0])
    ids, windows = key_windows(segment_ids, real)
    query_ids = ids.astype(F32).reshape(rows // QB, QB)

    if not paired:
        me = jnp.zeros((1,), jnp.int32)
        att, mlp = gather_plainly(params, att_rows, width)
        n1, qkv, small = project_qkv(me, tokens, att)
        mixed, x1, branch, n2, dm, stats, gb2 = attend(
            me, windows, qkv, tokens, cotangent, query_ids, small, att
        )
        u, dz, gb1, *gmlp = feed_forward(me, n2, dm, small, mlp)
        output, gs2 = feed_forward_out(me, u, x1, cotangent, small, mlp)
        dx1, da, gwo0, gwo1, others = split(
            me, dz, x1, cotangent, branch, mixed, small, mlp, att
        )
        small_mlp = jnp.concatenate([others[:12], gb1, gb2, gs2])
        small_proj = others[12:]
        dqkv0 = attend_back(0, windows, qkv, da, stats, query_ids)
        dqkv1 = attend_back(1, windows, qkv, da, stats, query_ids)
        gatt0 = weight_grad(me, n1, dqkv0, gwo0)
        grad_input, *gatt1 = qkv_back(
            me, tokens, n1, dx1, dqkv0, dqkv1, small, small_proj, small_mlp, gwo1, att
        )
        owned = reduce_plainly(gatt0, gatt1, gmlp, att_rows, mlp_rows, width, devices)
        return output, grad_input, owned * scale

    me = lax.axis_index(AXES).astype(jnp.int32).reshape(1)
    tails = jnp.concatenate([params[att_rows - ATT_BEFORE : att_rows], params[-MLP_BEFORE:]])
    heads = jnp.concatenate([params[:ATT_AFTER], params[att_rows : att_rows + MLP_AFTER]])
    before, beyond = overhangs(att_rows, mlp_rows)
    heads = lax.ppermute(heads.astype(BF16), AXES, [(d + 1, d) for d in beyond])
    tails = lax.ppermute(tails.astype(BF16), AXES, [(d - 1, d) for d in before])
    att_own, mlp_own = pack(me, params, tails, heads, att_rows)

    got = [exchange(att_own, k * Z0) for k in range(1, 4)]
    a, b = along_z(att_own[0], att_own[1], got)
    a, b, mlp_own, windows, query_ids = together(a, b, mlp_own, windows, query_ids)
    ax, by = exchange(a, X), exchange(b, Y)
    z1, z3 = exchange(mlp_own, Z0), exchange(mlp_own, 3 * Z0)
    a, b = joined(a, ax), joined(b, by)
    a, b, z1, z3, mlp_own = together(a, b, z1, z3, mlp_own)
    ay, bx = exchange(a, Y), exchange(b, X)
    ac, bc = exchange(a, C), exchange(b, C)
    z2 = exchange(mlp_own, 2 * Z0)
    m, n = along_z(mlp_own[0], mlp_own[1], [z1, z2, z3])
    ay, bx, ac, bc, m, n = together(ay, bx, ac, bc, m, n)
    ayc, bxc = exchange(ay, C), exchange(bx, C)
    att = together(a, ay, ac, ayc, b, bx, bc, bxc, m, n, tokens)
    *att, m, n, tokens_now = att
    mx, ny = exchange(m, X), exchange(n, Y)
    n1, qkv, small = project_qkv(me, tokens_now, att)
    m, n = joined(m, mx), joined(n, ny)
    m, n, qkv = together(m, n, qkv)
    my, nx = exchange(m, Y), exchange(n, X)
    mc, nc = exchange(m, C), exchange(n, C)
    mixed, x1, branch, n2, dm, stats, gb2 = attend(
        me, windows, qkv, tokens, cotangent, query_ids, small, att
    )
    m, n, my, nx, mc, nc, n2 = together(m, n, my, nx, mc, nc, n2)
    myc, nxc = exchange(my, C), exchange(nx, C)
    mlp = (m, my, mc, myc, n, nx, nc, nxc)

    u, dz, gb1, *gmlp = feed_forward(me, n2, dm, small, mlp)

    mc, nc = exchange(gmlp[1], C), exchange(gmlp[3], C)
    output, gs2 = feed_forward_out(me, u, x1, cotangent, small, mlp)
    mc, nc, dz, gs2 = together(mc, nc, dz, gs2)
    m, n = [gmlp[0], mc], [gmlp[2], nc]
    my, nx, dz = together(sent(m), sent(n), dz)
    my, nx = exchange(my, Y), exchange(nx, X)
    dx1, da, gwo0, gwo1, others = split(
        me, dz, x1, cotangent, branch, mixed, small, mlp, att
    )
    dqkv0 = attend_back(0, windows, qkv, da, stats, query_ids)
    gatt0 = weight_grad(me, n1, dqkv0, gwo0)
    my, nx, da, *gatt0 = together(my, nx, da, *gatt0)
    m, n = kept(m) + [my], kept(n) + [nx]
    mx, ny, da, *gatt0 = together(sent(m), sent(n), da, *gatt0)
    mx, ny = exchange(mx, X), exchange(ny, Y)
    ac, bc = exchange(gatt0[1], C), exchange(gatt0[3], C)
    dqkv1 = attend_back(1, windows, qkv, da, stats, query_ids)
    mx, ny, ac, bc, dqkv1 = together(mx, ny, ac, bc, dqkv1)
    m, n = kept(m) + [mx], kept(n) + [ny]
    z1, z2, z3 = [z_part(m, n, k).astype(BF16) for k in range(1, 4)]
    a, b = [gatt0[0], ac], [gatt0[2], bc]
    ay, bx, z1, z2, z3, dqkv1 = together(sent(a), sent(b), z1, z2, z3, dqkv1)
    z1, z2 = exchange(z1, Z0), exchange(z2, 2 * Z0)
    ay, bx = exchange(ay, Y), exchange(bx, X)
    small_mlp = jnp.concatenate([others[:12], gb1, gb2, gs2])
    grad_input, *gatt1 = qkv_back(
        me, tokens, n1, dx1, dqkv0, dqkv1, small, others[12:], small_mlp, gwo1, att
    )
    ay, bx, z1, z2, *gatt1 = together(ay, bx, z1, z2, *gatt1)
    a, b = kept(a) + [ay], kept(b) + [bx]
    ax, by, c1, d1, z3 = together(sent(a), sent(b), gatt1[1], gatt1[3], z3)
    c1, d1 = exchange(c1, C), exchange(d1, C)
    ax, by = exchange(ax, X), exchange(by, Y)
    z3a = exchange(z3[0], 3 * Z0)
    c, d = [gatt1[0], c1], [gatt1[2], d1]
    a, b = kept(a) + [ax], kept(b) + [by]
    sends = [z_part(a, b, k).astype(BF16) for k in range(1, 4)]
    cy, dx, z3a, z3, *sends = together(sent(c), sent(d), z3a, z3, *sends)
    cy, dx = exchange(cy, Y), exchange(dx, X)
    got = [exchange(part, (k + 1) * Z0) for k, part in enumerate(sends)]
    c, d = kept(c) + [cy], kept(d) + [dx]
    cx, dy, z3, *got = together(sent(c), sent(d), z3, *got)
    z3b = exchange(z3[1], 3 * Z0)
    group0 = sum_terms([z_part(a, b, 0)] + got)
    cx, dy = exchange(cx, X), exchange(dy, Y)
    c, d = kept(c) + [cx], kept(d) + [dy]
    m_own = sum_terms([z_part(m, n, 0), z1, z2, jnp.stack([z3a, z3b])])
    sends = [z_part(c, d, k).astype(BF16) for k in range(1, 4)]
    group0, m_own, *sends = together(group0, m_own, *sends)
    got = [exchange(part, (k + 1) * Z0) for k, part in enumerate(sends)]
    group1 = sum_terms([z_part(c, d, 0)] + got)
    mine, to_before, to_after = spread(me, group0, group1, m_own, att_rows, mlp_rows, scale)
    below = lax.ppermute(to_after, AXES, [(d, d + 1) for d in beyond])
    above = lax.ppermute(to_before, AXES, [(d, d - 1) for d in before])
    grad_params = close(mine, below, above, att_rows)
    return output, grad_input, grad_params


def solution(mesh):
    return jax.shard_map(
        local,
        mesh=mesh,
        in_specs=(
            P(AXES, None),
            P(AXES, None),
            P(AXES),
            P(AXES),
            P(AXES),
            P(AXES, None),
        ),
        out_specs=(P(AXES, None), P(AXES, None), P(AXES, None)),
        check_vma=False,
    )
```

```python
import math
from functools import partial

import jax
import jax.numpy as jnp
from jax import lax
from jax.experimental import pallas as pl
from jax.experimental.pallas import tpu as pltpu
from jax.sharding import PartitionSpec as P

FF = 3072
HEADS = 12
EPSILON = 1e-06
NEGATIVE = -1e30
AXES = ("wide", "narrow")
LANES = 128
SUB = 16
QB = 128
MEGA = 1 << 20
GRANT = 58 * MEGA
F32 = jnp.float32
BF16 = jnp.bfloat16

BLOCKS = 32
QKV_BLOCKS, QKV_RT, QKV_CT = 24, 2, 18
WO_BLOCKS, WO_RT, WO_CT = 8, 6, 6
W1_BLOCKS, W1_RT, W1_CT = 16, 3, 24
W2_BLOCKS, W2_RT, W2_CT = 16, 12, 6
ATT_HALF, MLP_HALF = 18, 36
ATT_SENT = ATT_HALF + 1
ATT_PART = 9
HALF_BLOCKS = BLOCKS // 2
CHUNK = 768
CHUNKS = FF // CHUNK

G1, C1, BQ, BV, BO, S1 = 0, 6, 12, 18, 24, 30
G2, C2, B1, B2, S2 = 36, 42, 48, 72, 78
SMALL = 88

NT = (((1,), (1,)), ((), ()))
NN = (((1,), (0,)), ((), ()))
TN = (((0,), (0,)), ((), ()))


def mm(lhs, rhs, dims):
    return lax.dot_general(lhs, rhs, dims, preferred_element_type=F32)


def row_of(ref, first, count):
    return jnp.concatenate([ref[first + k : first + k + 1, :] for k in range(count)], axis=1)


def put_row(ref, first, values):
    for k in range(values.shape[1] // LANES):
        ref[first + k : first + k + 1, :] = values[:, k * LANES : (k + 1) * LANES]


def fold8(values):
    rows, columns = values.shape
    return jnp.sum(values.reshape(rows // 8, 8, columns), axis=0)


def total(values):
    return jnp.sum(values, axis=0, keepdims=True)


def vmem():
    return pl.BlockSpec(memory_space=pltpu.VMEM)


def smem():
    return pl.BlockSpec(memory_space=pltpu.SMEM)


def hbm():
    return pl.BlockSpec(memory_space=pltpu.HBM)


def shape(dims, kind):
    return jax.ShapeDtypeStruct(dims, kind)


def cost(flops, moved, exps=0):
    return pl.CostEstimate(flops=int(flops), transcendentals=int(exps), bytes_accessed=int(moved))


def normalized(values):
    center = values - jnp.mean(values, axis=-1, keepdims=True)
    inverse = lax.rsqrt(jnp.mean(center * center, axis=-1, keepdims=True) + EPSILON)
    return center * inverse, inverse


def norm_pullback(unit, inverse, grad, gain):
    scaled = grad * gain
    first = jnp.mean(scaled, axis=-1, keepdims=True)
    second = jnp.mean(scaled * unit, axis=-1, keepdims=True)
    return inverse * (scaled - first - unit * second)


def gelu_pair(z):
    magnitude = jnp.abs(z)
    t = 1.0 / (1.0 + (0.3275911 * math.sqrt(0.5)) * magnitude)
    density = jnp.exp(z * z * -0.5)
    tail = 0.5 * 1.061405429
    tail = tail * t + 0.5 * -1.453152027
    tail = tail * t + 0.5 * 1.421413741
    tail = tail * t + 0.5 * -0.284496736
    tail = tail * t + 0.5 * 0.254829592
    tail = tail * t * density
    cumulative = jnp.where(z < 0, tail, 1.0 - tail)
    return z * cumulative, cumulative + z * density * (1.0 / math.sqrt(2.0 * math.pi))


def fetch(copies):
    for copy in copies:
        copy.start()


def settle(copies):
    for copy in copies:
        copy.wait()


ATT_BEFORE, ATT_AFTER = 64, 32
MLP_BEFORE, MLP_AFTER = 64, 40


def window_offsets(me, att_rows, mlp_rows):
    att = ATT_BEFORE + 12 + me * (576 - att_rows) + jnp.where(me < QKV_BLOCKS, 0, 12)
    mlp = MLP_BEFORE + 12 + me * (1152 - mlp_rows) + jnp.where(me < W1_BLOCKS, 0, 24)
    return att, mlp


def each_tile(me, act):
    for name, blocks, rt_count, ct_count, mine in (
        ("qkv", QKV_BLOCKS, QKV_RT, QKV_CT, me < QKV_BLOCKS),
        ("wo", WO_BLOCKS, WO_RT, WO_CT, me >= QKV_BLOCKS),
        ("w1", W1_BLOCKS, W1_RT, W1_CT, me < W1_BLOCKS),
        ("w2", W2_BLOCKS, W2_RT, W2_CT, me >= W1_BLOCKS),
    ):

        @pl.when(mine)
        def _(name=name, rt_count=rt_count, ct_count=ct_count):
            for ct in range(ct_count):
                for rt in range(rt_count):
                    act(name, rt, ct, rt * SUB * ct_count + ct, ct_count)


def half_place(name, rt, ct):
    if name == "qkv":
        return ct // 9, ct % 9 * QKV_RT + rt
    if name == "wo":
        return rt // 3, rt % 3 * WO_CT + ct
    if name == "w1":
        return ct // 12, ct % 12 * W1_RT + rt
    return rt // 6, rt % 6 * W2_CT + ct


def part_place(name, rt, ct):
    if name == "qkv":
        return ct % 6 // 3, rt, ct // 6 * 3 + ct % 3
    place = rt * WO_CT + ct
    return place // 18, place // ATT_PART % 2, place % ATT_PART


def qkv_group(g):
    return [6 * third + 3 * g + i for third in range(3) for i in range(3)]


def small_rows(me, act):
    @pl.when(me == 0)
    def _():
        act("att", True, 12, G1)
        act("mlp", True, 12, G2)

    @pl.when(me == QKV_BLOCKS - 1)
    def _():
        act("att", False, 12, BQ)

    @pl.when(me == W1_BLOCKS - 1)
    def _():
        act("mlp", False, 24, B1)

    @pl.when(me == BLOCKS - 1)
    def _():
        act("att", False, 12, BO)
        act("mlp", False, 12, B2)


OWNERS = (0, W1_BLOCKS - 1, QKV_BLOCKS - 1, BLOCKS - 1)


def sent_rows(kind, first):
    return 12 if kind == "mlp" and first in (G2, B2) else 0


def pack_kernel(att_rows, me_ref, own, tails, heads, att, mlp, win_a, win_m, table):
    me = me_ref[0]
    mlp_rows = own.shape[0] - att_rows
    win_a[0:ATT_BEFORE, :] = tails[0:ATT_BEFORE, :].astype(F32)
    win_a[ATT_BEFORE : ATT_BEFORE + att_rows, :] = own[0:att_rows, :]
    win_a[ATT_BEFORE + att_rows :, :] = heads[0:ATT_AFTER, :].astype(F32)
    win_m[0:MLP_BEFORE, :] = tails[ATT_BEFORE:, :].astype(F32)
    win_m[MLP_BEFORE : MLP_BEFORE + mlp_rows, :] = own[att_rows:, :]
    win_m[MLP_BEFORE + mlp_rows :, :] = heads[ATT_AFTER:, :].astype(F32)
    att_off, mlp_off = window_offsets(me, att_rows, mlp_rows)

    def tile(name, rt, ct, first, stride):
        attention = name in ("qkv", "wo")
        window, out, off = (win_a, att, att_off) if attention else (win_m, mlp, mlp_off)
        values = window[pl.ds(off + first, SUB, stride=stride), :]
        out[half_place(name, rt, ct)] = values.astype(BF16)

    each_tile(me, tile)
    table[...] = jnp.zeros_like(table)

    def vector(kind, before, rows, first):
        window, off, size = (win_a, att_off, 576) if kind == "att" else (win_m, mlp_off, 1152)
        start = off - 12 if before else off + size
        place = sent_rows(kind, first)
        table[place : place + rows, :] = window[pl.ds(start, rows), :]

    small_rows(me, vector)
    att[0, ATT_HALF] = table[0:SUB, :].astype(BF16)
    att[1, ATT_HALF] = table[SUB : 2 * SUB, :].astype(BF16)


def pack(me, own, tails, heads, att_rows):
    mlp_rows = own.shape[0] - att_rows
    return pl.pallas_call(
        partial(pack_kernel, att_rows),
        out_shape=(
            shape((2, ATT_SENT, SUB, LANES), BF16),
            shape((2, MLP_HALF, SUB, LANES), BF16),
        ),
        in_specs=[smem(), vmem(), vmem(), vmem()],
        out_specs=(vmem(), vmem()),
        scratch_shapes=[
            pltpu.VMEM((ATT_BEFORE + att_rows + ATT_AFTER, LANES), F32),
            pltpu.VMEM((MLP_BEFORE + mlp_rows + MLP_AFTER, LANES), F32),
            pltpu.VMEM((2 * SUB, LANES), F32),
        ],
        name="pack",
    )(me, own, tails, heads)


def spread_kernel(
    att_rows, scale, me_ref, group0, group1, mlp, mine, to_before, to_after, win_a, win_m, table
):
    me = me_ref[0]
    mlp_rows = mine.shape[0] - att_rows
    att_off, mlp_off = window_offsets(me, att_rows, mlp_rows)
    win_a[...] = jnp.zeros_like(win_a)
    win_m[...] = jnp.zeros_like(win_m)

    def tile(name, rt, ct, first, stride):
        if name in ("qkv", "wo"):
            g, half, index = part_place(name, rt, ct)
            values = (group0, group1)[g][half, index]
            win_a[pl.ds(att_off + first, SUB, stride=stride), :] = values * scale
        else:
            values = mlp[half_place(name, rt, ct)]
            win_m[pl.ds(mlp_off + first, SUB, stride=stride), :] = values * scale

    each_tile(me, tile)
    for h in range(2):
        table[SUB * h : SUB * h + SUB, :] = group1[h, ATT_PART] * scale

    def vector(kind, before, rows, first):
        window, off, size = (win_a, att_off, 576) if kind == "att" else (win_m, mlp_off, 1152)
        start = off - 12 if before else off + size
        place = sent_rows(kind, first)
        window[pl.ds(start, rows), :] = table[place : place + rows, :]

    small_rows(me, vector)
    mine[0:att_rows, :] = win_a[ATT_BEFORE : ATT_BEFORE + att_rows, :]
    mine[att_rows:, :] = win_m[MLP_BEFORE : MLP_BEFORE + mlp_rows, :]
    to_before[0:ATT_BEFORE, :] = win_a[0:ATT_BEFORE, :]
    to_before[ATT_BEFORE:, :] = win_m[0:MLP_BEFORE, :]
    to_after[0:ATT_AFTER, :] = win_a[ATT_BEFORE + att_rows :, :]
    to_after[ATT_AFTER:, :] = win_m[MLP_BEFORE + mlp_rows :, :]


def spread(me, group0, group1, mlp, att_rows, mlp_rows, scale):
    return pl.pallas_call(
        partial(spread_kernel, att_rows, scale),
        out_shape=(
            shape((att_rows + mlp_rows, LANES), F32),
            shape((ATT_BEFORE + MLP_BEFORE, LANES), F32),
            shape((ATT_AFTER + MLP_AFTER, LANES), F32),
        ),
        in_specs=[smem(), vmem(), vmem(), vmem()],
        out_specs=(vmem(), vmem(), vmem()),
        scratch_shapes=[
            pltpu.VMEM((ATT_BEFORE + att_rows + ATT_AFTER, LANES), F32),
            pltpu.VMEM((MLP_BEFORE + mlp_rows + MLP_AFTER, LANES), F32),
            pltpu.VMEM((2 * SUB, LANES), F32),
        ],
        name="spread",
    )(me, group0, group1, mlp)


def close_kernel(att_rows, mine, below, above, out):
    rows = mine.shape[0]
    out[...] = mine[...]
    out[0:ATT_AFTER, :] += below[0:ATT_AFTER, :]
    out[att_rows : att_rows + MLP_AFTER, :] += below[ATT_AFTER:, :]
    out[att_rows - ATT_BEFORE : att_rows, :] += above[0:ATT_BEFORE, :]
    out[rows - MLP_BEFORE : rows, :] += above[ATT_BEFORE:, :]


def close(mine, below, above, att_rows):
    return pl.pallas_call(
        partial(close_kernel, att_rows),
        out_shape=shape(mine.shape, F32),
        in_specs=[vmem()] * 3,
        out_specs=vmem(),
        name="close",
    )(mine, below, above)


def spot(h, d):
    x, c, z, y = d >> 4, (d >> 3) & 1, (d >> 1) & 3, d & 1
    return c * 16 + (y * 8 + x * 4 if h == 0 else x * 8 + y * 4) + z


SLOTS = [sorted(range(BLOCKS), key=partial(spot, h)) for h in range(2)]


def fill_spots(me, spots):
    for h in range(2):
        mine = spot(h, me)
        for d in range(BLOCKS):
            spots[h, d] = jnp.bitwise_xor(mine, spot(h, d))


def slots_scratch(tiles):
    return pltpu.VMEM((2, BLOCKS, tiles, SUB, LANES), BF16)


def spots_scratch():
    return pltpu.SMEM((2, BLOCKS), jnp.int32)


def arriving_slots(buffers, w, sems):
    return [
        pltpu.make_async_copy(buffers[i], w.at[i // 4, pl.ds(i % 4 * 8, 8)], sems.at[i])
        for i in range(8)
    ]


def leaving_slots(buffers, w, sems):
    return [
        pltpu.make_async_copy(w.at[i // 2, pl.ds(i % 2 * 16, 16)], buffers[i], sems.at[i])
        for i in range(4)
    ]


def qkv_column(w, spots, ct):
    h, place = ct // 9, ct % 9 * QKV_RT
    tiles = [w[h, spots[h, d], place + rt] for d in range(QKV_BLOCKS) for rt in range(QKV_RT)]
    return jnp.concatenate(tiles, axis=0)


def wo_matrix(w, spots):
    columns = []
    for ct in range(WO_CT):
        tiles = [
            w[rt // 3, spots[rt // 3, QKV_BLOCKS + i] & 7, rt % 3 * WO_CT + ct]
            for i in range(WO_BLOCKS)
            for rt in range(WO_RT)
        ]
        columns.append(jnp.concatenate(tiles, axis=0))
    return jnp.concatenate(columns, axis=1)


def dma(count):
    return pltpu.SemaphoreType.DMA((count,))


def norm_rows(rows, gain, shift, source, target, step=256):
    def one(i, carry):
        at = pl.ds(pl.multiple_of(i * step, step), step)
        unit, _ = normalized(source[at, :].astype(F32))
        target[at, :] = (unit * gain + shift).astype(BF16)
        return carry

    lax.fori_loop(0, rows // step, one, 0)


def qkv_kernel(me_ref, tokens, *refs):
    buffers, (n1, qkv, small, w, spots, x, unit, triple, sems, own) = refs[:8], refs[8:]
    coming = pltpu.make_async_copy(tokens, x, own.at[0])
    coming.start()
    weights = arriving_slots(buffers, w, sems)
    fetch(weights)
    fill_spots(me_ref[0], spots)
    settle(weights)
    tables = [
        jnp.concatenate([w[h, spots[h, d], ATT_HALF] for h in range(2)], axis=0).astype(F32)
        for d in OWNERS
    ]
    small[G1 : G1 + 12, :] = tables[0][0:12]
    small[G2 : G2 + 12, :] = tables[0][12:24]
    small[B1 : B1 + 24, :] = tables[1][0:24]
    small[BQ : BQ + 12, :] = tables[2][0:12]
    small[BO : BO + 12, :] = tables[3][0:12]
    small[B2 : B2 + 12, :] = tables[3][12:24]
    small[SMALL - 4 :, :] = jnp.zeros((4, LANES), F32)
    coming.wait()
    norm_rows(x.shape[0], row_of(small, G1, 6), row_of(small, C1, 6), x, unit)
    going = [pltpu.make_async_copy(unit, n1, own.at[0])]
    going[0].start()
    bias = jnp.concatenate(
        [row_of(small, BQ, 6), jnp.zeros((1, 768), F32), row_of(small, BV, 6)], axis=1
    )
    for c in range(QKV_CT // 2):
        weight = jnp.concatenate([qkv_column(w, spots, 2 * c + i) for i in range(2)], axis=1)
        lanes = slice(256 * c, 256 * c + 256)
        triple[:, lanes] = (mm(unit[...], weight, NN) + bias[:, lanes]).astype(BF16)
        going.append(
            pltpu.make_async_copy(triple.at[:, lanes], qkv.at[:, lanes], own.at[1 + c])
        )
        going[-1].start()
    settle(going)


def project_qkv(me, tokens, att):
    rows, width = tokens.shape
    return pl.pallas_call(
        qkv_kernel,
        out_shape=(
            shape((rows, width), BF16),
            shape((rows, 3 * width), BF16),
            shape((SMALL, LANES), F32),
        ),
        in_specs=[smem(), hbm()] + [hbm()] * 8,
        out_specs=(hbm(), hbm(), vmem()),
        scratch_shapes=[
            slots_scratch(ATT_SENT),
            spots_scratch(),
            pltpu.VMEM((rows, width), BF16),
            pltpu.VMEM((rows, width), BF16),
            pltpu.VMEM((rows, 3 * width), BF16),
            dma(8),
            dma(1 + QKV_CT // 2),
        ],
        compiler_params=pltpu.CompilerParams(vmem_limit_bytes=GRANT),
        cost_estimate=cost(6 * rows * width * width, 12 * rows * width),
        name="qkv_forward",
    )(me, tokens, *att)


CLASSES = (128, 256, 320, 384, 448, 512, 768)


def head_masked(block):
    lane = lax.broadcasted_iota(jnp.int32, block.shape, 1)
    zero = jnp.zeros_like(block)
    return jnp.concatenate(
        [jnp.where(lane < 64, block, zero), jnp.where(lane >= 64, block, zero)], axis=0
    )


def pick_heads(both):
    return jnp.concatenate([both[0:64, 0:QB], both[64:128, QB : 2 * QB]], axis=0)


def pieces_of_window(width):
    return [slice(first, min(first + QB, width)) for first in range(0, width, QB)]


def spread_ids(query_ids, key_ids):
    for b in range(query_ids.shape[0]):
        row = jnp.broadcast_to(query_ids[b : b + 1, :], (QB, QB))
        key_ids[b * QB : (b + 1) * QB, :] = row.T


def mask_bias(start, width, b, key_ids, query_ids, bias):
    for piece in pieces_of_window(width):
        size = piece.stop - piece.start
        at = pl.ds(pl.multiple_of(start + piece.start, SUB), size)
        same = key_ids[at, :] == query_ids[pl.ds(b, 1), :]
        bias[piece, :] = jnp.where(same, 0.0, NEGATIVE)


PAIRS = HEADS // 2


def attend_block(b, start, width, qkv, mixed, stats, bias, scores):
    rows = pl.ds(pl.multiple_of(b * QB, QB), QB)
    pieces = pieces_of_window(width)
    for p in range(PAIRS):
        lanes, key_lanes, value_lanes = [
            slice(LANES * (PAIRS * third + p), LANES * (PAIRS * third + p + 1))
            for third in range(3)
        ]
        queries = head_masked(qkv[rows, lanes] * 0.125)
        highest = jnp.full((8, 2 * QB), NEGATIVE, F32)
        for piece in pieces:
            size = piece.stop - piece.start
            at = pl.ds(pl.multiple_of(start + piece.start, SUB), size)
            part = mm(qkv[at, key_lanes], queries, NT)
            part = part + jnp.concatenate([bias[piece, :]] * 2, axis=1)
            scores[p, piece, :] = part
            highest = jnp.maximum(highest, jnp.max(part.reshape(size // 8, 8, 2 * QB), axis=0))
        highest = jnp.max(highest, axis=0, keepdims=True)
        summed = jnp.zeros((8, 2 * QB), F32)
        both = jnp.zeros((LANES, 2 * QB), F32)
        for piece in pieces:
            size = piece.stop - piece.start
            at = pl.ds(pl.multiple_of(start + piece.start, SUB), size)
            raised = jnp.exp(scores[p, piece, :] - highest)
            summed = summed + fold8(raised)
            both = both + mm(qkv[at, value_lanes], raised.astype(BF16), TN)
        inverse = 1.0 / total(summed)
        mixed[rows, lanes] = pick_heads(both * inverse).T.astype(BF16)
        stats[b * PAIRS + p, 0:1, :] = highest
        stats[b * PAIRS + p, 1:2, :] = inverse


def wo_scratch():
    return pltpu.VMEM((2, WO_BLOCKS, ATT_SENT, SUB, LANES), BF16)


def wo_copies(buffers, w, sems, core, x):
    copies = []
    for y in range(2):
        source = buffers[2 * core + y].at[pl.ds(4 * x, 4)]
        copies.append(pltpu.make_async_copy(source, w.at[0, pl.ds(4 * y, 4)], sems.at[y]))
    copies.append(pltpu.make_async_copy(buffers[4 + 2 * core + x], w.at[1], sems.at[2]))
    return copies


def fetch_wo(me, buffers, w, spots, sems):
    fill_spots(me, spots)
    for h in range(2):
        for i in range(WO_BLOCKS):
            place = spot(h, jnp.bitwise_xor(me, QKV_BLOCKS + i) & 7)
            spots[h, QKV_BLOCKS + i] = (place >> (1 if h == 0 else 0)) & 4 | place & 3
    far = jnp.bitwise_xor(me, QKV_BLOCKS)
    for core in range(2):
        for x in range(2):

            @pl.when((far >> 3) == 2 * x + core)
            def _(core=core, x=x):
                fetch(wo_copies(buffers, w, sems, core, x))


def wait_wo(buffers, w, sems):
    settle(wo_copies(buffers, w, sems, 0, 0))


def attend_kernel(me_ref, windows, qkv, tokens, cot, query_ids, small, *refs):
    buffers, refs = refs[:8], refs[8:]
    mixed, x1, branch, n2, dm, stats, gb2 = refs[:7]
    key_ids, triple, x, g, mix, mid, out, unit, scaled, bias, scores, w, spots = refs[7:20]
    sems, own, chunk_sems = refs[20:]
    rows = tokens.shape[0]
    blocks = rows // QB

    def chunk(i):
        at = pl.ds(pl.multiple_of(i * QB, QB), QB)
        return pltpu.make_async_copy(qkv.at[at, :], triple.at[at, :], chunk_sems.at[i])

    for i in range(blocks):
        chunk(i).start()
    coming = [
        pltpu.make_async_copy(tokens, x, own.at[0]),
        pltpu.make_async_copy(cot, g, own.at[1]),
    ]
    fetch(coming)
    fetch_wo(me_ref[0], buffers, w, spots, sems)
    spread_ids(query_ids, key_ids)

    def one_block(b, loaded):
        start = pl.multiple_of(windows[0, b], SUB)
        needed = jnp.maximum(windows[2, b], loaded)

        def arrived(i, carry):
            chunk(i).wait()
            return carry

        lax.fori_loop(loaded, needed, arrived, 0)
        for index, width in enumerate(CLASSES):

            @pl.when(windows[1, b] == index)
            def _(width=width):
                mask_bias(start, width, b, key_ids, query_ids, bias)
                attend_block(b, start, width, triple, mix, stats, bias, scores)

        return needed

    loaded = lax.fori_loop(0, blocks, one_block, jnp.int32(0))

    def arrived(i, carry):
        chunk(i).wait()
        return carry

    lax.fori_loop(loaded, blocks, arrived, 0)
    going = [pltpu.make_async_copy(mix, mixed, own.at[2])]
    going[0].start()
    wait_wo(buffers, w, sems)
    settle(coming)
    bo, s1 = row_of(small, BO, 6), row_of(small, S1, 6)
    gain, shift = row_of(small, G2, 6), row_of(small, C2, 6)
    s2 = row_of(small, S2, 6)
    weight = wo_matrix(w, spots)
    step = 256
    sums = jnp.zeros((8, 768), F32)
    for i in range(rows // step):
        at = slice(i * step, (i + 1) * step)
        made = mm(mix[at, :], weight, NN) + bo
        out[at, :] = made.astype(BF16)
        values = x[at, :].astype(F32) + s1 * made
        mid[at, :] = values
        normal, _ = normalized(values)
        unit[at, :] = (normal * gain + shift).astype(BF16)
        rounded = (g[at, :].astype(F32) * s2).astype(BF16)
        scaled[at, :] = rounded
        sums = sums + fold8(rounded.astype(F32))
        for k, (source, target) in enumerate(
            ((out, branch), (mid, x1), (unit, n2), (scaled, dm))
        ):
            sem = own.at[3 + 4 * i + k]
            going.append(pltpu.make_async_copy(source.at[at, :], target.at[at, :], sem))
            going[-1].start()
    put_row(gb2, 0, total(sums))
    settle(going)


def attend(me, windows, qkv, tokens, cot, query_ids, small, att):
    rows, width = tokens.shape
    row = lambda kind: pltpu.VMEM((rows, width), kind)
    return pl.pallas_call(
        attend_kernel,
        out_shape=(
            shape((rows, width), BF16),
            shape((rows, width), F32),
            shape((rows, width), BF16),
            shape((rows, width), BF16),
            shape((rows, width), BF16),
            shape((rows // QB * PAIRS, 2, 2 * QB), F32),
            shape((6, LANES), F32),
        ),
        in_specs=[smem(), smem(), hbm(), hbm(), hbm(), vmem(), vmem()] + [hbm()] * 8,
        out_specs=(hbm(),) * 5 + (vmem(), vmem()),
        scratch_shapes=[
            pltpu.VMEM((rows, QB), F32),
            pltpu.VMEM((rows, 3 * width), BF16),
            row(BF16),
            row(BF16),
            row(BF16),
            row(F32),
            row(BF16),
            row(BF16),
            row(BF16),
            pltpu.VMEM((CLASSES[-1], QB), F32),
            pltpu.VMEM((PAIRS, CLASSES[-1], 2 * QB), F32),
            wo_scratch(),
            spots_scratch(),
            dma(3),
            dma(3 + 4 * rows // 256),
            dma(rows // QB),
        ],
        compiler_params=pltpu.CompilerParams(vmem_limit_bytes=GRANT),
        cost_estimate=cost(2 * rows * rows * width, 20 * rows * width, 4 * rows * rows),
        name="attend_forward",
    )(me, windows, qkv, tokens, cot, query_ids, small, *att)


def lay_matrix(w, spots, name, blocks, first, rt_count, columns, out):
    def one_block(d, carry):
        places = [spots[h, first + d] for h in range(2)]
        base = pl.multiple_of(d * rt_count * SUB, SUB)
        for rt in range(rt_count):
            for column, ct in enumerate(columns):
                h, index = half_place(name, rt, ct)
                at = pl.ds(pl.multiple_of(base + rt * SUB, SUB), SUB)
                out[at, LANES * column : LANES * (column + 1)] = w[h, places[h], index]
        return carry

    lax.fori_loop(0, blocks, one_block, 0)


def lay_w1(w, spots, out):
    lay_matrix(w, spots, "w1", W1_BLOCKS, 0, W1_RT, range(W1_CT), out)


def lay_w2(w, spots, out):
    lay_matrix(w, spots, "w2", W2_BLOCKS, W1_BLOCKS, W2_RT, range(W2_CT), out)


def w2_place(spots, f, row, ct):
    rt = row % W2_RT
    h = rt // 6
    return h, spots[h, W1_BLOCKS + 4 * f + row // W2_RT], rt % 6 * W2_CT + ct


TALL = 256
PARTS = CHUNK // 256


def device_of(x, c, z, y):
    return x * 16 + c * 8 + z * 2 + y


W1_RUNS = [
    [(0, device_of(0, c, 0, y), 4) for c in range(2) for y in range(2)],
    [(1, device_of(0, c, 0, 0), 8) for c in range(2)],
]
W2_RUNS = [
    [(h, device_of(1, f >> 1, 2 * (f & 1), y), 2) for h in range(2) for y in range(2)]
    for f in range(CHUNKS)
]
RUN_ORDER = W1_RUNS[0] + W2_RUNS[0] + W2_RUNS[1] + W1_RUNS[1] + W2_RUNS[2] + W2_RUNS[3]


class Runs:
    def __init__(self, buffers, w, spots, sems, out=False):
        self.buffers, self.w, self.spots, self.sems, self.out = buffers, w, spots, sems, out
        self.each = len(buffers) // 2

    def copy(self, run, which, index, place):
        h, first, size = run
        outer = self.buffers[self.each * h + which].at[pl.ds(index, size)]
        inner = self.w.at[h, pl.ds(place, size)]
        sem = self.sems.at[RUN_ORDER.index(run)]
        ends = (inner, outer) if self.out else (outer, inner)
        return pltpu.make_async_copy(*ends, sem)

    def start(self, runs):
        length = BLOCKS // self.each
        for run in runs:
            h, first, size = run
            place = self.spots[h, first] & (BLOCKS - size)
            for which in range(self.each):

                @pl.when(place // length == which)
                def _(run=run, which=which, place=place):
                    self.copy(run, which, place & (length - 1), place).start()

    def wait(self, runs):
        for run in runs:
            self.copy(run, 0, 0, 0).wait()


def mlp_kernel(me_ref, n2_in, dm_in, small, *refs):
    arriving, refs = refs[:8], refs[8:]
    u_out, dz_out, vectors, *leaving = refs[:7]
    w, first, second, spots, n2, dm, u, dz, zs, dus, bias_sums, b1_lines, sems, own = refs[7:]
    rows, width = n2.shape
    tiles = rows // TALL
    coming = [
        pltpu.make_async_copy(n2_in, n2, own.at[0]),
        pltpu.make_async_copy(dm_in, dm, own.at[1]),
    ]
    fetch(coming)
    fill_spots(me_ref[0], spots)
    incoming = Runs(arriving, w, spots, sems)
    incoming.start(RUN_ORDER)
    bias_sums[...] = jnp.zeros_like(bias_sums)
    for f in range(CHUNKS):
        b1_lines[f : f + 1, :] = row_of(small, B1 + 6 * f, 6)
    def lay_chunk(f, side):
        h, base = f >> 1, MLP_HALF // 2 * (f & 1)
        for d in range(W1_BLOCKS):
            place = spots[h, d]
            for rt in range(W1_RT):
                at = slice((d * W1_RT + rt) * SUB, (d * W1_RT + rt + 1) * SUB)
                for ct in range(6):
                    lanes = slice(LANES * ct, LANES * ct + LANES)
                    first[side, at, lanes] = w[h, place, base + ct * W1_RT + rt]
        for k in range(4):
            places = [spots[i, W1_BLOCKS + 4 * f + k] for i in range(2)]
            for rt in range(W2_RT):
                at = slice((k * W2_RT + rt) * SUB, (k * W2_RT + rt + 1) * SUB)
                for ct in range(W2_CT):
                    lanes = slice(LANES * ct, LANES * ct + LANES)
                    i, index = half_place("w2", rt, ct)
                    second[side, at, lanes] = w[i, places[i], index]

    incoming.wait(W1_RUNS[0] + W2_RUNS[0])
    lay_chunk(jnp.int32(0), jnp.int32(0))
    settle(coming)

    units = [(t, c) for c in range(PARTS) for t in range(tiles)]

    def lanes_of(f, c):
        return pl.ds(pl.multiple_of(CHUNK * f + 256 * c, 256), 256)

    def outward(f):
        chunk = pl.ds(pl.multiple_of(CHUNK * f, CHUNK), CHUNK)
        return [
            pltpu.make_async_copy(u.at[:, chunk], u_out.at[:, chunk], own.at[2 * f]),
            pltpu.make_async_copy(dz.at[:, chunk], dz_out.at[:, chunk], own.at[2 * f + 1]),
        ]

    def one_chunk(f, carry):
        for index in range(CHUNKS - 1):

            @pl.when(f == index)
            def _(index=index):
                incoming.wait(W2_RUNS[index + 1] + (W1_RUNS[1] if index == 1 else []))

        side = f & 1
        lay_chunk(jnp.minimum(f + 1, CHUNKS - 1), 1 - side)

        def multiply(unit, slot):
            t, c = unit
            at = slice(TALL * t, TALL * t + TALL)
            zs[slot] = mm(n2[at, :], first[side, :, 256 * c : 256 * c + 256], NN)
            dus[slot] = mm(dm[at, :], second[side, 256 * c : 256 * c + 256, :], NT)

        def activate(unit, slot):
            t, c = unit
            lanes = slice(256 * c, 256 * c + 256)
            bias = b1_lines[pl.ds(f, 1), lanes]
            folded = jnp.zeros((8, 256), F32)
            for r in range(TALL // 32):
                part = slice(32 * r, 32 * r + 32)
                place = slice(TALL * t + 32 * r, TALL * t + 32 * r + 32)
                value, slope = gelu_pair(zs[slot, part, :] + bias)
                u[place, lanes_of(f, c)] = value.astype(BF16)
                rounded = (dus[slot, part, :] * slope).astype(BF16)
                dz[place, lanes_of(f, c)] = rounded
                folded = folded + fold8(rounded.astype(F32))
            bias_sums[:, lanes_of(f, c)] += folded

        multiply(units[0], 0)
        for i, unit in enumerate(units):
            if i + 1 < len(units):
                multiply(units[i + 1], (i + 1) % 2)
            activate(unit, i % 2)
        fetch(outward(f))
        return carry

    lax.fori_loop(0, CHUNKS, one_chunk, 0)
    put_row(vectors, 0, total(bias_sums[...]))

    outgoing = Runs(leaving, w, spots, sems, out=True)

    def one_grad(f, carry):
        h, base = f >> 1, MLP_HALF // 2 * (f & 1)
        chunk = pl.ds(pl.multiple_of(CHUNK * f, CHUNK), CHUNK)
        for c in range(PARTS):
            lanes = slice(256 * c, 256 * c + 256)
            grad = mm(n2[:, lanes], dz[:, chunk], TN)
            for r in range(SUB):
                d, rt = (SUB * c + r) // W1_RT, (SUB * c + r) % W1_RT
                for ct in range(6):
                    tile = grad[SUB * r : SUB * r + SUB, LANES * ct : LANES * ct + LANES]
                    w[h, spots[h, d], base + ct * W1_RT + rt] = tile.astype(BF16)
        for side in range(2):

            @pl.when(f == 2 * side + 1)
            def _(side=side):
                outgoing.start(W1_RUNS[side])

        for c in range(PARTS):
            grad = mm(u[:, lanes_of(f, c)], dm[...], TN)
            for r in range(SUB):
                for ct in range(W2_CT):
                    tile = grad[SUB * r : SUB * r + SUB, LANES * ct : LANES * ct + LANES]
                    w[w2_place(spots, f, SUB * c + r, ct)] = tile.astype(BF16)
        for index in range(CHUNKS):

            @pl.when(f == index)
            def _(index=index):
                outgoing.start(W2_RUNS[index])

        return carry

    lax.fori_loop(0, CHUNKS, one_grad, 0)
    for f in range(CHUNKS):
        settle(outward(f))
    outgoing.wait(RUN_ORDER)


def feed_forward(me, n2, dm, small, mlp):
    rows, width = n2.shape
    half = shape((HALF_BLOCKS, MLP_HALF, SUB, LANES), BF16)
    return pl.pallas_call(
        mlp_kernel,
        out_shape=(
            shape((rows, FF), BF16),
            shape((rows, FF), BF16),
            shape((24, LANES), F32),
            half,
            half,
            half,
            half,
        ),
        in_specs=[smem(), hbm(), hbm(), vmem()] + [hbm()] * 8,
        out_specs=(hbm(), hbm(), vmem()) + (hbm(),) * 4,
        scratch_shapes=[
            slots_scratch(MLP_HALF),
            pltpu.VMEM((2, width, CHUNK), BF16),
            pltpu.VMEM((2, CHUNK, width), BF16),
            spots_scratch(),
            pltpu.VMEM((rows, width), BF16),
            pltpu.VMEM((rows, width), BF16),
            pltpu.VMEM((rows, FF), BF16),
            pltpu.VMEM((rows, FF), BF16),
            pltpu.VMEM((2, TALL, 256), F32),
            pltpu.VMEM((2, TALL, 256), F32),
            pltpu.VMEM((8, FF), F32),
            pltpu.VMEM((CHUNKS, CHUNK), F32),
            dma(len(RUN_ORDER)),
            dma(2 * CHUNKS),
        ],
        compiler_params=pltpu.CompilerParams(vmem_limit_bytes=42 * MEGA),
        cost_estimate=cost(8 * rows * width * FF, 40 * MEGA),
        name="feed_forward",
    )(me, n2, dm, small, *mlp)


def matrix_copies(buffers, w, sems, x):
    copies = []
    for i in range(4):
        source = buffers[i].at[pl.ds(4 * x, 4)]
        copies.append(pltpu.make_async_copy(source, w.at[0, pl.ds(4 * i, 4)], sems.at[i]))
    for c in range(2):
        source = buffers[4 + 2 * c + x]
        copies.append(pltpu.make_async_copy(source, w.at[1, pl.ds(8 * c, 8)], sems.at[4 + c]))
    return copies


def fetch_matrix(me, buffers, w, spots, sems, first):
    def place(d):
        return ((d >> 3) & 1) * 8 + (d & 1) * 4 + ((d >> 1) & 3)

    for x in range(2):

        @pl.when((me >> 4) == (x ^ (first >> 4)))
        def _(x=x):
            fetch(matrix_copies(buffers, w, sems, x))

    mine = place(me)
    for d in range(W1_BLOCKS):
        for h in range(2):
            spots[h, first + d] = jnp.bitwise_xor(mine, place(d))


def wait_matrix(buffers, w, sems):
    settle(matrix_copies(buffers, w, sems, 0))


def matrix_scratch():
    return pltpu.VMEM((2, W1_BLOCKS, MLP_HALF, SUB, LANES), BF16)


def mlp_out_kernel(me_ref, u_in, x1_in, cot_in, small, *refs):
    arriving, refs = refs[:8], refs[8:]
    out, vectors, w, second, spots, u, x1, cot, macc, done, sums, sems, own = refs
    rows, width = x1.shape
    tiles = rows // TALL

    def tile_copy(source, target, t, k):
        at = pl.ds(pl.multiple_of(TALL * t, TALL), TALL)
        return pltpu.make_async_copy(source.at[at, :], target.at[at, :], own.at[k, t])

    fetch_matrix(me_ref[0], arriving, w, spots, sems, W1_BLOCKS)
    for t in range(tiles):
        tile_copy(u_in, u, t, 0).start()
    for t in range(tiles):
        tile_copy(x1_in, x1, t, 1).start()
        tile_copy(cot_in, cot, t, 2).start()
    bias, scale = row_of(small, B2, 6), row_of(small, S2, 6)
    sums[...] = jnp.zeros_like(sums)
    wait_matrix(arriving, w, sems)
    lay_w2(w, spots, second)

    def contract(t):
        at = pl.ds(pl.multiple_of(TALL * t, TALL), TALL)
        tile_copy(u_in, u, t, 0).wait()
        macc[at, :] = mm(u[at, :], second[...], NN)

    def finish(t):
        tile_copy(x1_in, x1, t, 1).wait()
        tile_copy(cot_in, cot, t, 2).wait()
        for part in range(TALL // 64):
            at = pl.ds(pl.multiple_of(TALL * t + 64 * part, 64), 64)
            contracted = macc[at, :] + bias
            done[at, :] = (x1[at, :] + scale * contracted).astype(BF16)
            sums[...] += fold8(cot[at, :].astype(F32) * contracted)
        tile_copy(done, out, t, 3).start()

    def one_tile(t, carry):
        contract(t)
        finish(t - 1)
        return carry

    contract(0)
    lax.fori_loop(1, tiles, one_tile, 0)
    finish(tiles - 1)
    put_row(vectors, 0, total(sums[...]))
    for t in range(tiles):
        tile_copy(done, out, t, 3).wait()


def feed_forward_out(me, u, x1, cot, small, mlp):
    rows, width = x1.shape
    row = lambda kind: pltpu.VMEM((rows, width), kind)
    return pl.pallas_call(
        mlp_out_kernel,
        out_shape=(shape((rows, width), BF16), shape((6, LANES), F32)),
        in_specs=[smem()] + [hbm()] * 3 + [vmem()] + [hbm()] * 8,
        out_specs=(hbm(), vmem()),
        scratch_shapes=[
            matrix_scratch(),
            pltpu.VMEM((FF, width), BF16),
            spots_scratch(),
            pltpu.VMEM((rows, FF), BF16),
            row(F32),
            row(BF16),
            row(F32),
            row(BF16),
            pltpu.VMEM((8, width), F32),
            dma(6),
            pltpu.SemaphoreType.DMA((4, rows // TALL)),
        ],
        compiler_params=pltpu.CompilerParams(vmem_limit_bytes=32 * MEGA),
        cost_estimate=cost(2 * rows * width * FF, 20 * MEGA),
        name="feed_forward_out",
    )(me, u, x1, cot, small, *mlp)


def split_kernel(me_ref, dz_in, x1_in, cot_in, branch_in, mixed_in, small, *refs):
    buffers, att_buffers, refs = refs[:8], refs[8:16], refs[16:]
    dx1_out, da_out, gwo0, gwo1, vectors = refs[:5]
    w, first, spots, wo, wo_spots, dz, x1, cot, dnacc, dx1, branch, mixed, db, da = refs[5:19]
    parts, sums, sems, wo_sems, own = refs[19:]
    me = me_ref[0]
    rows, width = x1.shape
    tiles = rows // TALL

    def tile_copy(source, target, t, k):
        at = pl.ds(pl.multiple_of(TALL * t, TALL), TALL)
        return pltpu.make_async_copy(source.at[at, :], target.at[at, :], own.at[k, t])

    fetch_matrix(me, buffers, w, spots, sems, 0)
    for t in range(tiles):
        tile_copy(dz_in, dz, t, 0).start()
    for t in range(tiles):
        tile_copy(x1_in, x1, t, 1).start()
        tile_copy(cot_in, cot, t, 2).start()
        tile_copy(branch_in, branch, t, 3).start()
    fetch_wo(me, att_buffers, wo, wo_spots, wo_sems)
    late = pltpu.make_async_copy(mixed_in, mixed, own.at[4, 0])
    late.start()
    gain, scale = row_of(small, G2, 6), row_of(small, S1, 6)
    sums[...] = jnp.zeros_like(sums)
    wait_matrix(buffers, w, sems)
    lay_w1(w, spots, first)

    def contract(t):
        at = pl.ds(pl.multiple_of(TALL * t, TALL), TALL)
        tile_copy(dz_in, dz, t, 0).wait()
        dnacc[at, :] = mm(dz[at, :], first[...], NT)

    def finish(t):
        tile_copy(x1_in, x1, t, 1).wait()
        tile_copy(cot_in, cot, t, 2).wait()
        tile_copy(branch_in, branch, t, 3).wait()
        for half in range(2):
            at = pl.ds(pl.multiple_of(TALL * t + TALL // 2 * half, TALL // 2), TALL // 2)
            unit, inverse = normalized(x1[at, :])
            grad = dnacc[at, :]
            middle = cot[at, :].astype(F32) + norm_pullback(unit, inverse, grad, gain)
            dx1[at, :] = middle
            rounded = (middle * scale).astype(BF16)
            db[at, :] = rounded
            sums[0:8, :] += fold8(grad * unit)
            sums[8:16, :] += fold8(grad)
            sums[16:24, :] += fold8(rounded.astype(F32))
            sums[24:32, :] += fold8(middle * branch[at, :].astype(F32))
        tile_copy(dx1, dx1_out, t, 1).start()

    def one_tile(t, carry):
        contract(t)
        finish(t - 1)
        return carry

    contract(0)
    lax.fori_loop(1, tiles, one_tile, 0)
    finish(tiles - 1)
    for k in range(4):
        put_row(vectors, 6 * k, total(sums[8 * k : 8 * k + 8, :]))
    wait_wo(att_buffers, wo, wo_sems)
    weight = wo_matrix(wo, wo_spots)
    going = []
    for c in range(3):
        lanes = slice(256 * c, 256 * c + 256)
        da[:, lanes] = mm(db[...], weight[lanes, :], NT).astype(BF16)
        going.append(pltpu.make_async_copy(da.at[:, lanes], da_out.at[:, lanes], own.at[0, c]))
        going[-1].start()
    late.wait()
    for c in range(3):
        grad = mm(mixed[:, 256 * c : 256 * c + 256], db[...], TN)
        for r in range(SUB):
            i, rt = (SUB * c + r) // WO_RT, (SUB * c + r) % WO_RT
            for ct in range(WO_CT):
                tile = grad[SUB * r : SUB * r + SUB, LANES * ct : LANES * ct + LANES]
                g, half, index = part_place("wo", rt, ct)
                parts[g, half, i, index] = tile.astype(BF16)
    for g, target in enumerate((gwo0, gwo1)):
        going.append(pltpu.make_async_copy(parts.at[g], target, own.at[4, g]))
        going[-1].start()
    settle(going)
    for t in range(tiles):
        tile_copy(dx1, dx1_out, t, 1).wait()


def split(me, dz, x1, cot, branch, mixed, small, mlp, att):
    rows, width = x1.shape
    part = (2, WO_BLOCKS, ATT_PART, SUB, LANES)
    row = lambda kind: pltpu.VMEM((rows, width), kind)
    return pl.pallas_call(
        split_kernel,
        out_shape=(
            shape((rows, width), F32),
            shape((rows, width), BF16),
            shape(part, BF16),
            shape(part, BF16),
            shape((24, LANES), F32),
        ),
        in_specs=[smem()] + [hbm()] * 5 + [vmem()] + [hbm()] * 16,
        out_specs=(hbm(),) * 4 + (vmem(),),
        scratch_shapes=[
            matrix_scratch(),
            pltpu.VMEM((width, FF), BF16),
            spots_scratch(),
            wo_scratch(),
            spots_scratch(),
            pltpu.VMEM((rows, FF), BF16),
            row(F32),
            row(BF16),
            row(F32),
            row(F32),
            row(BF16),
            row(BF16),
            row(BF16),
            row(BF16),
            pltpu.VMEM((2,) + part, BF16),
            pltpu.VMEM((32, width), F32),
            dma(6),
            dma(3),
            pltpu.SemaphoreType.DMA((5, rows // TALL)),
        ],
        compiler_params=pltpu.CompilerParams(vmem_limit_bytes=44 * MEGA),
        cost_estimate=cost(2 * rows * width * FF + 4 * rows * width * width, 40 * MEGA),
        name="feed_forward_in",
    )(me, dz, x1, cot, branch, mixed, small, *mlp, *att)


GROUP = PAIRS // 2
GROUP_LANES = GROUP * LANES


def attend_back_block(b, start, width, group, refs):
    q, k, v, da, stats, dq, dkeys, dvalues, bias = refs
    rows = pl.ds(pl.multiple_of(b * QB, QB), QB)
    at = pl.ds(start, width)
    mask = jnp.concatenate([bias[0:width, :]] * 2, axis=1)
    pairs = []
    for p in range(GROUP):
        lanes = slice(LANES * p, LANES * p + LANES)
        place = b * PAIRS + GROUP * group + p
        queries = head_masked(q[rows, lanes] * 0.125)
        grads = head_masked(da[rows, lanes])
        keys, values = k[at, lanes], v[at, lanes]
        scores = mm(keys, queries, NT)
        dweight = mm(values, grads, NT)
        pairs.append((lanes, place, queries, grads, keys, scores, dweight))
    later = []
    for lanes, place, queries, grads, keys, scores, dweight in pairs:
        highest = stats[place, 0:1, :]
        inverse = stats[place, 1:2, :]
        weight = jnp.exp(scores + mask - highest) * inverse
        inner_sum = total(fold8(weight * dweight))
        dvalues[at, lanes] += mm(weight.astype(BF16), grads, NN)
        dscore = (weight * (dweight - inner_sum)).astype(BF16)
        later.append((lanes, queries, keys, dscore))
    for lanes, queries, keys, dscore in later:
        dkeys[at, lanes] += mm(dscore, queries, NN)
        both = mm(keys, dscore, TN)
        dq[rows, lanes] = (pick_heads(both) * 0.125).T.astype(BF16)


def attend_back_kernel(group, windows, qkv, da_in, stats, query_ids, dqkv, *refs):
    q, k, v, da, out, dkeys, dvalues, bias, key_ids, own = refs
    rows = q.shape[0]
    blocks = rows // QB
    lanes = slice(GROUP_LANES * group, GROUP_LANES * group + GROUP_LANES)
    coming = [pltpu.make_async_copy(da_in.at[:, lanes], da, own.at[3])]
    for third, target in enumerate((q, k, v)):
        first = LANES * PAIRS * third + GROUP_LANES * group
        source = qkv.at[:, first : first + GROUP_LANES]
        coming.append(pltpu.make_async_copy(source, target, own.at[third]))
    fetch(coming)
    dkeys[...] = jnp.zeros_like(dkeys)
    dvalues[...] = jnp.zeros_like(dvalues)
    spread_ids(query_ids, key_ids)
    settle(coming)
    dq = out.at[:, 0:GROUP_LANES]

    def one_block(b, carry):
        start = pl.multiple_of(windows[0, b], SUB)
        for index, width in enumerate(CLASSES):

            @pl.when(windows[1, b] == index)
            def _(width=width):
                mask_bias(start, width, b, key_ids, query_ids, bias)
                parts = (q, k, v, da, stats, dq, dkeys, dvalues, bias)
                attend_back_block(b, start, width, group, parts)

        return carry

    lax.fori_loop(0, blocks, one_block, 0)
    going = []
    for i in range(rows // 256):
        at = slice(256 * i, 256 * i + 256)
        out[at, GROUP_LANES : 2 * GROUP_LANES] = dkeys[at, :].astype(BF16)
        out[at, 2 * GROUP_LANES :] = dvalues[at, :].astype(BF16)
        going.append(pltpu.make_async_copy(out.at[at, :], dqkv.at[at, :], own.at[i]))
        going[-1].start()
    settle(going)


def attend_back(group, windows, qkv, da, stats, query_ids):
    rows = qkv.shape[0]
    part = lambda kind: pltpu.VMEM((rows, GROUP_LANES), kind)
    return pl.pallas_call(
        partial(attend_back_kernel, group),
        out_shape=shape((rows, 3 * GROUP_LANES), BF16),
        in_specs=[smem(), hbm(), hbm(), vmem(), vmem()],
        out_specs=hbm(),
        scratch_shapes=[
            part(BF16),
            part(BF16),
            part(BF16),
            part(BF16),
            pltpu.VMEM((rows, 3 * GROUP_LANES), BF16),
            part(F32),
            part(F32),
            pltpu.VMEM((CLASSES[-1], QB), F32),
            pltpu.VMEM((rows, QB), F32),
            dma(4),
        ],
        compiler_params=pltpu.CompilerParams(vmem_limit_bytes=32 * MEGA),
        cost_estimate=cost(3 * rows * rows * rows, 14 * rows * rows, 4 * rows * rows),
        name="attend_backward",
    )(windows, qkv, da, stats, query_ids)


def put_qkv_grad(n1, dqkv, w, spots):
    for c in range(3):
        grad = mm(n1[:, 256 * c : 256 * c + 256], dqkv[...], TN)
        for r in range(SUB):
            d, rt = (SUB * c + r) // QKV_RT, (SUB * c + r) % QKV_RT
            place = spots[rt, d]
            for index in range(ATT_PART):
                tile = grad[SUB * r : SUB * r + SUB, LANES * index : LANES * index + LANES]
                w[rt, place, index] = tile.astype(BF16)


def put_wo_grad(gwo, w, spots):
    for h in range(2):
        for i in range(WO_BLOCKS):
            w[h, spots[h, QKV_BLOCKS + i], 0:ATT_PART] = gwo[h, i]


def weight_grad_kernel(me_ref, n1_in, dqkv_in, gwo_in, *refs):
    leaving, (w, spots, n1, dqkv, gwo, sems, own) = refs[:4], refs[4:]
    coming = [
        pltpu.make_async_copy(n1_in, n1, own.at[0]),
        pltpu.make_async_copy(dqkv_in, dqkv, own.at[1]),
        pltpu.make_async_copy(gwo_in, gwo, own.at[2]),
    ]
    fetch(coming)
    fill_spots(me_ref[0], spots)
    settle(coming)
    put_wo_grad(gwo, w, spots)
    put_qkv_grad(n1, dqkv, w, spots)
    copies = leaving_slots(leaving, w, sems)
    fetch(copies)
    settle(copies)


def weight_grad(me, n1, dqkv, gwo):
    rows, width = n1.shape
    half = shape((HALF_BLOCKS, ATT_PART, SUB, LANES), BF16)
    return pl.pallas_call(
        weight_grad_kernel,
        out_shape=(half,) * 4,
        in_specs=[smem()] + [hbm()] * 3,
        out_specs=(hbm(),) * 4,
        scratch_shapes=[
            slots_scratch(ATT_PART),
            spots_scratch(),
            pltpu.VMEM((rows, width), BF16),
            pltpu.VMEM(dqkv.shape, BF16),
            pltpu.VMEM(gwo.shape, BF16),
            dma(4),
            dma(3),
        ],
        compiler_params=pltpu.CompilerParams(vmem_limit_bytes=20 * MEGA),
        cost_estimate=cost(3 * rows * width * width, 10 * rows * width),
        name="qkv_weight_grad",
    )(me, n1, dqkv, gwo)


def qkv_back_kernel(
    me_ref, tokens_in, n1_in, dx1_in, dqkv0_in, dqkv1_in, small, proj, mlp, gwo_in, *refs
):
    arriving, refs = refs[:8], refs[8:]
    dx_out, *leaving = refs[:5]
    w, gw, weight, spots, gwo, tokens, n1, dx1, dqkv0, dqkv1, dn, dx, sums, table = refs[5:19]
    sems, out_sems, own = refs[19:]
    rows = tokens.shape[0]
    tiles = rows // TALL

    def tile_copy(source, target, t, k):
        at = pl.ds(pl.multiple_of(TALL * t, TALL), TALL)
        return pltpu.make_async_copy(source.at[at, :], target.at[at, :], own.at[k, t])

    for t in range(tiles):
        tile_copy(dqkv0_in, dqkv0, t, 0).start()
        tile_copy(dqkv1_in, dqkv1, t, 1).start()
    weights = arriving_slots(arriving, w, sems)
    fetch(weights)
    for t in range(tiles):
        tile_copy(tokens_in, tokens, t, 2).start()
        tile_copy(dx1_in, dx1, t, 3).start()
    late = [
        pltpu.make_async_copy(n1_in, n1, own.at[4, 0]),
        pltpu.make_async_copy(gwo_in, gwo, own.at[4, 1]),
    ]
    fetch(late)
    sums[...] = jnp.zeros_like(sums)
    gain = row_of(small, G1, 6)
    fill_spots(me_ref[0], spots)
    settle(weights)
    columns = qkv_group(0) + qkv_group(1)
    lay_matrix(w, spots, "qkv", QKV_BLOCKS, 0, QKV_RT, columns, weight)

    def contract(t):
        at = pl.ds(pl.multiple_of(TALL * t, TALL), TALL)
        for g, (source, part) in enumerate(((dqkv0_in, dqkv0), (dqkv1_in, dqkv1))):
            tile_copy(source, part, t, g).wait()
            lanes = slice(384 * g, 384 * g + 384)
            sums[16:24, lanes] += fold8(part[at, 0:384].astype(F32))
            sums[24:32, lanes] += fold8(part[at, 768:1152].astype(F32))
        both = jnp.concatenate([dqkv0[at, :], dqkv1[at, :]], axis=1)
        dn[at, :] = mm(both, weight[...], NT)

    def finish(t):
        tile_copy(tokens_in, tokens, t, 2).wait()
        tile_copy(dx1_in, dx1, t, 3).wait()
        for half in range(2):
            at = pl.ds(pl.multiple_of(TALL * t + TALL // 2 * half, TALL // 2), TALL // 2)
            unit, inverse = normalized(tokens[at, :].astype(F32))
            grad = dn[at, :]
            dx[at, :] = dx1[at, :] + norm_pullback(unit, inverse, grad, gain)
            sums[0:8, :] += fold8(grad * unit)
            sums[8:16, :] += fold8(grad)
        tile_copy(dx, dx_out, t, 3).start()

    def one_tile(t, carry):
        contract(t)
        finish(t - 1)
        return carry

    contract(0)
    lax.fori_loop(1, tiles, one_tile, 0)
    finish(tiles - 1)

    def put_table(owner, *places):
        table[...] = jnp.zeros_like(table)
        for place, values in places:
            if values.shape[1] == LANES:
                table[place : place + values.shape[0], :] = values
            else:
                put_row(table, place, values)
        for h in range(2):
            gw[h, spots[h, owner], ATT_PART] = table[SUB * h : SUB * h + SUB, :].astype(BF16)

    put_table(
        OWNERS[0], (0, total(sums[0:8, :])), (6, total(sums[8:16, :])), (12, mlp[0:12, :])
    )
    put_table(OWNERS[1], (0, mlp[12:36, :]))
    put_table(OWNERS[2], (0, total(sums[16:24, :])), (6, total(sums[24:32, :])))
    put_table(OWNERS[3], (0, proj[...]), (12, mlp[36:48, :]))
    settle(late)
    put_wo_grad(gwo, gw, spots)
    put_qkv_grad(n1, dqkv1, gw, spots)
    copies = leaving_slots(leaving, gw, out_sems)
    fetch(copies)
    for t in range(tiles):
        tile_copy(dx, dx_out, t, 3).wait()
    settle(copies)


def qkv_back(me, tokens, n1, dx1, dqkv0, dqkv1, small, proj, mlp, gwo, att):
    rows, width = tokens.shape
    tiles = ATT_PART + 1
    half = shape((HALF_BLOCKS, tiles, SUB, LANES), BF16)
    row = lambda kind: pltpu.VMEM((rows, width), kind)
    return pl.pallas_call(
        qkv_back_kernel,
        out_shape=(shape((rows, width), F32), half, half, half, half),
        in_specs=[smem()] + [hbm()] * 5 + [vmem()] * 3 + [hbm()] * 9,
        out_specs=(hbm(),) * 5,
        scratch_shapes=[
            slots_scratch(ATT_SENT),
            slots_scratch(tiles),
            pltpu.VMEM((width, 3 * width), BF16),
            spots_scratch(),
            pltpu.VMEM(gwo.shape, BF16),
            row(BF16),
            row(BF16),
            row(F32),
            pltpu.VMEM(dqkv0.shape, BF16),
            pltpu.VMEM(dqkv1.shape, BF16),
            row(F32),
            row(F32),
            pltpu.VMEM((32, width), F32),
            pltpu.VMEM((2 * SUB, LANES), F32),
            dma(8),
            dma(4),
            pltpu.SemaphoreType.DMA((5, rows // TALL)),
        ],
        compiler_params=pltpu.CompilerParams(vmem_limit_bytes=46 * MEGA),
        cost_estimate=cost(9 * rows * width * width, 30 * rows * width),
        name="qkv_backward",
    )(me, tokens, n1, dx1, dqkv0, dqkv1, small, proj, mlp, gwo, *att)


X, C, Z1, Z0, Y = 16, 8, 4, 2, 1


def exchange(values, bit):
    return lax.ppermute(values, AXES, [(d, d ^ bit) for d in range(BLOCKS)])


def overhangs(att_rows, mlp_rows):
    before, after = [], []
    for d in range(BLOCKS):
        att = 12 + d * (576 - att_rows) + (0 if d < QKV_BLOCKS else 12)
        mlp = 12 + d * (1152 - mlp_rows) + (0 if d < W1_BLOCKS else 24)
        ahead = 12 if d == 0 else 0
        att_end = att + 576 + (12 if d in (QKV_BLOCKS - 1, BLOCKS - 1) else 0)
        mlp_end = mlp + 1152 + (24 if d == W1_BLOCKS - 1 else 12 if d == BLOCKS - 1 else 0)
        if min(att, mlp) < ahead:
            before.append(d)
        if att_end > att_rows or mlp_end > mlp_rows:
            after.append(d)
    return before, after


def together(*values):
    return lax.optimization_barrier(values)


def along_z(first, second, received):
    return (
        jnp.stack([first] + [r[0] for r in received]),
        jnp.stack([second] + [r[1] for r in received]),
    )


def joined(own, received):
    return jnp.concatenate([own, received])


def sum_terms(terms):
    summed = terms[0].astype(F32)
    for term in terms[1:]:
        summed = summed + term.astype(F32)
    return summed


def kept(terms):
    return [t[: t.shape[0] // 2] for t in terms]


def z_part(first, second, k):
    return jnp.stack([sum_terms([t[k] for t in terms]) for terms in (first, second)])


def sent(terms):
    return sum_terms([t[t.shape[0] // 2 :] for t in terms]).astype(BF16)


def attention_amounts(width):
    return [width, width, 3 * width * width, width, width, width * width, width, width]


def feedforward_amounts(width):
    return [width, width, width * FF, FF, FF * width, width, width]


def pieces_of(vector, amounts):
    out, offset = [], 0
    for amount in amounts:
        out.append(vector[offset : offset + amount])
        offset += amount
    return out


def tiles_by_column(matrix, blocks, rt):
    ct = matrix.shape[1] // LANES
    return matrix.reshape(blocks, rt, SUB, ct, LANES).transpose(0, 3, 1, 2, 4)


def tiles_by_row(matrix, blocks, rt):
    ct = matrix.shape[1] // LANES
    return matrix.reshape(blocks, rt, SUB, ct, LANES).transpose(0, 1, 3, 2, 4)


def gather_plainly(params, att_rows, width):
    rounded = params.astype(BF16)
    att = lax.all_gather(rounded[:att_rows], AXES, axis=0, tiled=True).reshape(-1)
    mlp = lax.all_gather(rounded[att_rows:], AXES, axis=0, tiled=True).reshape(-1)
    g1, c1, wqkv, bq, bv, wo, bo, s1 = pieces_of(att, attention_amounts(width))
    g2, c2, w1, b1, w2, b2, s2 = pieces_of(mlp, feedforward_amounts(width))
    tile = (SUB, LANES)
    att = jnp.concatenate(
        [
            tiles_by_column(wqkv.reshape(width, -1), QKV_BLOCKS, QKV_RT).reshape((-1, 36) + tile),
            tiles_by_row(wo.reshape(width, -1), WO_BLOCKS, WO_RT).reshape((-1, 36) + tile),
        ]
    )
    mlp = jnp.concatenate(
        [
            tiles_by_column(w1.reshape(width, -1), W1_BLOCKS, W1_RT).reshape((-1, 72) + tile),
            tiles_by_row(w2.reshape(FF, -1), W2_BLOCKS, W2_RT).reshape((-1, 72) + tile),
        ]
    )
    vectors = jnp.concatenate([g1, c1, bq, bv, bo, s1, g2, c2, b1, b2, s2]).astype(F32)
    lines = vectors.reshape(-1, LANES)
    sent = jnp.zeros((BLOCKS, 2 * SUB, LANES), F32)
    for owner, place, first, count in (
        (OWNERS[0], 0, G1, 12),
        (OWNERS[0], 12, G2, 12),
        (OWNERS[1], 0, B1, 24),
        (OWNERS[2], 0, BQ, 12),
        (OWNERS[3], 0, BO, 12),
        (OWNERS[3], 12, B2, 12),
    ):
        sent = sent.at[owner, place : place + count].set(lines[first : first + count])
    sent = sent.astype(BF16).reshape((BLOCKS, 2, 1) + tile)
    att = [jnp.concatenate([att[:, 18 * h : 18 * h + 18], sent[:, h]], axis=1) for h in range(2)]
    return by_slot(*att), by_slot(mlp[:, :36], mlp[:, 36:])


def by_slot(first, second):
    halves = (first, second)
    return [
        jnp.stack([halves[i // 4][slot] for slot in SLOTS[i // 4][i % 4 * 8 : i % 4 * 8 + 8]])
        for i in range(8)
    ]


def from_slots(buffers):
    halves = []
    for h in range(2):
        slots = jnp.concatenate(buffers[2 * h : 2 * h + 2])
        halves.append(jnp.stack([slots[spot(h, d)] for d in range(BLOCKS)]))
    return halves


def reduce_plainly(gatt0, gatt1, gmlp, att_rows, mlp_rows, width, devices):
    groups = [from_slots(gatt0), from_slots(gatt1)]
    vectors = jnp.concatenate([groups[1][h][:, ATT_PART:] for h in range(2)], axis=1)
    vectors = vectors.astype(F32).reshape(BLOCKS, 2 * SUB, LANES)

    def matrix(name, first, last, rt_count, ct_count):
        rows = []
        for rt in range(rt_count):
            places = [part_place(name, rt, ct) for ct in range(ct_count)]
            rows.append(jnp.stack([groups[g][h][first:last, i] for g, h, i in places], axis=2))
        return jnp.stack(rows, axis=1).astype(F32).reshape(-1)

    wqkv = matrix("qkv", 0, QKV_BLOCKS, QKV_RT, QKV_CT)
    wo = matrix("wo", QKV_BLOCKS, BLOCKS, WO_RT, WO_CT)
    mlp = jnp.concatenate(from_slots(gmlp), axis=1).astype(F32)
    five = lambda v, dims: v.reshape((v.shape[0],) + dims + (SUB, LANES))
    w1 = five(mlp[:W1_BLOCKS], (W1_CT, W1_RT)).transpose(0, 2, 3, 1, 4).reshape(-1)
    w2 = five(mlp[W1_BLOCKS:], (W2_RT, W2_CT)).transpose(0, 1, 3, 2, 4).reshape(-1)
    line = lambda owner, first, count: vectors[owner, first : first + count].reshape(-1)
    att = [line(OWNERS[0], 0, 12), wqkv, line(OWNERS[2], 0, 12), wo, line(OWNERS[3], 0, 12)]
    mlp = [line(OWNERS[0], 12, 12), w1, line(OWNERS[1], 0, 24), w2, line(OWNERS[3], 12, 12)]

    def lay(parts, rows):
        vector = jnp.concatenate(parts)
        vector = jnp.pad(vector, (0, devices * rows * LANES - vector.shape[0]))
        return vector.reshape(devices, rows, LANES)

    whole = jnp.concatenate([lay(att, att_rows), lay(mlp, mlp_rows)], axis=1)
    return lax.psum_scatter(whole.reshape(-1, LANES), AXES, scatter_dimension=0, tiled=True)


def key_windows(segments, real):
    length = segments.shape[0]
    position = jnp.arange(length, dtype=jnp.int32)
    ids = jnp.where(real, segments, length + position)
    first = segments[0::QB]
    final = segments[QB - 1 :: QB]
    begin = jnp.sum((segments[None, :] < first[:, None]).astype(jnp.int32), axis=1)
    begin = jnp.where(real[0::QB], begin, position[0::QB])
    end = jnp.sum(((segments[None, :] <= final[:, None]) & real[None, :]).astype(jnp.int32), axis=1)
    end = jnp.where(real[QB - 1 :: QB], end, position[QB - 1 :: QB] + 1)
    begin = begin // SUB * SUB
    need = end - begin
    kind = sum((need > width).astype(jnp.int32) for width in CLASSES[:-1])
    widths = sum(
        jnp.where(kind == i, width, 0) for i, width in enumerate(CLASSES)
    )
    begin = jnp.minimum(begin, length - widths)
    chunks = (begin + widths + QB - 1) // QB
    return ids, jnp.stack([begin, kind, chunks]).astype(jnp.int32)


def local(tokens, cotangent, segment_ids, pad_mask, lengths, params):
    rows, width = tokens.shape
    wide, narrow = lax.axis_size("wide"), lax.axis_size("narrow")
    devices = wide * narrow
    att_count = 4 * width * width + 6 * width
    att_rows = (att_count // LANES + devices - 1) // devices
    mlp_rows = params.shape[0] - att_rows
    paired = (wide, narrow) == (4, 8)
    scale = 1.0 / math.sqrt(rows * devices)

    def attention_windows(segments, pads, lengths):
        real = (pads > 0) & (jnp.arange(rows, dtype=jnp.int32) < lengths[0])
        ids, windows = key_windows(segments, real)
        return windows, ids.astype(F32).reshape(rows // QB, QB)

    if not paired:
        windows, query_ids = attention_windows(segment_ids, pad_mask, lengths)
        me = jnp.zeros((1,), jnp.int32)
        att, mlp = gather_plainly(params, att_rows, width)
        n1, qkv, small = project_qkv(me, tokens, att)
        mixed, x1, branch, n2, dm, stats, gb2 = attend(
            me, windows, qkv, tokens, cotangent, query_ids, small, att
        )
        u, dz, gb1, *gmlp = feed_forward(me, n2, dm, small, mlp)
        output, gs2 = feed_forward_out(me, u, x1, cotangent, small, mlp)
        dx1, da, gwo0, gwo1, others = split(
            me, dz, x1, cotangent, branch, mixed, small, mlp, att
        )
        small_mlp = jnp.concatenate([others[:12], gb1, gb2, gs2])
        small_proj = others[12:]
        dqkv0 = attend_back(0, windows, qkv, da, stats, query_ids)
        dqkv1 = attend_back(1, windows, qkv, da, stats, query_ids)
        gatt0 = weight_grad(me, n1, dqkv0, gwo0)
        grad_input, *gatt1 = qkv_back(
            me, tokens, n1, dx1, dqkv0, dqkv1, small, small_proj, small_mlp, gwo1, att
        )
        owned = reduce_plainly(gatt0, gatt1, gmlp, att_rows, mlp_rows, width, devices)
        return output, grad_input, owned * scale

    me = lax.axis_index(AXES).astype(jnp.int32).reshape(1)
    tails = jnp.concatenate([params[att_rows - ATT_BEFORE : att_rows], params[-MLP_BEFORE:]])
    heads = jnp.concatenate([params[:ATT_AFTER], params[att_rows : att_rows + MLP_AFTER]])
    before, beyond = overhangs(att_rows, mlp_rows)
    heads = lax.ppermute(heads.astype(BF16), AXES, [(d + 1, d) for d in beyond])
    tails = lax.ppermute(tails.astype(BF16), AXES, [(d - 1, d) for d in before])
    att_own, mlp_own = pack(me, params, tails, heads, att_rows)

    got = [exchange(att_own, k * Z0) for k in range(1, 4)]
    a, b = along_z(att_own[0], att_own[1], got)
    a, b, mlp_own, *tables = together(a, b, mlp_own, segment_ids, pad_mask, lengths)
    windows, query_ids = attention_windows(*tables)
    ax, by = exchange(a, X), exchange(b, Y)
    z1, z3 = exchange(mlp_own, Z0), exchange(mlp_own, 3 * Z0)
    a, b = joined(a, ax), joined(b, by)
    a, b, z1, z3, mlp_own, windows, query_ids = together(
        a, b, z1, z3, mlp_own, windows, query_ids
    )
    ay, bx = exchange(a, Y), exchange(b, X)
    ac, bc = exchange(a, C), exchange(b, C)
    z2 = exchange(mlp_own, 2 * Z0)
    m, n = along_z(mlp_own[0], mlp_own[1], [z1, z2, z3])
    ay, bx, ac, bc, m, n = together(ay, bx, ac, bc, m, n)
    ayc, bxc = exchange(ay, C), exchange(bx, C)
    att = together(a, ay, ac, ayc, b, bx, bc, bxc, m, n, tokens)
    *att, m, n, tokens_now = att
    mx, ny = exchange(m, X), exchange(n, Y)
    n1, qkv, small = project_qkv(me, tokens_now, att)
    m, n = joined(m, mx), joined(n, ny)
    m, n, qkv = together(m, n, qkv)
    my, nx = exchange(m, Y), exchange(n, X)
    mc, nc = exchange(m, C), exchange(n, C)
    mixed, x1, branch, n2, dm, stats, gb2 = attend(
        me, windows, qkv, tokens, cotangent, query_ids, small, att
    )
    m, n, my, nx, mc, nc, n2 = together(m, n, my, nx, mc, nc, n2)
    myc, nxc = exchange(my, C), exchange(nx, C)
    mlp = (m, my, mc, myc, n, nx, nc, nxc)

    u, dz, gb1, *gmlp = feed_forward(me, n2, dm, small, mlp)

    mc, nc = exchange(gmlp[1], C), exchange(gmlp[3], C)
    output, gs2 = feed_forward_out(me, u, x1, cotangent, small, mlp)
    mc, nc, dz, gs2 = together(mc, nc, dz, gs2)
    m, n = [gmlp[0], mc], [gmlp[2], nc]
    my, nx, dz = together(sent(m), sent(n), dz)
    my, nx = exchange(my, Y), exchange(nx, X)
    dx1, da, gwo0, gwo1, others = split(
        me, dz, x1, cotangent, branch, mixed, small, mlp, att
    )
    dqkv0 = attend_back(0, windows, qkv, da, stats, query_ids)
    gatt0 = weight_grad(me, n1, dqkv0, gwo0)
    my, nx, da, *gatt0 = together(my, nx, da, *gatt0)
    m, n = kept(m) + [my], kept(n) + [nx]
    mx, ny, da, *gatt0 = together(sent(m), sent(n), da, *gatt0)
    mx, ny = exchange(mx, X), exchange(ny, Y)
    ac, bc = exchange(gatt0[1], C), exchange(gatt0[3], C)
    dqkv1 = attend_back(1, windows, qkv, da, stats, query_ids)
    mx, ny, ac, bc, dqkv1 = together(mx, ny, ac, bc, dqkv1)
    m, n = kept(m) + [mx], kept(n) + [ny]
    z1, z2, z3 = [z_part(m, n, k).astype(BF16) for k in range(1, 4)]
    a, b = [gatt0[0], ac], [gatt0[2], bc]
    ay, bx, z1, z2, z3, dqkv1 = together(sent(a), sent(b), z1, z2, z3, dqkv1)
    z1, z2 = exchange(z1, Z0), exchange(z2, 2 * Z0)
    ay, bx = exchange(ay, Y), exchange(bx, X)
    small_mlp = jnp.concatenate([others[:12], gb1, gb2, gs2])
    grad_input, *gatt1 = qkv_back(
        me, tokens, n1, dx1, dqkv0, dqkv1, small, others[12:], small_mlp, gwo1, att
    )
    ay, bx, z1, z2, *gatt1 = together(ay, bx, z1, z2, *gatt1)
    a, b = kept(a) + [ay], kept(b) + [bx]
    ax, by, c1, d1, z3 = together(sent(a), sent(b), gatt1[1], gatt1[3], z3)
    c1, d1 = exchange(c1, C), exchange(d1, C)
    ax, by = exchange(ax, X), exchange(by, Y)
    z3a = exchange(z3[0], 3 * Z0)
    c, d = [gatt1[0], c1], [gatt1[2], d1]
    a, b = kept(a) + [ax], kept(b) + [by]
    sends = [z_part(a, b, k).astype(BF16) for k in range(1, 4)]
    cy, dx, z3a, z3, *sends = together(sent(c), sent(d), z3a, z3, *sends)
    cy, dx = exchange(cy, Y), exchange(dx, X)
    got = [exchange(part, (k + 1) * Z0) for k, part in enumerate(sends)]
    c, d = kept(c) + [cy], kept(d) + [dx]
    cx, dy, z3, *got = together(sent(c), sent(d), z3, *got)
    z3b = exchange(z3[1], 3 * Z0)
    group0 = sum_terms([z_part(a, b, 0)] + got)
    cx, dy = exchange(cx, X), exchange(dy, Y)
    c, d = kept(c) + [cx], kept(d) + [dy]
    m_own = sum_terms([z_part(m, n, 0), z1, z2, jnp.stack([z3a, z3b])])
    sends = [z_part(c, d, k).astype(BF16) for k in range(1, 4)]
    group0, m_own, *sends = together(group0, m_own, *sends)
    got = [exchange(part, (k + 1) * Z0) for k, part in enumerate(sends)]
    group1 = sum_terms([z_part(c, d, 0)] + got)
    mine, to_before, to_after = spread(me, group0, group1, m_own, att_rows, mlp_rows, scale)
    below = lax.ppermute(to_after, AXES, [(d, d + 1) for d in beyond])
    above = lax.ppermute(to_before, AXES, [(d, d - 1) for d in before])
    grad_params = close(mine, below, above, att_rows)
    return output, grad_input, grad_params


def solution(mesh):
    return jax.shard_map(
        local,
        mesh=mesh,
        in_specs=(
            P(AXES, None),
            P(AXES, None),
            P(AXES),
            P(AXES),
            P(AXES),
            P(AXES, None),
        ),
        out_specs=(P(AXES, None), P(AXES, None), P(AXES, None)),
        check_vma=False,
    )
```

```python
import math
from functools import partial

import jax
import jax.numpy as jnp
from jax import lax
from jax.experimental import pallas as pl
from jax.experimental.pallas import tpu as pltpu
from jax.sharding import PartitionSpec as P

FF = 3072
HEADS = 12
EPSILON = 1e-06
NEGATIVE = -1e30
AXES = ("wide", "narrow")
LANES = 128
SUB = 16
QB = 128
MEGA = 1 << 20
GRANT = 58 * MEGA
F32 = jnp.float32
BF16 = jnp.bfloat16

BLOCKS = 32
QKV_BLOCKS, QKV_RT, QKV_CT = 24, 2, 18
WO_BLOCKS, WO_RT, WO_CT = 8, 6, 6
W1_BLOCKS, W1_RT, W1_CT = 16, 3, 24
W2_BLOCKS, W2_RT, W2_CT = 16, 12, 6
ATT_HALF, MLP_HALF = 18, 36
ATT_SENT = ATT_HALF + 1
ATT_PART = 9
HALF_BLOCKS = BLOCKS // 2
CHUNK = 768
CHUNKS = FF // CHUNK

G1, C1, BQ, BV, BO, S1 = 0, 6, 12, 18, 24, 30
G2, C2, B1, B2, S2 = 36, 42, 48, 72, 78
SMALL = 88

NT = (((1,), (1,)), ((), ()))
NN = (((1,), (0,)), ((), ()))
TN = (((0,), (0,)), ((), ()))


def mm(lhs, rhs, dims):
    return lax.dot_general(lhs, rhs, dims, preferred_element_type=F32)


def row_of(ref, first, count):
    return jnp.concatenate([ref[first + k : first + k + 1, :] for k in range(count)], axis=1)


def put_row(ref, first, values):
    for k in range(values.shape[1] // LANES):
        ref[first + k : first + k + 1, :] = values[:, k * LANES : (k + 1) * LANES]


def fold8(values):
    rows, columns = values.shape
    return jnp.sum(values.reshape(rows // 8, 8, columns), axis=0)


def total(values):
    return jnp.sum(values, axis=0, keepdims=True)


def vmem():
    return pl.BlockSpec(memory_space=pltpu.VMEM)


def smem():
    return pl.BlockSpec(memory_space=pltpu.SMEM)


def hbm():
    return pl.BlockSpec(memory_space=pltpu.HBM)


def shape(dims, kind):
    return jax.ShapeDtypeStruct(dims, kind)


def cost(flops, moved, exps=0):
    return pl.CostEstimate(flops=int(flops), transcendentals=int(exps), bytes_accessed=int(moved))


def normalized(values):
    center = values - jnp.mean(values, axis=-1, keepdims=True)
    inverse = lax.rsqrt(jnp.mean(center * center, axis=-1, keepdims=True) + EPSILON)
    return center * inverse, inverse


def norm_pullback(unit, inverse, grad, gain):
    scaled = grad * gain
    first = jnp.mean(scaled, axis=-1, keepdims=True)
    second = jnp.mean(scaled * unit, axis=-1, keepdims=True)
    return inverse * (scaled - first - unit * second)


def gelu_pair(z):
    magnitude = jnp.abs(z)
    t = 1.0 / (1.0 + (0.3275911 * math.sqrt(0.5)) * magnitude)
    density = jnp.exp(z * z * -0.5)
    tail = 0.5 * 1.061405429
    tail = tail * t + 0.5 * -1.453152027
    tail = tail * t + 0.5 * 1.421413741
    tail = tail * t + 0.5 * -0.284496736
    tail = tail * t + 0.5 * 0.254829592
    tail = tail * t * density
    cumulative = jnp.where(z < 0, tail, 1.0 - tail)
    return z * cumulative, cumulative + z * density * (1.0 / math.sqrt(2.0 * math.pi))


def fetch(copies):
    for copy in copies:
        copy.start()


def settle(copies):
    for copy in copies:
        copy.wait()


ATT_BEFORE, ATT_AFTER = 64, 32
MLP_BEFORE, MLP_AFTER = 64, 40


def window_offsets(me, att_rows, mlp_rows):
    att = ATT_BEFORE + 12 + me * (576 - att_rows) + jnp.where(me < QKV_BLOCKS, 0, 12)
    mlp = MLP_BEFORE + 12 + me * (1152 - mlp_rows) + jnp.where(me < W1_BLOCKS, 0, 24)
    return att, mlp


def each_tile(me, act):
    for name, blocks, rt_count, ct_count, mine in (
        ("qkv", QKV_BLOCKS, QKV_RT, QKV_CT, me < QKV_BLOCKS),
        ("wo", WO_BLOCKS, WO_RT, WO_CT, me >= QKV_BLOCKS),
        ("w1", W1_BLOCKS, W1_RT, W1_CT, me < W1_BLOCKS),
        ("w2", W2_BLOCKS, W2_RT, W2_CT, me >= W1_BLOCKS),
    ):

        @pl.when(mine)
        def _(name=name, rt_count=rt_count, ct_count=ct_count):
            for ct in range(ct_count):
                for rt in range(rt_count):
                    act(name, rt, ct, rt * SUB * ct_count + ct, ct_count)


def half_place(name, rt, ct):
    if name == "qkv":
        return ct // 9, ct % 9 * QKV_RT + rt
    if name == "wo":
        return rt // 3, rt % 3 * WO_CT + ct
    if name == "w1":
        return ct // 12, ct % 12 * W1_RT + rt
    return rt // 6, rt % 6 * W2_CT + ct


def part_place(name, rt, ct):
    if name == "qkv":
        return ct % 6 // 3, rt, ct // 6 * 3 + ct % 3
    place = rt * WO_CT + ct
    return place // 18, place // ATT_PART % 2, place % ATT_PART


def qkv_group(g):
    return [6 * third + 3 * g + i for third in range(3) for i in range(3)]


def small_rows(me, act):
    @pl.when(me == 0)
    def _():
        act("att", True, 12, G1)
        act("mlp", True, 12, G2)

    @pl.when(me == QKV_BLOCKS - 1)
    def _():
        act("att", False, 12, BQ)

    @pl.when(me == W1_BLOCKS - 1)
    def _():
        act("mlp", False, 24, B1)

    @pl.when(me == BLOCKS - 1)
    def _():
        act("att", False, 12, BO)
        act("mlp", False, 12, B2)


OWNERS = (0, W1_BLOCKS - 1, QKV_BLOCKS - 1, BLOCKS - 1)


def sent_rows(kind, first):
    return 12 if kind == "mlp" and first in (G2, B2) else 0


def pack_kernel(att_rows, me_ref, own, tails, heads, att, mlp, win_a, win_m, table):
    me = me_ref[0]
    mlp_rows = own.shape[0] - att_rows
    win_a[0:ATT_BEFORE, :] = tails[0:ATT_BEFORE, :].astype(F32)
    win_a[ATT_BEFORE : ATT_BEFORE + att_rows, :] = own[0:att_rows, :]
    win_a[ATT_BEFORE + att_rows :, :] = heads[0:ATT_AFTER, :].astype(F32)
    win_m[0:MLP_BEFORE, :] = tails[ATT_BEFORE:, :].astype(F32)
    win_m[MLP_BEFORE : MLP_BEFORE + mlp_rows, :] = own[att_rows:, :]
    win_m[MLP_BEFORE + mlp_rows :, :] = heads[ATT_AFTER:, :].astype(F32)
    att_off, mlp_off = window_offsets(me, att_rows, mlp_rows)

    def tile(name, rt, ct, first, stride):
        attention = name in ("qkv", "wo")
        window, out, off = (win_a, att, att_off) if attention else (win_m, mlp, mlp_off)
        values = window[pl.ds(off + first, SUB, stride=stride), :]
        out[half_place(name, rt, ct)] = values.astype(BF16)

    each_tile(me, tile)
    table[...] = jnp.zeros_like(table)

    def vector(kind, before, rows, first):
        window, off, size = (win_a, att_off, 576) if kind == "att" else (win_m, mlp_off, 1152)
        start = off - 12 if before else off + size
        place = sent_rows(kind, first)
        table[place : place + rows, :] = window[pl.ds(start, rows), :]

    small_rows(me, vector)
    att[0, ATT_HALF] = table[0:SUB, :].astype(BF16)
    att[1, ATT_HALF] = table[SUB : 2 * SUB, :].astype(BF16)


def pack(me, own, tails, heads, att_rows):
    mlp_rows = own.shape[0] - att_rows
    return pl.pallas_call(
        partial(pack_kernel, att_rows),
        out_shape=(
            shape((2, ATT_SENT, SUB, LANES), BF16),
            shape((2, MLP_HALF, SUB, LANES), BF16),
        ),
        in_specs=[smem(), vmem(), vmem(), vmem()],
        out_specs=(vmem(), vmem()),
        scratch_shapes=[
            pltpu.VMEM((ATT_BEFORE + att_rows + ATT_AFTER, LANES), F32),
            pltpu.VMEM((MLP_BEFORE + mlp_rows + MLP_AFTER, LANES), F32),
            pltpu.VMEM((2 * SUB, LANES), F32),
        ],
        name="pack",
    )(me, own, tails, heads)


def spread_kernel(
    att_rows, scale, me_ref, group0, group1, mlp, mine, to_before, to_after, win_a, win_m, table
):
    me = me_ref[0]
    mlp_rows = mine.shape[0] - att_rows
    att_off, mlp_off = window_offsets(me, att_rows, mlp_rows)
    win_a[...] = jnp.zeros_like(win_a)
    win_m[...] = jnp.zeros_like(win_m)

    def tile(name, rt, ct, first, stride):
        if name in ("qkv", "wo"):
            g, half, index = part_place(name, rt, ct)
            values = (group0, group1)[g][half, index]
            win_a[pl.ds(att_off + first, SUB, stride=stride), :] = values * scale
        else:
            values = mlp[half_place(name, rt, ct)]
            win_m[pl.ds(mlp_off + first, SUB, stride=stride), :] = values * scale

    each_tile(me, tile)
    for h in range(2):
        table[SUB * h : SUB * h + SUB, :] = group1[h, ATT_PART] * scale

    def vector(kind, before, rows, first):
        window, off, size = (win_a, att_off, 576) if kind == "att" else (win_m, mlp_off, 1152)
        start = off - 12 if before else off + size
        place = sent_rows(kind, first)
        window[pl.ds(start, rows), :] = table[place : place + rows, :]

    small_rows(me, vector)
    mine[0:att_rows, :] = win_a[ATT_BEFORE : ATT_BEFORE + att_rows, :]
    mine[att_rows:, :] = win_m[MLP_BEFORE : MLP_BEFORE + mlp_rows, :]
    to_before[0:ATT_BEFORE, :] = win_a[0:ATT_BEFORE, :]
    to_before[ATT_BEFORE:, :] = win_m[0:MLP_BEFORE, :]
    to_after[0:ATT_AFTER, :] = win_a[ATT_BEFORE + att_rows :, :]
    to_after[ATT_AFTER:, :] = win_m[MLP_BEFORE + mlp_rows :, :]


def spread(me, group0, group1, mlp, att_rows, mlp_rows, scale):
    return pl.pallas_call(
        partial(spread_kernel, att_rows, scale),
        out_shape=(
            shape((att_rows + mlp_rows, LANES), F32),
            shape((ATT_BEFORE + MLP_BEFORE, LANES), F32),
            shape((ATT_AFTER + MLP_AFTER, LANES), F32),
        ),
        in_specs=[smem(), vmem(), vmem(), vmem()],
        out_specs=(vmem(), vmem(), vmem()),
        scratch_shapes=[
            pltpu.VMEM((ATT_BEFORE + att_rows + ATT_AFTER, LANES), F32),
            pltpu.VMEM((MLP_BEFORE + mlp_rows + MLP_AFTER, LANES), F32),
            pltpu.VMEM((2 * SUB, LANES), F32),
        ],
        name="spread",
    )(me, group0, group1, mlp)


def close_kernel(att_rows, mine, below, above, out):
    rows = mine.shape[0]
    out[...] = mine[...]
    out[0:ATT_AFTER, :] += below[0:ATT_AFTER, :]
    out[att_rows : att_rows + MLP_AFTER, :] += below[ATT_AFTER:, :]
    out[att_rows - ATT_BEFORE : att_rows, :] += above[0:ATT_BEFORE, :]
    out[rows - MLP_BEFORE : rows, :] += above[ATT_BEFORE:, :]


def close(mine, below, above, att_rows):
    return pl.pallas_call(
        partial(close_kernel, att_rows),
        out_shape=shape(mine.shape, F32),
        in_specs=[vmem()] * 3,
        out_specs=vmem(),
        name="close",
    )(mine, below, above)


def spot(h, d):
    x, c, z, y = d >> 4, (d >> 3) & 1, (d >> 1) & 3, d & 1
    return c * 16 + (y * 8 + x * 4 if h == 0 else x * 8 + y * 4) + z


SLOTS = [sorted(range(BLOCKS), key=partial(spot, h)) for h in range(2)]


def fill_spots(me, spots):
    for h in range(2):
        mine = spot(h, me)
        for d in range(BLOCKS):
            spots[h, d] = jnp.bitwise_xor(mine, spot(h, d))


def slots_scratch(tiles):
    return pltpu.VMEM((2, BLOCKS, tiles, SUB, LANES), BF16)


def spots_scratch():
    return pltpu.SMEM((2, BLOCKS), jnp.int32)


def arriving_slots(buffers, w, sems):
    return [
        pltpu.make_async_copy(buffers[i], w.at[i // 4, pl.ds(i % 4 * 8, 8)], sems.at[i])
        for i in range(8)
    ]


def leaving_slots(buffers, w, sems):
    return [
        pltpu.make_async_copy(w.at[i // 2, pl.ds(i % 2 * 16, 16)], buffers[i], sems.at[i])
        for i in range(4)
    ]


def qkv_column(w, spots, ct):
    h, place = ct // 9, ct % 9 * QKV_RT
    tiles = [w[h, spots[h, d], place + rt] for d in range(QKV_BLOCKS) for rt in range(QKV_RT)]
    return jnp.concatenate(tiles, axis=0)


def wo_matrix(w, spots):
    columns = []
    for ct in range(WO_CT):
        tiles = [
            w[rt // 3, spots[rt // 3, QKV_BLOCKS + i] & 7, rt % 3 * WO_CT + ct]
            for i in range(WO_BLOCKS)
            for rt in range(WO_RT)
        ]
        columns.append(jnp.concatenate(tiles, axis=0))
    return jnp.concatenate(columns, axis=1)


def dma(count):
    return pltpu.SemaphoreType.DMA((count,))


def norm_rows(rows, gain, shift, source, target, step=256):
    def one(i, carry):
        at = pl.ds(pl.multiple_of(i * step, step), step)
        unit, _ = normalized(source[at, :].astype(F32))
        target[at, :] = (unit * gain + shift).astype(BF16)
        return carry

    lax.fori_loop(0, rows // step, one, 0)


def qkv_kernel(me_ref, tokens, *refs):
    buffers, (n1, qkv, small, w, spots, x, unit, triple, sems, own) = refs[:8], refs[8:]
    coming = pltpu.make_async_copy(tokens, x, own.at[0])
    coming.start()
    weights = arriving_slots(buffers, w, sems)
    fetch(weights)
    fill_spots(me_ref[0], spots)
    settle(weights)
    tables = [
        jnp.concatenate([w[h, spots[h, d], ATT_HALF] for h in range(2)], axis=0).astype(F32)
        for d in OWNERS
    ]
    small[G1 : G1 + 12, :] = tables[0][0:12]
    small[G2 : G2 + 12, :] = tables[0][12:24]
    small[B1 : B1 + 24, :] = tables[1][0:24]
    small[BQ : BQ + 12, :] = tables[2][0:12]
    small[BO : BO + 12, :] = tables[3][0:12]
    small[B2 : B2 + 12, :] = tables[3][12:24]
    small[SMALL - 4 :, :] = jnp.zeros((4, LANES), F32)
    coming.wait()
    norm_rows(x.shape[0], row_of(small, G1, 6), row_of(small, C1, 6), x, unit)
    going = [pltpu.make_async_copy(unit, n1, own.at[0])]
    going[0].start()
    bias = jnp.concatenate(
        [row_of(small, BQ, 6), jnp.zeros((1, 768), F32), row_of(small, BV, 6)], axis=1
    )
    for c in range(QKV_CT // 2):
        weight = jnp.concatenate([qkv_column(w, spots, 2 * c + i) for i in range(2)], axis=1)
        lanes = slice(256 * c, 256 * c + 256)
        triple[:, lanes] = (mm(unit[...], weight, NN) + bias[:, lanes]).astype(BF16)
        going.append(
            pltpu.make_async_copy(triple.at[:, lanes], qkv.at[:, lanes], own.at[1 + c])
        )
        going[-1].start()
    settle(going)


def project_qkv(me, tokens, att):
    rows, width = tokens.shape
    return pl.pallas_call(
        qkv_kernel,
        out_shape=(
            shape((rows, width), BF16),
            shape((rows, 3 * width), BF16),
            shape((SMALL, LANES), F32),
        ),
        in_specs=[smem(), hbm()] + [hbm()] * 8,
        out_specs=(hbm(), hbm(), vmem()),
        scratch_shapes=[
            slots_scratch(ATT_SENT),
            spots_scratch(),
            pltpu.VMEM((rows, width), BF16),
            pltpu.VMEM((rows, width), BF16),
            pltpu.VMEM((rows, 3 * width), BF16),
            dma(8),
            dma(1 + QKV_CT // 2),
        ],
        compiler_params=pltpu.CompilerParams(vmem_limit_bytes=GRANT),
        cost_estimate=cost(6 * rows * width * width, 12 * rows * width),
        name="qkv_forward",
    )(me, tokens, *att)


CLASSES = (128, 256, 320, 384, 448, 512, 768)


def head_masked(block):
    lane = lax.broadcasted_iota(jnp.int32, block.shape, 1)
    zero = jnp.zeros_like(block)
    return jnp.concatenate(
        [jnp.where(lane < 64, block, zero), jnp.where(lane >= 64, block, zero)], axis=0
    )


def pick_heads(both):
    return jnp.concatenate([both[0:64, 0:QB], both[64:128, QB : 2 * QB]], axis=0)


def pieces_of_window(width):
    return [slice(first, min(first + QB, width)) for first in range(0, width, QB)]


def spread_ids(query_ids, key_ids):
    for b in range(query_ids.shape[0]):
        row = jnp.broadcast_to(query_ids[b : b + 1, :], (QB, QB))
        key_ids[b * QB : (b + 1) * QB, :] = row.T


def mask_bias(start, width, b, key_ids, query_ids, bias):
    for piece in pieces_of_window(width):
        size = piece.stop - piece.start
        at = pl.ds(pl.multiple_of(start + piece.start, SUB), size)
        same = key_ids[at, :] == query_ids[pl.ds(b, 1), :]
        bias[piece, :] = jnp.where(same, 0.0, NEGATIVE)


PAIRS = HEADS // 2


def attend_block(b, start, width, qkv, mixed, stats, bias, scores):
    rows = pl.ds(pl.multiple_of(b * QB, QB), QB)
    pieces = pieces_of_window(width)
    for p in range(PAIRS):
        lanes, key_lanes, value_lanes = [
            slice(LANES * (PAIRS * third + p), LANES * (PAIRS * third + p + 1))
            for third in range(3)
        ]
        queries = head_masked(qkv[rows, lanes] * 0.125)
        highest = jnp.full((8, 2 * QB), NEGATIVE, F32)
        for piece in pieces:
            size = piece.stop - piece.start
            at = pl.ds(pl.multiple_of(start + piece.start, SUB), size)
            part = mm(qkv[at, key_lanes], queries, NT)
            part = part + jnp.concatenate([bias[piece, :]] * 2, axis=1)
            scores[p, piece, :] = part
            highest = jnp.maximum(highest, jnp.max(part.reshape(size // 8, 8, 2 * QB), axis=0))
        highest = jnp.max(highest, axis=0, keepdims=True)
        summed = jnp.zeros((8, 2 * QB), F32)
        both = jnp.zeros((LANES, 2 * QB), F32)
        for piece in pieces:
            size = piece.stop - piece.start
            at = pl.ds(pl.multiple_of(start + piece.start, SUB), size)
            raised = jnp.exp(scores[p, piece, :] - highest)
            summed = summed + fold8(raised)
            both = both + mm(qkv[at, value_lanes], raised.astype(BF16), TN)
        inverse = 1.0 / total(summed)
        mixed[rows, lanes] = pick_heads(both * inverse).T.astype(BF16)
        stats[b * PAIRS + p, 0:1, :] = highest
        stats[b * PAIRS + p, 1:2, :] = inverse


def wo_scratch():
    return pltpu.VMEM((2, WO_BLOCKS, ATT_SENT, SUB, LANES), BF16)


def wo_copies(buffers, w, sems, core, x):
    copies = []
    for y in range(2):
        source = buffers[2 * core + y].at[pl.ds(4 * x, 4)]
        copies.append(pltpu.make_async_copy(source, w.at[0, pl.ds(4 * y, 4)], sems.at[y]))
    copies.append(pltpu.make_async_copy(buffers[4 + 2 * core + x], w.at[1], sems.at[2]))
    return copies


def fetch_wo(me, buffers, w, spots, sems):
    fill_spots(me, spots)
    for h in range(2):
        for i in range(WO_BLOCKS):
            place = spot(h, jnp.bitwise_xor(me, QKV_BLOCKS + i) & 7)
            spots[h, QKV_BLOCKS + i] = (place >> (1 if h == 0 else 0)) & 4 | place & 3
    far = jnp.bitwise_xor(me, QKV_BLOCKS)
    for core in range(2):
        for x in range(2):

            @pl.when((far >> 3) == 2 * x + core)
            def _(core=core, x=x):
                fetch(wo_copies(buffers, w, sems, core, x))


def wait_wo(buffers, w, sems):
    settle(wo_copies(buffers, w, sems, 0, 0))


def attend_kernel(me_ref, windows, qkv, tokens, cot, query_ids, small, *refs):
    buffers, refs = refs[:8], refs[8:]
    mixed, x1, branch, n2, dm, stats, gb2 = refs[:7]
    key_ids, triple, x, g, mix, mid, out, unit, scaled, bias, scores, w, spots = refs[7:20]
    sems, own, chunk_sems = refs[20:]
    rows = tokens.shape[0]
    blocks = rows // QB

    def chunk(i):
        at = pl.ds(pl.multiple_of(i * QB, QB), QB)
        return pltpu.make_async_copy(qkv.at[at, :], triple.at[at, :], chunk_sems.at[i])

    for i in range(blocks):
        chunk(i).start()
    coming = [
        pltpu.make_async_copy(tokens, x, own.at[0]),
        pltpu.make_async_copy(cot, g, own.at[1]),
    ]
    fetch(coming)
    fetch_wo(me_ref[0], buffers, w, spots, sems)
    spread_ids(query_ids, key_ids)

    def one_block(b, loaded):
        start = pl.multiple_of(windows[0, b], SUB)
        needed = jnp.maximum(windows[2, b], loaded)

        def arrived(i, carry):
            chunk(i).wait()
            return carry

        lax.fori_loop(loaded, needed, arrived, 0)
        for index, width in enumerate(CLASSES):

            @pl.when(windows[1, b] == index)
            def _(width=width):
                mask_bias(start, width, b, key_ids, query_ids, bias)
                attend_block(b, start, width, triple, mix, stats, bias, scores)

        return needed

    loaded = lax.fori_loop(0, blocks, one_block, jnp.int32(0))

    def arrived(i, carry):
        chunk(i).wait()
        return carry

    lax.fori_loop(loaded, blocks, arrived, 0)
    going = [pltpu.make_async_copy(mix, mixed, own.at[2])]
    going[0].start()
    wait_wo(buffers, w, sems)
    settle(coming)
    bo, s1 = row_of(small, BO, 6), row_of(small, S1, 6)
    gain, shift = row_of(small, G2, 6), row_of(small, C2, 6)
    s2 = row_of(small, S2, 6)
    weight = wo_matrix(w, spots)
    step = 256
    sums = jnp.zeros((8, 768), F32)
    for i in range(rows // step):
        at = slice(i * step, (i + 1) * step)
        made = mm(mix[at, :], weight, NN) + bo
        out[at, :] = made.astype(BF16)
        values = x[at, :].astype(F32) + s1 * made
        mid[at, :] = values
        normal, _ = normalized(values)
        unit[at, :] = (normal * gain + shift).astype(BF16)
        rounded = (g[at, :].astype(F32) * s2).astype(BF16)
        scaled[at, :] = rounded
        sums = sums + fold8(rounded.astype(F32))
        for k, (source, target) in enumerate(
            ((out, branch), (mid, x1), (unit, n2), (scaled, dm))
        ):
            sem = own.at[3 + 4 * i + k]
            going.append(pltpu.make_async_copy(source.at[at, :], target.at[at, :], sem))
            going[-1].start()
    put_row(gb2, 0, total(sums))
    settle(going)


def attend(me, windows, qkv, tokens, cot, query_ids, small, att):
    rows, width = tokens.shape
    row = lambda kind: pltpu.VMEM((rows, width), kind)
    return pl.pallas_call(
        attend_kernel,
        out_shape=(
            shape((rows, width), BF16),
            shape((rows, width), F32),
            shape((rows, width), BF16),
            shape((rows, width), BF16),
            shape((rows, width), BF16),
            shape((rows // QB * PAIRS, 2, 2 * QB), F32),
            shape((6, LANES), F32),
        ),
        in_specs=[smem(), smem(), hbm(), hbm(), hbm(), vmem(), vmem()] + [hbm()] * 8,
        out_specs=(hbm(),) * 5 + (vmem(), vmem()),
        scratch_shapes=[
            pltpu.VMEM((rows, QB), F32),
            pltpu.VMEM((rows, 3 * width), BF16),
            row(BF16),
            row(BF16),
            row(BF16),
            row(F32),
            row(BF16),
            row(BF16),
            row(BF16),
            pltpu.VMEM((CLASSES[-1], QB), F32),
            pltpu.VMEM((PAIRS, CLASSES[-1], 2 * QB), F32),
            wo_scratch(),
            spots_scratch(),
            dma(3),
            dma(3 + 4 * rows // 256),
            dma(rows // QB),
        ],
        compiler_params=pltpu.CompilerParams(vmem_limit_bytes=GRANT),
        cost_estimate=cost(2 * rows * rows * width, 20 * rows * width, 4 * rows * rows),
        name="attend_forward",
    )(me, windows, qkv, tokens, cot, query_ids, small, *att)


def lay_matrix(w, spots, name, blocks, first, rt_count, columns, out):
    def one_block(d, carry):
        places = [spots[h, first + d] for h in range(2)]
        base = pl.multiple_of(d * rt_count * SUB, SUB)
        for rt in range(rt_count):
            for column, ct in enumerate(columns):
                h, index = half_place(name, rt, ct)
                at = pl.ds(pl.multiple_of(base + rt * SUB, SUB), SUB)
                out[at, LANES * column : LANES * (column + 1)] = w[h, places[h], index]
        return carry

    lax.fori_loop(0, blocks, one_block, 0)


def lay_w1(w, spots, out):
    lay_matrix(w, spots, "w1", W1_BLOCKS, 0, W1_RT, range(W1_CT), out)


def lay_w2(w, spots, out):
    lay_matrix(w, spots, "w2", W2_BLOCKS, W1_BLOCKS, W2_RT, range(W2_CT), out)


def w2_place(spots, f, row, ct):
    rt = row % W2_RT
    h = rt // 6
    return h, spots[h, W1_BLOCKS + 4 * f + row // W2_RT], rt % 6 * W2_CT + ct


TALL = 256
PARTS = CHUNK // 256


def device_of(x, c, z, y):
    return x * 16 + c * 8 + z * 2 + y


W1_RUNS = [
    [(0, device_of(0, c, 0, y), 4) for c in range(2) for y in range(2)],
    [(1, device_of(0, c, 0, 0), 8) for c in range(2)],
]
W2_RUNS = [
    [(h, device_of(1, f >> 1, 2 * (f & 1), y), 2) for h in range(2) for y in range(2)]
    for f in range(CHUNKS)
]
RUN_ORDER = W1_RUNS[0] + W2_RUNS[0] + W2_RUNS[1] + W1_RUNS[1] + W2_RUNS[2] + W2_RUNS[3]


class Runs:
    def __init__(self, buffers, w, spots, sems, out=False):
        self.buffers, self.w, self.spots, self.sems, self.out = buffers, w, spots, sems, out
        self.each = len(buffers) // 2

    def copy(self, run, which, index, place):
        h, first, size = run
        outer = self.buffers[self.each * h + which].at[pl.ds(index, size)]
        inner = self.w.at[h, pl.ds(place, size)]
        sem = self.sems.at[RUN_ORDER.index(run)]
        ends = (inner, outer) if self.out else (outer, inner)
        return pltpu.make_async_copy(*ends, sem)

    def start(self, runs):
        length = BLOCKS // self.each
        for run in runs:
            h, first, size = run
            place = self.spots[h, first] & (BLOCKS - size)
            for which in range(self.each):

                @pl.when(place // length == which)
                def _(run=run, which=which, place=place):
                    self.copy(run, which, place & (length - 1), place).start()

    def wait(self, runs):
        for run in runs:
            self.copy(run, 0, 0, 0).wait()


def mlp_kernel(me_ref, n2_in, dm_in, small, *refs):
    arriving, refs = refs[:8], refs[8:]
    u_out, dz_out, vectors, *leaving = refs[:7]
    w, first, second, spots, n2, dm, u, dz, zs, dus, bias_sums, b1_lines, sems, own = refs[7:]
    rows, width = n2.shape
    tiles = rows // TALL
    coming = [
        pltpu.make_async_copy(n2_in, n2, own.at[0]),
        pltpu.make_async_copy(dm_in, dm, own.at[1]),
    ]
    fetch(coming)
    fill_spots(me_ref[0], spots)
    incoming = Runs(arriving, w, spots, sems)
    incoming.start(RUN_ORDER)
    bias_sums[...] = jnp.zeros_like(bias_sums)
    for f in range(CHUNKS):
        b1_lines[f : f + 1, :] = row_of(small, B1 + 6 * f, 6)
    def lay_chunk(f, side):
        h, base = f >> 1, MLP_HALF // 2 * (f & 1)
        for d in range(W1_BLOCKS):
            place = spots[h, d]
            for rt in range(W1_RT):
                at = slice((d * W1_RT + rt) * SUB, (d * W1_RT + rt + 1) * SUB)
                for ct in range(6):
                    lanes = slice(LANES * ct, LANES * ct + LANES)
                    first[side, at, lanes] = w[h, place, base + ct * W1_RT + rt]
        for k in range(4):
            places = [spots[i, W1_BLOCKS + 4 * f + k] for i in range(2)]
            for rt in range(W2_RT):
                at = slice((k * W2_RT + rt) * SUB, (k * W2_RT + rt + 1) * SUB)
                for ct in range(W2_CT):
                    lanes = slice(LANES * ct, LANES * ct + LANES)
                    i, index = half_place("w2", rt, ct)
                    second[side, at, lanes] = w[i, places[i], index]

    incoming.wait(W1_RUNS[0] + W2_RUNS[0])
    lay_chunk(jnp.int32(0), jnp.int32(0))
    settle(coming)

    units = [(t, c) for c in range(PARTS) for t in range(tiles)]

    def lanes_of(f, c):
        return pl.ds(pl.multiple_of(CHUNK * f + 256 * c, 256), 256)

    def outward(f):
        chunk = pl.ds(pl.multiple_of(CHUNK * f, CHUNK), CHUNK)
        return [
            pltpu.make_async_copy(u.at[:, chunk], u_out.at[:, chunk], own.at[2 * f]),
            pltpu.make_async_copy(dz.at[:, chunk], dz_out.at[:, chunk], own.at[2 * f + 1]),
        ]

    def one_chunk(f, carry):
        for index in range(CHUNKS - 1):

            @pl.when(f == index)
            def _(index=index):
                incoming.wait(W2_RUNS[index + 1] + (W1_RUNS[1] if index == 1 else []))

        side = f & 1
        lay_chunk(jnp.minimum(f + 1, CHUNKS - 1), 1 - side)

        def multiply(unit, slot):
            t, c = unit
            at = slice(TALL * t, TALL * t + TALL)
            zs[slot] = mm(n2[at, :], first[side, :, 256 * c : 256 * c + 256], NN)
            dus[slot] = mm(dm[at, :], second[side, 256 * c : 256 * c + 256, :], NT)

        def activate(unit, slot):
            t, c = unit
            lanes = slice(256 * c, 256 * c + 256)
            bias = b1_lines[pl.ds(f, 1), lanes]
            folded = jnp.zeros((8, 256), F32)
            for r in range(TALL // 32):
                part = slice(32 * r, 32 * r + 32)
                place = slice(TALL * t + 32 * r, TALL * t + 32 * r + 32)
                value, slope = gelu_pair(zs[slot, part, :] + bias)
                u[place, lanes_of(f, c)] = value.astype(BF16)
                rounded = (dus[slot, part, :] * slope).astype(BF16)
                dz[place, lanes_of(f, c)] = rounded
                folded = folded + fold8(rounded.astype(F32))
            bias_sums[:, lanes_of(f, c)] += folded

        multiply(units[0], 0)
        for i, unit in enumerate(units):
            if i + 1 < len(units):
                multiply(units[i + 1], (i + 1) % 2)
            activate(unit, i % 2)
        fetch(outward(f))
        return carry

    lax.fori_loop(0, CHUNKS, one_chunk, 0)
    put_row(vectors, 0, total(bias_sums[...]))

    outgoing = Runs(leaving, w, spots, sems, out=True)

    def one_grad(f, carry):
        h, base = f >> 1, MLP_HALF // 2 * (f & 1)
        chunk = pl.ds(pl.multiple_of(CHUNK * f, CHUNK), CHUNK)
        for c in range(PARTS):
            lanes = slice(256 * c, 256 * c + 256)
            grad = mm(n2[:, lanes], dz[:, chunk], TN)
            for r in range(SUB):
                d, rt = (SUB * c + r) // W1_RT, (SUB * c + r) % W1_RT
                for ct in range(6):
                    tile = grad[SUB * r : SUB * r + SUB, LANES * ct : LANES * ct + LANES]
                    w[h, spots[h, d], base + ct * W1_RT + rt] = tile.astype(BF16)
        for side in range(2):

            @pl.when(f == 2 * side + 1)
            def _(side=side):
                outgoing.start(W1_RUNS[side])

        for c in range(PARTS):
            grad = mm(u[:, lanes_of(f, c)], dm[...], TN)
            for r in range(SUB):
                for ct in range(W2_CT):
                    tile = grad[SUB * r : SUB * r + SUB, LANES * ct : LANES * ct + LANES]
                    w[w2_place(spots, f, SUB * c + r, ct)] = tile.astype(BF16)
        for index in range(CHUNKS):

            @pl.when(f == index)
            def _(index=index):
                outgoing.start(W2_RUNS[index])

        return carry

    lax.fori_loop(0, CHUNKS, one_grad, 0)
    for f in range(CHUNKS):
        settle(outward(f))
    outgoing.wait(RUN_ORDER)


def feed_forward(me, n2, dm, small, mlp):
    rows, width = n2.shape
    half = shape((HALF_BLOCKS, MLP_HALF, SUB, LANES), BF16)
    return pl.pallas_call(
        mlp_kernel,
        out_shape=(
            shape((rows, FF), BF16),
            shape((rows, FF), BF16),
            shape((24, LANES), F32),
            half,
            half,
            half,
            half,
        ),
        in_specs=[smem(), hbm(), hbm(), vmem()] + [hbm()] * 8,
        out_specs=(hbm(), hbm(), vmem()) + (hbm(),) * 4,
        scratch_shapes=[
            slots_scratch(MLP_HALF),
            pltpu.VMEM((2, width, CHUNK), BF16),
            pltpu.VMEM((2, CHUNK, width), BF16),
            spots_scratch(),
            pltpu.VMEM((rows, width), BF16),
            pltpu.VMEM((rows, width), BF16),
            pltpu.VMEM((rows, FF), BF16),
            pltpu.VMEM((rows, FF), BF16),
            pltpu.VMEM((2, TALL, 256), F32),
            pltpu.VMEM((2, TALL, 256), F32),
            pltpu.VMEM((8, FF), F32),
            pltpu.VMEM((CHUNKS, CHUNK), F32),
            dma(len(RUN_ORDER)),
            dma(2 * CHUNKS),
        ],
        compiler_params=pltpu.CompilerParams(vmem_limit_bytes=42 * MEGA),
        cost_estimate=cost(8 * rows * width * FF, 40 * MEGA),
        name="feed_forward",
    )(me, n2, dm, small, *mlp)


def matrix_copies(buffers, w, sems, x):
    copies = []
    for i in range(4):
        source = buffers[i].at[pl.ds(4 * x, 4)]
        copies.append(pltpu.make_async_copy(source, w.at[0, pl.ds(4 * i, 4)], sems.at[i]))
    for c in range(2):
        source = buffers[4 + 2 * c + x]
        copies.append(pltpu.make_async_copy(source, w.at[1, pl.ds(8 * c, 8)], sems.at[4 + c]))
    return copies


def fetch_matrix(me, buffers, w, spots, sems, first):
    def place(d):
        return ((d >> 3) & 1) * 8 + (d & 1) * 4 + ((d >> 1) & 3)

    for x in range(2):

        @pl.when((me >> 4) == (x ^ (first >> 4)))
        def _(x=x):
            fetch(matrix_copies(buffers, w, sems, x))

    mine = place(me)
    for d in range(W1_BLOCKS):
        for h in range(2):
            spots[h, first + d] = jnp.bitwise_xor(mine, place(d))


def wait_matrix(buffers, w, sems):
    settle(matrix_copies(buffers, w, sems, 0))


def matrix_scratch():
    return pltpu.VMEM((2, W1_BLOCKS, MLP_HALF, SUB, LANES), BF16)


def mlp_out_kernel(me_ref, u_in, x1_in, cot_in, small, *refs):
    arriving, refs = refs[:8], refs[8:]
    out, vectors, w, second, spots, u, x1, cot, macc, done, sums, sems, own = refs
    rows, width = x1.shape
    tiles = rows // TALL

    def tile_copy(source, target, t, k):
        at = pl.ds(pl.multiple_of(TALL * t, TALL), TALL)
        return pltpu.make_async_copy(source.at[at, :], target.at[at, :], own.at[k, t])

    fetch_matrix(me_ref[0], arriving, w, spots, sems, W1_BLOCKS)
    for t in range(tiles):
        tile_copy(u_in, u, t, 0).start()
    for t in range(tiles):
        tile_copy(x1_in, x1, t, 1).start()
        tile_copy(cot_in, cot, t, 2).start()
    bias, scale = row_of(small, B2, 6), row_of(small, S2, 6)
    sums[...] = jnp.zeros_like(sums)
    wait_matrix(arriving, w, sems)
    lay_w2(w, spots, second)

    def contract(t):
        at = pl.ds(pl.multiple_of(TALL * t, TALL), TALL)
        tile_copy(u_in, u, t, 0).wait()
        macc[at, :] = mm(u[at, :], second[...], NN)

    def finish(t):
        tile_copy(x1_in, x1, t, 1).wait()
        tile_copy(cot_in, cot, t, 2).wait()
        for part in range(TALL // 64):
            at = pl.ds(pl.multiple_of(TALL * t + 64 * part, 64), 64)
            contracted = macc[at, :] + bias
            done[at, :] = (x1[at, :] + scale * contracted).astype(BF16)
            sums[...] += fold8(cot[at, :].astype(F32) * contracted)
        tile_copy(done, out, t, 3).start()

    def one_tile(t, carry):
        contract(t)
        finish(t - 1)
        return carry

    contract(0)
    lax.fori_loop(1, tiles, one_tile, 0)
    finish(tiles - 1)
    put_row(vectors, 0, total(sums[...]))
    for t in range(tiles):
        tile_copy(done, out, t, 3).wait()


def feed_forward_out(me, u, x1, cot, small, mlp):
    rows, width = x1.shape
    row = lambda kind: pltpu.VMEM((rows, width), kind)
    return pl.pallas_call(
        mlp_out_kernel,
        out_shape=(shape((rows, width), BF16), shape((6, LANES), F32)),
        in_specs=[smem()] + [hbm()] * 3 + [vmem()] + [hbm()] * 8,
        out_specs=(hbm(), vmem()),
        scratch_shapes=[
            matrix_scratch(),
            pltpu.VMEM((FF, width), BF16),
            spots_scratch(),
            pltpu.VMEM((rows, FF), BF16),
            row(F32),
            row(BF16),
            row(F32),
            row(BF16),
            pltpu.VMEM((8, width), F32),
            dma(6),
            pltpu.SemaphoreType.DMA((4, rows // TALL)),
        ],
        compiler_params=pltpu.CompilerParams(vmem_limit_bytes=46 * MEGA),
        cost_estimate=cost(2 * rows * width * FF, 20 * MEGA),
        name="feed_forward_out",
    )(me, u, x1, cot, small, *mlp)


def split_kernel(me_ref, dz_in, x1_in, cot_in, branch_in, mixed_in, small, *refs):
    buffers, att_buffers, refs = refs[:8], refs[8:16], refs[16:]
    dx1_out, da_out, gwo0, gwo1, vectors = refs[:5]
    w, first, spots, wo, wo_spots, dz, x1, cot, dnacc, dx1, branch, mixed, db, da = refs[5:19]
    parts, sums, sems, wo_sems, own = refs[19:]
    me = me_ref[0]
    rows, width = x1.shape
    tiles = rows // TALL

    def tile_copy(source, target, t, k):
        at = pl.ds(pl.multiple_of(TALL * t, TALL), TALL)
        return pltpu.make_async_copy(source.at[at, :], target.at[at, :], own.at[k, t])

    fetch_matrix(me, buffers, w, spots, sems, 0)
    for t in range(tiles):
        tile_copy(dz_in, dz, t, 0).start()
    for t in range(tiles):
        tile_copy(x1_in, x1, t, 1).start()
        tile_copy(cot_in, cot, t, 2).start()
        tile_copy(branch_in, branch, t, 3).start()
    fetch_wo(me, att_buffers, wo, wo_spots, wo_sems)
    late = pltpu.make_async_copy(mixed_in, mixed, own.at[4, 0])
    late.start()
    gain, scale = row_of(small, G2, 6), row_of(small, S1, 6)
    sums[...] = jnp.zeros_like(sums)
    wait_matrix(buffers, w, sems)
    lay_w1(w, spots, first)

    def contract(t):
        at = pl.ds(pl.multiple_of(TALL * t, TALL), TALL)
        tile_copy(dz_in, dz, t, 0).wait()
        dnacc[at, :] = mm(dz[at, :], first[...], NT)

    def finish(t):
        tile_copy(x1_in, x1, t, 1).wait()
        tile_copy(cot_in, cot, t, 2).wait()
        tile_copy(branch_in, branch, t, 3).wait()
        for half in range(2):
            at = pl.ds(pl.multiple_of(TALL * t + TALL // 2 * half, TALL // 2), TALL // 2)
            unit, inverse = normalized(x1[at, :])
            grad = dnacc[at, :]
            middle = cot[at, :].astype(F32) + norm_pullback(unit, inverse, grad, gain)
            dx1[at, :] = middle
            rounded = (middle * scale).astype(BF16)
            db[at, :] = rounded
            sums[0:8, :] += fold8(grad * unit)
            sums[8:16, :] += fold8(grad)
            sums[16:24, :] += fold8(rounded.astype(F32))
            sums[24:32, :] += fold8(middle * branch[at, :].astype(F32))
        tile_copy(dx1, dx1_out, t, 1).start()

    def one_tile(t, carry):
        contract(t)
        finish(t - 1)
        return carry

    contract(0)
    lax.fori_loop(1, tiles, one_tile, 0)
    finish(tiles - 1)
    for k in range(4):
        put_row(vectors, 6 * k, total(sums[8 * k : 8 * k + 8, :]))
    wait_wo(att_buffers, wo, wo_sems)
    weight = wo_matrix(wo, wo_spots)
    going = []
    for c in range(3):
        lanes = slice(256 * c, 256 * c + 256)
        da[:, lanes] = mm(db[...], weight[lanes, :], NT).astype(BF16)
        going.append(pltpu.make_async_copy(da.at[:, lanes], da_out.at[:, lanes], own.at[0, c]))
        going[-1].start()
    late.wait()
    for c in range(3):
        grad = mm(mixed[:, 256 * c : 256 * c + 256], db[...], TN)
        for r in range(SUB):
            i, rt = (SUB * c + r) // WO_RT, (SUB * c + r) % WO_RT
            for ct in range(WO_CT):
                tile = grad[SUB * r : SUB * r + SUB, LANES * ct : LANES * ct + LANES]
                g, half, index = part_place("wo", rt, ct)
                parts[g, half, i, index] = tile.astype(BF16)
    for g, target in enumerate((gwo0, gwo1)):
        going.append(pltpu.make_async_copy(parts.at[g], target, own.at[4, g]))
        going[-1].start()
    settle(going)
    for t in range(tiles):
        tile_copy(dx1, dx1_out, t, 1).wait()


def split(me, dz, x1, cot, branch, mixed, small, mlp, att):
    rows, width = x1.shape
    part = (2, WO_BLOCKS, ATT_PART, SUB, LANES)
    row = lambda kind: pltpu.VMEM((rows, width), kind)
    return pl.pallas_call(
        split_kernel,
        out_shape=(
            shape((rows, width), F32),
            shape((rows, width), BF16),
            shape(part, BF16),
            shape(part, BF16),
            shape((24, LANES), F32),
        ),
        in_specs=[smem()] + [hbm()] * 5 + [vmem()] + [hbm()] * 16,
        out_specs=(hbm(),) * 4 + (vmem(),),
        scratch_shapes=[
            matrix_scratch(),
            pltpu.VMEM((width, FF), BF16),
            spots_scratch(),
            wo_scratch(),
            spots_scratch(),
            pltpu.VMEM((rows, FF), BF16),
            row(F32),
            row(BF16),
            row(F32),
            row(F32),
            row(BF16),
            row(BF16),
            row(BF16),
            row(BF16),
            pltpu.VMEM((2,) + part, BF16),
            pltpu.VMEM((32, width), F32),
            dma(6),
            dma(3),
            pltpu.SemaphoreType.DMA((5, rows // TALL)),
        ],
        compiler_params=pltpu.CompilerParams(vmem_limit_bytes=44 * MEGA),
        cost_estimate=cost(2 * rows * width * FF + 4 * rows * width * width, 40 * MEGA),
        name="feed_forward_in",
    )(me, dz, x1, cot, branch, mixed, small, *mlp, *att)


GROUP = PAIRS // 2
GROUP_LANES = GROUP * LANES


def attend_back_block(b, start, width, group, refs):
    q, k, v, da, stats, dq, dkeys, dvalues, bias = refs
    rows = pl.ds(pl.multiple_of(b * QB, QB), QB)
    at = pl.ds(start, width)
    mask = jnp.concatenate([bias[0:width, :]] * 2, axis=1)
    pairs = []
    for p in range(GROUP):
        lanes = slice(LANES * p, LANES * p + LANES)
        place = b * PAIRS + GROUP * group + p
        queries = head_masked(q[rows, lanes] * 0.125)
        grads = head_masked(da[rows, lanes])
        keys, values = k[at, lanes], v[at, lanes]
        scores = mm(keys, queries, NT)
        dweight = mm(values, grads, NT)
        pairs.append((lanes, place, queries, grads, keys, scores, dweight))
    later = []
    for lanes, place, queries, grads, keys, scores, dweight in pairs:
        highest = stats[place, 0:1, :]
        inverse = stats[place, 1:2, :]
        weight = jnp.exp(scores + mask - highest) * inverse
        inner_sum = total(fold8(weight * dweight))
        dvalues[at, lanes] += mm(weight.astype(BF16), grads, NN)
        dscore = (weight * (dweight - inner_sum)).astype(BF16)
        later.append((lanes, queries, keys, dscore))
    for lanes, queries, keys, dscore in later:
        dkeys[at, lanes] += mm(dscore, queries, NN)
        both = mm(keys, dscore, TN)
        dq[rows, lanes] = (pick_heads(both) * 0.125).T.astype(BF16)


def attend_back_kernel(group, windows, qkv, da_in, stats, query_ids, dqkv, *refs):
    q, k, v, da, out, dkeys, dvalues, bias, key_ids, own = refs
    rows = q.shape[0]
    blocks = rows // QB
    lanes = slice(GROUP_LANES * group, GROUP_LANES * group + GROUP_LANES)
    coming = [pltpu.make_async_copy(da_in.at[:, lanes], da, own.at[3])]
    for third, target in enumerate((q, k, v)):
        first = LANES * PAIRS * third + GROUP_LANES * group
        source = qkv.at[:, first : first + GROUP_LANES]
        coming.append(pltpu.make_async_copy(source, target, own.at[third]))
    fetch(coming)
    dkeys[...] = jnp.zeros_like(dkeys)
    dvalues[...] = jnp.zeros_like(dvalues)
    spread_ids(query_ids, key_ids)
    settle(coming)
    dq = out.at[:, 0:GROUP_LANES]

    def one_block(b, carry):
        start = pl.multiple_of(windows[0, b], SUB)
        for index, width in enumerate(CLASSES):

            @pl.when(windows[1, b] == index)
            def _(width=width):
                mask_bias(start, width, b, key_ids, query_ids, bias)
                parts = (q, k, v, da, stats, dq, dkeys, dvalues, bias)
                attend_back_block(b, start, width, group, parts)

        return carry

    lax.fori_loop(0, blocks, one_block, 0)
    going = []
    for i in range(rows // 256):
        at = slice(256 * i, 256 * i + 256)
        out[at, GROUP_LANES : 2 * GROUP_LANES] = dkeys[at, :].astype(BF16)
        out[at, 2 * GROUP_LANES :] = dvalues[at, :].astype(BF16)
        going.append(pltpu.make_async_copy(out.at[at, :], dqkv.at[at, :], own.at[i]))
        going[-1].start()
    settle(going)


def attend_back(group, windows, qkv, da, stats, query_ids):
    rows = qkv.shape[0]
    part = lambda kind: pltpu.VMEM((rows, GROUP_LANES), kind)
    return pl.pallas_call(
        partial(attend_back_kernel, group),
        out_shape=shape((rows, 3 * GROUP_LANES), BF16),
        in_specs=[smem(), hbm(), hbm(), vmem(), vmem()],
        out_specs=hbm(),
        scratch_shapes=[
            part(BF16),
            part(BF16),
            part(BF16),
            part(BF16),
            pltpu.VMEM((rows, 3 * GROUP_LANES), BF16),
            part(F32),
            part(F32),
            pltpu.VMEM((CLASSES[-1], QB), F32),
            pltpu.VMEM((rows, QB), F32),
            dma(4),
        ],
        compiler_params=pltpu.CompilerParams(vmem_limit_bytes=32 * MEGA),
        cost_estimate=cost(3 * rows * rows * rows, 14 * rows * rows, 4 * rows * rows),
        name="attend_backward",
    )(windows, qkv, da, stats, query_ids)


def put_qkv_grad(n1, dqkv, w, spots):
    for c in range(3):
        grad = mm(n1[:, 256 * c : 256 * c + 256], dqkv[...], TN)
        for r in range(SUB):
            d, rt = (SUB * c + r) // QKV_RT, (SUB * c + r) % QKV_RT
            place = spots[rt, d]
            for index in range(ATT_PART):
                tile = grad[SUB * r : SUB * r + SUB, LANES * index : LANES * index + LANES]
                w[rt, place, index] = tile.astype(BF16)


def put_wo_grad(gwo, w, spots):
    for h in range(2):
        for i in range(WO_BLOCKS):
            w[h, spots[h, QKV_BLOCKS + i], 0:ATT_PART] = gwo[h, i]


def weight_grad_kernel(me_ref, n1_in, dqkv_in, gwo_in, *refs):
    leaving, (w, spots, n1, dqkv, gwo, sems, own) = refs[:4], refs[4:]
    coming = [
        pltpu.make_async_copy(n1_in, n1, own.at[0]),
        pltpu.make_async_copy(dqkv_in, dqkv, own.at[1]),
        pltpu.make_async_copy(gwo_in, gwo, own.at[2]),
    ]
    fetch(coming)
    fill_spots(me_ref[0], spots)
    settle(coming)
    put_wo_grad(gwo, w, spots)
    put_qkv_grad(n1, dqkv, w, spots)
    copies = leaving_slots(leaving, w, sems)
    fetch(copies)
    settle(copies)


def weight_grad(me, n1, dqkv, gwo):
    rows, width = n1.shape
    half = shape((HALF_BLOCKS, ATT_PART, SUB, LANES), BF16)
    return pl.pallas_call(
        weight_grad_kernel,
        out_shape=(half,) * 4,
        in_specs=[smem()] + [hbm()] * 3,
        out_specs=(hbm(),) * 4,
        scratch_shapes=[
            slots_scratch(ATT_PART),
            spots_scratch(),
            pltpu.VMEM((rows, width), BF16),
            pltpu.VMEM(dqkv.shape, BF16),
            pltpu.VMEM(gwo.shape, BF16),
            dma(4),
            dma(3),
        ],
        compiler_params=pltpu.CompilerParams(vmem_limit_bytes=20 * MEGA),
        cost_estimate=cost(3 * rows * width * width, 10 * rows * width),
        name="qkv_weight_grad",
    )(me, n1, dqkv, gwo)


def qkv_back_kernel(
    me_ref, tokens_in, n1_in, dx1_in, dqkv0_in, dqkv1_in, small, proj, mlp, gwo_in, *refs
):
    arriving, refs = refs[:8], refs[8:]
    dx_out, *leaving = refs[:5]
    w, gw, weight, spots, gwo, tokens, n1, dx1, dqkv0, dqkv1, dn, dx, sums, table = refs[5:19]
    sems, out_sems, own = refs[19:]
    rows = tokens.shape[0]
    tiles = rows // TALL

    def tile_copy(source, target, t, k):
        at = pl.ds(pl.multiple_of(TALL * t, TALL), TALL)
        return pltpu.make_async_copy(source.at[at, :], target.at[at, :], own.at[k, t])

    for t in range(tiles):
        tile_copy(dqkv0_in, dqkv0, t, 0).start()
        tile_copy(dqkv1_in, dqkv1, t, 1).start()
    weights = arriving_slots(arriving, w, sems)
    fetch(weights)
    for t in range(tiles):
        tile_copy(tokens_in, tokens, t, 2).start()
        tile_copy(dx1_in, dx1, t, 3).start()
    late = [
        pltpu.make_async_copy(n1_in, n1, own.at[4, 0]),
        pltpu.make_async_copy(gwo_in, gwo, own.at[4, 1]),
    ]
    fetch(late)
    sums[...] = jnp.zeros_like(sums)
    gain = row_of(small, G1, 6)
    fill_spots(me_ref[0], spots)
    settle(weights)
    columns = qkv_group(0) + qkv_group(1)
    lay_matrix(w, spots, "qkv", QKV_BLOCKS, 0, QKV_RT, columns, weight)

    def contract(t):
        at = pl.ds(pl.multiple_of(TALL * t, TALL), TALL)
        for g, (source, part) in enumerate(((dqkv0_in, dqkv0), (dqkv1_in, dqkv1))):
            tile_copy(source, part, t, g).wait()
            lanes = slice(384 * g, 384 * g + 384)
            sums[16:24, lanes] += fold8(part[at, 0:384].astype(F32))
            sums[24:32, lanes] += fold8(part[at, 768:1152].astype(F32))
        both = jnp.concatenate([dqkv0[at, :], dqkv1[at, :]], axis=1)
        dn[at, :] = mm(both, weight[...], NT)

    def finish(t):
        tile_copy(tokens_in, tokens, t, 2).wait()
        tile_copy(dx1_in, dx1, t, 3).wait()
        for half in range(2):
            at = pl.ds(pl.multiple_of(TALL * t + TALL // 2 * half, TALL // 2), TALL // 2)
            unit, inverse = normalized(tokens[at, :].astype(F32))
            grad = dn[at, :]
            dx[at, :] = dx1[at, :] + norm_pullback(unit, inverse, grad, gain)
            sums[0:8, :] += fold8(grad * unit)
            sums[8:16, :] += fold8(grad)
        tile_copy(dx, dx_out, t, 3).start()

    def one_tile(t, carry):
        contract(t)
        finish(t - 1)
        return carry

    contract(0)
    lax.fori_loop(1, tiles, one_tile, 0)
    finish(tiles - 1)

    def put_table(owner, *places):
        table[...] = jnp.zeros_like(table)
        for place, values in places:
            if values.shape[1] == LANES:
                table[place : place + values.shape[0], :] = values
            else:
                put_row(table, place, values)
        for h in range(2):
            gw[h, spots[h, owner], ATT_PART] = table[SUB * h : SUB * h + SUB, :].astype(BF16)

    put_table(
        OWNERS[0], (0, total(sums[0:8, :])), (6, total(sums[8:16, :])), (12, mlp[0:12, :])
    )
    put_table(OWNERS[1], (0, mlp[12:36, :]))
    put_table(OWNERS[2], (0, total(sums[16:24, :])), (6, total(sums[24:32, :])))
    put_table(OWNERS[3], (0, proj[...]), (12, mlp[36:48, :]))
    settle(late)
    put_wo_grad(gwo, gw, spots)
    put_qkv_grad(n1, dqkv1, gw, spots)
    copies = leaving_slots(leaving, gw, out_sems)
    fetch(copies)
    for t in range(tiles):
        tile_copy(dx, dx_out, t, 3).wait()
    settle(copies)


def qkv_back(me, tokens, n1, dx1, dqkv0, dqkv1, small, proj, mlp, gwo, att):
    rows, width = tokens.shape
    tiles = ATT_PART + 1
    half = shape((HALF_BLOCKS, tiles, SUB, LANES), BF16)
    row = lambda kind: pltpu.VMEM((rows, width), kind)
    return pl.pallas_call(
        qkv_back_kernel,
        out_shape=(shape((rows, width), F32), half, half, half, half),
        in_specs=[smem()] + [hbm()] * 5 + [vmem()] * 3 + [hbm()] * 9,
        out_specs=(hbm(),) * 5,
        scratch_shapes=[
            slots_scratch(ATT_SENT),
            slots_scratch(tiles),
            pltpu.VMEM((width, 3 * width), BF16),
            spots_scratch(),
            pltpu.VMEM(gwo.shape, BF16),
            row(BF16),
            row(BF16),
            row(F32),
            pltpu.VMEM(dqkv0.shape, BF16),
            pltpu.VMEM(dqkv1.shape, BF16),
            row(F32),
            row(F32),
            pltpu.VMEM((32, width), F32),
            pltpu.VMEM((2 * SUB, LANES), F32),
            dma(8),
            dma(4),
            pltpu.SemaphoreType.DMA((5, rows // TALL)),
        ],
        compiler_params=pltpu.CompilerParams(vmem_limit_bytes=46 * MEGA),
        cost_estimate=cost(9 * rows * width * width, 30 * rows * width),
        name="qkv_backward",
    )(me, tokens, n1, dx1, dqkv0, dqkv1, small, proj, mlp, gwo, *att)


X, C, Z1, Z0, Y = 16, 8, 4, 2, 1


def exchange(values, bit):
    return lax.ppermute(values, AXES, [(d, d ^ bit) for d in range(BLOCKS)])


def overhangs(att_rows, mlp_rows):
    before, after = [], []
    for d in range(BLOCKS):
        att = 12 + d * (576 - att_rows) + (0 if d < QKV_BLOCKS else 12)
        mlp = 12 + d * (1152 - mlp_rows) + (0 if d < W1_BLOCKS else 24)
        ahead = 12 if d == 0 else 0
        att_end = att + 576 + (12 if d in (QKV_BLOCKS - 1, BLOCKS - 1) else 0)
        mlp_end = mlp + 1152 + (24 if d == W1_BLOCKS - 1 else 12 if d == BLOCKS - 1 else 0)
        if min(att, mlp) < ahead:
            before.append(d)
        if att_end > att_rows or mlp_end > mlp_rows:
            after.append(d)
    return before, after


def together(*values):
    return lax.optimization_barrier(values)


def along_z(first, second, received):
    return (
        jnp.stack([first] + [r[0] for r in received]),
        jnp.stack([second] + [r[1] for r in received]),
    )


def joined(own, received):
    return jnp.concatenate([own, received])


def sum_terms(terms):
    summed = terms[0].astype(F32)
    for term in terms[1:]:
        summed = summed + term.astype(F32)
    return summed


def kept(terms):
    return [t[: t.shape[0] // 2] for t in terms]


def z_part(first, second, k):
    return jnp.stack([sum_terms([t[k] for t in terms]) for terms in (first, second)])


def sent(terms):
    return sum_terms([t[t.shape[0] // 2 :] for t in terms]).astype(BF16)


def attention_amounts(width):
    return [width, width, 3 * width * width, width, width, width * width, width, width]


def feedforward_amounts(width):
    return [width, width, width * FF, FF, FF * width, width, width]


def pieces_of(vector, amounts):
    out, offset = [], 0
    for amount in amounts:
        out.append(vector[offset : offset + amount])
        offset += amount
    return out


def tiles_by_column(matrix, blocks, rt):
    ct = matrix.shape[1] // LANES
    return matrix.reshape(blocks, rt, SUB, ct, LANES).transpose(0, 3, 1, 2, 4)


def tiles_by_row(matrix, blocks, rt):
    ct = matrix.shape[1] // LANES
    return matrix.reshape(blocks, rt, SUB, ct, LANES).transpose(0, 1, 3, 2, 4)


def gather_plainly(params, att_rows, width):
    rounded = params.astype(BF16)
    att = lax.all_gather(rounded[:att_rows], AXES, axis=0, tiled=True).reshape(-1)
    mlp = lax.all_gather(rounded[att_rows:], AXES, axis=0, tiled=True).reshape(-1)
    g1, c1, wqkv, bq, bv, wo, bo, s1 = pieces_of(att, attention_amounts(width))
    g2, c2, w1, b1, w2, b2, s2 = pieces_of(mlp, feedforward_amounts(width))
    tile = (SUB, LANES)
    att = jnp.concatenate(
        [
            tiles_by_column(wqkv.reshape(width, -1), QKV_BLOCKS, QKV_RT).reshape((-1, 36) + tile),
            tiles_by_row(wo.reshape(width, -1), WO_BLOCKS, WO_RT).reshape((-1, 36) + tile),
        ]
    )
    mlp = jnp.concatenate(
        [
            tiles_by_column(w1.reshape(width, -1), W1_BLOCKS, W1_RT).reshape((-1, 72) + tile),
            tiles_by_row(w2.reshape(FF, -1), W2_BLOCKS, W2_RT).reshape((-1, 72) + tile),
        ]
    )
    vectors = jnp.concatenate([g1, c1, bq, bv, bo, s1, g2, c2, b1, b2, s2]).astype(F32)
    lines = vectors.reshape(-1, LANES)
    sent = jnp.zeros((BLOCKS, 2 * SUB, LANES), F32)
    for owner, place, first, count in (
        (OWNERS[0], 0, G1, 12),
        (OWNERS[0], 12, G2, 12),
        (OWNERS[1], 0, B1, 24),
        (OWNERS[2], 0, BQ, 12),
        (OWNERS[3], 0, BO, 12),
        (OWNERS[3], 12, B2, 12),
    ):
        sent = sent.at[owner, place : place + count].set(lines[first : first + count])
    sent = sent.astype(BF16).reshape((BLOCKS, 2, 1) + tile)
    att = [jnp.concatenate([att[:, 18 * h : 18 * h + 18], sent[:, h]], axis=1) for h in range(2)]
    return by_slot(*att), by_slot(mlp[:, :36], mlp[:, 36:])


def by_slot(first, second):
    halves = (first, second)
    return [
        jnp.stack([halves[i // 4][slot] for slot in SLOTS[i // 4][i % 4 * 8 : i % 4 * 8 + 8]])
        for i in range(8)
    ]


def from_slots(buffers):
    halves = []
    for h in range(2):
        slots = jnp.concatenate(buffers[2 * h : 2 * h + 2])
        halves.append(jnp.stack([slots[spot(h, d)] for d in range(BLOCKS)]))
    return halves


def reduce_plainly(gatt0, gatt1, gmlp, att_rows, mlp_rows, width, devices):
    groups = [from_slots(gatt0), from_slots(gatt1)]
    vectors = jnp.concatenate([groups[1][h][:, ATT_PART:] for h in range(2)], axis=1)
    vectors = vectors.astype(F32).reshape(BLOCKS, 2 * SUB, LANES)

    def matrix(name, first, last, rt_count, ct_count):
        rows = []
        for rt in range(rt_count):
            places = [part_place(name, rt, ct) for ct in range(ct_count)]
            rows.append(jnp.stack([groups[g][h][first:last, i] for g, h, i in places], axis=2))
        return jnp.stack(rows, axis=1).astype(F32).reshape(-1)

    wqkv = matrix("qkv", 0, QKV_BLOCKS, QKV_RT, QKV_CT)
    wo = matrix("wo", QKV_BLOCKS, BLOCKS, WO_RT, WO_CT)
    mlp = jnp.concatenate(from_slots(gmlp), axis=1).astype(F32)
    five = lambda v, dims: v.reshape((v.shape[0],) + dims + (SUB, LANES))
    w1 = five(mlp[:W1_BLOCKS], (W1_CT, W1_RT)).transpose(0, 2, 3, 1, 4).reshape(-1)
    w2 = five(mlp[W1_BLOCKS:], (W2_RT, W2_CT)).transpose(0, 1, 3, 2, 4).reshape(-1)
    line = lambda owner, first, count: vectors[owner, first : first + count].reshape(-1)
    att = [line(OWNERS[0], 0, 12), wqkv, line(OWNERS[2], 0, 12), wo, line(OWNERS[3], 0, 12)]
    mlp = [line(OWNERS[0], 12, 12), w1, line(OWNERS[1], 0, 24), w2, line(OWNERS[3], 12, 12)]

    def lay(parts, rows):
        vector = jnp.concatenate(parts)
        vector = jnp.pad(vector, (0, devices * rows * LANES - vector.shape[0]))
        return vector.reshape(devices, rows, LANES)

    whole = jnp.concatenate([lay(att, att_rows), lay(mlp, mlp_rows)], axis=1)
    return lax.psum_scatter(whole.reshape(-1, LANES), AXES, scatter_dimension=0, tiled=True)


def key_windows(segments, real):
    length = segments.shape[0]
    position = jnp.arange(length, dtype=jnp.int32)
    ids = jnp.where(real, segments, length + position)
    first = segments[0::QB]
    final = segments[QB - 1 :: QB]
    begin = jnp.sum((segments[None, :] < first[:, None]).astype(jnp.int32), axis=1)
    begin = jnp.where(real[0::QB], begin, position[0::QB])
    end = jnp.sum(((segments[None, :] <= final[:, None]) & real[None, :]).astype(jnp.int32), axis=1)
    end = jnp.where(real[QB - 1 :: QB], end, position[QB - 1 :: QB] + 1)
    begin = begin // SUB * SUB
    need = end - begin
    kind = sum((need > width).astype(jnp.int32) for width in CLASSES[:-1])
    widths = sum(
        jnp.where(kind == i, width, 0) for i, width in enumerate(CLASSES)
    )
    begin = jnp.minimum(begin, length - widths)
    chunks = (begin + widths + QB - 1) // QB
    return ids, jnp.stack([begin, kind, chunks]).astype(jnp.int32)


def local(tokens, cotangent, segment_ids, pad_mask, lengths, params):
    rows, width = tokens.shape
    wide, narrow = lax.axis_size("wide"), lax.axis_size("narrow")
    devices = wide * narrow
    att_count = 4 * width * width + 6 * width
    att_rows = (att_count // LANES + devices - 1) // devices
    mlp_rows = params.shape[0] - att_rows
    paired = (wide, narrow) == (4, 8)
    scale = 1.0 / math.sqrt(rows * devices)

    def attention_windows(segments, pads, lengths):
        real = (pads > 0) & (jnp.arange(rows, dtype=jnp.int32) < lengths[0])
        ids, windows = key_windows(segments, real)
        return windows, ids.astype(F32).reshape(rows // QB, QB)

    if not paired:
        windows, query_ids = attention_windows(segment_ids, pad_mask, lengths)
        me = jnp.zeros((1,), jnp.int32)
        att, mlp = gather_plainly(params, att_rows, width)
        n1, qkv, small = project_qkv(me, tokens, att)
        mixed, x1, branch, n2, dm, stats, gb2 = attend(
            me, windows, qkv, tokens, cotangent, query_ids, small, att
        )
        u, dz, gb1, *gmlp = feed_forward(me, n2, dm, small, mlp)
        output, gs2 = feed_forward_out(me, u, x1, cotangent, small, mlp)
        dx1, da, gwo0, gwo1, others = split(
            me, dz, x1, cotangent, branch, mixed, small, mlp, att
        )
        small_mlp = jnp.concatenate([others[:12], gb1, gb2, gs2])
        small_proj = others[12:]
        dqkv0 = attend_back(0, windows, qkv, da, stats, query_ids)
        dqkv1 = attend_back(1, windows, qkv, da, stats, query_ids)
        gatt0 = weight_grad(me, n1, dqkv0, gwo0)
        grad_input, *gatt1 = qkv_back(
            me, tokens, n1, dx1, dqkv0, dqkv1, small, small_proj, small_mlp, gwo1, att
        )
        owned = reduce_plainly(gatt0, gatt1, gmlp, att_rows, mlp_rows, width, devices)
        return output, grad_input, owned * scale

    me = lax.axis_index(AXES).astype(jnp.int32).reshape(1)
    tails = jnp.concatenate([params[att_rows - ATT_BEFORE : att_rows], params[-MLP_BEFORE:]])
    heads = jnp.concatenate([params[:ATT_AFTER], params[att_rows : att_rows + MLP_AFTER]])
    before, beyond = overhangs(att_rows, mlp_rows)
    heads = lax.ppermute(heads.astype(BF16), AXES, [(d + 1, d) for d in beyond])
    tails = lax.ppermute(tails.astype(BF16), AXES, [(d - 1, d) for d in before])
    att_own, mlp_own = pack(me, params, tails, heads, att_rows)

    got = [exchange(att_own, k * Z0) for k in range(1, 4)]
    a, b = along_z(att_own[0], att_own[1], got)
    a, b, mlp_own, *tables = together(a, b, mlp_own, segment_ids, pad_mask, lengths)
    windows, query_ids = attention_windows(*tables)
    ax, by = exchange(a, X), exchange(b, Y)
    z1, z3 = exchange(mlp_own, Z0), exchange(mlp_own, 3 * Z0)
    a, b = joined(a, ax), joined(b, by)
    a, b, z1, z3, mlp_own, windows, query_ids = together(
        a, b, z1, z3, mlp_own, windows, query_ids
    )
    ay, bx = exchange(a, Y), exchange(b, X)
    ac, bc = exchange(a, C), exchange(b, C)
    z2 = exchange(mlp_own, 2 * Z0)
    m, n = along_z(mlp_own[0], mlp_own[1], [z1, z2, z3])
    ay, bx, ac, bc, m, n = together(ay, bx, ac, bc, m, n)
    ayc, bxc = exchange(ay, C), exchange(bx, C)
    att = together(a, ay, ac, ayc, b, bx, bc, bxc, m, n, tokens)
    *att, m, n, tokens_now = att
    mx, ny = exchange(m, X), exchange(n, Y)
    n1, qkv, small = project_qkv(me, tokens_now, att)
    m, n = joined(m, mx), joined(n, ny)
    m, n, qkv = together(m, n, qkv)
    my, nx = exchange(m, Y), exchange(n, X)
    mc, nc = exchange(m, C), exchange(n, C)
    mixed, x1, branch, n2, dm, stats, gb2 = attend(
        me, windows, qkv, tokens, cotangent, query_ids, small, att
    )
    m, n, my, nx, mc, nc, n2 = together(m, n, my, nx, mc, nc, n2)
    myc, nxc = exchange(my, C), exchange(nx, C)
    mlp = (m, my, mc, myc, n, nx, nc, nxc)

    u, dz, gb1, *gmlp = feed_forward(me, n2, dm, small, mlp)

    mc, nc = exchange(gmlp[1], C), exchange(gmlp[3], C)
    output, gs2 = feed_forward_out(me, u, x1, cotangent, small, mlp)
    mc, nc, dz, gs2 = together(mc, nc, dz, gs2)
    m, n = [gmlp[0], mc], [gmlp[2], nc]
    my, nx, dz = together(sent(m), sent(n), dz)
    my, nx = exchange(my, Y), exchange(nx, X)
    dx1, da, gwo0, gwo1, others = split(
        me, dz, x1, cotangent, branch, mixed, small, mlp, att
    )
    dqkv0 = attend_back(0, windows, qkv, da, stats, query_ids)
    gatt0 = weight_grad(me, n1, dqkv0, gwo0)
    my, nx, da, *gatt0 = together(my, nx, da, *gatt0)
    m, n = kept(m) + [my], kept(n) + [nx]
    mx, ny, da, *gatt0 = together(sent(m), sent(n), da, *gatt0)
    mx, ny = exchange(mx, X), exchange(ny, Y)
    ac, bc = exchange(gatt0[1], C), exchange(gatt0[3], C)
    dqkv1 = attend_back(1, windows, qkv, da, stats, query_ids)
    mx, ny, ac, bc, dqkv1 = together(mx, ny, ac, bc, dqkv1)
    m, n = kept(m) + [mx], kept(n) + [ny]
    z1, z2, z3 = [z_part(m, n, k).astype(BF16) for k in range(1, 4)]
    a, b = [gatt0[0], ac], [gatt0[2], bc]
    ay, bx, z1, z2, z3, dqkv1 = together(sent(a), sent(b), z1, z2, z3, dqkv1)
    z1, z2 = exchange(z1, Z0), exchange(z2, 2 * Z0)
    ay, bx = exchange(ay, Y), exchange(bx, X)
    small_mlp = jnp.concatenate([others[:12], gb1, gb2, gs2])
    grad_input, *gatt1 = qkv_back(
        me, tokens, n1, dx1, dqkv0, dqkv1, small, others[12:], small_mlp, gwo1, att
    )
    ay, bx, z1, z2, *gatt1 = together(ay, bx, z1, z2, *gatt1)
    a, b = kept(a) + [ay], kept(b) + [bx]
    ax, by, c1, d1, z3 = together(sent(a), sent(b), gatt1[1], gatt1[3], z3)
    c1, d1 = exchange(c1, C), exchange(d1, C)
    ax, by = exchange(ax, X), exchange(by, Y)
    z3a = exchange(z3[0], 3 * Z0)
    c, d = [gatt1[0], c1], [gatt1[2], d1]
    a, b = kept(a) + [ax], kept(b) + [by]
    sends = [z_part(a, b, k).astype(BF16) for k in range(1, 4)]
    cy, dx, z3a, z3, *sends = together(sent(c), sent(d), z3a, z3, *sends)
    cy, dx = exchange(cy, Y), exchange(dx, X)
    got = [exchange(part, (k + 1) * Z0) for k, part in enumerate(sends)]
    c, d = kept(c) + [cy], kept(d) + [dx]
    cx, dy, z3, *got = together(sent(c), sent(d), z3, *got)
    z3b = exchange(z3[1], 3 * Z0)
    group0 = sum_terms([z_part(a, b, 0)] + got)
    cx, dy = exchange(cx, X), exchange(dy, Y)
    c, d = kept(c) + [cx], kept(d) + [dy]
    m_own = sum_terms([z_part(m, n, 0), z1, z2, jnp.stack([z3a, z3b])])
    sends = [z_part(c, d, k).astype(BF16) for k in range(1, 4)]
    group0, m_own, *sends = together(group0, m_own, *sends)
    got = [exchange(part, (k + 1) * Z0) for k, part in enumerate(sends)]
    group1 = sum_terms([z_part(c, d, 0)] + got)
    mine, to_before, to_after = spread(me, group0, group1, m_own, att_rows, mlp_rows, scale)
    below = lax.ppermute(to_after, AXES, [(d, d + 1) for d in beyond])
    above = lax.ppermute(to_before, AXES, [(d, d - 1) for d in before])
    grad_params = close(mine, below, above, att_rows)
    return output, grad_input, grad_params


def solution(mesh):
    return jax.shard_map(
        local,
        mesh=mesh,
        in_specs=(
            P(AXES, None),
            P(AXES, None),
            P(AXES),
            P(AXES),
            P(AXES),
            P(AXES, None),
        ),
        out_specs=(P(AXES, None), P(AXES, None), P(AXES, None)),
        check_vma=False,
    )
```
